32 devices in a mesh: fsdp: 4 (over y, x), ctx: 4 (over z), tp: 2 (over core).
Axes of the slice: x: 2, y: 2, z: 4, core: 2. Of those that a mesh axis runs over, the one named last changes fastest.
Arguments:
- image_input: bfloat16 [4, 2048, 768], P('fsdp', 'ctx'), may hold values from -6 to 6
- image_segments: int32 [4, 2048], P('fsdp'), may hold values from 0 to 5, never falling along the last dimension, each value on 1 to 1536 neighbouring positions
- image_cotangent: bfloat16 [4, 2048, 768], P('fsdp', 'ctx'), may hold values from -6 to 6
- image_gains: bfloat16 [2, 768], P(None, 'fsdp'), may hold values from 0.099609375 to 1.8984375
- image_shifts: bfloat16 [4, 768], P(None, 'fsdp'), may hold values from -3 to 3
- image_head_bias: bfloat16 [2, 2304], P('tp', 'fsdp'), may hold values from -3 to 3
- image_qkv_weight: bfloat16 [3, 768, 768], P(None, 'fsdp', 'tp'), may hold values from -0.21875 to 0.21875
- image_proj_weight: bfloat16 [768, 768], P('tp', 'fsdp'), may hold values from -0.875 to 0.875
- image_up_weight: bfloat16 [768, 3072], P('fsdp', 'tp'), may hold values from -0.21875 to 0.21875
- image_down_weight: bfloat16 [3072, 768], P('tp', 'fsdp'), may hold values from -0.109375 to 0.109375
- text_input: bfloat16 [4, 2048, 512], P('fsdp', 'ctx'), may hold values from -6 to 6
- text_segments: int32 [4, 2048], P('fsdp'), may hold values from 0 to 5, never falling along the last dimension, each value on 1 to 1536 neighbouring positions
- text_cotangent: bfloat16 [4, 2048, 512], P('fsdp', 'ctx'), may hold values from -6 to 6
- text_gains: bfloat16 [2, 512], P(None, 'fsdp'), may hold values from 0.099609375 to 1.8984375
- text_shifts: bfloat16 [4, 512], P(None, 'fsdp'), may hold values from -3 to 3
- text_head_bias: bfloat16 [2, 1536], P('tp', 'fsdp'), may hold values from -3 to 3
- text_qkv_weight: bfloat16 [3, 512, 512], P(None, 'fsdp', 'tp'), may hold values from -0.25 to 0.25
- text_proj_weight: bfloat16 [512, 512], P('tp', 'fsdp'), may hold values from -1 to 1
- text_up_weight: bfloat16 [512, 2048], P('fsdp', 'tp'), may hold values from -0.25 to 0.25
- text_down_weight: bfloat16 [2048, 512], P('tp', 'fsdp'), may hold values from -0.125 to 0.125
Outputs:
- image_output: bfloat16 [4, 2048, 768], P('fsdp', 'ctx')
- image_input_grad: float32 [4, 2048, 768], P('fsdp', 'ctx')
- image_gains_grad: float32 [2, 768], P(None, 'fsdp')
- image_shifts_grad: float32 [4, 768], P(None, 'fsdp')
- image_head_bias_grad: float32 [2, 2304], P('tp', 'fsdp')
- image_qkv_grad: float32 [3, 768, 768], P(None, 'fsdp', 'tp')
- image_proj_grad: float32 [768, 768], P('tp', 'fsdp')
- image_up_grad: float32 [768, 3072], P('fsdp', 'tp')
- image_down_grad: float32 [3072, 768], P('tp', 'fsdp')
- text_output: bfloat16 [4, 2048, 512], P('fsdp', 'ctx')
- text_input_grad: float32 [4, 2048, 512], P('fsdp', 'ctx')
- text_gains_grad: float32 [2, 512], P(None, 'fsdp')
- text_shifts_grad: float32 [4, 512], P(None, 'fsdp')
- text_head_bias_grad: float32 [2, 1536], P('tp', 'fsdp')
- text_qkv_grad: float32 [3, 512, 512], P(None, 'fsdp', 'tp')
- text_proj_grad: float32 [512, 512], P('tp', 'fsdp')
- text_up_grad: float32 [512, 2048], P('fsdp', 'tp')
- text_down_grad: float32 [2048, 512], P('tp', 'fsdp')
The draws below stay inside these ranges and needn't reach their ends.
Inputs may be any that keep to these rules, and one draw needn't show every extreme that they name: `image_segments`: along each sequence segment numbers never fall; every document has 1 to 1536 tokens, and one has exactly that many. `text_segments`: along each sequence segment numbers never fall; every document has 1 to 1536 tokens, and one has exactly that many.
All inputs are finite; a program needn't handle non-finite values.
Results may differ from the reference program's by a relative error of at most 0.012.
Values may be sent and summed in bfloat16 or wider, within the bound.
A program may use at most 128 MiB of HBM per device.

```python
import math
import jax
import jax.numpy as jnp
import numpy as np
from jax import lax

D = 768
FF = 3072
TD = 512
TFF = 2048
HD = 64
SEQ_LEN = 2048
SEQS = 4
IBIAS = 2304
TBIAS = 1536
N_TP = 2


def shard_levels(own_key, dims, shards, low, largest):
    def one(position, blocks):
        steps = jax.random.uniform(jax.random.fold_in(jax.random.fold_in(own_key, 6), position), (blocks,), jnp.float32, low / len(shards), largest / len(shards))
        return jnp.repeat(jnp.exp(steps), dims[position] // blocks).reshape((-1,) + (1,) * (len(dims) - position - 1))

    level = one(*shards[0])
    for cut in shards[1:]:
        level = level * one(*cut)
    return level


def length_profile(amount, total, bound, skew):
    loads = [(1 << 20) // math.isqrt(standing ** skew) + 1 for standing in range(2, amount + 1)]
    surplus, holding = total - bound - (amount - 1), [1] * (amount - 1)
    while surplus > 0:
        candidates = [i for i in range(amount - 1) if holding[i] < bound]
        pool, budget = sum([loads[i] for i in candidates]), surplus
        for i in candidates:
            extra = min(bound - holding[i], max(1, budget * loads[i] // pool), surplus)
            holding[i] = holding[i] + extra
            surplus = surplus - extra
    return np.array([bound] + holding)


def ragged(stream_key, count, total, bound, skew):
    if count == 2:
        one = jax.random.randint(stream_key, (), max(1, total - bound), min(bound, total - 1) + 1)
        return jnp.stack([one, total - one])
    lengths = jnp.asarray(length_profile(count, total, bound, skew), jnp.int32)
    couples = (count - 1) // 2
    donor, sink = lengths[1:1 + 2 * couples:2], lengths[2:2 + 2 * couples:2]
    room = jnp.minimum(donor - 1, bound - sink)
    passed = jax.random.randint(jax.random.fold_in(stream_key, 1), (couples,), 0, 1 << 20) % (room + 1)
    lengths = lengths.at[1:1 + 2 * couples:2].set(donor - passed).at[2:2 + 2 * couples:2].set(sink + passed)
    return lengths[jax.random.permutation(jax.random.fold_in(stream_key, 2), count)]


def scatter_about(stream_key, shape, scale, limit, split=(), kind=jnp.bfloat16):
    level = shard_levels(stream_key, shape, split, -0.22, 0.18) if split else 1.0
    array = jax.random.normal(stream_key, shape, jnp.float32) * scale * level
    return jnp.minimum(jnp.maximum(array, -limit), limit).astype(kind)


def setup_inputs(seed: int = 0) -> dict:
    seeds = jax.random.split(jax.random.key(seed), 21)
    return {
        "image_input": scatter_about(seeds[0], (SEQS, SEQ_LEN, D), 1.0, 6.0, ((0, 4), (1, 4))),
        "image_segments": jax.vmap(lambda own: jnp.searchsorted(jnp.cumsum(ragged(own, 6, SEQ_LEN, 3 * SEQ_LEN // 4, 1)), jnp.arange(SEQ_LEN), side="right"))(jax.random.split(seeds[1], SEQS)).reshape((SEQS, SEQ_LEN)).astype(jnp.int32),
        "image_cotangent": scatter_about(seeds[2], (SEQS, SEQ_LEN, D), 1.0, 6.0, ((0, 4), (1, 4))),
        "image_gains": jnp.clip(1.0 + 0.18 * jax.random.normal(seeds[3], (2, D), jnp.float32), 0.099609375, 1.8984375).astype(jnp.bfloat16),
        "image_shifts": scatter_about(seeds[4], (4, D), 0.5, 3.0, ((1, 4),)),
        "image_head_bias": scatter_about(seeds[5], (N_TP, IBIAS), 0.5, 3.0, ((0, 2), (1, 4))),
        "image_qkv_weight": scatter_about(seeds[6], (3, D, D), D ** -0.5, 0.21875, ((1, 4), (2, 2))),
        "image_proj_weight": scatter_about(seeds[7], (D, D), (D // 16) ** -0.5, 0.875, ((0, 2), (1, 4))),
        "image_up_weight": scatter_about(seeds[8], (D, FF), D ** -0.5, 0.21875, ((0, 4), (1, 2))),
        "image_down_weight": scatter_about(seeds[9], (FF, D), FF ** -0.5, 0.109375, ((0, 2), (1, 4))),
        "text_input": scatter_about(seeds[10], (SEQS, SEQ_LEN, TD), 1.0, 6.0, ((0, 4), (1, 4))),
        "text_segments": jax.vmap(lambda own: jnp.searchsorted(jnp.cumsum(ragged(own, 6, SEQ_LEN, 3 * SEQ_LEN // 4, 1)), jnp.arange(SEQ_LEN), side="right"))(jax.random.split(seeds[11], SEQS)).reshape((SEQS, SEQ_LEN)).astype(jnp.int32),
        "text_cotangent": scatter_about(seeds[12], (SEQS, SEQ_LEN, TD), 1.0, 6.0, ((0, 4), (1, 4))),
        "text_gains": jnp.clip(1.0 + 0.18 * jax.random.normal(seeds[13], (2, TD), jnp.float32), 0.099609375, 1.8984375).astype(jnp.bfloat16),
        "text_shifts": scatter_about(seeds[14], (4, TD), 0.5, 3.0, ((1, 4),)),
        "text_head_bias": scatter_about(seeds[15], (N_TP, TBIAS), 0.5, 3.0, ((0, 2), (1, 4))),
        "text_qkv_weight": scatter_about(seeds[16], (3, TD, TD), TD ** -0.5, 0.25, ((1, 4), (2, 2))),
        "text_proj_weight": scatter_about(seeds[17], (TD, TD), (TD // 16) ** -0.5, 1.0, ((0, 2), (1, 4))),
        "text_up_weight": scatter_about(seeds[18], (TD, TFF), TD ** -0.5, 0.25, ((0, 4), (1, 2))),
        "text_down_weight": scatter_about(seeds[19], (TFF, TD), TFF ** -0.5, 0.125, ((0, 2), (1, 4))),
    }


@jax.custom_vjp
def low(v):
    return lax.optimization_barrier(v.astype(jnp.bfloat16)).astype(jnp.float32)

@jax.custom_vjp
def low_back(v):
    return v

def low_keep(v):
    return (low(v), None)

def low_pass(kept, grad):
    return (grad,)

def back_keep(v):
    return (v, None)

def back_low(kept, grad):
    return (low(grad),)
low.defvjp(low_keep, low_pass)
low_back.defvjp(back_keep, back_low)

def matmul_high(left, right):
    return jnp.dot(left, right, precision=lax.Precision.HIGHEST, preferred_element_type=jnp.float32)

def both_round(value):
    return low(low_back(value))

def normalize(rows, gain, shift):
    row_mean = lax.optimization_barrier(jnp.mean(rows, axis=-1, keepdims=True))
    centred = rows - row_mean
    inv_std = lax.rsqrt(lax.optimization_barrier(jnp.mean(centred * centred, axis=-1, keepdims=True)) + 1e-05)
    return centred * inv_std * gain + shift

def block_forward(rows, seg_row, params, causal):
    gains, shifts, head_bias, qkv_weight, proj_weight, up_weight, down_weight = params
    length = rows.shape[0]
    width = rows.shape[1]
    head_count = width // HD
    tp_width = width // N_TP
    bias_query = head_bias[:, :tp_width].reshape(-1)
    bias_value = head_bias[:, tp_width:2 * tp_width].reshape(-1)
    bias_up = head_bias[:, 2 * tp_width:].reshape(-1)
    normed = low(normalize(rows, gains[0], shifts[0]))
    queries = both_round(matmul_high(normed, qkv_weight[0]) + bias_query)
    key_rows = both_round(matmul_high(normed, qkv_weight[1]))
    values = both_round(matmul_high(normed, qkv_weight[2]) + bias_value)
    positions = jnp.arange(length, dtype=jnp.int32)
    allowed = seg_row[:, None] == seg_row[None, :]
    if causal:
        allowed = jnp.logical_and(allowed, positions[None, :] <= positions[:, None])

    def one_head(head_items):
        query_h, key_h, value_h = head_items
        scores = matmul_high(query_h, key_h.T) * 0.125
        scores = low_back(jnp.where(allowed, scores, -1e+30))
        weights_low = low(jax.nn.softmax(scores, axis=-1))
        return matmul_high(weights_low, value_h)

    def split_heads(matrix):
        return matrix.reshape(length, head_count, HD).transpose(1, 0, 2)
    mixed = lax.map(jax.checkpoint(one_head), (split_heads(queries), split_heads(key_rows), split_heads(values)))
    mixed = both_round(mixed.transpose(1, 0, 2).reshape(length, width))
    middle = rows + low_back(matmul_high(mixed, proj_weight)) + shifts[1]
    normed_two = low(normalize(middle, gains[1], shifts[2]))
    hidden = low_back(matmul_high(normed_two, up_weight) + bias_up)
    activated = low(hidden * jax.nn.sigmoid(1.702 * hidden))
    return middle + low_back(matmul_high(activated, down_weight)) + shifts[3]

def run_stream(inputs, segments, cotangent, params, causal):
    params_wide = tuple((item.astype(jnp.float32) for item in params))
    zero_grads = tuple((jnp.zeros_like(item) for item in params_wide))

    def per_sequence(carry, seq_items):
        rows, seg_row, cot_row = seq_items

        def forward(rows_in, params_in):
            return block_forward(rows_in, seg_row, params_in, causal)
        output, pullback = jax.vjp(forward, rows.astype(jnp.float32), params_wide)
        grad_rows, grad_params = pullback(cot_row.astype(jnp.float32))
        carry = tuple((total + part for total, part in zip(carry, grad_params)))
        return (carry, (output.astype(jnp.bfloat16), grad_rows))
    totals, stacked = lax.scan(per_sequence, zero_grads, (inputs, segments, cotangent))
    return (stacked[0], stacked[1], totals)

def reference(image_input, image_segments, image_cotangent, image_gains, image_shifts, image_head_bias, image_qkv_weight, image_proj_weight, image_up_weight, image_down_weight, text_input, text_segments, text_cotangent, text_gains, text_shifts, text_head_bias, text_qkv_weight, text_proj_weight, text_up_weight, text_down_weight):
    image_params = (image_gains, image_shifts, image_head_bias, image_qkv_weight, image_proj_weight, image_up_weight, image_down_weight)
    text_params = (text_gains, text_shifts, text_head_bias, text_qkv_weight, text_proj_weight, text_up_weight, text_down_weight)
    image_out, image_grad, image_totals = run_stream(image_input, image_segments, image_cotangent, image_params, False)
    text_out, text_grad, text_totals = run_stream(text_input, text_segments, text_cotangent, text_params, True)
    return (image_out, image_grad, image_totals[0], image_totals[1], image_totals[2], image_totals[3], image_totals[4], image_totals[5], image_totals[6], text_out, text_grad, text_totals[0], text_totals[1], text_totals[2], text_totals[3], text_totals[4], text_totals[5], text_totals[6])
```

```python
import functools

import jax
import jax.numpy as jnp
from jax import lax
from jax.experimental import pallas as pl
from jax.experimental.pallas import tpu as pltpu
from jax.sharding import PartitionSpec as P

HD = 64
LANES = 128
QB = 256
KB = 512
NEG = -1e30
F32 = jnp.float32
BF16 = jnp.bfloat16
ACROSS_X = [(i, i ^ 1) for i in range(4)]
ACROSS_Y = [(i, i ^ 2) for i in range(4)]


def dot(left, right, dims=((1,), (0,))):
    return lax.dot_general(left, right, (dims, ((), ())), preferred_element_type=F32)


def gather_rows(piece):
    group = lax.axis_index("fsdp")
    rows = piece.shape[0]
    half = rows // 2
    from_x = lax.ppermute(piece, "fsdp", ACROSS_X)
    from_y = lax.ppermute(piece, "fsdp", ACROSS_Y)
    far_top = lax.ppermute(from_y[:half], "fsdp", ACROSS_X)
    far_low = lax.ppermute(from_x[half:], "fsdp", ACROSS_Y)
    whole = jnp.zeros((4 * rows,) + piece.shape[1:], piece.dtype)

    def put(whole, part, owner, offset=0):
        return lax.dynamic_update_slice_in_dim(whole, part, owner * rows + offset, 0)

    whole = put(whole, piece, group)
    whole = put(whole, from_x, group ^ 1)
    whole = put(whole, from_y, group ^ 2)
    whole = put(whole, far_top, group ^ 3)
    return put(whole, far_low, group ^ 3, half)


def swap_blocks(blocks):
    here = lax.axis_index("ctx")

    def pick(index):
        return lax.dynamic_index_in_dim(blocks, index, 0, keepdims=True)

    out = jnp.zeros_like(blocks)
    out = lax.dynamic_update_slice_in_dim(out, pick(here), here, 0)
    for step in (1, 2, 3):
        pairs = [(i, i ^ step) for i in range(4)]
        out = lax.dynamic_update_slice_in_dim(
            out, lax.ppermute(pick(here ^ step), "ctx", pairs), here ^ step, 0
        )
    return out


def other_core(rows):
    return lax.ppermute(rows, "tp", [(0, 1), (1, 0)])


def tensor_sum(rows):
    return rows + other_core(rows)


def reduce_owned(partial):
    group = lax.axis_index("fsdp")
    here = lax.axis_index("ctx")
    rows = partial.shape[0] // 4
    half = rows // 2
    low = partial.astype(BF16)

    def take(array, owner, offset):
        return lax.dynamic_slice_in_dim(array, owner * rows + offset, half, 0)

    def pair(owner_one, owner_two, offset):
        return jnp.concatenate([take(low, owner_one, offset), take(low, owner_two, offset)])

    top = lax.ppermute(pair(group ^ 1, group ^ 3, 0), "fsdp", ACROSS_X).astype(F32)
    bottom = lax.ppermute(pair(group ^ 2, group ^ 3, half), "fsdp", ACROSS_Y).astype(F32)
    top_pass = (take(partial, group ^ 2, 0).astype(F32) + top[half:]).astype(BF16)
    low_pass = (take(partial, group ^ 1, half).astype(F32) + bottom[half:]).astype(BF16)
    top_back = lax.ppermute(top_pass, "fsdp", ACROSS_Y).astype(F32)
    low_back = lax.ppermute(low_pass, "fsdp", ACROSS_X).astype(F32)
    top_sum = take(partial, group, 0).astype(F32) + top[:half] + top_back
    low_sum = take(partial, group, half).astype(F32) + bottom[:half] + low_back
    owned = jnp.concatenate([top_sum, low_sum])
    quarter = rows // 4
    owned_low = owned.astype(BF16)

    def cut(array, index):
        return lax.dynamic_slice_in_dim(array, index * quarter, quarter, 0)

    total = cut(owned, here)
    for step in (1, 2, 3):
        pairs = [(i, i ^ step) for i in range(4)]
        total = total + lax.ppermute(cut(owned_low, here ^ step), "ctx", pairs).astype(F32)
    total = total.astype(BF16)
    out = jnp.zeros((4, quarter, partial.shape[1]), BF16)
    out = lax.dynamic_update_slice_in_dim(out, total[None], here, 0)
    for step in (1, 2, 3):
        pairs = [(i, i ^ step) for i in range(4)]
        out = lax.dynamic_update_slice_in_dim(
            out, lax.ppermute(total, "ctx", pairs)[None], here ^ step, 0
        )
    return out.reshape(rows, partial.shape[1]).astype(F32)


def reduce_small(vector):
    for axis, pairs in (
        ("fsdp", ACROSS_X),
        ("fsdp", ACROSS_Y),
        ("ctx", [(i, i ^ 1) for i in range(4)]),
        ("ctx", [(i, i ^ 2) for i in range(4)]),
    ):
        vector = vector + lax.ppermute(vector, axis, pairs)
    return vector


def lane_marks():
    lane = lax.broadcasted_iota(jnp.int32, (1, LANES), 1)
    first = (lane < HD).astype(F32).astype(BF16)
    second = (lane >= HD).astype(F32).astype(BF16)
    return first, second


def attend_kernel(
    causal, bounds, q_ref, kv_ref, extra_ref, segcol_ref, segrow_ref, o_ref, lse_ref
):
    block = pl.program_id(0)
    low, high, active = bounds[0, block], bounds[1, block], bounds[2, block]
    first, second = lane_marks()
    lane = lax.broadcasted_iota(jnp.int32, (QB, LANES), 1)
    query = q_ref[...]
    seg_query = segcol_ref[...]

    def one(query, keys_ref, own, other):
        def step(index, carry):
            top, acc = carry
            start = pl.multiple_of(index * KB, KB)
            keys = keys_ref[pl.ds(start, KB), :]
            scores = dot(query * own, keys, ((1,), (1,)))
            ok = seg_query == segrow_ref[:, pl.ds(start, KB)]
            if causal:
                key_pos = start + lax.broadcasted_iota(jnp.int32, (QB, KB), 1)
                query_pos = block * QB + lax.broadcasted_iota(jnp.int32, (QB, KB), 0)
                ok = jnp.logical_and(ok, key_pos <= query_pos)
            scores = jnp.where(ok, scores, NEG)
            new_top = jnp.maximum(top, jnp.max(scores, axis=1, keepdims=True))
            weights = jnp.exp(scores - new_top).astype(BF16)
            acc = acc * jnp.exp(top - new_top) + dot(weights, keys * other + own)
            return new_top, acc

        top, acc = lax.fori_loop(
            low, high, step, (jnp.full((QB, 1), NEG, F32), jnp.zeros((QB, LANES), F32))
        )
        return acc / pltpu.roll(acc, HD, 1), top + jnp.log(acc)

    mixed, lse = one(query, kv_ref, first, second)
    if extra_ref is None:
        o_ref[...] = mixed.astype(BF16)
        lse_ref[0] = jnp.transpose(lse)[:16]
    else:

        @pl.when(active == 0)
        def _():
            o_ref[...] = mixed.astype(BF16)
            lse_ref[0, :8] = jnp.transpose(lse)[:8]
            lse_ref[0, 8:] = jnp.zeros((8, QB), F32)

        @pl.when(active != 0)
        def _():
            mixed_two, lse_two = one(query, extra_ref, second, first)
            o_ref[...] = jnp.where(lane < HD, mixed_two, mixed).astype(BF16)
            lse_ref[0, :8] = jnp.transpose(lse)[:8]
            lse_ref[0, 8:] = jnp.transpose(lse_two)[HD : HD + 8]


def attend(causal, bounds, q, kv, extra, segcol, segrow):
    rows = q.shape[0]
    body = functools.partial(attend_kernel, causal)
    if extra is None:

        def kernel(bounds, q_ref, kv_ref, *rest):
            body(bounds, q_ref, kv_ref, None, *rest)

        wide = [kv]
    else:
        kernel = body
        wide = [kv, extra]
    whole = pl.BlockSpec((rows, LANES), lambda i, b: (0, 0))
    block = pl.BlockSpec((QB, LANES), lambda i, b: (i, 0))
    blocks = rows // QB
    heads = len(wide)
    return pl.pallas_call(
        kernel,
        grid_spec=pltpu.PrefetchScalarGridSpec(
            num_scalar_prefetch=1,
            grid=(blocks,),
            in_specs=[block]
            + [whole] * heads
            + [
                pl.BlockSpec((QB, 1), lambda i, b: (i, 0)),
                pl.BlockSpec((1, rows), lambda i, b: (0, 0)),
            ],
            out_specs=[block, pl.BlockSpec((1, 16, QB), lambda i, b: (i, 0, 0))],
        ),
        out_shape=[
            jax.ShapeDtypeStruct((rows, LANES), BF16),
            jax.ShapeDtypeStruct((blocks, 16, QB), F32),
        ],
        cost_estimate=pl.CostEstimate(
            flops=heads * 4 * rows * rows * LANES, bytes_accessed=6 * rows * LANES, transcendentals=heads * rows * rows
        ),
        name="attend_causal" if causal else "attend_full",
    )(bounds, q, *wide, segcol, segrow)


def attend_back_kernel(
    causal,
    bounds,
    q_ref,
    do_ref,
    o_ref,
    lse_ref,
    kv_ref,
    extra_ref,
    segcol_ref,
    segrow_ref,
    dq_ref,
    dkv_ref,
    dextra_ref,
    acc_ref,
    acc_extra_ref,
):
    block = pl.program_id(0)
    low, high, active = bounds[0, block], bounds[1, block], bounds[2, block]
    first, second = lane_marks()
    lane = lax.broadcasted_iota(jnp.int32, (QB, LANES), 1)

    @pl.when(block == 0)
    def _():
        acc_ref[...] = jnp.zeros_like(acc_ref)
        if acc_extra_ref is not None:
            acc_extra_ref[...] = jnp.zeros_like(acc_extra_ref)

    query = q_ref[...]
    grad_o = do_ref[...]
    product = jnp.transpose(grad_o.astype(F32) * o_ref[...].astype(F32))
    seg_query = segrow_ref[:, pl.ds(pl.multiple_of(block * QB, QB), QB)]

    def one(keys_ref, total_ref, own, other, lse, delta):
        query_own = query * own
        grad_own = grad_o * other

        def step(index, grad_query):
            start = pl.multiple_of(index * KB, KB)
            keys = keys_ref[pl.ds(start, KB), :]
            scores = dot(keys, query_own, ((1,), (1,)))
            ok = segcol_ref[pl.ds(start, KB), :] == seg_query
            if causal:
                key_pos = start + lax.broadcasted_iota(jnp.int32, (KB, QB), 0)
                query_pos = block * QB + lax.broadcasted_iota(jnp.int32, (KB, QB), 1)
                ok = jnp.logical_and(ok, key_pos <= query_pos)
            weights = jnp.where(ok, jnp.exp(scores - lse), 0.0)
            grad_weights = dot(keys, grad_own, ((1,), (1,)))
            grad_scores = (weights * (grad_weights - delta)).astype(BF16)
            total_ref[pl.ds(start, KB), :] += dot(grad_scores, query_own) + dot(
                weights.astype(BF16), grad_own
            )
            return grad_query + dot(grad_scores, keys, ((0,), (0,)))

        return lax.fori_loop(low, high, step, jnp.zeros((QB, LANES), F32))

    grad_query = one(
        kv_ref,
        acc_ref,
        first,
        second,
        lse_ref[0, :1],
        jnp.sum(product[HD:], axis=0, keepdims=True),
    )
    if extra_ref is None:
        dq_ref[...] = (grad_query * 0.125).astype(BF16)
    else:

        @pl.when(active == 0)
        def _():
            dq_ref[...] = (grad_query * 0.125).astype(BF16)

        @pl.when(active != 0)
        def _():
            grad_two = one(
                extra_ref,
                acc_extra_ref,
                second,
                first,
                lse_ref[0, 8:9],
                jnp.sum(product[:HD], axis=0, keepdims=True),
            )
            dq_ref[...] = (jnp.where(lane < HD, grad_query, grad_two) * 0.125).astype(BF16)

    @pl.when(block == pl.num_programs(0) - 1)
    def _():
        dkv_ref[...] = acc_ref[...].astype(BF16)
        if dextra_ref is not None:
            dextra_ref[...] = acc_extra_ref[...].astype(BF16)


def attend_back(causal, bounds, q, do, o, lse, kv, extra, segcol, segrow):
    rows = q.shape[0]
    body = functools.partial(attend_back_kernel, causal)
    if extra is None:

        def kernel(bounds, q, do, o, lse, kv, sc, sr, dq, dkv, acc):
            body(bounds, q, do, o, lse, kv, None, sc, sr, dq, dkv, None, acc, None)

        wide = [kv]
    else:
        kernel = body
        wide = [kv, extra]
    whole = pl.BlockSpec((rows, LANES), lambda i, b: (0, 0))
    block = pl.BlockSpec((QB, LANES), lambda i, b: (i, 0))
    blocks = rows // QB
    heads = len(wide)
    return pl.pallas_call(
        kernel,
        grid_spec=pltpu.PrefetchScalarGridSpec(
            num_scalar_prefetch=1,
            grid=(blocks,),
            in_specs=[block] * 3
            + [pl.BlockSpec((1, 16, QB), lambda i, b: (i, 0, 0))]
            + [whole] * heads
            + [
                pl.BlockSpec((rows, 1), lambda i, b: (0, 0)),
                pl.BlockSpec((1, rows), lambda i, b: (0, 0)),
            ],
            out_specs=[block] + [whole] * heads,
            scratch_shapes=[pltpu.VMEM((rows, LANES), F32)] * heads,
        ),
        out_shape=[jax.ShapeDtypeStruct((rows, LANES), BF16)] * (1 + heads),
        cost_estimate=pl.CostEstimate(
            flops=heads * 10 * rows * rows * LANES, bytes_accessed=12 * rows * LANES, transcendentals=heads * rows * rows
        ),
        name="attend_back_causal" if causal else "attend_back_full",
    )(bounds, q, do, o, lse, *wide, segcol, segrow)


def block_bounds(seg, causal):
    blocks = seg.reshape(-1, QB)
    begin = jnp.sum(seg[None, :] < blocks[:, :1], axis=1, dtype=jnp.int32)
    end = jnp.sum(seg[None, :] <= blocks[:, -1:], axis=1, dtype=jnp.int32)
    if causal:
        end = jnp.minimum(end, (jnp.arange(blocks.shape[0], dtype=jnp.int32) + 1) * QB)
    half = lax.axis_index("ctx") % 2
    count = blocks.shape[0]
    active = (jnp.arange(count, dtype=jnp.int32) // (count // 2) == half).astype(jnp.int32)
    return jnp.stack([begin // KB, (end + KB - 1) // KB, active])


def layer_stats(rows):
    row_mean = jnp.mean(rows, axis=-1, keepdims=True)
    centred = rows - row_mean
    inv_std = lax.rsqrt(jnp.mean(centred * centred, axis=-1, keepdims=True) + 1e-05)
    return (centred * inv_std, inv_std)


def norm_back(grad_normed_out, normed, inv_std, gain):
    scaled = grad_normed_out * gain
    return inv_std * (
        scaled
        - jnp.mean(scaled, axis=-1, keepdims=True)
        - normed * jnp.mean(scaled * normed, axis=-1, keepdims=True)
    )


def head(array, index):
    return array[:, index * HD : (index + 1) * HD]


def gather_first(gains, shifts, head_bias, qkv_weight):
    rows, columns = qkv_weight.shape[1], 3 * qkv_weight.shape[2]
    weight = qkv_weight.transpose(1, 0, 2).reshape(rows, columns)
    small = jnp.concatenate([gains.reshape(-1), shifts.reshape(-1), head_bias.reshape(-1)])
    small = jnp.pad(small, (0, 16 * columns - small.size)).reshape(16, columns)
    whole = gather_rows(jnp.concatenate([weight, small])).reshape(4, rows + 16, columns)
    small = whole[:, rows:].reshape(4, -1)
    g, s = gains.size, shifts.size
    gain_vals = small[:, :g].reshape(4, 2, rows).transpose(1, 0, 2).reshape(2, -1)
    shift_vals = small[:, g : g + s].reshape(4, 4, rows).transpose(1, 0, 2).reshape(4, -1)
    bias_vals = small[:, g + s : g + s + head_bias.size].reshape(-1)
    return (
        whole[:, :rows].reshape(4 * rows, columns),
        gain_vals.astype(F32),
        shift_vals.astype(F32),
        bias_vals.astype(F32),
    )


def forward_first(rows_in, params, weight_first, heads):
    gain_vals, shift_vals, bias_vals = params
    rows = rows_in[0].astype(F32)
    width = heads * HD
    normed, inv = layer_stats(rows)
    first_in = (normed * gain_vals[0] + shift_vals[0]).astype(BF16)
    qkv = dot(first_in, weight_first)
    q = (qkv[:, :width] + bias_vals[:width]).astype(BF16) * jnp.asarray(0.125, BF16)
    k = qkv[:, width : 2 * width].astype(BF16)
    v = (qkv[:, 2 * width :] + bias_vals[width : 2 * width]).astype(BF16)
    return first_in, q, k, v


def pack_qkv(q, k, v, heads):
    out = []
    for c in range(4):
        if heads == 4:
            parts = [(head(q, c), jnp.zeros_like(head(q, c))), (head(k, c), head(v, c))]
        else:
            e = 4 + c // 2
            parts = [
                (head(q, c), head(q, e)),
                (head(k, c), head(v, c)),
                (head(v, e), head(k, e)),
            ]
        out.append(jnp.stack([jnp.concatenate(p, axis=1) for p in parts]))
    return jnp.stack(out)


def unpack_o(blocks, heads):
    columns = [blocks[c][:, HD:] for c in range(4)]
    if heads == 6:
        part = lax.axis_index("ctx") // 2
        for h in range(2):
            columns.append(
                lax.dynamic_index_in_dim(blocks[2 * h : 2 * h + 2], part, 0, keepdims=False)[:, :HD]
            )
    return jnp.concatenate(columns, axis=1)


def pack_do(do, heads):
    out = []
    for c in range(4):
        other = jnp.zeros_like(head(do, c)) if heads == 4 else head(do, 4 + c // 2)
        out.append(jnp.concatenate([other, head(do, c)], axis=1))
    return jnp.stack(out)


def unpack_dqkv(blocks, heads):
    dq = [blocks[c, 0][:, :HD] for c in range(4)]
    dk = [blocks[c, 1][:, :HD] for c in range(4)]
    dv = [blocks[c, 1][:, HD:] for c in range(4)]
    if heads == 6:
        part = lax.axis_index("ctx") // 2
        for h in range(2):
            dq.append(
                lax.dynamic_index_in_dim(blocks[2 * h : 2 * h + 2, 0], part, 0, keepdims=False)[:, HD:]
            )
            both = (
                blocks[2 * h, 2].astype(F32) + blocks[2 * h + 1, 2].astype(F32)
            ).astype(BF16)
            dk.append(both[:, HD:])
            dv.append(both[:, :HD])
    return (
        jnp.concatenate(dq, axis=1),
        jnp.concatenate(dk, axis=1),
        jnp.concatenate(dv, axis=1),
    )


def blocks_of(array):
    return array.reshape(4, -1, array.shape[-1])


def middle_part(rows_in, cotangent, mixed, params, rest, heads):
    gain_vals, shift_vals, bias_vals = params
    width = heads * HD
    hidden_width = bias_vals.shape[0] - 2 * width
    up = rest[:, :hidden_width]
    down_t = rest[:, hidden_width : 2 * hidden_width]
    proj_t = rest[:, 2 * hidden_width :]
    rows = rows_in[0].astype(F32)
    grad_out = cotangent[0].astype(F32)
    middle = rows + tensor_sum(dot(mixed, proj_t, ((1,), (1,)))) + shift_vals[1]
    normed_two, inv_two = layer_stats(middle)
    second_in = (normed_two * gain_vals[1] + shift_vals[2]).astype(BF16)
    hidden = dot(second_in, up) + bias_vals[2 * width :]
    sigma = jax.nn.sigmoid(1.702 * hidden)
    activated = (hidden * sigma).astype(BF16)
    grad_branch = cotangent[0]
    grad_act = dot(grad_branch, down_t)
    grad_hidden = (grad_act * (sigma + 1.702 * hidden * sigma * (1.0 - sigma))).astype(BF16)
    grad_second = tensor_sum(dot(grad_hidden, up, ((1,), (1,))))
    output = (
        middle + tensor_sum(dot(activated, down_t, ((1,), (1,)))) + shift_vals[3]
    ).astype(BF16)
    grad_middle = grad_out + norm_back(grad_second, normed_two, inv_two, gain_vals[1])
    grad_attn = grad_middle.astype(BF16)
    grad_mixed = dot(grad_attn, proj_t).astype(BF16)
    over_rows = ((0,), (0,))
    grad_rest = jnp.concatenate(
        [
            dot(second_in, grad_hidden, over_rows).astype(BF16),
            dot(grad_branch, activated, over_rows).astype(BF16),
            dot(grad_attn, mixed, over_rows).astype(BF16),
        ],
        axis=1,
    )
    small = (
        jnp.sum(grad_second * normed_two, axis=0),
        jnp.sum(grad_middle, axis=0),
        jnp.sum(grad_second, axis=0),
        jnp.sum(grad_out, axis=0),
        jnp.sum(grad_hidden.astype(F32), axis=0),
    )
    return output, grad_middle, grad_mixed, grad_rest, small


def last_part(rows_in, params, weight_first, first_in, dq, dk, dv, grad_middle):
    gain_vals = params[0]
    dqkv = jnp.concatenate([dq, dk, dv], axis=1)
    grad_first = tensor_sum(dot(dqkv, weight_first, ((1,), (1,))))
    grad_weight = dot(first_in, dqkv, ((0,), (0,))).astype(BF16)
    normed, inv = layer_stats(rows_in[0].astype(F32))
    grad_rows = grad_middle + norm_back(grad_first, normed, inv, gain_vals[0])
    small = (
        jnp.sum(grad_first * normed, axis=0),
        jnp.sum(grad_first, axis=0),
        jnp.sum(dq.astype(F32), axis=0),
        jnp.sum(dv.astype(F32), axis=0),
    )
    return grad_rows, grad_weight, small


class Stream:
    def __init__(self, args, causal):
        (
            self.rows_in,
            seg_row,
            self.cotangent,
            gains,
            shifts,
            head_bias,
            qkv_weight,
            proj_weight,
            up_weight,
            down_weight,
        ) = args
        self.causal = causal
        self.heads = qkv_weight.shape[2] // HD
        self.segrow = seg_row
        self.segcol = seg_row.reshape(-1, 1)
        self.bounds = block_bounds(seg_row[0], causal)
        self.first = (gains, shifts, head_bias, qkv_weight)
        self.rest = jnp.concatenate(
            [up_weight, down_weight.T, proj_weight.T], axis=1
        )

    def gather_first(self):
        weight, *params = gather_first(*self.first)
        self.weight_first, self.params = weight, params

    def qkv(self):
        self.first_in, q, k, v = forward_first(
            self.rows_in, self.params, self.weight_first, self.heads
        )
        got = swap_blocks(pack_qkv(q, k, v, self.heads))
        parts = [got[:, i].reshape(-1, LANES) for i in range(got.shape[1])]
        self.q, self.kv = parts[0], parts[1]
        self.extra = parts[2] if self.heads == 6 else None

    def gather_rest(self):
        self.rest_full = gather_rows(self.rest)

    def attend(self):
        self.o, self.lse = attend(
            self.causal, self.bounds, self.q, self.kv, self.extra, self.segcol, self.segrow
        )
        self.mixed = unpack_o(swap_blocks(blocks_of(self.o)), self.heads)

    def middle(self):
        self.output, self.grad_middle, grad_mixed, self.grad_rest, self.small = middle_part(
            self.rows_in, self.cotangent, self.mixed, self.params, self.rest_full, self.heads
        )
        self.do = swap_blocks(pack_do(grad_mixed, self.heads)).reshape(-1, LANES)

    def back(self):
        grads = attend_back(
            self.causal,
            self.bounds,
            self.q,
            self.do,
            self.o,
            self.lse,
            self.kv,
            self.extra,
            self.segcol,
            self.segrow,
        )
        got = swap_blocks(jnp.stack([blocks_of(g) for g in grads], axis=1))
        self.dqkv = unpack_dqkv(got, self.heads)

    def last(self):
        self.grad_rows, self.grad_first, self.small_last = last_part(
            self.rows_in,
            self.params,
            self.weight_first,
            self.first_in,
            *self.dqkv,
            self.grad_middle,
        )

    def small_vector(self):
        gain_two, shift_proj, shift_two, shift_down, bias_up = self.small
        gain_one, shift_one, bias_q, bias_v = self.small_last
        return jnp.concatenate(
            [
                gain_one,
                gain_two,
                shift_one,
                shift_proj,
                shift_two,
                shift_down,
                bias_q,
                bias_v,
                bias_up,
            ]
        )

    def outputs(self, small):
        group = lax.axis_index("fsdp")
        full = self.rows_in.shape[2]
        width = self.heads * HD
        hidden = (self.rest.shape[1] - width) // 2

        def own(array):
            columns = array.shape[1] // 4
            return lax.dynamic_slice_in_dim(array, group * columns, columns, 1)

        gains = own(small[: 2 * full].reshape(2, full))
        shifts = own(small[2 * full : 6 * full].reshape(4, full))
        bias = own(small[6 * full :].reshape(1, -1))
        rest = reduce_owned(self.grad_rest)
        first = reduce_owned(self.grad_first)
        rows = first.shape[0]
        return (
            self.output[None],
            self.grad_rows[None],
            gains,
            shifts,
            bias,
            first.reshape(rows, 3, width).transpose(1, 0, 2),
            rest[:, 2 * hidden :].T,
            rest[:, :hidden],
            rest[:, hidden : 2 * hidden].T,
        )


def on_device(*args):
    image = Stream(args[:10], False)
    text = Stream(args[10:], True)
    for stage in ("gather_first", "qkv", "gather_rest", "attend", "middle", "back", "last"):
        for stream in (text, image):
            getattr(stream, stage)()
    small_image, small_text = image.small_vector(), text.small_vector()
    small = reduce_small(jnp.concatenate([small_image, small_text]))
    cut = small_image.shape[0]
    return image.outputs(small[:cut]) + text.outputs(small[cut:])


def tensor_psum(partial_rows):
    return lax.psum(partial_rows, "tp")


def any_mesh_block(
    rows_in,
    seg_row,
    cotangent,
    gains,
    shifts,
    head_bias,
    qkv_weight,
    proj_weight,
    up_weight,
    down_weight,
    causal,
):
    gain_full, shift_full, bias_full, qkv_full, proj_full, up_full, down_full = (
        lax.all_gather(gains, "fsdp", axis=1, tiled=True),
        lax.all_gather(shifts, "fsdp", axis=1, tiled=True),
        lax.all_gather(head_bias, "fsdp", axis=1, tiled=True),
        lax.all_gather(qkv_weight, "fsdp", axis=1, tiled=True),
        lax.all_gather(proj_weight, "fsdp", axis=1, tiled=True),
        lax.all_gather(up_weight, "fsdp", axis=0, tiled=True),
        lax.all_gather(down_weight, "fsdp", axis=1, tiled=True),
    )
    gain_vals = gain_full.astype(jnp.float32)
    shift_vals = shift_full.astype(jnp.float32)
    bias_vals = bias_full[0].astype(jnp.float32)
    tp_width = qkv_full.shape[2]
    local_rows = rows_in.shape[1]
    seq_length = seg_row.shape[1]
    head_local = tp_width // HD
    rows = rows_in[0].astype(jnp.float32)
    row_start = lax.axis_index("ctx") * local_rows
    seg_all = seg_row[0]
    seg_query = lax.dynamic_slice_in_dim(seg_all, row_start, local_rows)
    query_pos = row_start + jnp.arange(local_rows, dtype=jnp.int32)
    key_pos = jnp.arange(seq_length, dtype=jnp.int32)
    allowed = seg_query[:, None] == seg_all[None, :]
    if causal:
        allowed = jnp.logical_and(allowed, key_pos[None, :] <= query_pos[:, None])

    def to_heads(matrix):
        return matrix.reshape(matrix.shape[0], head_local, HD).transpose(1, 0, 2)

    def from_heads(stacked):
        return stacked.transpose(1, 0, 2).reshape(stacked.shape[1], head_local * HD)

    normed_one, inv_one = layer_stats(rows)
    first_in = (normed_one * gain_vals[0] + shift_vals[0]).astype(jnp.bfloat16)
    queries = (
        jnp.dot(first_in, qkv_full[0], preferred_element_type=jnp.float32) + bias_vals[:tp_width]
    ).astype(jnp.bfloat16)
    key_rows = jnp.dot(first_in, qkv_full[1], preferred_element_type=jnp.float32).astype(
        jnp.bfloat16
    )
    values = (
        jnp.dot(first_in, qkv_full[2], preferred_element_type=jnp.float32)
        + bias_vals[tp_width : 2 * tp_width]
    ).astype(jnp.bfloat16)
    key_all, value_all = (
        lax.all_gather(key_rows, "ctx", axis=0, tiled=True),
        lax.all_gather(values, "ctx", axis=0, tiled=True),
    )
    query_heads = to_heads(queries)
    key_heads = to_heads(key_all)
    value_heads = to_heads(value_all)

    def attend(head_items):
        query_h, key_h, value_h = head_items
        scores = jnp.einsum("qd,kd->qk", query_h, key_h, preferred_element_type=jnp.float32) * 0.125
        scores = jnp.where(allowed, scores, -1e30)
        row_top = jnp.max(scores, axis=-1, keepdims=True)
        weights = jnp.exp(scores - row_top)
        row_total = jnp.sum(weights, axis=-1, keepdims=True)
        weights_low = (weights / row_total).astype(jnp.bfloat16)
        mixed_h = jnp.einsum("qk,kd->qd", weights_low, value_h, preferred_element_type=jnp.float32)
        return (mixed_h.astype(jnp.bfloat16), row_top[:, 0] + jnp.log(row_total[:, 0]))

    mixed_heads, log_totals = lax.map(attend, (query_heads, key_heads, value_heads))
    mixed = from_heads(mixed_heads)
    middle = (
        rows
        + tensor_psum(jnp.dot(mixed, proj_full, preferred_element_type=jnp.float32))
        + shift_vals[1]
    )
    normed_two, inv_two = layer_stats(middle)
    second_in = (normed_two * gain_vals[1] + shift_vals[2]).astype(jnp.bfloat16)
    hidden = (
        jnp.dot(second_in, up_full, preferred_element_type=jnp.float32) + bias_vals[2 * tp_width :]
    )
    sigma = jax.nn.sigmoid(1.702 * hidden)
    activated = (hidden * sigma).astype(jnp.bfloat16)
    output = (
        middle
        + tensor_psum(jnp.dot(activated, down_full, preferred_element_type=jnp.float32))
        + shift_vals[3]
    )
    grad_out = cotangent[0].astype(jnp.float32)
    grad_down_bias = jnp.sum(grad_out, axis=0)
    grad_branch = grad_out.astype(jnp.bfloat16)
    grad_down = jnp.einsum("tf,td->fd", activated, grad_branch, preferred_element_type=jnp.float32)
    grad_act = jnp.einsum("td,fd->tf", grad_branch, down_full, preferred_element_type=jnp.float32)
    grad_hidden = (grad_act * (sigma + 1.702 * hidden * sigma * (1.0 - sigma))).astype(jnp.bfloat16)
    grad_up_bias = jnp.sum(grad_hidden.astype(jnp.float32), axis=0)
    grad_up = jnp.einsum("td,tf->df", second_in, grad_hidden, preferred_element_type=jnp.float32)
    grad_second = tensor_psum(
        jnp.einsum("tf,df->td", grad_hidden, up_full, preferred_element_type=jnp.float32)
    )
    grad_gain_two = jnp.sum(grad_second * normed_two, axis=0)
    grad_shift_two = jnp.sum(grad_second, axis=0)
    grad_middle = grad_out + norm_back(grad_second, normed_two, inv_two, gain_vals[1])
    grad_proj_bias = jnp.sum(grad_middle, axis=0)
    grad_attn = grad_middle.astype(jnp.bfloat16)
    grad_proj = jnp.einsum("tc,td->cd", mixed, grad_attn, preferred_element_type=jnp.float32)
    grad_mixed = jnp.einsum(
        "td,cd->tc", grad_attn, proj_full, preferred_element_type=jnp.float32
    ).astype(jnp.bfloat16)

    def attend_back(head_items):
        query_h, key_h, value_h, grad_h, log_total = head_items
        scores = jnp.einsum("qd,kd->qk", query_h, key_h, preferred_element_type=jnp.float32) * 0.125
        weights = jnp.where(allowed, jnp.exp(scores - log_total[:, None]), 0.0)
        grad_weights = jnp.einsum("qd,kd->qk", grad_h, value_h, preferred_element_type=jnp.float32)
        row_delta = jnp.sum(weights * grad_weights, axis=-1, keepdims=True)
        grad_scores = (weights * (grad_weights - row_delta)).astype(jnp.bfloat16)
        grad_query_h = (
            jnp.einsum("qk,kd->qd", grad_scores, key_h, preferred_element_type=jnp.float32) * 0.125
        )
        grad_key_h = (
            jnp.einsum("qk,qd->kd", grad_scores, query_h, preferred_element_type=jnp.float32)
            * 0.125
        )
        grad_value_h = jnp.einsum(
            "qk,qd->kd", weights.astype(jnp.bfloat16), grad_h, preferred_element_type=jnp.float32
        )
        return (grad_query_h, grad_key_h, grad_value_h)

    query_parts, key_parts, value_parts = lax.map(
        attend_back, (query_heads, key_heads, value_heads, to_heads(grad_mixed), log_totals)
    )
    key_sum, value_sum = (
        lax.psum_scatter(from_heads(key_parts), "ctx", scatter_dimension=0, tiled=True),
        lax.psum_scatter(from_heads(value_parts), "ctx", scatter_dimension=0, tiled=True),
    )
    grad_query = from_heads(query_parts).astype(jnp.bfloat16)
    grad_key = key_sum.astype(jnp.bfloat16)
    grad_value = value_sum.astype(jnp.bfloat16)
    grad_qkv = jnp.stack(
        [
            jnp.einsum("td,tc->dc", first_in, grad_query, preferred_element_type=jnp.float32),
            jnp.einsum("td,tc->dc", first_in, grad_key, preferred_element_type=jnp.float32),
            jnp.einsum("td,tc->dc", first_in, grad_value, preferred_element_type=jnp.float32),
        ]
    )
    grad_head = jnp.concatenate(
        [
            jnp.sum(grad_query.astype(jnp.float32), axis=0),
            jnp.sum(grad_value.astype(jnp.float32), axis=0),
            grad_up_bias,
        ]
    )[None, :]
    grad_first_part = jnp.einsum(
        "tc,dc->td", grad_query, qkv_full[0], preferred_element_type=jnp.float32
    )
    grad_first_part = grad_first_part + jnp.einsum(
        "tc,dc->td", grad_key, qkv_full[1], preferred_element_type=jnp.float32
    )
    grad_first_part = grad_first_part + jnp.einsum(
        "tc,dc->td", grad_value, qkv_full[2], preferred_element_type=jnp.float32
    )
    grad_first = tensor_psum(grad_first_part)
    grad_gain_one = jnp.sum(grad_first * normed_one, axis=0)
    grad_shift_one = jnp.sum(grad_first, axis=0)
    grad_rows = grad_middle + norm_back(grad_first, normed_one, inv_one, gain_vals[0])
    grad_gains = jnp.stack([grad_gain_one, grad_gain_two])
    grad_shifts = jnp.stack([grad_shift_one, grad_proj_bias, grad_shift_two, grad_down_bias])
    share_gains, share_shifts, share_head, share_qkv, share_proj, share_up, share_down = (
        lax.psum_scatter(grad_gains, "fsdp", scatter_dimension=1, tiled=True),
        lax.psum_scatter(grad_shifts, "fsdp", scatter_dimension=1, tiled=True),
        lax.psum_scatter(grad_head, "fsdp", scatter_dimension=1, tiled=True),
        lax.psum_scatter(grad_qkv, "fsdp", scatter_dimension=1, tiled=True),
        lax.psum_scatter(grad_proj, "fsdp", scatter_dimension=1, tiled=True),
        lax.psum_scatter(grad_up, "fsdp", scatter_dimension=0, tiled=True),
        lax.psum_scatter(grad_down, "fsdp", scatter_dimension=1, tiled=True),
    )
    owned = lax.psum(
        (share_gains, share_shifts, share_head, share_qkv, share_proj, share_up, share_down), "ctx"
    )
    return (output.astype(jnp.bfloat16)[None], grad_rows[None]) + tuple(owned)


def on_any_mesh(
    image_input,
    image_segments,
    image_cotangent,
    image_gains,
    image_shifts,
    image_head_bias,
    image_qkv_weight,
    image_proj_weight,
    image_up_weight,
    image_down_weight,
    text_input,
    text_segments,
    text_cotangent,
    text_gains,
    text_shifts,
    text_head_bias,
    text_qkv_weight,
    text_proj_weight,
    text_up_weight,
    text_down_weight,
):
    image_results = any_mesh_block(
        image_input,
        image_segments,
        image_cotangent,
        image_gains,
        image_shifts,
        image_head_bias,
        image_qkv_weight,
        image_proj_weight,
        image_up_weight,
        image_down_weight,
        False,
    )
    text_results = any_mesh_block(
        text_input,
        text_segments,
        text_cotangent,
        text_gains,
        text_shifts,
        text_head_bias,
        text_qkv_weight,
        text_proj_weight,
        text_up_weight,
        text_down_weight,
        True,
    )
    return image_results + text_results


def stream_specs():
    return (
        P("fsdp", "ctx", None),
        P("fsdp", None),
        P("fsdp", "ctx", None),
        P(None, "fsdp"),
        P(None, "fsdp"),
        P("tp", "fsdp"),
        P(None, "fsdp", "tp"),
        P("tp", "fsdp"),
        P("fsdp", "tp"),
        P("tp", "fsdp"),
    )


def solution(mesh):
    one = stream_specs()
    grads = (one[0], one[0]) + one[3:]
    body = on_device
    if (mesh.shape["fsdp"], mesh.shape["ctx"], mesh.shape["tp"]) != (4, 4, 2):
        body = on_any_mesh
    return jax.shard_map(
        body, mesh=mesh, in_specs=one + one, out_specs=grads + grads, check_vma=False
    )
```

```python
import functools

import jax
import jax.numpy as jnp
from jax import lax
from jax.experimental import pallas as pl
from jax.experimental.pallas import tpu as pltpu
from jax.sharding import PartitionSpec as P

HD = 64
LANES = 128
QB = 256
KB = 512
NEG = -1e30
F32 = jnp.float32
MESH = pl.DeviceIdType.MESH
FSDP, CTX, TP = "fsdp", "ctx", "tp"
BF16 = jnp.bfloat16


def dot(left, right, dims=((1,), (0,))):
    return lax.dot_general(left, right, (dims, ((), ())), preferred_element_type=F32)


def reduce_small(vector):
    for axis, step in ((FSDP, 1), (FSDP, 2), (CTX, 1), (CTX, 2)):
        vector = vector + lax.ppermute(vector, axis, [(i, i ^ step) for i in range(4)])
    return vector


def lane_marks():
    lane = lax.broadcasted_iota(jnp.int32, (1, LANES), 1)
    first = (lane < HD).astype(F32).astype(BF16)
    second = (lane >= HD).astype(F32).astype(BF16)
    return first, second


def turn(value, flag):
    return jnp.where(flag != 0, pltpu.roll(value, HD, 1), value)


def attend_kernel(causal, bounds, m_ref, segcol_ref, segrow_ref, o_ref, lse_ref):
    block = pl.program_id(0)
    low, high, active = bounds[0, block], bounds[1, block], bounds[2, block]
    source, half = block // 2, block % 2
    first, second = lane_marks()
    lane = lax.broadcasted_iota(jnp.int32, (QB, LANES), 1)
    seg_query = segcol_ref[...]

    def one(query, load, own, other):
        def step(index, carry):
            top, acc = carry
            keys = load(index)
            scores = dot(query * own, keys, ((1,), (1,)))
            start = index * KB
            ok = seg_query == segrow_ref[:, pl.ds(pl.multiple_of(start, KB), KB)]
            if causal:
                key_pos = start + lax.broadcasted_iota(jnp.int32, (QB, KB), 1)
                query_pos = block * QB + lax.broadcasted_iota(jnp.int32, (QB, KB), 0)
                ok = jnp.logical_and(ok, key_pos <= query_pos)
            scores = jnp.where(ok, scores, NEG)
            new_top = jnp.maximum(top, jnp.max(scores, axis=1, keepdims=True))
            weights = jnp.exp(scores - new_top).astype(BF16)
            acc = acc * jnp.exp(top - new_top) + dot(weights, keys * other + own)
            return new_top, acc

        top, acc = lax.fori_loop(
            low, high, step, (jnp.full((QB, 1), NEG, F32), jnp.zeros((QB, LANES), F32))
        )
        return acc / pltpu.roll(acc, HD, 1), top + jnp.log(acc)

    if causal:
        query = turn(m_ref[source, :QB].astype(F32), half).astype(BF16)
        mixed, lse = one(query, lambda i: m_ref[i, QB:], first, second)
        mixed = turn(mixed, 1 - half).astype(BF16)
        lse_ref[0] = jnp.transpose(lse)[:16]

        @pl.when(half == 0)
        def _():
            o_ref[0] = mixed

        @pl.when(half != 0)
        def _():
            o_ref[0] = jnp.where(lane < HD, o_ref[0], mixed)
    else:
        query = m_ref[source, 0, pl.ds(pl.multiple_of(half * QB, QB), QB)]
        mixed, lse = one(query, lambda i: m_ref[i, 1], first, second)

        @pl.when(active == 0)
        def _():
            o_ref[0] = mixed.astype(BF16)
            lse_ref[0, :8] = jnp.transpose(lse)[:8]
            lse_ref[0, 8:] = jnp.zeros((8, QB), F32)

        @pl.when(active != 0)
        def _():
            mixed_two, lse_two = one(query, lambda i: m_ref[i, 2], second, first)
            o_ref[0] = jnp.where(lane < HD, mixed_two, mixed).astype(BF16)
            lse_ref[0, :8] = jnp.transpose(lse)[:8]
            lse_ref[0, 8:] = jnp.transpose(lse_two)[HD : HD + 8]


def o_block(causal):
    if causal:
        return pl.BlockSpec((1, QB, LANES), lambda i, b: (i // 2, 0, 0))
    return pl.BlockSpec((1, QB, LANES), lambda i, b: (i // 2, i % 2, 0))


def attend(causal, bounds, messages, segcol, segrow):
    rows = segcol.shape[0]
    blocks = rows // QB
    heads = 1 if causal else 2
    o_shape = (4, QB if causal else KB, LANES)
    return pl.pallas_call(
        functools.partial(attend_kernel, causal),
        grid_spec=pltpu.PrefetchScalarGridSpec(
            num_scalar_prefetch=1,
            grid=(blocks,),
            in_specs=[
                pl.BlockSpec(messages.shape, lambda i, b: (0,) * messages.ndim),
                pl.BlockSpec((QB, 1), lambda i, b: (i, 0)),
                pl.BlockSpec((1, rows), lambda i, b: (0, 0)),
            ],
            out_specs=[o_block(causal), pl.BlockSpec((1, 16, QB), lambda i, b: (i, 0, 0))],
        ),
        out_shape=[
            jax.ShapeDtypeStruct(o_shape, BF16),
            jax.ShapeDtypeStruct((blocks, 16, QB), F32),
        ],
        cost_estimate=pl.CostEstimate(
            flops=heads * 4 * rows * rows * LANES,
            bytes_accessed=6 * rows * LANES,
            transcendentals=heads * rows * rows,
        ),
        name="attend_causal" if causal else "attend_full",
    )(bounds, messages, segcol, segrow)


def attend_back_kernel(
    causal, bounds, m_ref, do_ref, o_ref, lse_ref, segcol_ref, segrow_ref, out_ref, acc_ref
):
    block = pl.program_id(0)
    low, high, active = bounds[0, block], bounds[1, block], bounds[2, block]
    source, half = block // 2, block % 2
    first, second = lane_marks()
    lane = lax.broadcasted_iota(jnp.int32, (QB, LANES), 1)

    @pl.when(block == 0)
    def _():
        acc_ref[...] = jnp.zeros_like(acc_ref)

    seg_query = segrow_ref[:, pl.ds(pl.multiple_of(block * QB, QB), QB)]

    def one(query, grad_o, load, which, own, other, lse, delta):
        query_own = query * own
        grad_own = grad_o * other

        def step(index, grad_query):
            start = pl.multiple_of(index * KB, KB)
            keys = load(index)
            scores = dot(keys, query_own, ((1,), (1,)))
            ok = segcol_ref[pl.ds(start, KB), :] == seg_query
            if causal:
                key_pos = start + lax.broadcasted_iota(jnp.int32, (KB, QB), 0)
                query_pos = block * QB + lax.broadcasted_iota(jnp.int32, (KB, QB), 1)
                ok = jnp.logical_and(ok, key_pos <= query_pos)
            weights = jnp.where(ok, jnp.exp(scores - lse), 0.0)
            grad_weights = dot(keys, grad_own, ((1,), (1,)))
            grad_scores = (weights * (grad_weights - delta)).astype(BF16)
            acc_ref[which, pl.ds(start, KB), :] += dot(grad_scores, query_own) + dot(
                weights.astype(BF16), grad_own
            )
            return grad_query + dot(grad_scores, keys, ((0,), (0,)))

        return lax.fori_loop(low, high, step, jnp.zeros((QB, LANES), F32))

    grad_o = do_ref[0].astype(F32)
    mixed = o_ref[0].astype(F32)
    if causal:
        grad_o = turn(grad_o, 1 - half)
        product = jnp.transpose(grad_o * turn(mixed, 1 - half))
        query = turn(m_ref[source, :QB].astype(F32), half).astype(BF16)
        grad_query = one(
            query,
            grad_o.astype(BF16),
            lambda i: m_ref[i, QB:],
            0,
            first,
            second,
            lse_ref[0, :1],
            jnp.sum(product[HD:], axis=0, keepdims=True),
        )
        grad_query = turn(grad_query * 0.125, half).astype(BF16)

        @pl.when(half == 0)
        def _():
            out_ref[source, :QB] = grad_query

        @pl.when(half != 0)
        def _():
            out_ref[source, :QB] = jnp.where(lane < HD, out_ref[source, :QB], grad_query)
    else:
        product = jnp.transpose(grad_o * mixed)
        rows = pl.ds(pl.multiple_of(half * QB, QB), QB)
        query = m_ref[source, 0, rows]
        grad_query = one(
            query,
            do_ref[0],
            lambda i: m_ref[i, 1],
            0,
            first,
            second,
            lse_ref[0, :1],
            jnp.sum(product[HD:], axis=0, keepdims=True),
        )

        @pl.when(active == 0)
        def _():
            out_ref[source, 0, rows] = (grad_query * 0.125).astype(BF16)

        @pl.when(active != 0)
        def _():
            grad_two = one(
                query,
                do_ref[0],
                lambda i: m_ref[i, 2],
                1,
                second,
                first,
                lse_ref[0, 8:9],
                jnp.sum(product[:HD], axis=0, keepdims=True),
            )
            out_ref[source, 0, rows] = (
                jnp.where(lane < HD, grad_query, grad_two) * 0.125
            ).astype(BF16)

    @pl.when(block == pl.num_programs(0) - 1)
    def _():
        for index in range(4):
            keys = slice(index * KB, (index + 1) * KB)
            if causal:
                out_ref[index, QB:] = acc_ref[0, keys].astype(BF16)
            else:
                out_ref[index, 1] = acc_ref[0, keys].astype(BF16)
                out_ref[index, 2] = acc_ref[1, keys].astype(BF16)


def attend_back(causal, bounds, messages, do, o, lse, segcol, segrow):
    rows = segcol.shape[0]
    blocks = rows // QB
    heads = 1 if causal else 2
    whole = pl.BlockSpec(messages.shape, lambda i, b: (0,) * messages.ndim)
    return pl.pallas_call(
        functools.partial(attend_back_kernel, causal),
        grid_spec=pltpu.PrefetchScalarGridSpec(
            num_scalar_prefetch=1,
            grid=(blocks,),
            in_specs=[
                whole,
                o_block(causal),
                o_block(causal),
                pl.BlockSpec((1, 16, QB), lambda i, b: (i, 0, 0)),
                pl.BlockSpec((rows, 1), lambda i, b: (0, 0)),
                pl.BlockSpec((1, rows), lambda i, b: (0, 0)),
            ],
            out_specs=whole,
            scratch_shapes=[pltpu.VMEM((heads, rows, LANES), F32)],
        ),
        out_shape=jax.ShapeDtypeStruct(messages.shape, BF16),
        cost_estimate=pl.CostEstimate(
            flops=heads * 10 * rows * rows * LANES,
            bytes_accessed=12 * rows * LANES,
            transcendentals=heads * rows * rows,
        ),
        name="attend_back_causal" if causal else "attend_back_full",
    )(bounds, messages, do, o, lse, segcol, segrow)


def block_bounds(seg, causal):
    blocks = seg.reshape(-1, QB)
    begin = jnp.sum(seg[None, :] < blocks[:, :1], axis=1, dtype=jnp.int32)
    end = jnp.sum(seg[None, :] <= blocks[:, -1:], axis=1, dtype=jnp.int32)
    if causal:
        end = jnp.minimum(end, (jnp.arange(blocks.shape[0], dtype=jnp.int32) + 1) * QB)
    half = lax.axis_index(CTX) % 2
    count = blocks.shape[0]
    active = (jnp.arange(count, dtype=jnp.int32) // (count // 2) == half).astype(jnp.int32)
    return jnp.stack([begin // KB, (end + KB - 1) // KB, active])


class Bag:
    pass


def partners():
    at = Bag()
    group, here, core = lax.axis_index(FSDP), lax.axis_index(CTX), lax.axis_index(TP)
    at.group, at.here = group, here
    at.group_x = group + 1 - 2 * (group % 2)
    at.group_y = group + 2 - 4 * (group // 2)
    at.group_far = 3 - group
    at.here_low, at.here_high = here % 2, here // 2
    at.ctx = (here, here + 1 - 2 * (here % 2), here + 2 - 4 * (here // 2), 3 - here)
    at.to_x, at.to_y, at.to_far = ({FSDP: g} for g in (at.group_x, at.group_y, at.group_far))
    at.to_ctx = [{CTX: c} for c in at.ctx]
    at.to_core = {TP: 1 - core}
    return at


def meet(devices):
    barrier = pltpu.get_barrier_semaphore()
    for device in devices:
        pl.semaphore_signal(barrier, inc=1, device_id=device, device_id_type=MESH)
    pl.semaphore_wait(barrier, len(devices))


class Copies:
    def __init__(self, send_sems, recv_sems, local_sems):
        self.sems = (send_sems, recv_sems, local_sems)
        self.used = [0, 0]

    def remote(self, src, dst, device):
        index = self.used[0]
        self.used[0] += 1
        copy = pltpu.make_async_remote_copy(
            src_ref=src,
            dst_ref=dst,
            send_sem=self.sems[0].at[index],
            recv_sem=self.sems[1].at[index],
            device_id=device,
            device_id_type=MESH,
        )
        copy.start()
        return copy

    def local(self, src, dst):
        index = self.used[1]
        self.used[1] += 1
        copy = pltpu.make_async_copy(src, dst, self.sems[2].at[index])
        copy.start()
        return copy


def copy_sems(remote, local):
    return [
        pltpu.SemaphoreType.DMA((remote,)),
        pltpu.SemaphoreType.DMA((remote,)),
        pltpu.SemaphoreType.DMA((local,)),
    ]


class Gather:
    def __init__(self, copies, at, src, dst):
        self.copies, self.at, self.dst = copies, at, dst
        self.rows = src.shape[-2]
        own = self.part(at.group, 0, self.rows)
        self.own = copies.local(src, own)
        self.to_x = copies.remote(src, own, at.to_x)
        self.to_y = copies.remote(src, own, at.to_y)

    def part(self, owner, offset, size):
        rows = pl.ds(pl.multiple_of(owner * self.rows + offset, 8), size)
        return self.dst.at[:, rows, :] if len(self.dst.shape) == 3 else self.dst.at[rows, :]

    def forward(self):
        half = self.rows // 2
        self.to_x.wait_recv()
        self.to_y.wait_recv()
        top = self.part(self.at.group_y, 0, half)
        low = self.part(self.at.group_x, half, half)
        self.far_x = self.copies.remote(top, top, self.at.to_x)
        self.far_y = self.copies.remote(low, low, self.at.to_y)

    def arrived(self):
        self.own.wait()
        self.far_x.wait_recv()
        self.far_y.wait_recv()

    def sent(self):
        for copy in (self.to_x, self.to_y, self.far_x, self.far_y):
            copy.wait_send()


def normalise(rows):
    mean = jnp.mean(rows, axis=-1, keepdims=True)
    centred = rows - mean
    inv = lax.rsqrt(jnp.mean(centred * centred, axis=-1, keepdims=True) + 1e-05)
    return centred * inv, inv


def lane_pair(low, high):
    lane = lax.broadcasted_iota(jnp.int32, low[0].shape, 1)
    left = low[0] if low[1] == 0 else pltpu.roll(low[0], HD, 1)
    right = high[0] if high[1] == 1 else pltpu.roll(high[0], HD, 1)
    return jnp.where(lane < HD, left, right)


def head_tile(ref, start, index, rows=slice(None)):
    first = start + (index // 2) * LANES
    return ref[rows, first : first + LANES], index % 2


def write_messages(qkv, out, heads):
    width = heads * HD
    tokens = qkv.shape[0]
    for c in range(4):
        if heads == 4:
            half = tokens // 2
            out[c, :half] = lane_pair(
                head_tile(qkv, 0, c, slice(0, half)), head_tile(qkv, 0, c, slice(half, None))
            ).astype(BF16)
            out[c, half:] = lane_pair(
                head_tile(qkv, width, c), head_tile(qkv, 2 * width, c)
            ).astype(BF16)
        else:
            e = 4 + c // 2
            out[c, 0] = lane_pair(head_tile(qkv, 0, c), head_tile(qkv, 0, e)).astype(BF16)
            out[c, 1] = lane_pair(
                head_tile(qkv, width, c), head_tile(qkv, 2 * width, c)
            ).astype(BF16)
            out[c, 2] = lane_pair(
                head_tile(qkv, 2 * width, e), head_tile(qkv, width, e)
            ).astype(BF16)


def front_stream_sizes(width, heads, tokens):
    part = (tokens // 2 + tokens, LANES) if heads == 4 else (3, tokens, LANES)
    return (4,) + part


def first_rows(x_ref, small_ref, weight_ref, first_ref, qkv_ref, step):
    width = weight_ref.shape[2]
    rows = slice(step * 256, step * 256 + 256)
    normed, _ = normalise(x_ref[rows, :].astype(F32))
    first = (normed * small_ref[0:1] + small_ref[2:3]).astype(BF16)
    first_ref[:, rows] = jnp.transpose(first)
    bias = small_ref[6:7]
    qkv_ref[rows, :width] = (dot(first, weight_ref[0]) + bias[:, :width]) * 0.125
    qkv_ref[rows, width : 2 * width] = dot(first, weight_ref[1])
    qkv_ref[rows, 2 * width :] = dot(first, weight_ref[2]) + bias[:, width : 2 * width]


def front_kernel(*refs):
    at = partners()
    n = 6
    ins = [refs[:n], refs[n : 2 * n]]
    refs = refs[2 * n :]
    n = 7
    outs = [refs[:n], refs[n : 2 * n]]
    refs = refs[2 * n :]
    n = 5
    scratch = [refs[:n], refs[n : 2 * n]]
    copies = Copies(*refs[2 * n :])
    meet(
        [at.to_x, at.to_y, at.to_far]
        + at.to_ctx[1:]
    )
    small_copies, first_gathers = [], []
    for (x, small, qkv, up, down, proj), out, (small_in, *_) in zip(ins, outs, scratch):
        small_copies.append(
            [
                copies.remote(small, small_in.at[i], device)
                for i, device in enumerate((at.to_x, at.to_y, at.to_far))
            ]
        )
        first_gathers.append(Gather(copies, at, qkv, out[0]))
    for (x, small, qkv, up, down, proj), (_, _, _, down_t, proj_t) in zip(ins, scratch):
        if down.shape[0] > down.shape[1]:
            down_t[...] = jnp.transpose(down[...])
            proj_t[...] = jnp.transpose(proj[...])
    rest_gathers = []
    for gather in first_gathers:
        gather.forward()
    for (x, small, qkv, up, down, proj), out, (_, _, _, down_t, proj_t) in zip(ins, outs, scratch):
        flip = down.shape[0] > down.shape[1]
        for piece, full in zip((proj_t if flip else proj, up, down_t if flip else down), out[4:]):
            rest_gathers.append(Gather(copies, at, piece, full))
    sends = []
    for which in (0, 1):
        x, small = ins[which][:2]
        weight, small_full, first, messages = outs[which][:4]
        small_in, qkv, mine, _, _ = scratch[which]
        for copy in small_copies[which]:
            copy.wait_recv()
        small_full[...] = small[...] + small_in[0] + small_in[1] + small_in[2]
        first_gathers[which].arrived()
        for step in range(x.shape[0] // 256):
            first_rows(x, small_full, weight, first, qkv, step)
        heads = weight.shape[2] // HD
        write_messages(qkv, mine, heads)
        sends.append(copies.local(mine.at[at.here], messages.at[at.here]))
        for other in at.ctx[1:]:
            sends.append(
                copies.remote(mine.at[other], messages.at[at.here], {CTX: other})
            )
        for gather in rest_gathers[3 * which : 3 * which + 3]:
            gather.forward()
    for gather in rest_gathers:
        gather.arrived()
    for gather in first_gathers + rest_gathers:
        gather.sent()
    for copy in sends:
        copy.wait()
    for copy in small_copies[0] + small_copies[1]:
        copy.wait_send()


def front(streams):
    vmem, hbm = pl.BlockSpec(memory_space=pltpu.VMEM), pl.BlockSpec(memory_space=pl.ANY)
    out_shape, out_specs, scratch = [], [], []
    for x, small, qkv, up, down, proj in streams:
        tokens, width = x.shape
        heads = qkv.shape[2] // HD
        messages = front_stream_sizes(width, heads, tokens)
        hidden = up.shape[1]
        out_shape += [
            jax.ShapeDtypeStruct((3, width, heads * HD), BF16),
            jax.ShapeDtypeStruct(small.shape, F32),
            jax.ShapeDtypeStruct((width, tokens), BF16),
            jax.ShapeDtypeStruct(messages, BF16),
            jax.ShapeDtypeStruct((width, heads * HD), BF16),
            jax.ShapeDtypeStruct((width, hidden), BF16),
            jax.ShapeDtypeStruct((width, hidden), BF16),
        ]
        out_specs += [vmem, vmem, vmem, hbm, hbm, hbm, hbm]
        scratch += [
            pltpu.VMEM((3,) + small.shape, F32),
            pltpu.VMEM((tokens, 3 * heads * HD), F32),
            pltpu.VMEM(messages, BF16),
            pltpu.VMEM((width // 4, hidden), BF16),
            pltpu.VMEM((width // 4, heads * HD), BF16),
        ]
    results = pl.pallas_call(
        front_kernel,
        out_shape=out_shape,
        in_specs=[vmem] * 12,
        out_specs=out_specs,
        scratch_shapes=scratch + copy_sems(2 * (3 + 4 * 4 + 3), 2 * 5),
        compiler_params=pltpu.CompilerParams(
            collective_id=0, has_side_effects=True, vmem_limit_bytes=60 << 20
        ),
        name="front",
    )(*streams[0], *streams[1])
    return results[:7], results[7:]


def place_small(gains, shifts, head_bias):
    group = lax.axis_index(FSDP)
    width = 4 * gains.shape[1]

    def spread(array, columns):
        out = jnp.zeros((array.shape[0], columns), F32)
        return lax.dynamic_update_slice_in_dim(
            out, array.astype(F32), group * array.shape[1], 1
        )

    bias = spread(head_bias, 4 * head_bias.shape[1]).reshape(-1, width)
    rows = jnp.concatenate([spread(gains, width), spread(shifts, width), bias])
    return jnp.pad(rows, ((0, 16 - rows.shape[0]), (0, 0)))


def chunks(tokens, size=256):
    return [slice(start, start + size) for start in range(0, tokens, size)]


def as_f32(ref, index, rows=slice(None)):
    return ref[index, rows].astype(F32)


def take_mixed(got, mixed, at, heads):
    tokens = mixed.shape[0]
    if heads == 4:
        half = tokens // 2
        for tile in range(2):
            cols = slice(tile * LANES, (tile + 1) * LANES)
            one, two = as_f32(got, 2 * tile), as_f32(got, 2 * tile + 1)
            mixed[:half, cols] = lane_pair((one, 0), (two, 0)).astype(BF16)
            mixed[half:, cols] = lane_pair((one, 1), (two, 1)).astype(BF16)
        return
    for tile in range(2):
        cols = slice(tile * LANES, (tile + 1) * LANES)
        mixed[:, cols] = lane_pair(
            (as_f32(got, 2 * tile), 1), (as_f32(got, 2 * tile + 1), 1)
        ).astype(BF16)
    part = at.here // 2
    mixed[:, 2 * LANES :] = lane_pair((as_f32(got, part), 0), (as_f32(got, part + 2), 0)).astype(BF16)


def write_grad_o(grad, out, heads):
    tokens = grad.shape[0]
    half = tokens // 2
    for c in range(4):
        if heads == 4:
            out[c] = lane_pair(
                head_tile(grad, 0, c, slice(0, half)), head_tile(grad, 0, c, slice(half, None))
            ).astype(BF16)
        else:
            out[c] = lane_pair(head_tile(grad, 0, 4 + c // 2), head_tile(grad, 0, c)).astype(BF16)


def send_blocks(copies, at, mine, out):
    done = [copies.local(mine.at[at.here], out.at[at.here])]
    for other in at.ctx[1:]:
        done.append(copies.remote(mine.at[other], out.at[at.here], {CTX: other}))
    return done


def middle_kernel(*refs):
    at = partners()
    n = 7
    ins = [refs[:n], refs[n : 2 * n]]
    refs = refs[2 * n :]
    n = 5
    outs = [refs[:n], refs[n : 2 * n]]
    refs = refs[2 * n :]
    n = 16
    scratch = [refs[:n], refs[n : 2 * n]]
    copies = Copies(*refs[2 * n :])
    other_core = at.to_core
    meet(at.to_ctx[1:] + [other_core])
    streams = []
    for (o, x, dy, small, proj_in, up_in, down_in), out, own in zip(ins, outs, scratch):
        s = Bag()
        s.o, s.x, s.dy, s.small = o, x, dy, small
        s.y, s.dmid, s.do_out, s.rest, s.sums = out
        (
            s.proj, s.up, s.down, s.o_in, s.mixed, s.part, s.part_in, s.mid, s.first_t, s.dy_t,
            s.act, s.dz, s.grad, s.grad_in, s.do, s.do_mine,
        ) = own
        s.heads = proj_in.shape[1] // HD
        s.o_done = send_blocks(copies, at, o, s.o_in)
        s.proj_done = copies.local(proj_in, s.proj)
        streams.append(s)
    for s, (o, x, dy, small, proj_in, up_in, down_in) in zip(streams, ins):
        s.rest_done = [copies.local(up_in, s.up), copies.local(down_in, s.down)]
        s.sums[...] = jnp.zeros_like(s.sums)
        for rows in chunks(dy.shape[0]):
            s.dy_t[:, rows] = jnp.transpose(dy[rows, :])
    for s in streams:
        tokens, width = s.x.shape
        for copy in s.o_done:
            copy.wait()
        take_mixed(s.o_in, s.mixed, at, s.heads)
        s.proj_done.wait()
        for cols in chunks(width):
            s.part[:, cols] = dot(s.mixed[...], s.proj[cols, :], ((1,), (1,)))
        s.part_done = copies.remote(s.part, s.part_in, other_core)
    for s in streams:
        tokens, width = s.x.shape
        hidden = s.up.shape[1]
        small, mid, first_t, dy_t = s.small, s.mid, s.first_t, s.dy_t
        s.part_done.wait()
        for rows in chunks(tokens):
            middle = (
                s.x[rows, :].astype(F32) + s.part[rows, :] + s.part_in[rows, :] + small[3:4]
            )
            mid[rows, :] = middle
            normed, _ = normalise(middle)
            first_t[:, rows] = jnp.transpose((normed * small[1:2] + small[4:5]).astype(BF16))
        for copy in s.rest_done:
            copy.wait()
        act, dz = s.act, s.dz

        def tile(index, carry, s=s, act=act, dz=dz, first_t=first_t, dy_t=dy_t, small=small, tokens=tokens, width=width, hidden=hidden):
            cols = pl.ds(pl.multiple_of(index * 256, 256), 256)
            up, down = s.up[:, cols], s.down[:, cols]
            per_row = width // 256
            own = s.proj.shape[1]
            up_cols = pl.ds(pl.multiple_of(own + index * 256, LANES), 256)
            down_cols = pl.ds(pl.multiple_of(own + hidden + index * 256, LANES), 256)
            bias = small[pl.ds(7 + index // per_row, 1), pl.ds(pl.multiple_of((index % per_row) * 256, 256), 256)]
            total = jnp.zeros((1, 256), F32)
            for rows in chunks(tokens):
                z = dot(first_t[:, rows], up, ((0,), (0,))) + bias
                sg = jax.nn.sigmoid(1.702 * z)
                zs = z * sg
                act[rows, cols] = zs.astype(BF16)
                grad = dot(s.dy[rows, :], down)
                low = (grad * (sg + 1.702 * zs * (1.0 - sg))).astype(BF16)
                dz[rows, cols] = low
                total = total + jnp.sum(low.astype(F32), axis=0, keepdims=True)
            s.sums[pl.ds(7 + index // per_row, 1), pl.ds(pl.multiple_of((index % per_row) * 256, 256), 256)] = total
            s.rest[:, up_cols] = dot(first_t[...], dz[:, cols]).astype(BF16)
            s.rest[:, down_cols] = dot(dy_t[...], act[:, cols]).astype(BF16)
            return carry

        lax.fori_loop(0, hidden // 256, tile, 0)
        grad = s.grad
        for cols in chunks(width):
            grad[0, :, cols] = dot(dz[...], s.up[cols, :], ((1,), (1,)))
        s.grad_done = copies.remote(grad.at[0], s.grad_in.at[0], other_core)
        for cols in chunks(width):
            grad[1, :, cols] = dot(act[...], s.down[cols, :], ((1,), (1,)))
        s.y_done = copies.remote(grad.at[1], s.grad_in.at[1], other_core)
    for s in streams:
        tokens, width = s.x.shape
        small, sums = s.small, s.sums
        s.grad_done.wait()
        for rows in chunks(tokens):
            normed, inv = normalise(s.mid[rows, :])
            second = s.grad[0, rows, :] + s.grad_in[0, rows, :]
            scaled = second * small[1:2]
            dy = s.dy[rows, :].astype(F32)
            dmid = dy + inv * (
                scaled
                - jnp.mean(scaled, axis=-1, keepdims=True)
                - normed * jnp.mean(scaled * normed, axis=-1, keepdims=True)
            )
            s.dmid[rows, :] = dmid
            sums[1:2] += jnp.sum(second * normed, axis=0, keepdims=True)
            sums[3:4] += jnp.sum(dmid, axis=0, keepdims=True)
            sums[4:5] += jnp.sum(second, axis=0, keepdims=True)
            sums[5:6] += jnp.sum(dy, axis=0, keepdims=True)
            low = dmid.astype(BF16)
            s.first_t[:, rows] = jnp.transpose(low)
            s.do[rows, :] = dot(low, s.proj[...])
        write_grad_o(s.do, s.do_mine, s.heads)
        s.do_done = send_blocks(copies, at, s.do_mine, s.do_out)
        s.rest[:, : s.proj.shape[1]] = dot(s.first_t[...], s.mixed[...]).astype(BF16)
        s.y_done.wait()
        for rows in chunks(tokens):
            s.y[rows, :] = (
                s.mid[rows, :] + s.grad[1, rows, :] + s.grad_in[1, rows, :] + small[5:6]
            ).astype(BF16)
    for s in streams:
        for copy in s.do_done:
            copy.wait()


def middle(streams):
    vmem, hbm = pl.BlockSpec(memory_space=pltpu.VMEM), pl.BlockSpec(memory_space=pl.ANY)
    out_shape, out_specs, scratch = [], [], []
    for o, x, dy, small, proj, up, down in streams:
        tokens, width = x.shape
        hidden, own = up.shape[1], proj.shape[1]
        out_shape += [
            jax.ShapeDtypeStruct((tokens, width), BF16),
            jax.ShapeDtypeStruct((tokens, width), F32),
            jax.ShapeDtypeStruct(o.shape, BF16),
            jax.ShapeDtypeStruct((width, own + 2 * hidden), BF16),
            jax.ShapeDtypeStruct(small.shape, F32),
        ]
        out_specs += [vmem, vmem, hbm, vmem, vmem]
        scratch += [
            pltpu.VMEM(proj.shape, BF16),
            pltpu.VMEM(up.shape, BF16),
            pltpu.VMEM(down.shape, BF16),
            pltpu.VMEM(o.shape, BF16),
            pltpu.VMEM((tokens, own), BF16),
            pltpu.VMEM((tokens, width), F32),
            pltpu.VMEM((tokens, width), F32),
            pltpu.VMEM((tokens, width), F32),
            pltpu.VMEM((width, tokens), BF16),
            pltpu.VMEM((width, tokens), BF16),
            pltpu.VMEM((tokens, hidden), BF16),
            pltpu.VMEM((tokens, hidden), BF16),
            pltpu.VMEM((2, tokens, width), F32),
            pltpu.VMEM((2, tokens, width), F32),
            pltpu.VMEM((tokens, own), F32),
            pltpu.VMEM(o.shape, BF16),
        ]
    results = pl.pallas_call(
        middle_kernel,
        out_shape=out_shape,
        in_specs=([vmem] * 4 + [hbm] * 3) * 2,
        out_specs=out_specs,
        scratch_shapes=scratch + copy_sems(2 * 9, 2 * 5),
        compiler_params=pltpu.CompilerParams(
            collective_id=1, has_side_effects=True, vmem_limit_bytes=63 << 20
        ),
        name="middle",
    )(*streams[0], *streams[1])
    return results[:5], results[5:]


STEP = 384


def by_columns(columns, body):
    def one(index, carry):
        body(pl.ds(pl.multiple_of(index * STEP, STEP), STEP))
        return carry

    lax.fori_loop(0, columns // STEP, one, 0)


class Reduce:
    BUFFERS = 11

    def __init__(self, copies, at, src, buffers):
        self.copies, self.at = copies, at
        (
            self.own, self.pass_top, self.pass_low, self.in_x, self.in_y, self.in_top, self.in_low,
            self.total, self.half_out, self.quarter_out, self.final,
        ) = buffers[: self.BUFFERS]
        self.half_in, self.quarter_in = buffers[self.BUFFERS :]
        rows, self.columns = self.final.shape
        self.rows, half = rows, rows // 2
        self.half = half

        def block(owner, offset, size):
            return src.at[pl.ds(pl.multiple_of(owner * rows + offset, 8), size), :]

        self.loads = [
            copies.local(block(at.group_y, 0, half), self.pass_top),
            copies.local(block(at.group_x, half, half), self.pass_low),
            copies.local(block(at.group, 0, rows), self.own),
        ]
        self.first = [
            copies.remote(block(at.group_far, 0, half), self.in_x.at[1], at.to_x),
            copies.remote(block(at.group_far, half, half), self.in_y.at[1], at.to_y),
            copies.remote(block(at.group_x, 0, half), self.in_x.at[0], at.to_x),
            copies.remote(block(at.group_y, half, half), self.in_y.at[0], at.to_y),
        ]

    def cross(self):
        self.loads[0].wait()
        self.first[0].wait_recv()

        def top(cols):
            self.pass_top[:, cols] = (
                self.pass_top[:, cols].astype(F32) + self.in_x[1, :, cols].astype(F32)
            ).astype(BF16)

        by_columns(self.columns, top)
        self.second = [self.copies.remote(self.pass_top, self.in_top, self.at.to_y)]
        self.loads[1].wait()
        self.first[1].wait_recv()

        def low(cols):
            self.pass_low[:, cols] = (
                self.pass_low[:, cols].astype(F32) + self.in_y[1, :, cols].astype(F32)
            ).astype(BF16)

        by_columns(self.columns, low)
        self.second.append(self.copies.remote(self.pass_low, self.in_low, self.at.to_x))

    def along(self):
        half = self.half
        self.loads[2].wait()
        self.first[2].wait_recv()
        self.first[3].wait_recv()
        self.second[0].wait_recv()
        self.second[1].wait_recv()

        def plane(cols):
            self.total[:half, cols] = (
                self.own[:half, cols].astype(F32)
                + self.in_x[0, :, cols].astype(F32)
                + self.in_top[:, cols].astype(F32)
            )
            self.total[half:, cols] = (
                self.own[half:, cols].astype(F32)
                + self.in_y[0, :, cols].astype(F32)
                + self.in_low[:, cols].astype(F32)
            )

        by_columns(self.columns, plane)
        self.keep = pl.ds(pl.multiple_of(self.at.here_low * half, 8), half)
        give = pl.ds(pl.multiple_of((1 - self.at.here_low) * half, 8), half)

        def send(cols):
            self.half_out[:, cols] = self.total[give, cols].astype(BF16)

        by_columns(self.columns, send)
        self.third = self.copies.remote(self.half_out, self.half_in, self.at.to_ctx[1])

    def along_far(self):
        quarter = self.half // 2
        self.third.wait_recv()
        base = self.at.here_low * self.half
        mine = pl.ds(pl.multiple_of(self.at.here_high * quarter, 8), quarter)
        other = pl.ds(pl.multiple_of((1 - self.at.here_high) * quarter, 8), quarter)
        self.keep_low = pl.ds(pl.multiple_of(base + self.at.here_high * quarter, 8), quarter)
        give = pl.ds(pl.multiple_of(base + (1 - self.at.here_high) * quarter, 8), quarter)

        def send(cols):
            self.quarter_out[:, cols] = (
                self.total[give, cols] + self.half_in[other, cols].astype(F32)
            ).astype(BF16)

        by_columns(self.columns, send)
        self.fourth = self.copies.remote(self.quarter_out, self.quarter_in, self.at.to_ctx[2])
        self.mine = mine

    def back_far(self):
        self.fourth.wait_recv()

        def add(cols):
            self.final[self.keep_low, cols] = (
                self.total[self.keep_low, cols]
                + self.half_in[self.mine, cols].astype(F32)
                + self.quarter_in[:, cols].astype(F32)
            ).astype(BF16)

        by_columns(self.columns, add)
        rows = self.final.at[self.keep_low, :]
        self.fifth = self.copies.remote(rows, rows, self.at.to_ctx[2])

    def back_near(self):
        self.fifth.wait_recv()
        rows = self.final.at[self.keep, :]
        self.sixth = self.copies.remote(rows, rows, self.at.to_ctx[1])

    def finish(self):
        self.sixth.wait_recv()
        for copy in self.first + self.second + [self.third, self.fourth, self.fifth, self.sixth]:
            copy.wait_send()

    @staticmethod
    def scratch(rows, columns):
        half, quarter = rows // 2, rows // 4
        return [
            pltpu.VMEM((rows, columns), BF16),
            pltpu.VMEM((half, columns), BF16),
            pltpu.VMEM((half, columns), BF16),
            pltpu.VMEM((2, half, columns), BF16),
            pltpu.VMEM((2, half, columns), BF16),
            pltpu.VMEM((half, columns), BF16),
            pltpu.VMEM((half, columns), BF16),
            pltpu.VMEM((rows, columns), F32),
            pltpu.VMEM((half, columns), BF16),
            pltpu.VMEM((quarter, columns), BF16),
        ]

    @staticmethod
    def scratch_in(rows, columns):
        return [pltpu.VMEM((rows // 2, columns), BF16), pltpu.VMEM((rows // 4, columns), BF16)]


def take_dqkv(got, out, at, heads):
    tokens, width = out.shape[0], heads * HD

    def put(which, tile, rows, low, high):
        start = which * width + tile * LANES
        out[rows, start : start + LANES] = lane_pair(low, high).astype(BF16)

    every = slice(None)
    if heads == 4:
        half = tokens // 2
        top, low, keys = slice(0, half), slice(half, tokens), slice(half, half + tokens)
        for tile in range(2):
            one, two = 2 * tile, 2 * tile + 1
            for side, rows in ((0, top), (1, low)):
                put(0, tile, rows, (as_f32(got, one, top), side), (as_f32(got, two, top), side))
            for which in (1, 2):
                side = which - 1
                put(which, tile, every, (as_f32(got, one, keys), side), (as_f32(got, two, keys), side))
        return

    def part(position, index):
        return got[position, index].astype(F32)

    for tile in range(2):
        one, two = 2 * tile, 2 * tile + 1
        put(0, tile, every, (part(one, 0), 0), (part(two, 0), 0))
        put(1, tile, every, (part(one, 1), 0), (part(two, 1), 0))
        put(2, tile, every, (part(one, 1), 1), (part(two, 1), 1))
    put(0, 2, every, (part(at.here_high, 0), 1), (part(at.here_high + 2, 0), 1))
    one, two = part(0, 2) + part(1, 2), part(2, 2) + part(3, 2)
    put(1, 2, every, (one, 1), (two, 1))
    put(2, 2, every, (one, 0), (two, 0))


LAST_IN, LAST_OUT, LAST_SCRATCH = 8, 4, 9


def last_kernel(*refs):
    at = partners()
    ins = [refs[:LAST_IN], refs[LAST_IN : 2 * LAST_IN]]
    refs = refs[2 * LAST_IN :]
    outs = [refs[:LAST_OUT], refs[LAST_OUT : 2 * LAST_OUT]]
    refs = refs[2 * LAST_OUT :]
    count = LAST_SCRATCH + 2 * 12
    scratch = [refs[:count], refs[count : 2 * count]]
    copies = Copies(*refs[2 * count :])
    meet([at.to_x, at.to_y] + at.to_ctx[1:] + [at.to_core])
    streams = []
    for in_refs, out_refs, own in zip(ins, outs, scratch):
        s = Bag()
        s.back, s.first_in, s.x_in, s.small, s.weight_in, s.dmid_in, s.rest, s.sums_in = in_refs
        s.grad_rows, s.sums, rest_final, qkv_final = out_refs
        (
            s.got, s.dqkv, s.weight, s.first, s.x, s.dmid, s.part, s.part_in, s.g_qkv,
        ) = own[:LAST_SCRATCH]
        rest_buffers = list(own[LAST_SCRATCH : LAST_SCRATCH + 12])
        s.qkv_buffers = list(own[LAST_SCRATCH + 12 :])
        rest_buffers.insert(10, rest_final)
        s.qkv_buffers.insert(10, qkv_final)
        s.heads = s.weight.shape[2] // HD
        s.back_done = send_blocks(copies, at, s.back, s.got)
        s.loads = [
            copies.local(src, dst)
            for src, dst in (
                (s.weight_in, s.weight), (s.first_in, s.first), (s.x_in, s.x), (s.dmid_in, s.dmid),
            )
        ]
        s.rest_buffers = rest_buffers
        streams.append(s)
    for s in streams:
        s.reduce_rest = Reduce(copies, at, s.rest, s.rest_buffers)
    for s in streams:
        tokens, width = s.x.shape
        own = s.heads * HD
        for copy in s.back_done:
            copy.wait()
        for copy in s.loads:
            copy.wait()
        take_dqkv(s.got, s.dqkv, at, s.heads)
        for cols in chunks(width):
            total = dot(s.dqkv[:, :own], s.weight[0, cols, :], ((1,), (1,)))
            total = total + dot(s.dqkv[:, own : 2 * own], s.weight[1, cols, :], ((1,), (1,)))
            s.part[:, cols] = total + dot(s.dqkv[:, 2 * own :], s.weight[2, cols, :], ((1,), (1,)))
        s.part_done = copies.remote(s.part, s.part_in, at.to_core)
        for which in range(3):
            cols = slice(which * own, (which + 1) * own)
            s.g_qkv[:, cols] = dot(s.first[...], s.dqkv[:, cols]).astype(BF16)
        s.reduce_qkv = Reduce(copies, at, s.g_qkv, s.qkv_buffers)
        s.sums[...] = s.sums_in[...]
        s.sums[6:7, :own] = jnp.sum(s.dqkv[:, :own].astype(F32), axis=0, keepdims=True)
        s.sums[6:7, own:] = jnp.sum(s.dqkv[:, 2 * own :].astype(F32), axis=0, keepdims=True)
        s.reduce_rest.cross()
    for s in streams:
        tokens, width = s.x.shape
        s.part_done.wait()
        for rows in chunks(tokens):
            normed, inv = normalise(s.x[rows, :].astype(F32))
            first = s.part[rows, :] + s.part_in[rows, :]
            scaled = first * s.small[0:1]
            s.grad_rows[rows, :] = s.dmid[rows, :] + inv * (
                scaled
                - jnp.mean(scaled, axis=-1, keepdims=True)
                - normed * jnp.mean(scaled * normed, axis=-1, keepdims=True)
            )
            s.sums[0:1] += jnp.sum(first * normed, axis=0, keepdims=True)
            s.sums[2:3] += jnp.sum(first, axis=0, keepdims=True)
        s.reduce_rest.along()
    for s in streams:
        s.reduce_qkv.cross()
    for s in streams:
        s.reduce_rest.along_far()
    for s in streams:
        s.reduce_qkv.along()
    for s in streams:
        s.reduce_rest.back_far()
    for s in streams:
        s.reduce_qkv.along_far()
    for s in streams:
        s.reduce_rest.back_near()
    for s in streams:
        s.reduce_qkv.back_far()
    for s in streams:
        s.reduce_qkv.back_near()
    for s in streams:
        s.reduce_rest.finish()
    for s in streams:
        s.reduce_qkv.finish()


def last(streams):
    vmem, hbm = pl.BlockSpec(memory_space=pltpu.VMEM), pl.BlockSpec(memory_space=pl.ANY)
    out_shape, scratch = [], []
    for back, first, x, small, weight, dmid, rest, sums in streams:
        tokens, width = x.shape
        own = weight.shape[2]
        rest_shape, qkv_shape = (width // 4, rest.shape[1]), (width // 4, 3 * own)
        out_shape += [
            jax.ShapeDtypeStruct((tokens, width), F32),
            jax.ShapeDtypeStruct(small.shape, F32),
            jax.ShapeDtypeStruct(rest_shape, BF16),
            jax.ShapeDtypeStruct(qkv_shape, BF16),
        ]
        scratch += [
            pltpu.VMEM(back.shape, BF16),
            pltpu.VMEM((tokens, 3 * own), BF16),
            pltpu.VMEM(weight.shape, BF16),
            pltpu.VMEM(first.shape, BF16),
            pltpu.VMEM((tokens, width), BF16),
            pltpu.VMEM((tokens, width), F32),
            pltpu.VMEM((tokens, width), F32),
            pltpu.VMEM((tokens, width), F32),
            pltpu.VMEM((width, 3 * own), BF16),
        ]
        for shape in (rest_shape, qkv_shape):
            scratch += Reduce.scratch(*shape) + Reduce.scratch_in(*shape)
    results = pl.pallas_call(
        last_kernel,
        out_shape=out_shape,
        in_specs=[hbm, hbm, hbm, vmem, hbm, hbm, hbm, vmem] * 2,
        out_specs=[vmem] * 8,
        scratch_shapes=scratch + copy_sems(2 * (3 + 1 + 2 * 10), 2 * (1 + 4 + 2 * 3)),
        compiler_params=pltpu.CompilerParams(
            collective_id=2, has_side_effects=True, vmem_limit_bytes=63 << 20
        ),
        name="last",
    )(*streams[0], *streams[1])
    return results[:4], results[4:]


def finish_kernel(*refs):
    ins = [refs[:3], refs[3:6]]
    outs = [refs[6:13], refs[13:]]
    for (sums, rest, qkv), (gains, shifts, bias, qkv_out, proj, up, down) in zip(ins, outs):
        gains[...] = sums[0:2]
        shifts[...] = sums[2:6]
        bias[...] = sums[6:9]
        own = qkv.shape[1] // 3
        for which in range(3):
            qkv_out[which] = qkv[:, which * own : (which + 1) * own].astype(F32)
        hidden = up.shape[1]
        up[...] = rest[:, own : own + hidden].astype(F32)
        if down.shape[0] > down.shape[1]:
            proj[...] = jnp.transpose(rest[:, :own].astype(F32))
            down[...] = jnp.transpose(rest[:, own + hidden :].astype(F32))
        else:
            proj[...] = rest[:, :own].astype(F32)
            down[...] = rest[:, own + hidden :].astype(F32)


def finish(streams):
    out_shape = []
    for sums, rest, qkv, flip in streams:
        rows, own = qkv.shape[0], qkv.shape[1] // 3
        hidden = (rest.shape[1] - own) // 2
        shapes = [(2, 4 * rows), (4, 4 * rows), (3, 4 * rows), (3, rows, own)]
        shapes += [(own, rows), (rows, hidden), (hidden, rows)] if flip else [
            (rows, own), (rows, hidden), (rows, hidden)
        ]
        out_shape += [jax.ShapeDtypeStruct(shape, F32) for shape in shapes]
    results = pl.pallas_call(finish_kernel, out_shape=out_shape, name="finish")(
        *streams[0][:3], *streams[1][:3]
    )
    return results[:7], results[7:]


def own_columns(array):
    columns = array.shape[1] // 4
    return lax.dynamic_slice_in_dim(array, lax.axis_index(FSDP) * columns, columns, 1)


def on_device(*args):
    streams = []
    for item, causal in ((args[10:], True), (args[:10], False)):
        s = Bag()
        rows, s.segrow, cotangent, gains, shifts, head_bias, s.qkv, proj, s.up, down = item
        s.causal, s.x, s.dy = causal, rows[0], cotangent[0]
        s.segcol = s.segrow.reshape(-1, 1)
        s.bounds = block_bounds(s.segrow[0], causal)
        s.small = place_small(gains, shifts, head_bias)
        s.down, s.proj = (down, proj) if causal else (down.T, proj.T)
        streams.append(s)
    started = front([(s.x, s.small, s.qkv, s.up, s.down, s.proj) for s in streams])
    for s, (weight, small, first, messages, *rest) in zip(streams, started):
        s.weight, s.small, s.first, s.messages, s.weights = weight, small, first, messages, rest
        s.o, s.lse = attend(s.causal, s.bounds, messages, s.segcol, s.segrow)
    done = middle([(s.o, s.x, s.dy, s.small, *s.weights[:1], *s.weights[1:]) for s in streams])
    for s, (y, dmid, do, rest, sums) in zip(streams, done):
        s.y, s.dmid, s.rest, s.sums = y, dmid, rest, sums
        s.back = attend_back(
            s.causal, s.bounds, s.messages, do, s.o, s.lse, s.segcol, s.segrow
        )
    ended = last(
        [(s.back, s.first, s.x, s.small, s.weight, s.dmid, s.rest, s.sums) for s in streams]
    )
    totals = reduce_small(jnp.concatenate([sums for _, sums, _, _ in ended], axis=1))
    cut = streams[0].x.shape[1]
    final = finish(
        [
            (total, rest, qkv, s.causal)
            for s, total, (_, _, rest, qkv) in zip(
                streams, (totals[:, :cut], totals[:, cut:]), ended
            )
        ]
    )
    outputs = []
    for s, (grad_rows, *_), (gains, shifts, bias, qkv, proj, up, down) in zip(streams, ended, final):
        if not s.causal:
            proj, down = proj.T, down.T
        outputs.append(
            (
                s.y[None],
                grad_rows[None],
                own_columns(gains),
                own_columns(shifts),
                own_columns(bias.reshape(1, -1)),
                qkv,
                proj,
                up,
                down,
            )
        )
    return outputs[1] + outputs[0]


def layer_stats(rows):
    row_mean = jnp.mean(rows, axis=-1, keepdims=True)
    centred = rows - row_mean
    inv_std = lax.rsqrt(jnp.mean(centred * centred, axis=-1, keepdims=True) + 1e-05)
    return (centred * inv_std, inv_std)


def norm_back(grad_normed_out, normed, inv_std, gain):
    scaled = grad_normed_out * gain
    return inv_std * (
        scaled
        - jnp.mean(scaled, axis=-1, keepdims=True)
        - normed * jnp.mean(scaled * normed, axis=-1, keepdims=True)
    )


def tensor_psum(partial_rows):
    return lax.psum(partial_rows, TP)


def any_mesh_block(
    rows_in,
    seg_row,
    cotangent,
    gains,
    shifts,
    head_bias,
    qkv_weight,
    proj_weight,
    up_weight,
    down_weight,
    causal,
):
    gain_full, shift_full, bias_full, qkv_full, proj_full, up_full, down_full = (
        lax.all_gather(gains, FSDP, axis=1, tiled=True),
        lax.all_gather(shifts, FSDP, axis=1, tiled=True),
        lax.all_gather(head_bias, FSDP, axis=1, tiled=True),
        lax.all_gather(qkv_weight, FSDP, axis=1, tiled=True),
        lax.all_gather(proj_weight, FSDP, axis=1, tiled=True),
        lax.all_gather(up_weight, FSDP, axis=0, tiled=True),
        lax.all_gather(down_weight, FSDP, axis=1, tiled=True),
    )
    gain_vals = gain_full.astype(jnp.float32)
    shift_vals = shift_full.astype(jnp.float32)
    bias_vals = bias_full[0].astype(jnp.float32)
    tp_width = qkv_full.shape[2]
    local_rows = rows_in.shape[1]
    seq_length = seg_row.shape[1]
    head_local = tp_width // HD
    rows = rows_in[0].astype(jnp.float32)
    row_start = lax.axis_index(CTX) * local_rows
    seg_all = seg_row[0]
    seg_query = lax.dynamic_slice_in_dim(seg_all, row_start, local_rows)
    query_pos = row_start + jnp.arange(local_rows, dtype=jnp.int32)
    key_pos = jnp.arange(seq_length, dtype=jnp.int32)
    allowed = seg_query[:, None] == seg_all[None, :]
    if causal:
        allowed = jnp.logical_and(allowed, key_pos[None, :] <= query_pos[:, None])

    def to_heads(matrix):
        return matrix.reshape(matrix.shape[0], head_local, HD).transpose(1, 0, 2)

    def from_heads(stacked):
        return stacked.transpose(1, 0, 2).reshape(stacked.shape[1], head_local * HD)

    normed_one, inv_one = layer_stats(rows)
    first_in = (normed_one * gain_vals[0] + shift_vals[0]).astype(jnp.bfloat16)
    queries = (
        jnp.dot(first_in, qkv_full[0], preferred_element_type=jnp.float32) + bias_vals[:tp_width]
    ).astype(jnp.bfloat16)
    key_rows = jnp.dot(first_in, qkv_full[1], preferred_element_type=jnp.float32).astype(
        jnp.bfloat16
    )
    values = (
        jnp.dot(first_in, qkv_full[2], preferred_element_type=jnp.float32)
        + bias_vals[tp_width : 2 * tp_width]
    ).astype(jnp.bfloat16)
    key_all, value_all = (
        lax.all_gather(key_rows, CTX, axis=0, tiled=True),
        lax.all_gather(values, CTX, axis=0, tiled=True),
    )
    query_heads = to_heads(queries)
    key_heads = to_heads(key_all)
    value_heads = to_heads(value_all)

    def attend(head_items):
        query_h, key_h, value_h = head_items
        scores = dot(query_h, key_h, ((1,), (1,))) * 0.125
        scores = jnp.where(allowed, scores, -1e30)
        row_top = jnp.max(scores, axis=-1, keepdims=True)
        weights = jnp.exp(scores - row_top)
        row_total = jnp.sum(weights, axis=-1, keepdims=True)
        weights_low = (weights / row_total).astype(jnp.bfloat16)
        mixed_h = dot(weights_low, value_h, ((1,), (0,)))
        return (mixed_h.astype(jnp.bfloat16), row_top[:, 0] + jnp.log(row_total[:, 0]))

    mixed_heads, log_totals = lax.map(attend, (query_heads, key_heads, value_heads))
    mixed = from_heads(mixed_heads)
    middle = (
        rows
        + tensor_psum(jnp.dot(mixed, proj_full, preferred_element_type=jnp.float32))
        + shift_vals[1]
    )
    normed_two, inv_two = layer_stats(middle)
    second_in = (normed_two * gain_vals[1] + shift_vals[2]).astype(jnp.bfloat16)
    hidden = (
        jnp.dot(second_in, up_full, preferred_element_type=jnp.float32) + bias_vals[2 * tp_width :]
    )
    sigma = jax.nn.sigmoid(1.702 * hidden)
    activated = (hidden * sigma).astype(jnp.bfloat16)
    output = (
        middle
        + tensor_psum(jnp.dot(activated, down_full, preferred_element_type=jnp.float32))
        + shift_vals[3]
    )
    grad_out = cotangent[0].astype(jnp.float32)
    grad_down_bias = jnp.sum(grad_out, axis=0)
    grad_branch = grad_out.astype(jnp.bfloat16)
    grad_down = dot(activated, grad_branch, ((0,), (0,)))
    grad_act = dot(grad_branch, down_full, ((1,), (1,)))
    grad_hidden = (grad_act * (sigma + 1.702 * hidden * sigma * (1.0 - sigma))).astype(jnp.bfloat16)
    grad_up_bias = jnp.sum(grad_hidden.astype(jnp.float32), axis=0)
    grad_up = dot(second_in, grad_hidden, ((0,), (0,)))
    grad_second = tensor_psum(
        dot(grad_hidden, up_full, ((1,), (1,)))
    )
    grad_gain_two = jnp.sum(grad_second * normed_two, axis=0)
    grad_shift_two = jnp.sum(grad_second, axis=0)
    grad_middle = grad_out + norm_back(grad_second, normed_two, inv_two, gain_vals[1])
    grad_proj_bias = jnp.sum(grad_middle, axis=0)
    grad_attn = grad_middle.astype(jnp.bfloat16)
    grad_proj = dot(mixed, grad_attn, ((0,), (0,)))
    grad_mixed = dot(grad_attn, proj_full, ((1,), (1,))).astype(jnp.bfloat16)

    def attend_back(head_items):
        query_h, key_h, value_h, grad_h, log_total = head_items
        scores = dot(query_h, key_h, ((1,), (1,))) * 0.125
        weights = jnp.where(allowed, jnp.exp(scores - log_total[:, None]), 0.0)
        grad_weights = dot(grad_h, value_h, ((1,), (1,)))
        row_delta = jnp.sum(weights * grad_weights, axis=-1, keepdims=True)
        grad_scores = (weights * (grad_weights - row_delta)).astype(jnp.bfloat16)
        grad_query_h = (
            dot(grad_scores, key_h, ((1,), (0,))) * 0.125
        )
        grad_key_h = (
            dot(grad_scores, query_h, ((0,), (0,)))
            * 0.125
        )
        grad_value_h = dot(weights.astype(jnp.bfloat16), grad_h, ((0,), (0,)))
        return (grad_query_h, grad_key_h, grad_value_h)

    query_parts, key_parts, value_parts = lax.map(
        attend_back, (query_heads, key_heads, value_heads, to_heads(grad_mixed), log_totals)
    )
    key_sum, value_sum = (
        lax.psum_scatter(from_heads(key_parts), CTX, scatter_dimension=0, tiled=True),
        lax.psum_scatter(from_heads(value_parts), CTX, scatter_dimension=0, tiled=True),
    )
    grad_query = from_heads(query_parts).astype(jnp.bfloat16)
    grad_key = key_sum.astype(jnp.bfloat16)
    grad_value = value_sum.astype(jnp.bfloat16)
    grad_qkv = jnp.stack(
        [
            dot(first_in, grad_query, ((0,), (0,))),
            dot(first_in, grad_key, ((0,), (0,))),
            dot(first_in, grad_value, ((0,), (0,))),
        ]
    )
    grad_head = jnp.concatenate(
        [
            jnp.sum(grad_query.astype(jnp.float32), axis=0),
            jnp.sum(grad_value.astype(jnp.float32), axis=0),
            grad_up_bias,
        ]
    )[None, :]
    grad_first_part = dot(grad_query, qkv_full[0], ((1,), (1,)))
    grad_first_part = grad_first_part + dot(grad_key, qkv_full[1], ((1,), (1,)))
    grad_first_part = grad_first_part + dot(grad_value, qkv_full[2], ((1,), (1,)))
    grad_first = tensor_psum(grad_first_part)
    grad_gain_one = jnp.sum(grad_first * normed_one, axis=0)
    grad_shift_one = jnp.sum(grad_first, axis=0)
    grad_rows = grad_middle + norm_back(grad_first, normed_one, inv_one, gain_vals[0])
    grad_gains = jnp.stack([grad_gain_one, grad_gain_two])
    grad_shifts = jnp.stack([grad_shift_one, grad_proj_bias, grad_shift_two, grad_down_bias])
    share_gains, share_shifts, share_head, share_qkv, share_proj, share_up, share_down = (
        lax.psum_scatter(grad_gains, FSDP, scatter_dimension=1, tiled=True),
        lax.psum_scatter(grad_shifts, FSDP, scatter_dimension=1, tiled=True),
        lax.psum_scatter(grad_head, FSDP, scatter_dimension=1, tiled=True),
        lax.psum_scatter(grad_qkv, FSDP, scatter_dimension=1, tiled=True),
        lax.psum_scatter(grad_proj, FSDP, scatter_dimension=1, tiled=True),
        lax.psum_scatter(grad_up, FSDP, scatter_dimension=0, tiled=True),
        lax.psum_scatter(grad_down, FSDP, scatter_dimension=1, tiled=True),
    )
    owned = lax.psum(
        (share_gains, share_shifts, share_head, share_qkv, share_proj, share_up, share_down), CTX
    )
    return (output.astype(jnp.bfloat16)[None], grad_rows[None]) + tuple(owned)


def on_any_mesh(
    image_input,
    image_segments,
    image_cotangent,
    image_gains,
    image_shifts,
    image_head_bias,
    image_qkv_weight,
    image_proj_weight,
    image_up_weight,
    image_down_weight,
    text_input,
    text_segments,
    text_cotangent,
    text_gains,
    text_shifts,
    text_head_bias,
    text_qkv_weight,
    text_proj_weight,
    text_up_weight,
    text_down_weight,
):
    image_results = any_mesh_block(
        image_input,
        image_segments,
        image_cotangent,
        image_gains,
        image_shifts,
        image_head_bias,
        image_qkv_weight,
        image_proj_weight,
        image_up_weight,
        image_down_weight,
        False,
    )
    text_results = any_mesh_block(
        text_input,
        text_segments,
        text_cotangent,
        text_gains,
        text_shifts,
        text_head_bias,
        text_qkv_weight,
        text_proj_weight,
        text_up_weight,
        text_down_weight,
        True,
    )
    return image_results + text_results


def stream_specs():
    return (
        P(FSDP, CTX, None),
        P(FSDP, None),
        P(FSDP, CTX, None),
        P(None, FSDP),
        P(None, FSDP),
        P(TP, FSDP),
        P(None, FSDP, TP),
        P(TP, FSDP),
        P(FSDP, TP),
        P(TP, FSDP),
    )


def solution(mesh):
    one = stream_specs()
    grads = (one[0], one[0]) + one[3:]
    body = on_device
    if (mesh.shape[FSDP], mesh.shape[CTX], mesh.shape[TP]) != (4, 4, 2):
        body = on_any_mesh
    return jax.shard_map(
        body, mesh=mesh, in_specs=one + one, out_specs=grads + grads, check_vma=False
    )
```

```python
import functools

import jax
import jax.numpy as jnp
from jax import lax
from jax.experimental import pallas as pl
from jax.experimental.pallas import tpu as pltpu
from jax.sharding import PartitionSpec as P

HD = 64
LANES = 128
QB = 256
KB = 512
NEG = -1e30
F32 = jnp.float32
MESH = pl.DeviceIdType.MESH
FSDP, CTX, TP = "fsdp", "ctx", "tp"
BF16 = jnp.bfloat16


def dot(left, right, dims=((1,), (0,))):
    return lax.dot_general(left, right, (dims, ((), ())), preferred_element_type=F32)


def lane_marks():
    lane = lax.broadcasted_iota(jnp.int32, (1, LANES), 1)
    first = (lane < HD).astype(F32).astype(BF16)
    second = (lane >= HD).astype(F32).astype(BF16)
    return first, second


def document_columns(row_ref, out_ref):
    for start in range(0, out_ref.shape[0], LANES):
        row = row_ref[:, start : start + LANES].astype(F32)
        out_ref[start : start + LANES, :] = jnp.transpose(jnp.broadcast_to(row, (LANES, LANES)))


def swap_halves(value):
    return pltpu.roll(value, HD, 1)


def key_range(index):
    return slice(index * KB, (index + 1) * KB)


def mix_rows(query, seg_query, keys, seg_keys, own, other, diagonal=None):
    query = query * own
    scores = []
    for block, seg in zip(keys, seg_keys):
        score = dot(query, block, ((1,), (1,)))
        ok = seg_query == seg.astype(F32)
        if diagonal is not None and len(scores) == len(keys) - 1:
            key_pos = lax.broadcasted_iota(jnp.int32, score.shape, 1)
            query_pos = diagonal + lax.broadcasted_iota(jnp.int32, score.shape, 0)
            ok = jnp.logical_and(ok, key_pos <= query_pos)
        scores.append(jnp.where(ok, score, NEG))
    top = jnp.max(functools.reduce(jnp.maximum, scores), axis=1, keepdims=True)
    acc = jnp.zeros((query.shape[0], LANES), F32)
    for score, block in zip(scores, keys):
        acc = acc + dot(jnp.exp(score - top).astype(BF16), block * other + own)
    return acc / swap_halves(acc), top + jnp.log(acc)


def attend_text(m, seg_col, seg_row, o, lse):
    first, second = lane_marks()
    lane = lax.broadcasted_iota(jnp.int32, (QB, LANES), 1)
    for source in range(4):
        keys = [m[i, QB:] for i in range(source + 1)]
        segs = [seg_row[:, key_range(i)] for i in range(source + 1)]
        parts = []
        for half in range(2):
            query = m[source, :QB]
            if half:
                query = swap_halves(query.astype(F32)).astype(BF16)
            start = source * KB + half * QB
            mixed, log_total = mix_rows(
                query, seg_col[start : start + QB, :1], keys, segs, first, second, half * QB
            )
            lse[2 * source + half, :8] = jnp.transpose(log_total)[:8]
            parts.append(mixed if half else swap_halves(mixed))
        o[source] = jnp.where(lane < HD, parts[0], parts[1]).astype(BF16)


def image_rows(block):
    source, half = block // 2, block % 2
    return (
        source,
        pl.ds(pl.multiple_of(half * QB, QB), QB),
        pl.ds(pl.multiple_of(block * QB, QB), QB),
    )


def attend_image(at, m, seg_col, seg_row, o, lse):
    first, second = lane_marks()
    lane = lax.broadcasted_iota(jnp.int32, (QB, LANES), 1)
    segs = [seg_row[:, key_range(i)] for i in range(4)]
    o[...] = jnp.zeros_like(o)

    def extra(index, carry):
        block = at.here_low * 4 + index
        source, rows, tokens = image_rows(block)
        mixed, log_total = mix_rows(
            m[source, 0, rows], seg_col[tokens, :1], [m[i, 2] for i in range(4)], segs, second, first
        )
        lse[block, 8:] = jnp.transpose(log_total)[HD : HD + 8]
        o[source, rows] = mixed.astype(BF16)
        return carry

    lax.fori_loop(0, 4, extra, 0)

    def main(block, carry):
        source, rows, tokens = image_rows(block)
        mixed, log_total = mix_rows(
            m[source, 0, rows], seg_col[tokens, :1], [m[i, 1] for i in range(4)], segs, first, second
        )
        lse[block, :8] = jnp.transpose(log_total)[:8]
        o[source, rows] = jnp.where(lane < HD, o[source, rows], mixed.astype(BF16))
        return carry

    lax.fori_loop(0, 8, main, 0)


def unmix_rows(query, grad_o, seg_query, keys, seg_keys, totals, lse, delta, own, other, diagonal=None):
    query, grad_o = query * own, grad_o * other
    grad_query = jnp.zeros((query.shape[0], LANES), F32)
    for index, (block, seg, (total, rows)) in enumerate(zip(keys, seg_keys, totals)):
        score = dot(block, query, ((1,), (1,)))
        ok = seg == seg_query
        if diagonal is not None and index == len(keys) - 1:
            key_pos = lax.broadcasted_iota(jnp.int32, score.shape, 0)
            query_pos = diagonal + lax.broadcasted_iota(jnp.int32, score.shape, 1)
            ok = jnp.logical_and(ok, key_pos <= query_pos)
        weights = jnp.where(ok, jnp.exp(score - lse), 0.0)
        grad_weights = dot(block, grad_o, ((1,), (1,)))
        grad_scores = (weights * (grad_weights - delta)).astype(BF16)
        total[rows, :] += dot(grad_scores, query) + dot(weights.astype(BF16), grad_o)
        grad_query = grad_query + dot(grad_scores, block, ((0,), (0,)))
    return grad_query * 0.125


def unattend_text(m, do, o, lse, seg_col, seg_row, acc, out):
    first, second = lane_marks()
    lane = lax.broadcasted_iota(jnp.int32, (QB, LANES), 1)
    acc[...] = jnp.zeros_like(acc)
    for source in range(4):
        keys = [m[i, QB:] for i in range(source + 1)]
        segs = [seg_col[key_range(i), :1] for i in range(source + 1)]
        totals = [(acc, key_range(i)) for i in range(source + 1)]
        grads, mixed = do[source], o[source]
        product = jnp.transpose(grads.astype(F32) * mixed.astype(F32))
        parts = []
        for half in range(2):
            query, grad_o = m[source, :QB], grads
            if half:
                query = swap_halves(query.astype(F32)).astype(BF16)
            else:
                grad_o = swap_halves(grad_o.astype(F32)).astype(BF16)
            start = source * KB + half * QB
            grad_query = unmix_rows(
                query,
                grad_o,
                seg_row[:, start : start + QB].astype(F32),
                keys,
                segs,
                totals,
                lse[2 * source + half, :1],
                jnp.sum(product[half * HD : half * HD + HD], axis=0, keepdims=True),
                first,
                second,
                half * QB,
            )
            parts.append(swap_halves(grad_query) if half else grad_query)
        out[source, :QB] = jnp.where(lane < HD, parts[0], parts[1]).astype(BF16)
    for source in range(4):
        out[source, QB:] = acc[key_range(source)].astype(BF16)


def unattend_image(m, do, o, lse, seg_col, seg_row, acc, out, blocks, extra):
    first, second = lane_marks()
    lane = lax.broadcasted_iota(jnp.int32, (QB, LANES), 1)
    segs = [seg_col[key_range(i), :1] for i in range(4)]
    totals = [(acc, key_range(i)) for i in range(4)]

    def one(step, carry):
        block = blocks[0] + step
        source, rows, tokens = image_rows(block)
        grad_o = do[source, rows]
        product = jnp.transpose(grad_o.astype(F32) * o[source, rows].astype(F32))
        delta = jnp.sum(product[:HD] if extra else product[HD:], axis=0, keepdims=True)
        grad_query = unmix_rows(
            m[source, 0, rows],
            grad_o,
            seg_row[:, tokens].astype(F32),
            [m[i, 2 if extra else 1] for i in range(4)],
            segs,
            totals,
            lse[block, 8:9] if extra else lse[block, :1],
            delta,
            second if extra else first,
            first if extra else second,
        ).astype(BF16)
        if extra:
            out[source, 0, rows] = grad_query
        else:
            out[source, 0, rows] = jnp.where(lane < HD, grad_query, out[source, 0, rows])
        return carry

    lax.fori_loop(0, blocks[1], one, 0)


class Bag:
    pass


def partners():
    at = Bag()
    group, here, core = lax.axis_index(FSDP), lax.axis_index(CTX), lax.axis_index(TP)
    at.group, at.here = group, here
    at.group_x = group + 1 - 2 * (group % 2)
    at.group_y = group + 2 - 4 * (group // 2)
    at.group_far = 3 - group
    at.here_low, at.here_high = here % 2, here // 2
    at.ctx = (here, here + 1 - 2 * (here % 2), here + 2 - 4 * (here // 2), 3 - here)
    at.to_x, at.to_y, at.to_far = ({FSDP: g} for g in (at.group_x, at.group_y, at.group_far))
    at.to_ctx = [{CTX: c} for c in at.ctx]
    at.to_core = {TP: 1 - core}
    return at


def meet(devices):
    barrier = pltpu.get_barrier_semaphore()
    for device in devices:
        pl.semaphore_signal(barrier, inc=1, device_id=device, device_id_type=MESH)
    pl.semaphore_wait(barrier, len(devices))


class Copies:
    def __init__(self, send_sems, recv_sems, local_sems):
        self.sems = (send_sems, recv_sems, local_sems)
        self.used = [0, 0]

    def remote(self, src, dst, device):
        index = self.used[0]
        self.used[0] += 1
        copy = pltpu.make_async_remote_copy(
            src_ref=src,
            dst_ref=dst,
            send_sem=self.sems[0].at[index],
            recv_sem=self.sems[1].at[index],
            device_id=device,
            device_id_type=MESH,
        )
        copy.start()
        return copy

    def local(self, src, dst):
        index = self.used[1]
        self.used[1] += 1
        copy = pltpu.make_async_copy(src, dst, self.sems[2].at[index])
        copy.start()
        return copy


def copy_sems(remote, local):
    return [
        pltpu.SemaphoreType.DMA((remote,)),
        pltpu.SemaphoreType.DMA((remote,)),
        pltpu.SemaphoreType.DMA((local,)),
    ]


class Gather:
    def __init__(self, copies, at, src, dst):
        self.copies, self.at, self.dst = copies, at, dst
        self.rows = src.shape[-2]
        own = self.part(at.group, 0, self.rows)
        self.own = copies.local(src, own)
        self.to_x = copies.remote(src, own, at.to_x)
        self.to_y = copies.remote(src, own, at.to_y)

    def part(self, owner, offset, size):
        rows = pl.ds(pl.multiple_of(owner * self.rows + offset, 8), size)
        return self.dst.at[:, rows, :] if len(self.dst.shape) == 3 else self.dst.at[rows, :]

    def forward(self):
        half = self.rows // 2
        self.to_x.wait_recv()
        self.to_y.wait_recv()
        top = self.part(self.at.group_y, 0, half)
        low = self.part(self.at.group_x, half, half)
        self.far_x = self.copies.remote(top, top, self.at.to_x)
        self.far_y = self.copies.remote(low, low, self.at.to_y)

    def arrived(self):
        self.own.wait()
        self.far_x.wait_recv()
        self.far_y.wait_recv()

    def sent(self):
        for copy in (self.to_x, self.to_y, self.far_x, self.far_y):
            copy.wait_send()


def normalise(rows):
    mean = jnp.mean(rows, axis=-1, keepdims=True)
    centred = rows - mean
    inv = lax.rsqrt(jnp.mean(centred * centred, axis=-1, keepdims=True) + 1e-05)
    return centred * inv, inv


def lane_pair(low, high):
    lane = lax.broadcasted_iota(jnp.int32, low[0].shape, 1)
    left = low[0] if low[1] == 0 else pltpu.roll(low[0], HD, 1)
    right = high[0] if high[1] == 1 else pltpu.roll(high[0], HD, 1)
    return jnp.where(lane < HD, left, right)


def head_tile(ref, start, index, rows=slice(None)):
    first = start + (index // 2) * LANES
    return ref[rows, first : first + LANES], index % 2


def write_messages(qkv, out, heads):
    width = heads * HD
    tokens = qkv.shape[0]
    for c in range(4):
        if heads == 4:
            half = tokens // 2
            out[c, :half] = lane_pair(
                head_tile(qkv, 0, c, slice(0, half)), head_tile(qkv, 0, c, slice(half, None))
            ).astype(BF16)
            out[c, half:] = lane_pair(
                head_tile(qkv, width, c), head_tile(qkv, 2 * width, c)
            ).astype(BF16)
        else:
            e = 4 + c // 2
            out[c, 0] = lane_pair(head_tile(qkv, 0, c), head_tile(qkv, 0, e)).astype(BF16)
            out[c, 1] = lane_pair(
                head_tile(qkv, width, c), head_tile(qkv, 2 * width, c)
            ).astype(BF16)
            out[c, 2] = lane_pair(
                head_tile(qkv, 2 * width, e), head_tile(qkv, width, e)
            ).astype(BF16)


def message_shape(heads, tokens):
    part = (tokens // 2 + tokens, LANES) if heads == 4 else (3, tokens, LANES)
    return (4,) + part


def first_rows(x_ref, small_ref, weight_ref, first_ref, qkv_ref, step):
    width = weight_ref.shape[2]
    rows = slice(step * 256, step * 256 + 256)
    normed, _ = normalise(x_ref[rows, :].astype(F32))
    first = (normed * small_ref[0:1] + small_ref[2:3]).astype(BF16)
    first_ref[:, rows] = jnp.transpose(first)
    bias = small_ref[6:7]
    qkv_ref[rows, :width] = (dot(first, weight_ref[0]) + bias[:, :width]) * 0.125
    qkv_ref[rows, width : 2 * width] = dot(first, weight_ref[1])
    qkv_ref[rows, 2 * width :] = dot(first, weight_ref[2]) + bias[:, width : 2 * width]


def spread_small(at, gains, shifts, bias, wide, flat, out):
    width = wide.shape[1]
    columns, bias_columns = gains.shape[1], bias.shape[1]
    wide[...] = jnp.zeros_like(wide)
    flat[...] = jnp.zeros_like(flat)
    wide[0:2, :columns] = gains[...].astype(F32)
    wide[2:6, :columns] = shifts[...].astype(F32)
    flat[0:1, :bias_columns] = bias[...].astype(F32)
    out[0:8] = pltpu.roll(wide[...], at.group * columns, 1)
    line = pltpu.roll(flat[...], at.group * bias_columns, 1)
    out[8:16] = jnp.zeros((8, width), F32)
    for row in range(3):
        out[6 + row : 7 + row] = line[0:1, row * width : (row + 1) * width]


FRONT_IN, FRONT_OUT, FRONT_SCRATCH = 9, 9, 10


def front_kernel(*refs):
    at = partners()
    ins = [refs[:FRONT_IN], refs[FRONT_IN : 2 * FRONT_IN]]
    refs = refs[2 * FRONT_IN :]
    outs = [refs[:FRONT_OUT], refs[FRONT_OUT : 2 * FRONT_OUT]]
    refs = refs[2 * FRONT_OUT :]
    scratch = [refs[:FRONT_SCRATCH], refs[FRONT_SCRATCH : 2 * FRONT_SCRATCH]]
    copies = Copies(*refs[2 * FRONT_SCRATCH :])
    streams = []
    for in_refs, out_refs, own in zip(ins, outs, scratch):
        s = Bag()
        s.x, s.seg_row, s.gains, s.shifts, s.bias, s.qkv, s.up, s.down, s.proj = in_refs
        (
            s.weight, s.small, s.first, s.messages, s.proj_full, s.up_full, s.down_full, s.o, s.lse,
        ) = out_refs
        (
            s.small_in, s.small_own, s.wide, s.flat, s.rows, s.mine, s.got, s.down_t, s.proj_t, s.seg_col,
        ) = own
        s.heads = s.weight.shape[2] // HD
        streams.append(s)
    meet([at.to_x, at.to_y, at.to_far] + at.to_ctx[1:])
    for s in streams:
        s.gather = Gather(copies, at, s.qkv, s.weight)
    for s in streams:
        spread_small(at, s.gains, s.shifts, s.bias, s.wide, s.flat, s.small_own)
    for s in streams:
        s.small_done = [
            copies.remote(s.small_own, s.small_in.at[i], device)
            for i, device in enumerate((at.to_x, at.to_y, at.to_far))
        ]
        if s.heads == 4:
            s.down_t[...] = jnp.transpose(s.down[...])
            s.proj_t[...] = jnp.transpose(s.proj[...])
        document_columns(s.seg_row, s.seg_col)
    text, image = streams
    text.gather.forward()

    def project(s):
        for copy in s.small_done:
            copy.wait_recv()
        s.small[...] = s.small_own[...] + s.small_in[0] + s.small_in[1] + s.small_in[2]
        s.gather.arrived()
        for step in range(s.x.shape[0] // 256):
            first_rows(s.x, s.small, s.weight, s.first, s.rows, step)
        write_messages(s.rows, s.mine, s.heads)
        s.sends = send_blocks(copies, at, s.mine, s.got)

    project(text)
    image.gather.forward()
    for s in streams:
        pieces = (s.proj_t, s.up, s.down_t) if s.heads == 4 else (s.proj, s.up, s.down)
        s.rest = [
            Gather(copies, at, piece, full)
            for piece, full in zip(pieces, (s.proj_full, s.up_full, s.down_full))
        ]
    project(image)
    for gather in text.rest:
        gather.forward()
    for copy in text.sends:
        copy.wait()
    text.keep = copies.local(text.got, text.messages)
    attend_text(text.got, text.seg_col, text.seg_row, text.o, text.lse)
    for gather in image.rest:
        gather.forward()
    for copy in image.sends:
        copy.wait()
    image.keep = copies.local(image.got, image.messages)
    attend_image(at, image.got, image.seg_col, image.seg_row, image.o, image.lse)
    for s in streams:
        for gather in s.rest:
            gather.arrived()
        for gather in [s.gather] + s.rest:
            gather.sent()
        for copy in s.small_done:
            copy.wait_send()
        s.keep.wait()


def front(streams):
    vmem, hbm = pl.BlockSpec(memory_space=pltpu.VMEM), pl.BlockSpec(memory_space=pl.ANY)
    out_shape, out_specs, scratch = [], [], []
    for x, seg, gains, shifts, bias, qkv, up, down, proj in streams:
        tokens, width = x.shape
        own = qkv.shape[2]
        messages = message_shape(own // HD, tokens)
        hidden = up.shape[1]
        small = jax.ShapeDtypeStruct((16, width), F32)
        out_shape += [
            jax.ShapeDtypeStruct((3, width, own), BF16),
            small,
            jax.ShapeDtypeStruct((width, tokens), BF16),
            jax.ShapeDtypeStruct(messages, BF16),
            jax.ShapeDtypeStruct((width, own), BF16),
            jax.ShapeDtypeStruct((width, hidden), BF16),
            jax.ShapeDtypeStruct((width, hidden), BF16),
            jax.ShapeDtypeStruct((4, QB if own == 4 * HD else KB, LANES), BF16),
            jax.ShapeDtypeStruct((4 * tokens // QB, 16, QB), F32),
        ]
        out_specs += [vmem, vmem, vmem, hbm, hbm, hbm, hbm, vmem, vmem]
        scratch += [
            pltpu.VMEM((3, 16, width), F32),
            pltpu.VMEM((16, width), F32),
            pltpu.VMEM((8, width), F32),
            pltpu.VMEM((8, 3 * width), F32),
            pltpu.VMEM((tokens, 3 * own), F32),
            pltpu.VMEM(messages, BF16),
            pltpu.VMEM(messages, BF16),
            pltpu.VMEM((width // 4, hidden), BF16),
            pltpu.VMEM((width // 4, own), BF16),
            pltpu.VMEM((4 * tokens, LANES), F32),
        ]
    results = pl.pallas_call(
        front_kernel,
        out_shape=out_shape,
        in_specs=[vmem] * (2 * FRONT_IN),
        out_specs=out_specs,
        scratch_shapes=scratch + copy_sems(2 * (3 + 4 * 4 + 3), 2 * 6),
        compiler_params=pltpu.CompilerParams(
            collective_id=0, has_side_effects=True, vmem_limit_bytes=63 << 20
        ),
        name="front",
    )(*streams[0], *streams[1])
    return results[:FRONT_OUT], results[FRONT_OUT:]


def chunks(tokens, size=256):
    return [slice(start, start + size) for start in range(0, tokens, size)]


def as_f32(ref, index, rows=slice(None)):
    return ref[index, rows].astype(F32)


def take_mixed(got, mixed, at, heads):
    tokens = mixed.shape[0]
    if heads == 4:
        half = tokens // 2
        for tile in range(2):
            cols = slice(tile * LANES, (tile + 1) * LANES)
            one, two = as_f32(got, 2 * tile), as_f32(got, 2 * tile + 1)
            mixed[:half, cols] = lane_pair((one, 0), (two, 0)).astype(BF16)
            mixed[half:, cols] = lane_pair((one, 1), (two, 1)).astype(BF16)
        return
    for tile in range(2):
        cols = slice(tile * LANES, (tile + 1) * LANES)
        mixed[:, cols] = lane_pair(
            (as_f32(got, 2 * tile), 1), (as_f32(got, 2 * tile + 1), 1)
        ).astype(BF16)
    part = at.here // 2
    mixed[:, 2 * LANES :] = lane_pair((as_f32(got, part), 0), (as_f32(got, part + 2), 0)).astype(BF16)


def write_grad_o(grad, out, heads):
    tokens = grad.shape[0]
    half = tokens // 2
    for c in range(4):
        if heads == 4:
            out[c] = lane_pair(
                head_tile(grad, 0, c, slice(0, half)), head_tile(grad, 0, c, slice(half, None))
            ).astype(BF16)
        else:
            out[c] = lane_pair(head_tile(grad, 0, 4 + c // 2), head_tile(grad, 0, c)).astype(BF16)


def send_blocks(copies, at, mine, out):
    done = [copies.local(mine.at[at.here], out.at[at.here])]
    for other in at.ctx[1:]:
        done.append(copies.remote(mine.at[other], out.at[at.here], {CTX: other}))
    return done


def middle_kernel(*refs):
    at = partners()
    n = 7
    ins = [refs[:n], refs[n : 2 * n]]
    refs = refs[2 * n :]
    n = 5
    outs = [refs[:n], refs[n : 2 * n]]
    refs = refs[2 * n :]
    n = 17
    scratch = [refs[:n], refs[n : 2 * n]]
    copies = Copies(*refs[2 * n :])
    other_core = at.to_core
    meet(at.to_ctx[1:] + [other_core])
    streams = []
    for (o, x, dy, small, proj_in, up_in, down_in), out, own in zip(ins, outs, scratch):
        s = Bag()
        s.o, s.x, s.dy, s.small = o, x, dy, small
        s.y, s.dmid, s.do_out, s.rest, s.sums = out
        (
            s.proj, s.up, s.down, s.o_in, s.mixed, s.part, s.part_in, s.mid, s.first, s.first_t, s.dy_t,
            s.act, s.dz, s.grad, s.grad_in, s.do, s.do_mine,
        ) = own
        s.heads = proj_in.shape[1] // HD
        s.o_done = send_blocks(copies, at, o, s.o_in)
        s.proj_done = copies.local(proj_in, s.proj)
        streams.append(s)
    for s, (o, x, dy, small, proj_in, up_in, down_in) in zip(streams, ins):
        s.rest_done = [copies.local(up_in, s.up), copies.local(down_in, s.down)]
        s.sums[...] = jnp.zeros_like(s.sums)
        for rows in chunks(dy.shape[0]):
            s.dy_t[:, rows] = jnp.transpose(dy[rows, :])
    for s in streams:
        tokens, width = s.x.shape
        for copy in s.o_done:
            copy.wait()
        take_mixed(s.o_in, s.mixed, at, s.heads)
        s.proj_done.wait()
        for cols in chunks(width):
            s.part[:, cols] = dot(s.mixed[...], s.proj[cols, :], ((1,), (1,)))
        s.part_done = copies.remote(s.part, s.part_in, other_core)
    for s in streams:
        tokens, width = s.x.shape
        hidden = s.up.shape[1]
        small, mid, first_t, dy_t = s.small, s.mid, s.first_t, s.dy_t
        s.part_done.wait()
        for rows in chunks(tokens):
            middle = (
                s.x[rows, :].astype(F32) + s.part[rows, :] + s.part_in[rows, :] + small[3:4]
            )
            mid[rows, :] = middle
            normed, _ = normalise(middle)
            low = (normed * small[1:2] + small[4:5]).astype(BF16)
            s.first[rows, :] = low
            first_t[:, rows] = jnp.transpose(low)
        for copy in s.rest_done:
            copy.wait()
        act, dz = s.act, s.dz

        def tile(index, carry, s=s, act=act, dz=dz, first_t=first_t, dy_t=dy_t, small=small, tokens=tokens, width=width, hidden=hidden):
            cols = pl.ds(pl.multiple_of(index * 256, 256), 256)
            up, down = s.up[:, cols], s.down[:, cols]
            per_row = width // 256
            own = s.proj.shape[1]
            up_cols = pl.ds(pl.multiple_of(own + index * 256, LANES), 256)
            down_cols = pl.ds(pl.multiple_of(own + hidden + index * 256, LANES), 256)
            bias = small[pl.ds(7 + index // per_row, 1), pl.ds(pl.multiple_of((index % per_row) * 256, 256), 256)]
            total = jnp.zeros((1, 256), F32)
            for rows in chunks(tokens):
                z = dot(s.first[rows, :], up) + bias
                sg = jax.nn.sigmoid(1.702 * z)
                zs = z * sg
                act[rows, cols] = zs.astype(BF16)
                grad = dot(s.dy[rows, :], down)
                low = (grad * (sg + 1.702 * zs * (1.0 - sg))).astype(BF16)
                dz[rows, cols] = low
                total = total + jnp.sum(low.astype(F32), axis=0, keepdims=True)
            s.sums[pl.ds(7 + index // per_row, 1), pl.ds(pl.multiple_of((index % per_row) * 256, 256), 256)] = total
            s.rest[:, up_cols] = dot(first_t[...], dz[:, cols]).astype(BF16)
            s.rest[:, down_cols] = dot(dy_t[...], act[:, cols]).astype(BF16)
            return carry

        lax.fori_loop(0, hidden // 256, tile, 0)
        grad = s.grad
        for cols in chunks(width):
            grad[0, :, cols] = dot(dz[...], s.up[cols, :], ((1,), (1,)))
        s.grad_done = copies.remote(grad.at[0], s.grad_in.at[0], other_core)
        for cols in chunks(width):
            grad[1, :, cols] = dot(act[...], s.down[cols, :], ((1,), (1,)))
        s.y_done = copies.remote(grad.at[1], s.grad_in.at[1], other_core)
    for s in streams:
        tokens, width = s.x.shape
        small, sums = s.small, s.sums
        s.grad_done.wait()
        for rows in chunks(tokens):
            normed, inv = normalise(s.mid[rows, :])
            second = s.grad[0, rows, :] + s.grad_in[0, rows, :]
            scaled = second * small[1:2]
            dy = s.dy[rows, :].astype(F32)
            dmid = dy + inv * (
                scaled
                - jnp.mean(scaled, axis=-1, keepdims=True)
                - normed * jnp.mean(scaled * normed, axis=-1, keepdims=True)
            )
            s.dmid[rows, :] = dmid
            sums[1:2] += jnp.sum(second * normed, axis=0, keepdims=True)
            sums[3:4] += jnp.sum(dmid, axis=0, keepdims=True)
            sums[4:5] += jnp.sum(second, axis=0, keepdims=True)
            sums[5:6] += jnp.sum(dy, axis=0, keepdims=True)
            low = dmid.astype(BF16)
            s.first_t[:, rows] = jnp.transpose(low)
            s.do[rows, :] = dot(low, s.proj[...])
        write_grad_o(s.do, s.do_mine, s.heads)
        s.do_done = send_blocks(copies, at, s.do_mine, s.do_out)
        s.rest[:, : s.proj.shape[1]] = dot(s.first_t[...], s.mixed[...]).astype(BF16)
        s.y_done.wait()
        for rows in chunks(tokens):
            s.y[rows, :] = (
                s.mid[rows, :] + s.grad[1, rows, :] + s.grad_in[1, rows, :] + small[5:6]
            ).astype(BF16)
    for s in streams:
        for copy in s.do_done:
            copy.wait()


def middle(streams):
    vmem, hbm = pl.BlockSpec(memory_space=pltpu.VMEM), pl.BlockSpec(memory_space=pl.ANY)
    out_shape, out_specs, scratch = [], [], []
    for o, x, dy, small, proj, up, down in streams:
        tokens, width = x.shape
        hidden, own = up.shape[1], proj.shape[1]
        out_shape += [
            jax.ShapeDtypeStruct((tokens, width), BF16),
            jax.ShapeDtypeStruct((tokens, width), F32),
            jax.ShapeDtypeStruct(o.shape, BF16),
            jax.ShapeDtypeStruct((width, own + 2 * hidden), BF16),
            jax.ShapeDtypeStruct(small.shape, F32),
        ]
        out_specs += [vmem, vmem, hbm, vmem, vmem]
        scratch += [
            pltpu.VMEM(proj.shape, BF16),
            pltpu.VMEM(up.shape, BF16),
            pltpu.VMEM(down.shape, BF16),
            pltpu.VMEM(o.shape, BF16),
            pltpu.VMEM((tokens, own), BF16),
            pltpu.VMEM((tokens, width), F32),
            pltpu.VMEM((tokens, width), F32),
            pltpu.VMEM((tokens, width), F32),
            pltpu.VMEM((tokens, width), BF16),
            pltpu.VMEM((width, tokens), BF16),
            pltpu.VMEM((width, tokens), BF16),
            pltpu.VMEM((tokens, hidden), BF16),
            pltpu.VMEM((tokens, hidden), BF16),
            pltpu.VMEM((2, tokens, width), F32),
            pltpu.VMEM((2, tokens, width), F32),
            pltpu.VMEM((tokens, own), F32),
            pltpu.VMEM(o.shape, BF16),
        ]
    results = pl.pallas_call(
        middle_kernel,
        out_shape=out_shape,
        in_specs=([vmem] * 4 + [hbm] * 3) * 2,
        out_specs=out_specs,
        scratch_shapes=scratch + copy_sems(2 * 9, 2 * 5),
        compiler_params=pltpu.CompilerParams(
            collective_id=1, has_side_effects=True, vmem_limit_bytes=63 << 20
        ),
        name="middle",
    )(*streams[0], *streams[1])
    return results[:5], results[5:]


STEP = 384


def by_columns(columns, body):
    def one(index, carry):
        body(pl.ds(pl.multiple_of(index * STEP, STEP), STEP))
        return carry

    lax.fori_loop(0, columns // STEP, one, 0)


class Reduce:
    BUFFERS = 11

    def __init__(self, copies, at, src, buffers):
        self.copies, self.at = copies, at
        (
            self.own, self.pass_top, self.pass_low, self.in_x, self.in_y, self.in_top, self.in_low,
            self.total, self.half_out, self.quarter_out, self.final,
        ) = buffers[: self.BUFFERS]
        self.half_in, self.quarter_in = buffers[self.BUFFERS :]
        rows, self.columns = self.final.shape
        self.rows, half = rows, rows // 2
        self.half = half

        def block(owner, offset, size):
            return src.at[pl.ds(pl.multiple_of(owner * rows + offset, 8), size), :]

        self.loads = [
            copies.local(block(at.group_y, 0, half), self.pass_top),
            copies.local(block(at.group_x, half, half), self.pass_low),
            copies.local(block(at.group, 0, rows), self.own),
        ]
        self.first = [
            copies.remote(block(at.group_far, 0, half), self.in_x.at[1], at.to_x),
            copies.remote(block(at.group_far, half, half), self.in_y.at[1], at.to_y),
            copies.remote(block(at.group_x, 0, half), self.in_x.at[0], at.to_x),
            copies.remote(block(at.group_y, half, half), self.in_y.at[0], at.to_y),
        ]

    def cross(self):
        self.loads[0].wait()
        self.first[0].wait_recv()

        def top(cols):
            self.pass_top[:, cols] = (
                self.pass_top[:, cols].astype(F32) + self.in_x[1, :, cols].astype(F32)
            ).astype(BF16)

        by_columns(self.columns, top)
        self.second = [self.copies.remote(self.pass_top, self.in_top, self.at.to_y)]
        self.loads[1].wait()
        self.first[1].wait_recv()

        def low(cols):
            self.pass_low[:, cols] = (
                self.pass_low[:, cols].astype(F32) + self.in_y[1, :, cols].astype(F32)
            ).astype(BF16)

        by_columns(self.columns, low)
        self.second.append(self.copies.remote(self.pass_low, self.in_low, self.at.to_x))

    def along(self):
        half = self.half
        self.loads[2].wait()
        self.first[2].wait_recv()
        self.first[3].wait_recv()
        self.second[0].wait_recv()
        self.second[1].wait_recv()

        def plane(cols):
            self.total[:half, cols] = (
                self.own[:half, cols].astype(F32)
                + self.in_x[0, :, cols].astype(F32)
                + self.in_top[:, cols].astype(F32)
            )
            self.total[half:, cols] = (
                self.own[half:, cols].astype(F32)
                + self.in_y[0, :, cols].astype(F32)
                + self.in_low[:, cols].astype(F32)
            )

        by_columns(self.columns, plane)
        self.keep = pl.ds(pl.multiple_of(self.at.here_low * half, 8), half)
        give = pl.ds(pl.multiple_of((1 - self.at.here_low) * half, 8), half)

        def send(cols):
            self.half_out[:, cols] = self.total[give, cols].astype(BF16)

        by_columns(self.columns, send)
        self.third = self.copies.remote(self.half_out, self.half_in, self.at.to_ctx[1])

    def along_far(self):
        quarter = self.half // 2
        self.third.wait_recv()
        base = self.at.here_low * self.half
        mine = pl.ds(pl.multiple_of(self.at.here_high * quarter, 8), quarter)
        other = pl.ds(pl.multiple_of((1 - self.at.here_high) * quarter, 8), quarter)
        self.keep_low = pl.ds(pl.multiple_of(base + self.at.here_high * quarter, 8), quarter)
        give = pl.ds(pl.multiple_of(base + (1 - self.at.here_high) * quarter, 8), quarter)

        def send(cols):
            self.quarter_out[:, cols] = (
                self.total[give, cols] + self.half_in[other, cols].astype(F32)
            ).astype(BF16)

        by_columns(self.columns, send)
        self.fourth = self.copies.remote(self.quarter_out, self.quarter_in, self.at.to_ctx[2])
        self.mine = mine

    def back_far(self):
        self.fourth.wait_recv()

        def add(cols):
            self.final[self.keep_low, cols] = (
                self.total[self.keep_low, cols]
                + self.half_in[self.mine, cols].astype(F32)
                + self.quarter_in[:, cols].astype(F32)
            ).astype(BF16)

        by_columns(self.columns, add)
        rows = self.final.at[self.keep_low, :]
        self.fifth = self.copies.remote(rows, rows, self.at.to_ctx[2])

    def back_near(self):
        self.fifth.wait_recv()
        rows = self.final.at[self.keep, :]
        self.sixth = self.copies.remote(rows, rows, self.at.to_ctx[1])

    def finish(self):
        self.sixth.wait_recv()
        for copy in self.first + self.second + [self.third, self.fourth, self.fifth, self.sixth]:
            copy.wait_send()

    @staticmethod
    def scratch(rows, columns):
        half, quarter = rows // 2, rows // 4
        return [
            pltpu.VMEM((rows, columns), BF16),
            pltpu.VMEM((half, columns), BF16),
            pltpu.VMEM((half, columns), BF16),
            pltpu.VMEM((2, half, columns), BF16),
            pltpu.VMEM((2, half, columns), BF16),
            pltpu.VMEM((half, columns), BF16),
            pltpu.VMEM((half, columns), BF16),
            pltpu.VMEM((rows, columns), F32),
            pltpu.VMEM((half, columns), BF16),
            pltpu.VMEM((quarter, columns), BF16),
        ]

    @staticmethod
    def scratch_in(rows, columns):
        return [pltpu.VMEM((rows // 2, columns), BF16), pltpu.VMEM((rows // 4, columns), BF16)]


def take_dqkv(got, out, at, heads):
    tokens, width = out.shape[0], heads * HD

    def put(which, tile, rows, low, high):
        start = which * width + tile * LANES
        out[rows, start : start + LANES] = lane_pair(low, high).astype(BF16)

    every = slice(None)
    if heads == 4:
        half = tokens // 2
        top, low, keys = slice(0, half), slice(half, tokens), slice(half, half + tokens)
        for tile in range(2):
            one, two = 2 * tile, 2 * tile + 1
            for side, rows in ((0, top), (1, low)):
                put(0, tile, rows, (as_f32(got, one, top), side), (as_f32(got, two, top), side))
            for which in (1, 2):
                side = which - 1
                put(which, tile, every, (as_f32(got, one, keys), side), (as_f32(got, two, keys), side))
        return

    def part(position, index):
        return got[position, index].astype(F32)

    for tile in range(2):
        one, two = 2 * tile, 2 * tile + 1
        put(0, tile, every, (part(one, 0), 0), (part(two, 0), 0))
        put(1, tile, every, (part(one, 1), 0), (part(two, 1), 0))
        put(2, tile, every, (part(one, 1), 1), (part(two, 1), 1))
    put(0, 2, every, (part(at.here_high, 0), 1), (part(at.here_high + 2, 0), 1))
    one, two = part(0, 2) + part(1, 2), part(2, 2) + part(3, 2)
    put(1, 2, every, (one, 1), (two, 1))
    put(2, 2, every, (one, 0), (two, 0))


LAST_IN, LAST_OUT, LAST_SCRATCH = 12, 4, 18


def last_kernel(*refs):
    at = partners()
    ins = [refs[:LAST_IN], refs[LAST_IN : 2 * LAST_IN]]
    refs = refs[2 * LAST_IN :]
    outs = [refs[:LAST_OUT], refs[LAST_OUT : 2 * LAST_OUT]]
    refs = refs[2 * LAST_OUT :]
    count = LAST_SCRATCH + 2 * 12
    scratch = [refs[:count], refs[count : 2 * count]]
    copies = Copies(*refs[2 * count :])
    meet([at.to_x, at.to_y] + at.to_ctx[1:] + [at.to_core])
    streams = []
    for in_refs, out_refs, own in zip(ins, outs, scratch):
        s = Bag()
        (
            s.m_in, s.do_in, s.o_in, s.lse, s.seg_row, s.first_in, s.x_in, s.small, s.weight_in, s.dmid_in,
            s.rest, s.sums_in,
        ) = in_refs
        s.grad_rows, s.sums, rest_final, qkv_final = out_refs
        (
            s.m, s.do, s.o, s.seg_col, s.acc, s.back, s.got, s.dqkv, s.weight, s.first, s.x, s.dmid,
            s.part, s.part_in, s.g_qkv, s.sums_own, s.sums_out, s.sums_got,
        ) = own[:LAST_SCRATCH]
        rest_buffers = list(own[LAST_SCRATCH : LAST_SCRATCH + 12])
        s.qkv_buffers = list(own[LAST_SCRATCH + 12 :])
        rest_buffers.insert(10, rest_final)
        s.qkv_buffers.insert(10, qkv_final)
        s.heads = s.weight.shape[2] // HD
        s.reads = [
            copies.local(src, dst) for src, dst in ((s.m_in, s.m), (s.do_in, s.do), (s.o_in, s.o))
        ]
        s.rest_buffers = rest_buffers
        streams.append(s)
    text, image = streams
    for s in streams:
        s.reduce_rest = Reduce(copies, at, s.rest, s.rest_buffers)
    for s in streams:
        s.loads = [
            copies.local(src, dst)
            for src, dst in (
                (s.weight_in, s.weight), (s.first_in, s.first), (s.x_in, s.x), (s.dmid_in, s.dmid),
            )
        ]
        document_columns(s.seg_row, s.seg_col)
        for copy in s.reads:
            copy.wait()
    s = text
    unattend_text(s.m, s.do, s.o, s.lse, s.seg_col, s.seg_row, s.acc.at[0], s.back)
    text.sends = send_blocks(copies, at, text.back, text.got)

    def image_part(blocks, extra):
        s = image
        acc = s.acc.at[1 if extra else 0]
        unattend_image(s.m, s.do, s.o, s.lse, s.seg_col, s.seg_row, acc, s.back, blocks, extra)

    text.reduce_rest.cross()
    image.acc[...] = jnp.zeros_like(image.acc)
    image.back[...] = jnp.zeros_like(image.back)
    image_part((at.here_low * 4, 4), True)
    image_part((0, 4), False)
    image.reduce_rest.cross()
    text.reduce_rest.along()
    image_part((4, 4), False)
    for source in range(4):
        image.back[source, 1] = image.acc[0, key_range(source)].astype(BF16)
        image.back[source, 2] = image.acc[1, key_range(source)].astype(BF16)
    image.sends = send_blocks(copies, at, image.back, image.got)

    def project(s):
        tokens, width = s.x.shape
        own = s.heads * HD
        for copy in s.sends:
            copy.wait()
        for copy in s.loads:
            copy.wait()
        take_dqkv(s.got, s.dqkv, at, s.heads)
        for cols in chunks(width):
            total = dot(s.dqkv[:, :own], s.weight[0, cols, :], ((1,), (1,)))
            total = total + dot(s.dqkv[:, own : 2 * own], s.weight[1, cols, :], ((1,), (1,)))
            s.part[:, cols] = total + dot(s.dqkv[:, 2 * own :], s.weight[2, cols, :], ((1,), (1,)))
        s.part_done = copies.remote(s.part, s.part_in, at.to_core)
        for which in range(3):
            cols = slice(which * own, (which + 1) * own)
            s.g_qkv[:, cols] = dot(s.first[...], s.dqkv[:, cols]).astype(BF16)
        s.reduce_qkv = Reduce(copies, at, s.g_qkv, s.qkv_buffers)
        s.sums_own[...] = s.sums_in[...]
        s.sums_own[6:7, :own] = jnp.sum(s.dqkv[:, :own].astype(F32), axis=0, keepdims=True)
        s.sums_own[6:7, own:] = jnp.sum(s.dqkv[:, 2 * own :].astype(F32), axis=0, keepdims=True)

    def input_grad(s):
        tokens, width = s.x.shape
        s.part_done.wait()
        for rows in chunks(tokens):
            normed, inv = normalise(s.x[rows, :].astype(F32))
            first = s.part[rows, :] + s.part_in[rows, :]
            scaled = first * s.small[0:1]
            s.grad_rows[rows, :] = s.dmid[rows, :] + inv * (
                scaled
                - jnp.mean(scaled, axis=-1, keepdims=True)
                - normed * jnp.mean(scaled * normed, axis=-1, keepdims=True)
            )
            s.sums_own[0:1] += jnp.sum(first * normed, axis=0, keepdims=True)
            s.sums_own[2:3] += jnp.sum(first, axis=0, keepdims=True)
        s.sums_done = [copies.remote(s.sums_own, s.sums_got.at[0], at.to_x)]

    def add_sums(s, step):
        s.sums_done[-1].wait_recv()
        before = s.sums_own if step == 0 else s.sums_out.at[step - 1]
        after = s.sums if step == 3 else s.sums_out.at[step]
        after[...] = before[...] + s.sums_got[step]
        if step < 3:
            device = (at.to_y, at.to_ctx[1], at.to_ctx[2])[step]
            s.sums_done.append(copies.remote(after, s.sums_got.at[step + 1], device))

    project(text)
    text.reduce_rest.along_far()
    input_grad(text)
    image.reduce_rest.along()
    text.reduce_qkv.cross()
    text.reduce_rest.back_far()
    project(image)
    image.reduce_rest.along_far()
    text.reduce_qkv.along()
    text.reduce_rest.back_near()
    input_grad(image)
    image.reduce_qkv.cross()
    add_sums(text, 0)
    add_sums(image, 0)
    image.reduce_rest.back_far()
    text.reduce_qkv.along_far()
    add_sums(text, 1)
    add_sums(image, 1)
    image.reduce_qkv.along()
    image.reduce_rest.back_near()
    text.reduce_qkv.back_far()
    add_sums(text, 2)
    add_sums(image, 2)
    image.reduce_qkv.along_far()
    text.reduce_qkv.back_near()
    image.reduce_qkv.back_far()
    add_sums(text, 3)
    add_sums(image, 3)
    image.reduce_qkv.back_near()
    for s in streams:
        s.reduce_rest.finish()
        s.reduce_qkv.finish()
        for copy in s.sums_done:
            copy.wait_send()


def last(streams):
    vmem, hbm = pl.BlockSpec(memory_space=pltpu.VMEM), pl.BlockSpec(memory_space=pl.ANY)
    out_shape, scratch = [], []
    for messages, do, o, lse, seg, first, x, small, weight, dmid, rest, sums in streams:
        tokens, width = x.shape
        own = weight.shape[2]
        rest_shape, qkv_shape = (width // 4, rest.shape[1]), (width // 4, 3 * own)
        out_shape += [
            jax.ShapeDtypeStruct((tokens, width), F32),
            jax.ShapeDtypeStruct(small.shape, F32),
            jax.ShapeDtypeStruct(rest_shape, BF16),
            jax.ShapeDtypeStruct(qkv_shape, BF16),
        ]
        scratch += [
            pltpu.VMEM(messages.shape, BF16),
            pltpu.VMEM(do.shape, BF16),
            pltpu.VMEM(do.shape, BF16),
            pltpu.VMEM((4 * tokens, LANES), F32),
            pltpu.VMEM((1 if own == 4 * HD else 2, 4 * tokens, LANES), F32),
            pltpu.VMEM(messages.shape, BF16),
            pltpu.VMEM(messages.shape, BF16),
            pltpu.VMEM((tokens, 3 * own), BF16),
            pltpu.VMEM(weight.shape, BF16),
            pltpu.VMEM(first.shape, BF16),
            pltpu.VMEM((tokens, width), BF16),
            pltpu.VMEM((tokens, width), F32),
            pltpu.VMEM((tokens, width), F32),
            pltpu.VMEM((tokens, width), F32),
            pltpu.VMEM((width, 3 * own), BF16),
            pltpu.VMEM(small.shape, F32),
            pltpu.VMEM((3,) + small.shape, F32),
            pltpu.VMEM((4,) + small.shape, F32),
        ]
        for shape in (rest_shape, qkv_shape):
            scratch += Reduce.scratch(*shape) + Reduce.scratch_in(*shape)
    results = pl.pallas_call(
        last_kernel,
        out_shape=out_shape,
        in_specs=[hbm, hbm, hbm, vmem, vmem, hbm, hbm, vmem, hbm, hbm, hbm, vmem] * 2,
        out_specs=[vmem] * 8,
        scratch_shapes=scratch + copy_sems(2 * (3 + 1 + 4 + 2 * 10), 2 * (1 + 7 + 2 * 3)),
        compiler_params=pltpu.CompilerParams(
            collective_id=2, has_side_effects=True, vmem_limit_bytes=64 * 1024 * 1000
        ),
        name="last",
    )(*streams[0], *streams[1])
    return results[:4], results[4:]


def take_own(group, row):
    columns = row.shape[1] // 4
    return pltpu.roll(row, (4 - group) % 4 * columns, 1)[:, :columns]


def finish_kernel(*refs):
    ins = [refs[:3], refs[3:6]]
    outs = [refs[6:13], refs[13:]]
    for (sums, rest, qkv), (gains, shifts, bias, qkv_out, proj, up, down) in zip(ins, outs):
        group = lax.axis_index(FSDP)
        rows = take_own(group, sums[0:8])
        gains[...] = rows[0:2]
        shifts[...] = rows[2:6]
        line = jnp.concatenate([sums[6:7], sums[7:8], sums[8:9]], axis=1)
        bias[...] = take_own(group, jnp.broadcast_to(line, (8, line.shape[1])))[0:1]
        own = qkv.shape[1] // 3
        for which in range(3):
            qkv_out[which] = qkv[:, which * own : (which + 1) * own].astype(F32)
        hidden = up.shape[1]
        up[...] = rest[:, own : own + hidden].astype(F32)
        if down.shape[0] > down.shape[1]:
            proj[...] = jnp.transpose(rest[:, :own].astype(F32))
            down[...] = jnp.transpose(rest[:, own + hidden :].astype(F32))
        else:
            proj[...] = rest[:, :own].astype(F32)
            down[...] = rest[:, own + hidden :].astype(F32)


def finish(streams):
    out_shape = []
    for sums, rest, qkv, flip in streams:
        rows, own = qkv.shape[0], qkv.shape[1] // 3
        hidden = (rest.shape[1] - own) // 2
        shapes = [(2, rows), (4, rows), (1, 3 * rows), (3, rows, own)]
        shapes += [(own, rows), (rows, hidden), (hidden, rows)] if flip else [
            (rows, own), (rows, hidden), (rows, hidden)
        ]
        out_shape += [jax.ShapeDtypeStruct(shape, F32) for shape in shapes]
    results = pl.pallas_call(finish_kernel, out_shape=out_shape, name="finish")(
        *streams[0][:3], *streams[1][:3]
    )
    return results[:7], results[7:]


def on_device(*args):
    streams = []
    for item, causal in ((args[10:], True), (args[:10], False)):
        s = Bag()
        rows, s.seg, cotangent, s.gains, s.shifts, s.head_bias, s.qkv, proj, s.up, down = item
        s.flip, s.x, s.dy = causal, rows[0], cotangent[0]
        s.down, s.proj = (down, proj) if causal else (down.T, proj.T)
        streams.append(s)
    started = front(
        [(s.x, s.seg, s.gains, s.shifts, s.head_bias, s.qkv, s.up, s.down, s.proj) for s in streams]
    )
    for s, (weight, small, first, messages, proj, up, down, o, lse) in zip(streams, started):
        s.weight, s.small, s.first, s.messages, s.o, s.lse = weight, small, first, messages, o, lse
        s.weights = (proj, up, down)
    done = middle([(s.o, s.x, s.dy, s.small, *s.weights) for s in streams])
    ended = last(
        [
            (s.messages, do, s.o, s.lse, s.seg, s.first, s.x, s.small, s.weight, dmid, rest, sums)
            for s, (y, dmid, do, rest, sums) in zip(streams, done)
        ]
    )
    final = finish([(sums, rest, qkv, s.flip) for s, (_, sums, rest, qkv) in zip(streams, ended)])
    outputs = []
    for s, (y, *_), (grad_rows, *_), (gains, shifts, bias, qkv, proj, up, down) in zip(
        streams, done, ended, final
    ):
        if not s.flip:
            proj, down = proj.T, down.T
        outputs.append((y[None], grad_rows[None], gains, shifts, bias, qkv, proj, up, down))
    return outputs[1] + outputs[0]


def layer_stats(rows):
    row_mean = jnp.mean(rows, axis=-1, keepdims=True)
    centred = rows - row_mean
    inv_std = lax.rsqrt(jnp.mean(centred * centred, axis=-1, keepdims=True) + 1e-05)
    return (centred * inv_std, inv_std)


def norm_back(grad_normed_out, normed, inv_std, gain):
    scaled = grad_normed_out * gain
    return inv_std * (
        scaled
        - jnp.mean(scaled, axis=-1, keepdims=True)
        - normed * jnp.mean(scaled * normed, axis=-1, keepdims=True)
    )


def tensor_psum(partial_rows):
    return lax.psum(partial_rows, TP)


def any_mesh_block(
    rows_in,
    seg_row,
    cotangent,
    gains,
    shifts,
    head_bias,
    qkv_weight,
    proj_weight,
    up_weight,
    down_weight,
    causal,
):
    gain_full, shift_full, bias_full, qkv_full, proj_full, up_full, down_full = (
        lax.all_gather(gains, FSDP, axis=1, tiled=True),
        lax.all_gather(shifts, FSDP, axis=1, tiled=True),
        lax.all_gather(head_bias, FSDP, axis=1, tiled=True),
        lax.all_gather(qkv_weight, FSDP, axis=1, tiled=True),
        lax.all_gather(proj_weight, FSDP, axis=1, tiled=True),
        lax.all_gather(up_weight, FSDP, axis=0, tiled=True),
        lax.all_gather(down_weight, FSDP, axis=1, tiled=True),
    )
    gain_vals = gain_full.astype(jnp.float32)
    shift_vals = shift_full.astype(jnp.float32)
    bias_vals = bias_full[0].astype(jnp.float32)
    tp_width = qkv_full.shape[2]
    local_rows = rows_in.shape[1]
    seq_length = seg_row.shape[1]
    head_local = tp_width // HD
    rows = rows_in[0].astype(jnp.float32)
    row_start = lax.axis_index(CTX) * local_rows
    seg_all = seg_row[0]
    seg_query = lax.dynamic_slice_in_dim(seg_all, row_start, local_rows)
    query_pos = row_start + jnp.arange(local_rows, dtype=jnp.int32)
    key_pos = jnp.arange(seq_length, dtype=jnp.int32)
    allowed = seg_query[:, None] == seg_all[None, :]
    if causal:
        allowed = jnp.logical_and(allowed, key_pos[None, :] <= query_pos[:, None])

    def to_heads(matrix):
        return matrix.reshape(matrix.shape[0], head_local, HD).transpose(1, 0, 2)

    def from_heads(stacked):
        return stacked.transpose(1, 0, 2).reshape(stacked.shape[1], head_local * HD)

    normed_one, inv_one = layer_stats(rows)
    first_in = (normed_one * gain_vals[0] + shift_vals[0]).astype(jnp.bfloat16)
    queries = (
        jnp.dot(first_in, qkv_full[0], preferred_element_type=jnp.float32) + bias_vals[:tp_width]
    ).astype(jnp.bfloat16)
    key_rows = jnp.dot(first_in, qkv_full[1], preferred_element_type=jnp.float32).astype(
        jnp.bfloat16
    )
    values = (
        jnp.dot(first_in, qkv_full[2], preferred_element_type=jnp.float32)
        + bias_vals[tp_width : 2 * tp_width]
    ).astype(jnp.bfloat16)
    key_all, value_all = (
        lax.all_gather(key_rows, CTX, axis=0, tiled=True),
        lax.all_gather(values, CTX, axis=0, tiled=True),
    )
    query_heads = to_heads(queries)
    key_heads = to_heads(key_all)
    value_heads = to_heads(value_all)

    def attend(head_items):
        query_h, key_h, value_h = head_items
        scores = dot(query_h, key_h, ((1,), (1,))) * 0.125
        scores = jnp.where(allowed, scores, -1e30)
        row_top = jnp.max(scores, axis=-1, keepdims=True)
        weights = jnp.exp(scores - row_top)
        row_total = jnp.sum(weights, axis=-1, keepdims=True)
        weights_low = (weights / row_total).astype(jnp.bfloat16)
        mixed_h = dot(weights_low, value_h, ((1,), (0,)))
        return (mixed_h.astype(jnp.bfloat16), row_top[:, 0] + jnp.log(row_total[:, 0]))

    mixed_heads, log_totals = lax.map(attend, (query_heads, key_heads, value_heads))
    mixed = from_heads(mixed_heads)
    middle = (
        rows
        + tensor_psum(jnp.dot(mixed, proj_full, preferred_element_type=jnp.float32))
        + shift_vals[1]
    )
    normed_two, inv_two = layer_stats(middle)
    second_in = (normed_two * gain_vals[1] + shift_vals[2]).astype(jnp.bfloat16)
    hidden = (
        jnp.dot(second_in, up_full, preferred_element_type=jnp.float32) + bias_vals[2 * tp_width :]
    )
    sigma = jax.nn.sigmoid(1.702 * hidden)
    activated = (hidden * sigma).astype(jnp.bfloat16)
    output = (
        middle
        + tensor_psum(jnp.dot(activated, down_full, preferred_element_type=jnp.float32))
        + shift_vals[3]
    )
    grad_out = cotangent[0].astype(jnp.float32)
    grad_down_bias = jnp.sum(grad_out, axis=0)
    grad_branch = grad_out.astype(jnp.bfloat16)
    grad_down = dot(activated, grad_branch, ((0,), (0,)))
    grad_act = dot(grad_branch, down_full, ((1,), (1,)))
    grad_hidden = (grad_act * (sigma + 1.702 * hidden * sigma * (1.0 - sigma))).astype(jnp.bfloat16)
    grad_up_bias = jnp.sum(grad_hidden.astype(jnp.float32), axis=0)
    grad_up = dot(second_in, grad_hidden, ((0,), (0,)))
    grad_second = tensor_psum(
        dot(grad_hidden, up_full, ((1,), (1,)))
    )
    grad_gain_two = jnp.sum(grad_second * normed_two, axis=0)
    grad_shift_two = jnp.sum(grad_second, axis=0)
    grad_middle = grad_out + norm_back(grad_second, normed_two, inv_two, gain_vals[1])
    grad_proj_bias = jnp.sum(grad_middle, axis=0)
    grad_attn = grad_middle.astype(jnp.bfloat16)
    grad_proj = dot(mixed, grad_attn, ((0,), (0,)))
    grad_mixed = dot(grad_attn, proj_full, ((1,), (1,))).astype(jnp.bfloat16)

    def attend_back(head_items):
        query_h, key_h, value_h, grad_h, log_total = head_items
        scores = dot(query_h, key_h, ((1,), (1,))) * 0.125
        weights = jnp.where(allowed, jnp.exp(scores - log_total[:, None]), 0.0)
        grad_weights = dot(grad_h, value_h, ((1,), (1,)))
        row_delta = jnp.sum(weights * grad_weights, axis=-1, keepdims=True)
        grad_scores = (weights * (grad_weights - row_delta)).astype(jnp.bfloat16)
        grad_query_h = (
            dot(grad_scores, key_h, ((1,), (0,))) * 0.125
        )
        grad_key_h = (
            dot(grad_scores, query_h, ((0,), (0,)))
            * 0.125
        )
        grad_value_h = dot(weights.astype(jnp.bfloat16), grad_h, ((0,), (0,)))
        return (grad_query_h, grad_key_h, grad_value_h)

    query_parts, key_parts, value_parts = lax.map(
        attend_back, (query_heads, key_heads, value_heads, to_heads(grad_mixed), log_totals)
    )
    key_sum, value_sum = (
        lax.psum_scatter(from_heads(key_parts), CTX, scatter_dimension=0, tiled=True),
        lax.psum_scatter(from_heads(value_parts), CTX, scatter_dimension=0, tiled=True),
    )
    grad_query = from_heads(query_parts).astype(jnp.bfloat16)
    grad_key = key_sum.astype(jnp.bfloat16)
    grad_value = value_sum.astype(jnp.bfloat16)
    grad_qkv = jnp.stack(
        [
            dot(first_in, grad_query, ((0,), (0,))),
            dot(first_in, grad_key, ((0,), (0,))),
            dot(first_in, grad_value, ((0,), (0,))),
        ]
    )
    grad_head = jnp.concatenate(
        [
            jnp.sum(grad_query.astype(jnp.float32), axis=0),
            jnp.sum(grad_value.astype(jnp.float32), axis=0),
            grad_up_bias,
        ]
    )[None, :]
    grad_first_part = dot(grad_query, qkv_full[0], ((1,), (1,)))
    grad_first_part = grad_first_part + dot(grad_key, qkv_full[1], ((1,), (1,)))
    grad_first_part = grad_first_part + dot(grad_value, qkv_full[2], ((1,), (1,)))
    grad_first = tensor_psum(grad_first_part)
    grad_gain_one = jnp.sum(grad_first * normed_one, axis=0)
    grad_shift_one = jnp.sum(grad_first, axis=0)
    grad_rows = grad_middle + norm_back(grad_first, normed_one, inv_one, gain_vals[0])
    grad_gains = jnp.stack([grad_gain_one, grad_gain_two])
    grad_shifts = jnp.stack([grad_shift_one, grad_proj_bias, grad_shift_two, grad_down_bias])
    share_gains, share_shifts, share_head, share_qkv, share_proj, share_up, share_down = (
        lax.psum_scatter(grad_gains, FSDP, scatter_dimension=1, tiled=True),
        lax.psum_scatter(grad_shifts, FSDP, scatter_dimension=1, tiled=True),
        lax.psum_scatter(grad_head, FSDP, scatter_dimension=1, tiled=True),
        lax.psum_scatter(grad_qkv, FSDP, scatter_dimension=1, tiled=True),
        lax.psum_scatter(grad_proj, FSDP, scatter_dimension=1, tiled=True),
        lax.psum_scatter(grad_up, FSDP, scatter_dimension=0, tiled=True),
        lax.psum_scatter(grad_down, FSDP, scatter_dimension=1, tiled=True),
    )
    owned = lax.psum(
        (share_gains, share_shifts, share_head, share_qkv, share_proj, share_up, share_down), CTX
    )
    return (output.astype(jnp.bfloat16)[None], grad_rows[None]) + tuple(owned)


def on_any_mesh(
    image_input,
    image_segments,
    image_cotangent,
    image_gains,
    image_shifts,
    image_head_bias,
    image_qkv_weight,
    image_proj_weight,
    image_up_weight,
    image_down_weight,
    text_input,
    text_segments,
    text_cotangent,
    text_gains,
    text_shifts,
    text_head_bias,
    text_qkv_weight,
    text_proj_weight,
    text_up_weight,
    text_down_weight,
):
    image_results = any_mesh_block(
        image_input,
        image_segments,
        image_cotangent,
        image_gains,
        image_shifts,
        image_head_bias,
        image_qkv_weight,
        image_proj_weight,
        image_up_weight,
        image_down_weight,
        False,
    )
    text_results = any_mesh_block(
        text_input,
        text_segments,
        text_cotangent,
        text_gains,
        text_shifts,
        text_head_bias,
        text_qkv_weight,
        text_proj_weight,
        text_up_weight,
        text_down_weight,
        True,
    )
    return image_results + text_results


def stream_specs():
    return (
        P(FSDP, CTX, None),
        P(FSDP, None),
        P(FSDP, CTX, None),
        P(None, FSDP),
        P(None, FSDP),
        P(TP, FSDP),
        P(None, FSDP, TP),
        P(TP, FSDP),
        P(FSDP, TP),
        P(TP, FSDP),
    )


def solution(mesh):
    one = stream_specs()
    grads = (one[0], one[0]) + one[3:]
    body = on_device
    if (mesh.shape[FSDP], mesh.shape[CTX], mesh.shape[TP]) != (4, 4, 2):
        body = on_any_mesh
    return jax.shard_map(
        body, mesh=mesh, in_specs=one + one, out_specs=grads + grads, check_vma=False
    )
```

```python
import functools

import jax
import jax.numpy as jnp
from jax import lax
from jax.experimental import pallas as pl
from jax.experimental.pallas import tpu as pltpu
from jax.sharding import PartitionSpec as P

HD = 64
LANES = 128
QB = 256
KB = 512
NEG = -1e30
F32 = jnp.float32
MESH = pl.DeviceIdType.MESH
FSDP, CTX, TP = "fsdp", "ctx", "tp"
BF16 = jnp.bfloat16


def dot(left, right, dims=((1,), (0,))):
    return lax.dot_general(left, right, (dims, ((), ())), preferred_element_type=F32)


def lane_marks():
    lane = lax.broadcasted_iota(jnp.int32, (1, LANES), 1)
    first = (lane < HD).astype(F32).astype(BF16)
    second = (lane >= HD).astype(F32).astype(BF16)
    return first, second


def document_columns(row_ref, out_ref):
    for start in range(0, out_ref.shape[0], LANES):
        row = row_ref[:, start : start + LANES].astype(F32)
        out_ref[start : start + LANES, :] = jnp.transpose(jnp.broadcast_to(row, (LANES, LANES)))


def swap_halves(value):
    return pltpu.roll(value, HD, 1)


def key_range(index):
    return slice(index * KB, (index + 1) * KB)


def mix_rows(query, seg_query, keys, seg_keys, own, other, diagonal=None):
    query = query * own
    scores = []
    for block, seg in zip(keys, seg_keys):
        score = dot(query, block, ((1,), (1,)))
        ok = seg_query == seg.astype(F32)
        if diagonal is not None and len(scores) == len(keys) - 1:
            key_pos = lax.broadcasted_iota(jnp.int32, score.shape, 1)
            query_pos = diagonal + lax.broadcasted_iota(jnp.int32, score.shape, 0)
            ok = jnp.logical_and(ok, key_pos <= query_pos)
        scores.append(jnp.where(ok, score, NEG))
    top = jnp.max(functools.reduce(jnp.maximum, scores), axis=1, keepdims=True)
    acc = jnp.zeros((query.shape[0], LANES), F32)
    for score, block in zip(scores, keys):
        acc = acc + dot(jnp.exp(score - top).astype(BF16), block * other + own)
    return acc / swap_halves(acc), top + jnp.log(acc)


def pick(flag, one, zero):
    return jnp.where(flag == 1, one, zero)


def attend_text(m, seg_col, seg_row, o, lse):
    first, second = lane_marks()
    lane = lax.broadcasted_iota(jnp.int32, (QB, LANES), 1)
    o[...] = jnp.zeros_like(o)
    for source in range(4):
        keys = [m[i, QB:] for i in range(source + 1)]
        segs = [seg_row[:, key_range(i)] for i in range(source + 1)]

        def one(half, carry, source=source, keys=keys, segs=segs):
            query = m[source, :QB].astype(F32)
            query = pick(half, swap_halves(query), query).astype(BF16)
            tokens = pl.ds(pl.multiple_of(source * KB + half * QB, QB), QB)
            mixed, log_total = mix_rows(
                query, seg_col[tokens, :1], keys, segs, first, second, half * QB
            )
            lse[2 * source + half, :8] = jnp.transpose(log_total)[:8]
            mixed = pick(half, mixed, swap_halves(mixed))
            o[source] = jnp.where(lane // HD == half, mixed.astype(BF16), o[source])
            return carry

        lax.fori_loop(0, 2, one, 0)


def image_task(at, task):
    extra = 1 - (task + 8) // 12
    block = pick(extra, at.here_low * 4 + task, task - 4)
    source, half = block // 2, block % 2
    rows = pl.ds(pl.multiple_of(half * QB, QB), QB)
    tokens = pl.ds(pl.multiple_of(block * QB, QB), QB)
    return extra, block, source, rows, tokens


def task_marks(extra):
    first, second = lane_marks()
    return pick(extra, second, first), pick(extra, first, second)


def attend_image(at, m, seg_col, seg_row, o, lse):
    lane = lax.broadcasted_iota(jnp.int32, (QB, LANES), 1)
    segs = [seg_row[:, key_range(i)] for i in range(4)]
    o[...] = jnp.zeros_like(o)

    def one(task, carry):
        extra, block, source, rows, tokens = image_task(at, task)
        own, other = task_marks(extra)
        mixed, log_total = mix_rows(
            m[source, 0, rows],
            seg_col[tokens, :1],
            [m[i, 1 + extra] for i in range(4)],
            segs,
            own,
            other,
        )
        log_total = jnp.transpose(log_total)
        lse[block, pl.ds(pl.multiple_of(8 * extra, 8), 8)] = pick(
            extra, log_total[HD : HD + 8], log_total[:8]
        )
        o[source, rows] = jnp.where(lane // HD == 1 - extra, mixed.astype(BF16), o[source, rows])
        return carry

    lax.fori_loop(0, 12, one, 0)


def unmix_rows(query, grad_o, seg_query, keys, seg_keys, totals, lse, delta, own, other, diagonal=None):
    query, grad_o = query * own, grad_o * other
    grad_query = jnp.zeros((query.shape[0], LANES), F32)
    for index, (block, seg, (total, rows)) in enumerate(zip(keys, seg_keys, totals)):
        score = dot(block, query, ((1,), (1,)))
        ok = seg == seg_query
        if diagonal is not None and index == len(keys) - 1:
            key_pos = lax.broadcasted_iota(jnp.int32, score.shape, 0)
            query_pos = diagonal + lax.broadcasted_iota(jnp.int32, score.shape, 1)
            ok = jnp.logical_and(ok, key_pos <= query_pos)
        weights = jnp.where(ok, jnp.exp(score - lse), 0.0)
        grad_weights = dot(block, grad_o, ((1,), (1,)))
        grad_scores = (weights * (grad_weights - delta)).astype(BF16)
        total[rows, :] += dot(grad_scores, query) + dot(weights.astype(BF16), grad_o)
        grad_query = grad_query + dot(grad_scores, block, ((0,), (0,)))
    return grad_query * 0.125


def unattend_text(m, do, o, lse, seg_col, seg_row, acc, out):
    first, second = lane_marks()
    lane = lax.broadcasted_iota(jnp.int32, (QB, LANES), 1)
    acc[...] = jnp.zeros_like(acc)
    out[:, :QB] = jnp.zeros((4, QB, LANES), BF16)
    for source in range(4):
        keys = [m[i, QB:] for i in range(source + 1)]
        segs = [seg_col[key_range(i), :1] for i in range(source + 1)]
        totals = [(acc, key_range(i)) for i in range(source + 1)]

        def one(half, carry, source=source, keys=keys, segs=segs, totals=totals):
            query, grad_o = m[source, :QB].astype(F32), do[source].astype(F32)
            product = jnp.transpose(grad_o * o[source].astype(F32))
            query = pick(half, swap_halves(query), query).astype(BF16)
            grad_o = pick(half, grad_o, swap_halves(grad_o)).astype(BF16)
            tokens = pl.ds(pl.multiple_of(source * KB + half * QB, QB), QB)
            grad_query = unmix_rows(
                query,
                grad_o,
                seg_row[:, tokens].astype(F32),
                keys,
                segs,
                totals,
                lse[2 * source + half, :1],
                jnp.sum(pick(half, product[HD:], product[:HD]), axis=0, keepdims=True),
                first,
                second,
                half * QB,
            )
            grad_query = pick(half, swap_halves(grad_query), grad_query).astype(BF16)
            out[source, :QB] = jnp.where(lane // HD == half, grad_query, out[source, :QB])
            return carry

        lax.fori_loop(0, 2, one, 0)
    for source in range(4):
        out[source, QB:] = acc[key_range(source)].astype(BF16)


def unattend_image(at, m, do, o, lse, seg_col, seg_row, acc, out, begin, end):
    lane = lax.broadcasted_iota(jnp.int32, (QB, LANES), 1)
    segs = [seg_col[key_range(i), :1] for i in range(4)]

    def one(task, carry):
        extra, block, source, rows, tokens = image_task(at, task)
        own, other = task_marks(extra)
        grad_o = do[source, rows]
        product = jnp.transpose(grad_o.astype(F32) * o[source, rows].astype(F32))
        grad_query = unmix_rows(
            m[source, 0, rows],
            grad_o,
            seg_row[:, tokens].astype(F32),
            [m[i, 1 + extra] for i in range(4)],
            segs,
            [(acc.at[extra], key_range(i)) for i in range(4)],
            lse[block, pl.ds(pl.multiple_of(8 * extra, 8), 8)][:1],
            jnp.sum(pick(extra, product[:HD], product[HD:]), axis=0, keepdims=True),
            own,
            other,
        ).astype(BF16)
        out[source, 0, rows] = jnp.where(lane // HD == extra, grad_query, out[source, 0, rows])
        return carry

    lax.fori_loop(begin, end, one, 0)


class Bag:
    pass


def partners():
    at = Bag()
    group, here, core = lax.axis_index(FSDP), lax.axis_index(CTX), lax.axis_index(TP)
    at.group, at.here = group, here
    at.group_x = group + 1 - 2 * (group % 2)
    at.group_y = group + 2 - 4 * (group // 2)
    at.group_far = 3 - group
    at.here_low, at.here_high = here % 2, here // 2
    at.inner, at.outer = (here + 1) // 2 == 1, (here + 1) // 2 != 1
    at.ctx = (here, here + 1 - 2 * (here % 2), here + 2 - 4 * (here // 2), 3 - here)
    at.to_x, at.to_y, at.to_far = ({FSDP: g} for g in (at.group_x, at.group_y, at.group_far))
    at.to_ctx = [{CTX: c} for c in at.ctx]
    at.to_core = {TP: 1 - core}
    return at


def meet(devices):
    barrier = pltpu.get_barrier_semaphore()
    for device in devices:
        pl.semaphore_signal(barrier, inc=1, device_id=device, device_id_type=MESH)
    pl.semaphore_wait(barrier, len(devices))


class Copies:
    def __init__(self, send_sems, recv_sems, local_sems):
        self.sems = (send_sems, recv_sems, local_sems)
        self.used = [0, 0]

    def remote(self, src, dst, device, start=True):
        index = self.used[0]
        self.used[0] += 1
        copy = pltpu.make_async_remote_copy(
            src_ref=src,
            dst_ref=dst,
            send_sem=self.sems[0].at[index],
            recv_sem=self.sems[1].at[index],
            device_id=device,
            device_id_type=MESH,
        )
        if start:
            copy.start()
        return copy

    def local(self, src, dst):
        index = self.used[1]
        self.used[1] += 1
        copy = pltpu.make_async_copy(src, dst, self.sems[2].at[index])
        copy.start()
        return copy


def copy_sems(remote, local):
    return [
        pltpu.SemaphoreType.DMA((remote,)),
        pltpu.SemaphoreType.DMA((remote,)),
        pltpu.SemaphoreType.DMA((local,)),
    ]


class Gather:
    def __init__(self, copies, at, src, dst):
        self.copies, self.at, self.dst = copies, at, dst
        self.rows = src.shape[-2]
        own = self.part(at.group, 0, self.rows)
        self.own = copies.local(src, own)
        self.to_x = copies.remote(src, own, at.to_x)
        self.to_y = copies.remote(src, own, at.to_y)

    def part(self, owner, offset, size):
        rows = pl.ds(pl.multiple_of(owner * self.rows + offset, 8), size)
        return self.dst.at[:, rows, :] if len(self.dst.shape) == 3 else self.dst.at[rows, :]

    def forward(self):
        half = self.rows // 2
        self.to_x.wait_recv()
        self.to_y.wait_recv()
        top = self.part(self.at.group_y, 0, half)
        low = self.part(self.at.group_x, half, half)
        self.far_x = self.copies.remote(top, top, self.at.to_x)
        self.far_y = self.copies.remote(low, low, self.at.to_y)

    def arrived(self):
        self.own.wait()
        self.far_x.wait_recv()
        self.far_y.wait_recv()

    def sent(self):
        for copy in (self.to_x, self.to_y, self.far_x, self.far_y):
            copy.wait_send()


def normalise(rows):
    mean = jnp.mean(rows, axis=-1, keepdims=True)
    centred = rows - mean
    inv = lax.rsqrt(jnp.mean(centred * centred, axis=-1, keepdims=True) + 1e-05)
    return centred * inv, inv


def lane_pair(low, high):
    lane = lax.broadcasted_iota(jnp.int32, low[0].shape, 1)
    left = low[0] if low[1] == 0 else pltpu.roll(low[0], HD, 1)
    right = high[0] if high[1] == 1 else pltpu.roll(high[0], HD, 1)
    return jnp.where(lane < HD, left, right)


def head_tile(ref, start, index, rows=slice(None)):
    first = start + (index // 2) * LANES
    return ref[rows, first : first + LANES], index % 2


def write_messages(qkv, out, heads):
    width = heads * HD
    tokens = qkv.shape[0]
    for c in range(4):
        if heads == 4:
            half = tokens // 2
            out[c, :half] = lane_pair(
                head_tile(qkv, 0, c, slice(0, half)), head_tile(qkv, 0, c, slice(half, None))
            ).astype(BF16)
            out[c, half:] = lane_pair(
                head_tile(qkv, width, c), head_tile(qkv, 2 * width, c)
            ).astype(BF16)
        else:
            e = 4 + c // 2
            out[c, 0] = lane_pair(head_tile(qkv, 0, c), head_tile(qkv, 0, e)).astype(BF16)
            out[c, 1] = lane_pair(
                head_tile(qkv, width, c), head_tile(qkv, 2 * width, c)
            ).astype(BF16)
            out[c, 2] = lane_pair(
                head_tile(qkv, 2 * width, e), head_tile(qkv, width, e)
            ).astype(BF16)


def message_shape(heads, tokens):
    part = (tokens // 2 + tokens, LANES) if heads == 4 else (3, tokens, LANES)
    return (4,) + part


def first_rows(x_ref, small_ref, weight_ref, first_ref, qkv_ref, step):
    width = weight_ref.shape[2]
    rows = slice(step * 256, step * 256 + 256)
    normed, _ = normalise(x_ref[rows, :].astype(F32))
    first = (normed * small_ref[0:1] + small_ref[2:3]).astype(BF16)
    first_ref[:, rows] = jnp.transpose(first)
    bias = small_ref[6:7]
    qkv_ref[rows, :width] = (dot(first, weight_ref[0]) + bias[:, :width]) * 0.125
    qkv_ref[rows, width : 2 * width] = dot(first, weight_ref[1])
    qkv_ref[rows, 2 * width :] = dot(first, weight_ref[2]) + bias[:, width : 2 * width]


def spread_small(at, gains, shifts, bias, wide, flat, out):
    width = wide.shape[1]
    columns, bias_columns = gains.shape[1], bias.shape[1]
    wide[...] = jnp.zeros_like(wide)
    flat[...] = jnp.zeros_like(flat)
    wide[0:2, :columns] = gains[...].astype(F32)
    wide[2:6, :columns] = shifts[...].astype(F32)
    flat[0:1, :bias_columns] = bias[...].astype(F32)
    out[0:8] = pltpu.roll(wide[...], at.group * columns, 1)
    line = pltpu.roll(flat[...], at.group * bias_columns, 1)
    out[8:16] = jnp.zeros((8, width), F32)
    for row in range(3):
        out[6 + row : 7 + row] = line[0:1, row * width : (row + 1) * width]


FRONT_IN, FRONT_OUT, FRONT_SCRATCH = 9, 10, 10


def front_kernel(*refs):
    at = partners()
    ins = [refs[:FRONT_IN], refs[FRONT_IN : 2 * FRONT_IN]]
    refs = refs[2 * FRONT_IN :]
    outs = [refs[:FRONT_OUT], refs[FRONT_OUT : 2 * FRONT_OUT]]
    refs = refs[2 * FRONT_OUT :]
    scratch = [refs[:FRONT_SCRATCH], refs[FRONT_SCRATCH : 2 * FRONT_SCRATCH]]
    copies = Copies(*refs[2 * FRONT_SCRATCH :])
    streams = []
    for in_refs, out_refs, own in zip(ins, outs, scratch):
        s = Bag()
        s.x, s.seg_row, s.gains, s.shifts, s.bias, s.qkv, s.up, s.down, s.proj = in_refs
        (
            s.weight, s.small, s.first, s.messages, s.proj_full, s.up_full, s.down_full, s.o, s.lse,
            s.o_got,
        ) = out_refs
        (
            s.small_in, s.small_own, s.wide, s.flat, s.rows, s.mine, s.got, s.down_t, s.proj_t, s.seg_col,
        ) = own
        s.heads = s.weight.shape[2] // HD
        streams.append(s)
    meet([at.to_x, at.to_y, at.to_far] + at.to_ctx[1:])
    text, image = streams
    image.gather = Gather(copies, at, image.qkv, image.weight)
    for s in (image, text):
        spread_small(at, s.gains, s.shifts, s.bias, s.wide, s.flat, s.small_own)
    for s in (image, text):
        s.small_done = [
            copies.remote(s.small_own, s.small_in.at[i], device)
            for i, device in enumerate((at.to_x, at.to_y, at.to_far))
        ]
    image.gather.forward()
    text.gather = Gather(copies, at, text.qkv, text.weight)
    text.down_t[...] = jnp.transpose(text.down[...])
    text.proj_t[...] = jnp.transpose(text.proj[...])
    for s in (image, text):
        document_columns(s.seg_row, s.seg_col)

    def project(s):
        for copy in s.small_done:
            copy.wait_recv()
        s.small[...] = s.small_own[...] + s.small_in[0] + s.small_in[1] + s.small_in[2]
        s.gather.arrived()
        for step in range(s.x.shape[0] // 256):
            first_rows(s.x, s.small, s.weight, s.first, s.rows, step)
        write_messages(s.rows, s.mine, s.heads)
        s.sends = send_blocks(copies, at, s.mine, s.got)

    def gather_rest(s):
        pieces = (s.proj_t, s.up, s.down_t) if s.heads == 4 else (s.proj, s.up, s.down)
        s.rest = [
            Gather(copies, at, piece, full)
            for piece, full in zip(pieces, (s.proj_full, s.up_full, s.down_full))
        ]

    project(image)
    text.gather.forward()
    gather_rest(image)
    project(text)
    gather_rest(text)
    for gather in image.rest:
        gather.forward()
    for copy in image.sends:
        copy.wait()
    image.keep = copies.local(image.got, image.messages)
    attend_image(at, image.got, image.seg_col, image.seg_row, image.o, image.lse)
    image.o_done = send_blocks(copies, at, image.o, image.o_got)
    for gather in text.rest:
        gather.forward()
    for copy in text.sends:
        copy.wait()
    text.keep = copies.local(text.got, text.messages)
    attend_text(text.got, text.seg_col, text.seg_row, text.o, text.lse)
    text.o_done = send_blocks(copies, at, text.o, text.o_got)
    for s in (image, text):
        for gather in s.rest:
            gather.arrived()
        for gather in [s.gather] + s.rest:
            gather.sent()
        for copy in s.small_done:
            copy.wait_send()
        s.keep.wait()
        for copy in s.o_done:
            copy.wait()


def front(streams):
    vmem, hbm = pl.BlockSpec(memory_space=pltpu.VMEM), pl.BlockSpec(memory_space=pl.ANY)
    out_shape, out_specs, scratch = [], [], []
    for x, seg, gains, shifts, bias, qkv, up, down, proj in streams:
        tokens, width = x.shape
        own = qkv.shape[2]
        messages = message_shape(own // HD, tokens)
        hidden = up.shape[1]
        small = jax.ShapeDtypeStruct((16, width), F32)
        out_shape += [
            jax.ShapeDtypeStruct((3, width, own), BF16),
            small,
            jax.ShapeDtypeStruct((width, tokens), BF16),
            jax.ShapeDtypeStruct(messages, BF16),
            jax.ShapeDtypeStruct((width, own), BF16),
            jax.ShapeDtypeStruct((width, hidden), BF16),
            jax.ShapeDtypeStruct((width, hidden), BF16),
            jax.ShapeDtypeStruct((4, QB if own == 4 * HD else KB, LANES), BF16),
            jax.ShapeDtypeStruct((4 * tokens // QB, 16, QB), F32),
            jax.ShapeDtypeStruct((4, QB if own == 4 * HD else KB, LANES), BF16),
        ]
        out_specs += [vmem, vmem, vmem, hbm, hbm, hbm, hbm, vmem, vmem, hbm]
        scratch += [
            pltpu.VMEM((3, 16, width), F32),
            pltpu.VMEM((16, width), F32),
            pltpu.VMEM((8, width), F32),
            pltpu.VMEM((8, 3 * width), F32),
            pltpu.VMEM((tokens, 3 * own), F32),
            pltpu.VMEM(messages, BF16),
            pltpu.VMEM(messages, BF16),
            pltpu.VMEM((width // 4, hidden), BF16),
            pltpu.VMEM((width // 4, own), BF16),
            pltpu.VMEM((4 * tokens, LANES), F32),
        ]
    results = pl.pallas_call(
        front_kernel,
        out_shape=out_shape,
        in_specs=[vmem] * (2 * FRONT_IN),
        out_specs=out_specs,
        scratch_shapes=scratch + copy_sems(2 * (3 + 4 * 4 + 6), 2 * 7),
        compiler_params=pltpu.CompilerParams(
            collective_id=0, has_side_effects=True, vmem_limit_bytes=63 << 20
        ),
        name="front",
    )(*streams[0], *streams[1])
    return results[:FRONT_OUT], results[FRONT_OUT:]


STEP = 384


def by_columns(columns, body):
    def one(index, carry):
        body(pl.ds(pl.multiple_of(index * STEP, STEP), STEP))
        return carry

    lax.fori_loop(0, columns // STEP, one, 0)


class PlaneSum:
    def __init__(self, copies, at, src, arrivals, loads=None):
        self.copies, self.at = copies, at
        self.in_x, self.in_y, self.in_top, self.in_low = arrivals
        half, self.columns = self.in_top.shape
        self.half, rows = half, 2 * half

        def block(owner, offset, size=half):
            return src.at[pl.ds(pl.multiple_of(owner * rows + offset, 8), size), :]

        self.first = [
            copies.remote(block(at.group_far, 0), self.in_x.at[1], at.to_x),
            copies.remote(block(at.group_far, half), self.in_y.at[1], at.to_y),
            copies.remote(block(at.group_x, 0), self.in_x.at[0], at.to_x),
            copies.remote(block(at.group_y, half), self.in_y.at[0], at.to_y),
        ]
        parts = [block(at.group_y, 0), block(at.group_x, half), block(at.group, 0, rows)]
        if loads is None:
            self.loads = []
            self.pass_top, self.pass_low, self.own = parts
        else:
            self.loads = [copies.local(part, load) for part, load in zip(parts, loads)]
            self.pass_top, self.pass_low, self.own = loads

    def cross(self):
        for copy in self.loads:
            copy.wait()
        self.first[0].wait_recv()

        def top(cols):
            self.pass_top[:, cols] = (
                self.pass_top[:, cols].astype(F32) + self.in_x[1, :, cols].astype(F32)
            ).astype(BF16)

        by_columns(self.columns, top)
        self.second = [self.copies.remote(self.pass_top, self.in_top, self.at.to_y)]
        self.first[1].wait_recv()

        def low(cols):
            self.pass_low[:, cols] = (
                self.pass_low[:, cols].astype(F32) + self.in_y[1, :, cols].astype(F32)
            ).astype(BF16)

        by_columns(self.columns, low)
        self.second.append(self.copies.remote(self.pass_low, self.in_low, self.at.to_x))

    def arrived(self):
        for copy in self.first[2:] + self.second:
            copy.wait_recv()

    def halves(self, cols):
        half = self.half
        return (
            self.own[:half, cols].astype(F32)
            + self.in_x[0, :, cols].astype(F32)
            + self.in_top[:, cols].astype(F32),
            self.own[half:, cols].astype(F32)
            + self.in_y[0, :, cols].astype(F32)
            + self.in_low[:, cols].astype(F32),
        )

    def sent(self):
        for copy in self.first + self.second:
            copy.wait_send()

    @staticmethod
    def arrivals(rows, columns):
        half = rows // 2
        pair, one = pltpu.VMEM((2, half, columns), BF16), pltpu.VMEM((half, columns), BF16)
        return [pair, pair, one, one]

    @staticmethod
    def loads_scratch(rows, columns):
        half = rows // 2
        one = pltpu.VMEM((half, columns), BF16)
        return [one, one, pltpu.VMEM((rows, columns), BF16)]


class LineSum:
    def __init__(self, copies, at, values, buffers, final, begin, end):
        self.at, self.values, self.final, self.range = at, values, final, (begin, end)
        self.pair, self.outer_in, self.inner_in = buffers

        def part(ref):
            return ref.at[:, begin:end]

        self.up = copies.remote(part(self.pair), part(self.outer_in), at.to_ctx[1], False)
        self.across = copies.remote(part(self.pair), part(self.inner_in), at.to_ctx[3], False)
        self.down = copies.remote(part(final), part(final), at.to_ctx[1], False)

    def each(self, body):
        begin, end = self.range

        def one(index, carry):
            body(pl.ds(pl.multiple_of(begin + index * STEP, LANES), STEP))
            return carry

        lax.fori_loop(0, (end - begin) // STEP, one, 0)

    def gather(self):
        half = self.pair.shape[0] // 2

        @pl.when(self.at.outer)
        def _():
            def add(cols):
                top, low = self.values(cols)
                self.pair[:half, cols] = top.astype(BF16)
                self.pair[half:, cols] = low.astype(BF16)

            self.each(add)
            self.up.start()

    def join(self):
        half = self.pair.shape[0] // 2

        @pl.when(self.at.inner)
        def _():
            self.up.wait_recv()

            def add(cols):
                top, low = self.values(cols)
                self.pair[:half, cols] = (top + self.outer_in[:half, cols].astype(F32)).astype(BF16)
                self.pair[half:, cols] = (low + self.outer_in[half:, cols].astype(F32)).astype(BF16)

            self.each(add)
            self.across.start()

    def share(self):
        @pl.when(self.at.inner)
        def _():
            self.across.wait_recv()

            def add(cols):
                self.final[:, cols] = (
                    self.pair[:, cols].astype(F32) + self.inner_in[:, cols].astype(F32)
                ).astype(BF16)

            self.each(add)
            self.down.start()

    def finish(self):
        @pl.when(self.at.outer)
        def _():
            self.up.wait_send()
            self.down.wait_recv()

        @pl.when(self.at.inner)
        def _():
            self.across.wait_send()
            self.down.wait_send()

    @staticmethod
    def scratch(rows, columns):
        return [pltpu.VMEM((rows, columns), BF16)] * 3


def chunks(tokens, size=256):
    return [slice(start, start + size) for start in range(0, tokens, size)]


def as_f32(ref, index, rows=slice(None)):
    return ref[index, rows].astype(F32)


def take_mixed(got, mixed, at, heads):
    tokens = mixed.shape[0]
    if heads == 4:
        half = tokens // 2
        for tile in range(2):
            cols = slice(tile * LANES, (tile + 1) * LANES)
            one, two = as_f32(got, 2 * tile), as_f32(got, 2 * tile + 1)
            mixed[:half, cols] = lane_pair((one, 0), (two, 0)).astype(BF16)
            mixed[half:, cols] = lane_pair((one, 1), (two, 1)).astype(BF16)
        return
    for tile in range(2):
        cols = slice(tile * LANES, (tile + 1) * LANES)
        mixed[:, cols] = lane_pair(
            (as_f32(got, 2 * tile), 1), (as_f32(got, 2 * tile + 1), 1)
        ).astype(BF16)
    part = at.here // 2
    mixed[:, 2 * LANES :] = lane_pair((as_f32(got, part), 0), (as_f32(got, part + 2), 0)).astype(BF16)


def write_grad_o(grad, out, heads):
    tokens = grad.shape[0]
    half = tokens // 2
    for c in range(4):
        if heads == 4:
            out[c] = lane_pair(
                head_tile(grad, 0, c, slice(0, half)), head_tile(grad, 0, c, slice(half, None))
            ).astype(BF16)
        else:
            out[c] = lane_pair(head_tile(grad, 0, 4 + c // 2), head_tile(grad, 0, c)).astype(BF16)


def send_blocks(copies, at, mine, out):
    done = [copies.local(mine.at[at.here], out.at[at.here])]
    for other in at.ctx[1:]:
        done.append(copies.remote(mine.at[other], out.at[at.here], {CTX: other}))
    return done


MIDDLE_IN, MIDDLE_OUT, MIDDLE_SCRATCH = 7, 5, 17


def middle_kernel(*refs):
    at = partners()
    ins = [refs[:MIDDLE_IN], refs[MIDDLE_IN : 2 * MIDDLE_IN]]
    refs = refs[2 * MIDDLE_IN :]
    outs = [refs[:MIDDLE_OUT], refs[MIDDLE_OUT : 2 * MIDDLE_OUT]]
    refs = refs[2 * MIDDLE_OUT :]
    scratch = [refs[:MIDDLE_SCRATCH], refs[MIDDLE_SCRATCH : 2 * MIDDLE_SCRATCH]]
    arrivals = refs[2 * MIDDLE_SCRATCH : 2 * MIDDLE_SCRATCH + 4]
    copies = Copies(*refs[2 * MIDDLE_SCRATCH + 4 :])
    streams = []
    for in_refs, out_refs, own in zip(ins, outs, scratch):
        s = Bag()
        s.o, s.x, s.dy, s.small, proj_in, up_in, down_in = in_refs
        s.y, s.dmid, s.do_out, s.rest_out, s.sums = out_refs
        (
            s.proj, s.up, s.down, s.rest, s.mixed, s.part, s.part_in, s.mid, s.first, s.first_t, s.dy_t,
            s.act, s.dz, s.grad, s.grad_in, s.do, s.do_mine,
        ) = own
        s.heads = proj_in.shape[1] // HD
        s.proj_done = copies.local(proj_in, s.proj)
        s.rest_done = [copies.local(up_in, s.up), copies.local(down_in, s.down)]
        streams.append(s)
    text, image = streams
    meet([at.to_x, at.to_y] + at.to_ctx[1:] + [at.to_core])

    def project(s):
        take_mixed(s.o, s.mixed, at, s.heads)
        s.proj_done.wait()
        for cols in chunks(s.x.shape[1]):
            s.part[:, cols] = dot(s.mixed[...], s.proj[cols, :], ((1,), (1,)))
        s.part_done = copies.remote(s.part, s.part_in, at.to_core)
        s.sums[...] = jnp.zeros_like(s.sums)
        for rows in chunks(s.dy.shape[0]):
            s.dy_t[:, rows] = jnp.transpose(s.dy[rows, :])

    def second_norm(s):
        s.part_done.wait()
        for rows in chunks(s.x.shape[0]):
            middle = (
                s.x[rows, :].astype(F32) + s.part[rows, :] + s.part_in[rows, :] + s.small[3:4]
            )
            s.mid[rows, :] = middle
            normed, _ = normalise(middle)
            low = (normed * s.small[1:2] + s.small[4:5]).astype(BF16)
            s.first[rows, :] = low
            s.first_t[:, rows] = jnp.transpose(low)

    def feed_forward(s):
        tokens, width = s.x.shape
        hidden, own = s.up.shape[1], s.proj.shape[1]
        for copy in s.rest_done:
            copy.wait()

        def tile(index, carry):
            cols = pl.ds(pl.multiple_of(index * 256, 256), 256)
            up, down = s.up[:, cols], s.down[:, cols]
            per_row = width // 256
            up_cols = pl.ds(pl.multiple_of(own + index * 256, LANES), 256)
            down_cols = pl.ds(pl.multiple_of(own + hidden + index * 256, LANES), 256)
            row = pl.ds(7 + index // per_row, 1)
            place = pl.ds(pl.multiple_of((index % per_row) * 256, 256), 256)
            bias = s.small[row, place]
            total = jnp.zeros((1, 256), F32)
            for rows in chunks(tokens):
                z = dot(s.first[rows, :], up) + bias
                sg = jax.nn.sigmoid(1.702 * z)
                zs = z * sg
                s.act[rows, cols] = zs.astype(BF16)
                grad = dot(s.dy[rows, :], down)
                low = (grad * (sg + 1.702 * zs * (1.0 - sg))).astype(BF16)
                s.dz[rows, cols] = low
                total = total + jnp.sum(low.astype(F32), axis=0, keepdims=True)
            s.sums[row, place] = total
            s.rest[:, up_cols] = dot(s.first_t[...], s.dz[:, cols]).astype(BF16)
            s.rest[:, down_cols] = dot(s.dy_t[...], s.act[:, cols]).astype(BF16)
            return carry

        lax.fori_loop(0, hidden // 256, tile, 0)
        for cols in chunks(width):
            s.grad[0, :, cols] = dot(s.dz[...], s.up[cols, :], ((1,), (1,)))
        s.grad_done = copies.remote(s.grad.at[0], s.grad_in.at[0], at.to_core)
        for cols in chunks(width):
            s.grad[1, :, cols] = dot(s.act[...], s.down[cols, :], ((1,), (1,)))
        s.y_done = copies.remote(s.grad.at[1], s.grad_in.at[1], at.to_core)

    def back(s):
        sums = s.sums
        s.grad_done.wait()
        for rows in chunks(s.x.shape[0]):
            normed, inv = normalise(s.mid[rows, :])
            second = s.grad[0, rows, :] + s.grad_in[0, rows, :]
            scaled = second * s.small[1:2]
            dy = s.dy[rows, :].astype(F32)
            dmid = dy + inv * (
                scaled
                - jnp.mean(scaled, axis=-1, keepdims=True)
                - normed * jnp.mean(scaled * normed, axis=-1, keepdims=True)
            )
            s.dmid[rows, :] = dmid
            sums[1:2] += jnp.sum(second * normed, axis=0, keepdims=True)
            sums[3:4] += jnp.sum(dmid, axis=0, keepdims=True)
            sums[4:5] += jnp.sum(second, axis=0, keepdims=True)
            sums[5:6] += jnp.sum(dy, axis=0, keepdims=True)
            low = dmid.astype(BF16)
            s.first_t[:, rows] = jnp.transpose(low)
            s.do[rows, :] = dot(low, s.proj[...])
        write_grad_o(s.do, s.do_mine, s.heads)
        s.do_done = send_blocks(copies, at, s.do_mine, s.do_out)
        s.rest[:, : s.proj.shape[1]] = dot(s.first_t[...], s.mixed[...]).astype(BF16)

    def output(s):
        s.y_done.wait()
        for rows in chunks(s.x.shape[0]):
            s.y[rows, :] = (
                s.mid[rows, :] + s.grad[1, rows, :] + s.grad_in[1, rows, :] + s.small[5:6]
            ).astype(BF16)

    project(text)
    project(image)
    second_norm(text)
    feed_forward(text)
    second_norm(image)
    back(text)
    plane = PlaneSum(copies, at, text.rest, arrivals)
    feed_forward(image)
    back(image)
    keep = copies.local(image.rest, image.rest_out)
    plane.cross()
    output(text)
    output(image)
    plane.arrived()
    half = plane.half

    def put(cols):
        text.rest_out[:half, cols], text.rest_out[half:, cols] = plane.halves(cols)

    by_columns(plane.columns, put)
    plane.sent()
    keep.wait()
    for s in streams:
        for copy in s.do_done:
            copy.wait()


def middle(streams):
    vmem, hbm = pl.BlockSpec(memory_space=pltpu.VMEM), pl.BlockSpec(memory_space=pl.ANY)
    out_shape, out_specs, scratch = [], [], []
    arrivals = None
    for o, x, dy, small, proj, up, down in streams:
        tokens, width = x.shape
        hidden, own = up.shape[1], proj.shape[1]
        rest = (width, own + 2 * hidden)
        summed = arrivals is None
        if summed:
            arrivals = PlaneSum.arrivals(width // 4, rest[1])
        out_shape += [
            jax.ShapeDtypeStruct((tokens, width), BF16),
            jax.ShapeDtypeStruct((tokens, width), F32),
            jax.ShapeDtypeStruct(o.shape, BF16),
            jax.ShapeDtypeStruct((width // 4, rest[1]), F32)
            if summed
            else jax.ShapeDtypeStruct(rest, BF16),
            jax.ShapeDtypeStruct(small.shape, F32),
        ]
        out_specs += [vmem, vmem, hbm, vmem if summed else hbm, vmem]
        scratch += [
            pltpu.VMEM(proj.shape, BF16),
            pltpu.VMEM(up.shape, BF16),
            pltpu.VMEM(down.shape, BF16),
            pltpu.VMEM(rest, BF16),
            pltpu.VMEM((tokens, own), BF16),
            pltpu.VMEM((tokens, width), F32),
            pltpu.VMEM((tokens, width), F32),
            pltpu.VMEM((tokens, width), F32),
            pltpu.VMEM((tokens, width), BF16),
            pltpu.VMEM((width, tokens), BF16),
            pltpu.VMEM((width, tokens), BF16),
            pltpu.VMEM((tokens, hidden), BF16),
            pltpu.VMEM((tokens, hidden), BF16),
            pltpu.VMEM((2, tokens, width), F32),
            pltpu.VMEM((2, tokens, width), F32),
            pltpu.VMEM((tokens, own), F32),
            pltpu.VMEM(o.shape, BF16),
        ]
    results = pl.pallas_call(
        middle_kernel,
        out_shape=out_shape,
        in_specs=([vmem] * 4 + [hbm] * 3) * 2,
        out_specs=out_specs,
        scratch_shapes=scratch + arrivals + copy_sems(2 * 6 + 6, 2 * 4 + 1),
        compiler_params=pltpu.CompilerParams(
            collective_id=1, has_side_effects=True, vmem_limit_bytes=64 * 1024 * 1000
        ),
        name="middle",
    )(*streams[0], *streams[1])
    return results[:MIDDLE_OUT], results[MIDDLE_OUT:]


def take_dqkv(got, out, at, heads):
    tokens, width = out.shape[0], heads * HD

    def put(which, tile, rows, low, high):
        start = which * width + tile * LANES
        out[rows, start : start + LANES] = lane_pair(low, high).astype(BF16)

    every = slice(None)
    if heads == 4:
        half = tokens // 2
        top, low, keys = slice(0, half), slice(half, tokens), slice(half, half + tokens)
        for tile in range(2):
            one, two = 2 * tile, 2 * tile + 1
            for side, rows in ((0, top), (1, low)):
                put(0, tile, rows, (as_f32(got, one, top), side), (as_f32(got, two, top), side))
            for which in (1, 2):
                side = which - 1
                put(which, tile, every, (as_f32(got, one, keys), side), (as_f32(got, two, keys), side))
        return

    def part(position, index):
        return got[position, index].astype(F32)

    for tile in range(2):
        one, two = 2 * tile, 2 * tile + 1
        put(0, tile, every, (part(one, 0), 0), (part(two, 0), 0))
        put(1, tile, every, (part(one, 1), 0), (part(two, 1), 0))
        put(2, tile, every, (part(one, 1), 1), (part(two, 1), 1))
    put(0, 2, every, (part(at.here_high, 0), 1), (part(at.here_high + 2, 0), 1))
    one, two = part(0, 2) + part(1, 2), part(2, 2) + part(3, 2)
    put(1, 2, every, (one, 1), (two, 1))
    put(2, 2, every, (one, 0), (two, 0))


LAST_IN, LAST_OUT, LAST_SCRATCH = 12, 4, 18


def last_kernel(*refs):
    at = partners()
    ins = [refs[:LAST_IN], refs[LAST_IN : 2 * LAST_IN]]
    refs = refs[2 * LAST_IN :]
    outs = [refs[:LAST_OUT], refs[LAST_OUT : 2 * LAST_OUT]]
    refs = refs[2 * LAST_OUT :]
    count = LAST_SCRATCH + 10
    scratch = [refs[:count], refs[count : 2 * count]]
    refs = refs[2 * count :]
    rest_arrivals, rest_loads = refs[:4], refs[4:7]
    copies = Copies(*refs[7:])
    streams = []
    for in_refs, out_refs, own in zip(ins, outs, scratch):
        s = Bag()
        (
            s.m_in, s.do_in, s.o_in, s.lse, s.seg_row, s.first_in, s.x_in, s.small, s.weight_in, s.dmid_in,
            s.rest, s.sums_in,
        ) = in_refs
        s.grad_rows, s.sums, s.rest_final, s.qkv_final = out_refs
        (
            s.m, s.do, s.o, s.seg_col, s.acc, s.back, s.got, s.dqkv, s.weight, s.first, s.x, s.dmid,
            s.part, s.part_in, s.g_qkv, s.sums_own, s.sums_out, s.sums_got,
        ) = own[:LAST_SCRATCH]
        s.rest_line, s.qkv_line = own[LAST_SCRATCH : LAST_SCRATCH + 3], own[LAST_SCRATCH + 3 : LAST_SCRATCH + 6]
        s.qkv_arrivals = own[LAST_SCRATCH + 6 :]
        s.heads = s.weight.shape[2] // HD
        s.reads = [
            copies.local(src, dst) for src, dst in ((s.m_in, s.m), (s.do_in, s.do), (s.o_in, s.o))
        ]
        streams.append(s)
    text, image = streams
    meet([at.to_x, at.to_y] + at.to_ctx[1:] + [at.to_core])
    plane = PlaneSum(copies, at, image.rest, rest_arrivals, rest_loads)
    text_half = text.rest.shape[0] // 2

    def text_values(cols):
        return text.rest[:text_half, cols], text.rest[text_half:, cols]

    text_line = LineSum(
        copies, at, text_values, text.rest_line, text.rest_final, 0, text.rest.shape[1]
    )
    text_line.gather()
    for s in (image, text):
        document_columns(s.seg_row, s.seg_col)
    for s in streams:
        s.loads = [
            copies.local(src, dst)
            for src, dst in (
                (s.weight_in, s.weight), (s.first_in, s.first), (s.x_in, s.x), (s.dmid_in, s.dmid),
            )
        ]
    image.acc[...] = jnp.zeros_like(image.acc)
    image.back[...] = jnp.zeros_like(image.back)
    for s in (image, text):
        for copy in s.reads:
            copy.wait()

    def image_tasks(begin, end):
        s = image
        unattend_image(at, s.m, s.do, s.o, s.lse, s.seg_col, s.seg_row, s.acc, s.back, begin, end)

    image_tasks(0, 6)
    text_line.join()
    image_tasks(6, 12)
    for source in range(4):
        image.back[source, 1] = image.acc[0, key_range(source)].astype(BF16)
        image.back[source, 2] = image.acc[1, key_range(source)].astype(BF16)
    image.sends = send_blocks(copies, at, image.back, image.got)
    text_line.share()
    s = text
    unattend_text(s.m, s.do, s.o, s.lse, s.seg_col, s.seg_row, s.acc.at[0], s.back)
    text.sends = send_blocks(copies, at, text.back, text.got)
    plane.cross()

    def project(s):
        width = s.x.shape[1]
        own = s.heads * HD
        for copy in s.sends:
            copy.wait()
        for copy in s.loads:
            copy.wait()
        take_dqkv(s.got, s.dqkv, at, s.heads)
        for which in range(3):
            cols = slice(which * own, (which + 1) * own)
            s.g_qkv[:, cols] = dot(s.first[...], s.dqkv[:, cols]).astype(BF16)
        s.qkv_plane = PlaneSum(copies, at, s.g_qkv, s.qkv_arrivals)
        for cols in chunks(width):
            total = dot(s.dqkv[:, :own], s.weight[0, cols, :], ((1,), (1,)))
            total = total + dot(s.dqkv[:, own : 2 * own], s.weight[1, cols, :], ((1,), (1,)))
            s.part[:, cols] = total + dot(s.dqkv[:, 2 * own :], s.weight[2, cols, :], ((1,), (1,)))
        s.part_done = copies.remote(s.part, s.part_in, at.to_core)
        s.sums_own[...] = s.sums_in[...]
        s.sums_own[6:7, :own] = jnp.sum(s.dqkv[:, :own].astype(F32), axis=0, keepdims=True)
        s.sums_own[6:7, own:] = jnp.sum(s.dqkv[:, 2 * own :].astype(F32), axis=0, keepdims=True)
        s.qkv_sum = LineSum(
            copies, at, s.qkv_plane.halves, s.qkv_line, s.qkv_final, 0, 3 * own
        )

    def input_grad(s):
        s.part_done.wait()
        for rows in chunks(s.x.shape[0]):
            normed, inv = normalise(s.x[rows, :].astype(F32))
            first = s.part[rows, :] + s.part_in[rows, :]
            scaled = first * s.small[0:1]
            s.grad_rows[rows, :] = s.dmid[rows, :] + inv * (
                scaled
                - jnp.mean(scaled, axis=-1, keepdims=True)
                - normed * jnp.mean(scaled * normed, axis=-1, keepdims=True)
            )
            s.sums_own[0:1] += jnp.sum(first * normed, axis=0, keepdims=True)
            s.sums_own[2:3] += jnp.sum(first, axis=0, keepdims=True)
        s.sums_done = [copies.remote(s.sums_own, s.sums_got.at[0], at.to_x)]

    def add_sums(s, step):
        s.sums_done[-1].wait_recv()
        before = s.sums_own if step == 0 else s.sums_out.at[step - 1]
        after = s.sums if step == 3 else s.sums_out.at[step]
        after[...] = before[...] + s.sums_got[step]
        if step < 3:
            device = (at.to_y, at.to_ctx[1], at.to_ctx[2])[step]
            s.sums_done.append(copies.remote(after, s.sums_got.at[step + 1], device))

    project(image)
    plane.arrived()
    middle_column = plane.columns // (2 * STEP) * STEP
    rest_lines = [
        LineSum(copies, at, plane.halves, image.rest_line, image.rest_final, begin, end)
        for begin, end in ((0, middle_column), (middle_column, plane.columns))
    ]
    rest_lines[0].gather()
    input_grad(image)
    image.qkv_plane.cross()
    rest_lines[1].gather()
    project(text)
    rest_lines[0].join()
    input_grad(text)
    text.qkv_plane.cross()
    image.qkv_plane.arrived()
    image.qkv_sum.gather()
    rest_lines[1].join()
    add_sums(image, 0)
    rest_lines[0].share()
    add_sums(text, 0)
    text.qkv_plane.arrived()
    text.qkv_sum.gather()
    image.qkv_sum.join()
    add_sums(image, 1)
    add_sums(text, 1)
    rest_lines[1].share()
    text.qkv_sum.join()
    add_sums(image, 2)
    add_sums(text, 2)
    image.qkv_sum.share()
    text.qkv_sum.share()
    add_sums(image, 3)
    add_sums(text, 3)
    for line in [text_line] + rest_lines + [image.qkv_sum, text.qkv_sum]:
        line.finish()
    plane.sent()
    for s in streams:
        s.qkv_plane.sent()
        for copy in s.sums_done:
            copy.wait_send()


def last(streams):
    vmem, hbm = pl.BlockSpec(memory_space=pltpu.VMEM), pl.BlockSpec(memory_space=pl.ANY)
    out_shape, scratch = [], []
    for messages, do, o, lse, seg, first, x, small, weight, dmid, rest, sums in streams:
        tokens, width = x.shape
        own = weight.shape[2]
        rest_shape, qkv_shape = (width // 4, rest.shape[1]), (width // 4, 3 * own)
        out_shape += [
            jax.ShapeDtypeStruct((tokens, width), F32),
            jax.ShapeDtypeStruct(small.shape, F32),
            jax.ShapeDtypeStruct(rest_shape, BF16),
            jax.ShapeDtypeStruct(qkv_shape, BF16),
        ]
        scratch += [
            pltpu.VMEM(messages.shape, BF16),
            pltpu.VMEM(do.shape, BF16),
            pltpu.VMEM(do.shape, BF16),
            pltpu.VMEM((4 * tokens, LANES), F32),
            pltpu.VMEM((1 if own == 4 * HD else 2, 4 * tokens, LANES), F32),
            pltpu.VMEM(messages.shape, BF16),
            pltpu.VMEM(messages.shape, BF16),
            pltpu.VMEM((tokens, 3 * own), BF16),
            pltpu.VMEM(weight.shape, BF16),
            pltpu.VMEM(first.shape, BF16),
            pltpu.VMEM((tokens, width), BF16),
            pltpu.VMEM((tokens, width), F32),
            pltpu.VMEM((tokens, width), F32),
            pltpu.VMEM((tokens, width), F32),
            pltpu.VMEM((width, 3 * own), BF16),
            pltpu.VMEM(small.shape, F32),
            pltpu.VMEM((3,) + small.shape, F32),
            pltpu.VMEM((4,) + small.shape, F32),
        ]
        scratch += LineSum.scratch(*rest_shape) + LineSum.scratch(*qkv_shape)
        scratch += PlaneSum.arrivals(*qkv_shape)
    scratch += PlaneSum.arrivals(*rest_shape) + PlaneSum.loads_scratch(*rest_shape)
    specs = [hbm, hbm, hbm, vmem, vmem, hbm, hbm, vmem, hbm, hbm, vmem, vmem]
    specs += specs[:10] + [hbm, vmem]
    results = pl.pallas_call(
        last_kernel,
        out_shape=out_shape,
        in_specs=specs,
        out_specs=[vmem] * 8,
        scratch_shapes=scratch + copy_sems(2 * (3 + 1 + 4 + 6) + 6 + 3 * 5, 2 * (1 + 7) + 3),
        compiler_params=pltpu.CompilerParams(
            collective_id=2, has_side_effects=True, vmem_limit_bytes=64 * 1024 * 1000
        ),
        name="last",
    )(*streams[0], *streams[1])
    return results[:4], results[4:]


def take_own(group, row):
    columns = row.shape[1] // 4
    return pltpu.roll(row, (4 - group) % 4 * columns, 1)[:, :columns]


def finish_kernel(*refs):
    ins = [refs[:3], refs[3:6]]
    outs = [refs[6:13], refs[13:]]
    for (sums, rest, qkv), (gains, shifts, bias, qkv_out, proj, up, down) in zip(ins, outs):
        group = lax.axis_index(FSDP)
        rows = take_own(group, sums[0:8])
        gains[...] = rows[0:2]
        shifts[...] = rows[2:6]
        line = jnp.concatenate([sums[6:7], sums[7:8], sums[8:9]], axis=1)
        bias[...] = take_own(group, jnp.broadcast_to(line, (8, line.shape[1])))[0:1]
        own = qkv.shape[1] // 3
        for which in range(3):
            qkv_out[which] = qkv[:, which * own : (which + 1) * own].astype(F32)
        hidden = up.shape[1]
        up[...] = rest[:, own : own + hidden].astype(F32)
        if down.shape[0] > down.shape[1]:
            proj[...] = jnp.transpose(rest[:, :own].astype(F32))
            down[...] = jnp.transpose(rest[:, own + hidden :].astype(F32))
        else:
            proj[...] = rest[:, :own].astype(F32)
            down[...] = rest[:, own + hidden :].astype(F32)


def finish(streams):
    out_shape = []
    for sums, rest, qkv, flip in streams:
        rows, own = qkv.shape[0], qkv.shape[1] // 3
        hidden = (rest.shape[1] - own) // 2
        shapes = [(2, rows), (4, rows), (1, 3 * rows), (3, rows, own)]
        shapes += [(own, rows), (rows, hidden), (hidden, rows)] if flip else [
            (rows, own), (rows, hidden), (rows, hidden)
        ]
        out_shape += [jax.ShapeDtypeStruct(shape, F32) for shape in shapes]
    results = pl.pallas_call(finish_kernel, out_shape=out_shape, name="finish")(
        *streams[0][:3], *streams[1][:3]
    )
    return results[:7], results[7:]


def on_device(*args):
    streams = []
    for item, causal in ((args[10:], True), (args[:10], False)):
        s = Bag()
        rows, s.seg, cotangent, s.gains, s.shifts, s.head_bias, s.qkv, proj, s.up, down = item
        s.flip, s.x, s.dy = causal, rows[0], cotangent[0]
        s.down, s.proj = (down, proj) if causal else (down.T, proj.T)
        streams.append(s)
    started = front(
        [(s.x, s.seg, s.gains, s.shifts, s.head_bias, s.qkv, s.up, s.down, s.proj) for s in streams]
    )
    for s, (weight, small, first, messages, proj, up, down, o, lse, o_got) in zip(streams, started):
        s.weight, s.small, s.first, s.messages, s.o, s.lse = weight, small, first, messages, o, lse
        s.weights, s.o_got = (proj, up, down), o_got
    done = middle([(s.o_got, s.x, s.dy, s.small, *s.weights) for s in streams])
    ended = last(
        [
            (s.messages, do, s.o, s.lse, s.seg, s.first, s.x, s.small, s.weight, dmid, rest, sums)
            for s, (y, dmid, do, rest, sums) in zip(streams, done)
        ]
    )
    final = finish([(sums, rest, qkv, s.flip) for s, (_, sums, rest, qkv) in zip(streams, ended)])
    outputs = []
    for s, (y, *_), (grad_rows, *_), (gains, shifts, bias, qkv, proj, up, down) in zip(
        streams, done, ended, final
    ):
        if not s.flip:
            proj, down = proj.T, down.T
        outputs.append((y[None], grad_rows[None], gains, shifts, bias, qkv, proj, up, down))
    return outputs[1] + outputs[0]


def layer_stats(rows):
    row_mean = jnp.mean(rows, axis=-1, keepdims=True)
    centred = rows - row_mean
    inv_std = lax.rsqrt(jnp.mean(centred * centred, axis=-1, keepdims=True) + 1e-05)
    return (centred * inv_std, inv_std)


def norm_back(grad_normed_out, normed, inv_std, gain):
    scaled = grad_normed_out * gain
    return inv_std * (
        scaled
        - jnp.mean(scaled, axis=-1, keepdims=True)
        - normed * jnp.mean(scaled * normed, axis=-1, keepdims=True)
    )


def tensor_psum(partial_rows):
    return lax.psum(partial_rows, TP)


def any_mesh_block(
    rows_in,
    seg_row,
    cotangent,
    gains,
    shifts,
    head_bias,
    qkv_weight,
    proj_weight,
    up_weight,
    down_weight,
    causal,
):
    gain_full, shift_full, bias_full, qkv_full, proj_full, up_full, down_full = (
        lax.all_gather(gains, FSDP, axis=1, tiled=True),
        lax.all_gather(shifts, FSDP, axis=1, tiled=True),
        lax.all_gather(head_bias, FSDP, axis=1, tiled=True),
        lax.all_gather(qkv_weight, FSDP, axis=1, tiled=True),
        lax.all_gather(proj_weight, FSDP, axis=1, tiled=True),
        lax.all_gather(up_weight, FSDP, axis=0, tiled=True),
        lax.all_gather(down_weight, FSDP, axis=1, tiled=True),
    )
    gain_vals = gain_full.astype(jnp.float32)
    shift_vals = shift_full.astype(jnp.float32)
    bias_vals = bias_full[0].astype(jnp.float32)
    tp_width = qkv_full.shape[2]
    local_rows = rows_in.shape[1]
    seq_length = seg_row.shape[1]
    head_local = tp_width // HD
    rows = rows_in[0].astype(jnp.float32)
    row_start = lax.axis_index(CTX) * local_rows
    seg_all = seg_row[0]
    seg_query = lax.dynamic_slice_in_dim(seg_all, row_start, local_rows)
    query_pos = row_start + jnp.arange(local_rows, dtype=jnp.int32)
    key_pos = jnp.arange(seq_length, dtype=jnp.int32)
    allowed = seg_query[:, None] == seg_all[None, :]
    if causal:
        allowed = jnp.logical_and(allowed, key_pos[None, :] <= query_pos[:, None])

    def to_heads(matrix):
        return matrix.reshape(matrix.shape[0], head_local, HD).transpose(1, 0, 2)

    def from_heads(stacked):
        return stacked.transpose(1, 0, 2).reshape(stacked.shape[1], head_local * HD)

    normed_one, inv_one = layer_stats(rows)
    first_in = (normed_one * gain_vals[0] + shift_vals[0]).astype(jnp.bfloat16)
    queries = (
        jnp.dot(first_in, qkv_full[0], preferred_element_type=jnp.float32) + bias_vals[:tp_width]
    ).astype(jnp.bfloat16)
    key_rows = jnp.dot(first_in, qkv_full[1], preferred_element_type=jnp.float32).astype(
        jnp.bfloat16
    )
    values = (
        jnp.dot(first_in, qkv_full[2], preferred_element_type=jnp.float32)
        + bias_vals[tp_width : 2 * tp_width]
    ).astype(jnp.bfloat16)
    key_all, value_all = (
        lax.all_gather(key_rows, CTX, axis=0, tiled=True),
        lax.all_gather(values, CTX, axis=0, tiled=True),
    )
    query_heads = to_heads(queries)
    key_heads = to_heads(key_all)
    value_heads = to_heads(value_all)

    def attend(head_items):
        query_h, key_h, value_h = head_items
        scores = dot(query_h, key_h, ((1,), (1,))) * 0.125
        scores = jnp.where(allowed, scores, -1e30)
        row_top = jnp.max(scores, axis=-1, keepdims=True)
        weights = jnp.exp(scores - row_top)
        row_total = jnp.sum(weights, axis=-1, keepdims=True)
        weights_low = (weights / row_total).astype(jnp.bfloat16)
        mixed_h = dot(weights_low, value_h, ((1,), (0,)))
        return (mixed_h.astype(jnp.bfloat16), row_top[:, 0] + jnp.log(row_total[:, 0]))

    mixed_heads, log_totals = lax.map(attend, (query_heads, key_heads, value_heads))
    mixed = from_heads(mixed_heads)
    middle = (
        rows
        + tensor_psum(jnp.dot(mixed, proj_full, preferred_element_type=jnp.float32))
        + shift_vals[1]
    )
    normed_two, inv_two = layer_stats(middle)
    second_in = (normed_two * gain_vals[1] + shift_vals[2]).astype(jnp.bfloat16)
    hidden = (
        jnp.dot(second_in, up_full, preferred_element_type=jnp.float32) + bias_vals[2 * tp_width :]
    )
    sigma = jax.nn.sigmoid(1.702 * hidden)
    activated = (hidden * sigma).astype(jnp.bfloat16)
    output = (
        middle
        + tensor_psum(jnp.dot(activated, down_full, preferred_element_type=jnp.float32))
        + shift_vals[3]
    )
    grad_out = cotangent[0].astype(jnp.float32)
    grad_down_bias = jnp.sum(grad_out, axis=0)
    grad_branch = grad_out.astype(jnp.bfloat16)
    grad_down = dot(activated, grad_branch, ((0,), (0,)))
    grad_act = dot(grad_branch, down_full, ((1,), (1,)))
    grad_hidden = (grad_act * (sigma + 1.702 * hidden * sigma * (1.0 - sigma))).astype(jnp.bfloat16)
    grad_up_bias = jnp.sum(grad_hidden.astype(jnp.float32), axis=0)
    grad_up = dot(second_in, grad_hidden, ((0,), (0,)))
    grad_second = tensor_psum(
        dot(grad_hidden, up_full, ((1,), (1,)))
    )
    grad_gain_two = jnp.sum(grad_second * normed_two, axis=0)
    grad_shift_two = jnp.sum(grad_second, axis=0)
    grad_middle = grad_out + norm_back(grad_second, normed_two, inv_two, gain_vals[1])
    grad_proj_bias = jnp.sum(grad_middle, axis=0)
    grad_attn = grad_middle.astype(jnp.bfloat16)
    grad_proj = dot(mixed, grad_attn, ((0,), (0,)))
    grad_mixed = dot(grad_attn, proj_full, ((1,), (1,))).astype(jnp.bfloat16)

    def attend_back(head_items):
        query_h, key_h, value_h, grad_h, log_total = head_items
        scores = dot(query_h, key_h, ((1,), (1,))) * 0.125
        weights = jnp.where(allowed, jnp.exp(scores - log_total[:, None]), 0.0)
        grad_weights = dot(grad_h, value_h, ((1,), (1,)))
        row_delta = jnp.sum(weights * grad_weights, axis=-1, keepdims=True)
        grad_scores = (weights * (grad_weights - row_delta)).astype(jnp.bfloat16)
        grad_query_h = (
            dot(grad_scores, key_h, ((1,), (0,))) * 0.125
        )
        grad_key_h = (
            dot(grad_scores, query_h, ((0,), (0,)))
            * 0.125
        )
        grad_value_h = dot(weights.astype(jnp.bfloat16), grad_h, ((0,), (0,)))
        return (grad_query_h, grad_key_h, grad_value_h)

    query_parts, key_parts, value_parts = lax.map(
        attend_back, (query_heads, key_heads, value_heads, to_heads(grad_mixed), log_totals)
    )
    key_sum, value_sum = (
        lax.psum_scatter(from_heads(key_parts), CTX, scatter_dimension=0, tiled=True),
        lax.psum_scatter(from_heads(value_parts), CTX, scatter_dimension=0, tiled=True),
    )
    grad_query = from_heads(query_parts).astype(jnp.bfloat16)
    grad_key = key_sum.astype(jnp.bfloat16)
    grad_value = value_sum.astype(jnp.bfloat16)
    grad_qkv = jnp.stack(
        [
            dot(first_in, grad_query, ((0,), (0,))),
            dot(first_in, grad_key, ((0,), (0,))),
            dot(first_in, grad_value, ((0,), (0,))),
        ]
    )
    grad_head = jnp.concatenate(
        [
            jnp.sum(grad_query.astype(jnp.float32), axis=0),
            jnp.sum(grad_value.astype(jnp.float32), axis=0),
            grad_up_bias,
        ]
    )[None, :]
    grad_first_part = dot(grad_query, qkv_full[0], ((1,), (1,)))
    grad_first_part = grad_first_part + dot(grad_key, qkv_full[1], ((1,), (1,)))
    grad_first_part = grad_first_part + dot(grad_value, qkv_full[2], ((1,), (1,)))
    grad_first = tensor_psum(grad_first_part)
    grad_gain_one = jnp.sum(grad_first * normed_one, axis=0)
    grad_shift_one = jnp.sum(grad_first, axis=0)
    grad_rows = grad_middle + norm_back(grad_first, normed_one, inv_one, gain_vals[0])
    grad_gains = jnp.stack([grad_gain_one, grad_gain_two])
    grad_shifts = jnp.stack([grad_shift_one, grad_proj_bias, grad_shift_two, grad_down_bias])
    share_gains, share_shifts, share_head, share_qkv, share_proj, share_up, share_down = (
        lax.psum_scatter(grad_gains, FSDP, scatter_dimension=1, tiled=True),
        lax.psum_scatter(grad_shifts, FSDP, scatter_dimension=1, tiled=True),
        lax.psum_scatter(grad_head, FSDP, scatter_dimension=1, tiled=True),
        lax.psum_scatter(grad_qkv, FSDP, scatter_dimension=1, tiled=True),
        lax.psum_scatter(grad_proj, FSDP, scatter_dimension=1, tiled=True),
        lax.psum_scatter(grad_up, FSDP, scatter_dimension=0, tiled=True),
        lax.psum_scatter(grad_down, FSDP, scatter_dimension=1, tiled=True),
    )
    owned = lax.psum(
        (share_gains, share_shifts, share_head, share_qkv, share_proj, share_up, share_down), CTX
    )
    return (output.astype(jnp.bfloat16)[None], grad_rows[None]) + tuple(owned)


def on_any_mesh(
    image_input,
    image_segments,
    image_cotangent,
    image_gains,
    image_shifts,
    image_head_bias,
    image_qkv_weight,
    image_proj_weight,
    image_up_weight,
    image_down_weight,
    text_input,
    text_segments,
    text_cotangent,
    text_gains,
    text_shifts,
    text_head_bias,
    text_qkv_weight,
    text_proj_weight,
    text_up_weight,
    text_down_weight,
):
    image_results = any_mesh_block(
        image_input,
        image_segments,
        image_cotangent,
        image_gains,
        image_shifts,
        image_head_bias,
        image_qkv_weight,
        image_proj_weight,
        image_up_weight,
        image_down_weight,
        False,
    )
    text_results = any_mesh_block(
        text_input,
        text_segments,
        text_cotangent,
        text_gains,
        text_shifts,
        text_head_bias,
        text_qkv_weight,
        text_proj_weight,
        text_up_weight,
        text_down_weight,
        True,
    )
    return image_results + text_results


def stream_specs():
    return (
        P(FSDP, CTX, None),
        P(FSDP, None),
        P(FSDP, CTX, None),
        P(None, FSDP),
        P(None, FSDP),
        P(TP, FSDP),
        P(None, FSDP, TP),
        P(TP, FSDP),
        P(FSDP, TP),
        P(TP, FSDP),
    )


def solution(mesh):
    one = stream_specs()
    grads = (one[0], one[0]) + one[3:]
    body = on_device
    if (mesh.shape[FSDP], mesh.shape[CTX], mesh.shape[TP]) != (4, 4, 2):
        body = on_any_mesh
    return jax.shard_map(
        body, mesh=mesh, in_specs=one + one, out_specs=grads + grads, check_vma=False
    )
```

```python
import functools

import jax
import jax.numpy as jnp
from jax import lax
from jax.experimental import pallas as pl
from jax.experimental.pallas import tpu as pltpu
from jax.sharding import PartitionSpec as P

HD = 64
LANES = 128
QB = 256
KB = 512
NEG = -1e30
F32 = jnp.float32
MESH = pl.DeviceIdType.MESH
FSDP, CTX, TP = "fsdp", "ctx", "tp"
BF16 = jnp.bfloat16


def dot(left, right, dims=((1,), (0,))):
    return lax.dot_general(left, right, (dims, ((), ())), preferred_element_type=F32)


def lane_marks():
    lane = lax.broadcasted_iota(jnp.int32, (1, LANES), 1)
    first = (lane < HD).astype(F32).astype(BF16)
    second = (lane >= HD).astype(F32).astype(BF16)
    return first, second


def document_features(row_ref, query_out, key_out):
    lane = lax.broadcasted_iota(jnp.int32, (LANES, LANES), 1) % HD
    for start in range(0, query_out.shape[0], LANES):
        row = row_ref[:, start : start + LANES].astype(F32)
        same = jnp.transpose(jnp.broadcast_to(row, (LANES, LANES))) == lane.astype(F32)
        query_out[start : start + LANES, :] = jnp.where(same, 1.0, 0.0).astype(BF16)
        key_out[start : start + LANES, :] = jnp.where(same, 0.0, NEG).astype(BF16)


def swap_halves(value):
    return pltpu.roll(value, HD, 1)


def key_range(index):
    return slice(index * KB, (index + 1) * KB)


def pick(flag, one, zero):
    return jnp.where(flag == 1, one, zero)


def query_rows(head):
    return pl.ds(pl.multiple_of(head * (QB + 2 * KB), QB), QB)


def key_rows(head):
    return pl.ds(pl.multiple_of(QB + head * KB, QB), KB)


def mark_keys(m, features, heads, score_keys, value_keys):
    first, second = lane_marks()
    for head in range(heads):
        for index in range(4):
            block = m[index, key_rows(head)]
            score_keys[head, key_range(index)] = block * first + features[key_range(index), :] * second
            if value_keys is not None:
                value_keys[head, key_range(index)] = block * second + first


def later(index, shape, axis, query_start):
    key_pos = index * KB + lax.broadcasted_iota(jnp.int32, shape, axis)
    query_pos = query_start + lax.broadcasted_iota(jnp.int32, shape, 1 - axis)
    return key_pos > query_pos


def mix_rows(query, score_keys, value_keys, head, blocks, query_start=None):
    scores = []
    for index in range(blocks):
        score = dot(query, score_keys[head, key_range(index)], ((1,), (1,)))
        if query_start is not None:
            score = jnp.where(later(index, score.shape, 1, query_start), NEG, score)
        scores.append(score)
    top = jnp.max(functools.reduce(jnp.maximum, scores), axis=1, keepdims=True)
    acc = jnp.zeros((query.shape[0], LANES), F32)
    for index, score in enumerate(scores):
        acc = acc + dot(jnp.exp(score - top).astype(BF16), value_keys[head, key_range(index)])
    return acc / swap_halves(acc), top + jnp.log(acc)


def text_task(at, task):
    return 0, task // 2, task % 2


def image_task(at, task):
    shared = 1 - (task + 8) // 12
    return shared, pick(shared, at.here_high * 2 + task // 2, task // 2 - 2), task % 2


def attend(at, m, features, score_keys, value_keys, o, lse, task_of, begin, end, blocks, causal):
    first, second = lane_marks()
    lane = lax.broadcasted_iota(jnp.int32, (QB, LANES), 1)

    def one(task, carry):
        head, source, half = task_of(at, task)
        start = (source * 2 + half) * QB
        query = m[source, query_rows(head)].astype(F32)
        query = pick(half, swap_halves(query), query).astype(BF16)
        query = query * first + features[pl.ds(pl.multiple_of(start, QB), QB), :] * second
        mixed, log_total = mix_rows(
            query, score_keys, value_keys, head, blocks, start if causal else None
        )
        lse[task] = jnp.transpose(log_total)[:8]
        mixed = pick(half, mixed, swap_halves(mixed)).astype(BF16)
        rows = pl.ds(pl.multiple_of(head * QB, QB), QB)
        o[source, rows] = jnp.where(lane // HD == half, mixed, o[source, rows])
        return carry

    lax.fori_loop(begin, end, one, 0)


def unattend(at, m, do, o, lse, features, score_keys, acc, out, task_of, begin, end, blocks, causal):
    first, second = lane_marks()
    lane = lax.broadcasted_iota(jnp.int32, (QB, LANES), 1)

    def one(task, carry):
        head, source, half = task_of(at, task)
        start = (source * 2 + half) * QB
        rows = pl.ds(pl.multiple_of(head * QB, QB), QB)
        query, grad_o = m[source, query_rows(head)].astype(F32), do[source, rows].astype(F32)
        product = jnp.transpose(grad_o * o[source, rows].astype(F32))
        delta = jnp.sum(pick(half, product[HD:], product[:HD]), axis=0, keepdims=True)
        query = pick(half, swap_halves(query), query).astype(BF16) * first
        grad_o = pick(half, grad_o, swap_halves(grad_o)).astype(BF16) * second
        marked = query + features[pl.ds(pl.multiple_of(start, QB), QB), :] * second
        row_lse = lse[task, :1]
        grad_query = jnp.zeros((QB, LANES), F32)
        for index in range(blocks):
            keys = m[index, key_rows(head)]
            score = dot(score_keys[head, key_range(index)], marked, ((1,), (1,)))
            if causal:
                score = jnp.where(later(index, score.shape, 0, start), NEG, score)
            weights = jnp.exp(score - row_lse)
            grad_weights = dot(keys, grad_o, ((1,), (1,)))
            grad_scores = (weights * (grad_weights - delta)).astype(BF16)
            acc[head, key_range(index)] += dot(grad_scores, query) + dot(weights.astype(BF16), grad_o)
            grad_query = grad_query + dot(grad_scores, keys, ((0,), (0,)))
        grad_query = grad_query * 0.125
        grad_query = pick(half, swap_halves(grad_query), grad_query).astype(BF16)
        out[source, query_rows(head)] = jnp.where(
            lane // HD == half, grad_query, out[source, query_rows(head)]
        )
        return carry

    lax.fori_loop(begin, end, one, 0)


def key_gradients(acc, out):
    for head in range(acc.shape[0]):
        for index in range(4):
            out[index, key_rows(head)] = acc[head, key_range(index)].astype(BF16)


class Bag:
    pass


def partners():
    at = Bag()
    group, here, core = lax.axis_index(FSDP), lax.axis_index(CTX), lax.axis_index(TP)
    at.group, at.here = group, here
    at.group_x = group + 1 - 2 * (group % 2)
    at.group_y = group + 2 - 4 * (group // 2)
    at.group_far = 3 - group
    at.here_low, at.here_high = here % 2, here // 2
    at.inner, at.outer = (here + 1) // 2 == 1, (here + 1) // 2 != 1
    at.ctx = (here, here + 1 - 2 * (here % 2), here + 2 - 4 * (here // 2), 3 - here)
    at.to_x, at.to_y, at.to_far = ({FSDP: g} for g in (at.group_x, at.group_y, at.group_far))
    at.to_ctx = [{CTX: c} for c in at.ctx]
    at.to_core = {TP: 1 - core}
    return at


def meet(devices):
    barrier = pltpu.get_barrier_semaphore()
    for device in devices:
        pl.semaphore_signal(barrier, inc=1, device_id=device, device_id_type=MESH)
    pl.semaphore_wait(barrier, len(devices))


class Copies:
    def __init__(self, send_sems, recv_sems, local_sems):
        self.sems = (send_sems, recv_sems, local_sems)
        self.used = [0, 0]

    def remote(self, src, dst, device, start=True):
        index = self.used[0]
        self.used[0] += 1
        copy = pltpu.make_async_remote_copy(
            src_ref=src,
            dst_ref=dst,
            send_sem=self.sems[0].at[index],
            recv_sem=self.sems[1].at[index],
            device_id=device,
            device_id_type=MESH,
        )
        if start:
            copy.start()
        return copy

    def local(self, src, dst):
        index = self.used[1]
        self.used[1] += 1
        copy = pltpu.make_async_copy(src, dst, self.sems[2].at[index])
        copy.start()
        return copy


def copy_sems(remote, local):
    return [
        pltpu.SemaphoreType.DMA((remote,)),
        pltpu.SemaphoreType.DMA((remote,)),
        pltpu.SemaphoreType.DMA((local,)),
    ]


class Gather:
    def __init__(self, copies, at, src, dst):
        self.copies, self.at, self.dst = copies, at, dst
        self.rows = src.shape[-2]
        own = self.part(at.group, 0, self.rows)
        self.own = copies.local(src, own)
        self.to_x = copies.remote(src, own, at.to_x)
        self.to_y = copies.remote(src, own, at.to_y)

    def part(self, owner, offset, size):
        rows = pl.ds(pl.multiple_of(owner * self.rows + offset, 8), size)
        return self.dst.at[:, rows, :] if len(self.dst.shape) == 3 else self.dst.at[rows, :]

    def near(self):
        self.own.wait()
        self.to_x.wait()
        self.to_y.wait()

    def forward(self):
        half = self.rows // 2
        self.to_x.wait_recv()
        self.to_y.wait_recv()
        top = self.part(self.at.group_y, 0, half)
        low = self.part(self.at.group_x, half, half)
        self.far_x = self.copies.remote(top, top, self.at.to_x)
        self.far_y = self.copies.remote(low, low, self.at.to_y)

    def arrived(self):
        self.own.wait()
        self.far_x.wait_recv()
        self.far_y.wait_recv()

    def sent(self):
        for copy in (self.to_x, self.to_y, self.far_x, self.far_y):
            copy.wait_send()


def normalise(rows):
    mean = jnp.mean(rows, axis=-1, keepdims=True)
    centred = rows - mean
    inv = lax.rsqrt(jnp.mean(centred * centred, axis=-1, keepdims=True) + 1e-05)
    return centred * inv, inv


def lane_pair(low, high):
    lane = lax.broadcasted_iota(jnp.int32, low[0].shape, 1)
    left = low[0] if low[1] == 0 else pltpu.roll(low[0], HD, 1)
    right = high[0] if high[1] == 1 else pltpu.roll(high[0], HD, 1)
    return jnp.where(lane < HD, left, right)


def head_tile(ref, start, index, rows=slice(None)):
    first = start + (index // 2) * LANES
    return ref[rows, first : first + LANES], index % 2


def halves_pair(ref, start, index):
    half = ref.shape[0] // 2
    return lane_pair(
        head_tile(ref, start, index, slice(0, half)), head_tile(ref, start, index, slice(half, None))
    ).astype(BF16)


def write_messages(qkv, out, heads):
    width = heads * HD

    def keys_values(index):
        return lane_pair(head_tile(qkv, width, index), head_tile(qkv, 2 * width, index)).astype(BF16)

    for c in range(4):
        out[c, query_rows(0)] = halves_pair(qkv, 0, c)
        out[c, key_rows(0)] = keys_values(c)
        if heads == 6:
            out[c, key_rows(1)] = keys_values(4 + c % 2)
            out[c, query_rows(1)] = halves_pair(qkv, 0, 4 + c % 2)


def message_shape(heads, tokens):
    return (4, (heads // 2 - 1) * (QB + tokens), LANES)


def mixed_shape(heads):
    return (4, (heads // 2 - 1) * QB, LANES)


def first_rows(x_ref, small_ref, weight_ref, first_ref, qkv_ref, step):
    width = weight_ref.shape[2]
    rows = slice(step * 256, step * 256 + 256)
    normed, _ = normalise(x_ref[rows, :].astype(F32))
    first = (normed * small_ref[0:1] + small_ref[2:3]).astype(BF16)
    first_ref[:, rows] = jnp.transpose(first)
    bias = small_ref[6:7]
    qkv_ref[rows, :width] = (dot(first, weight_ref[0]) + bias[:, :width]) * 0.125
    qkv_ref[rows, width : 2 * width] = dot(first, weight_ref[1])
    qkv_ref[rows, 2 * width :] = dot(first, weight_ref[2]) + bias[:, width : 2 * width]


def spread_small(at, gains, shifts, bias, wide, flat, out):
    width = wide.shape[1]
    columns, bias_columns = gains.shape[1], bias.shape[1]
    wide[...] = jnp.zeros_like(wide)
    flat[...] = jnp.zeros_like(flat)
    wide[0:2, :columns] = gains[...].astype(F32)
    wide[2:6, :columns] = shifts[...].astype(F32)
    flat[0:1, :bias_columns] = bias[...].astype(F32)
    out[0:8] = pltpu.roll(wide[...], at.group * columns, 1)
    line = pltpu.roll(flat[...], at.group * bias_columns, 1)
    out[8:16] = jnp.zeros((8, width), F32)
    for row in range(3):
        out[6 + row : 7 + row] = line[0:1, row * width : (row + 1) * width]


FRONT_IN, FRONT_OUT, FRONT_SCRATCH = 9, 10, 20


def front_kernel(*refs):
    at = partners()
    ins = [refs[:FRONT_IN], refs[FRONT_IN : 2 * FRONT_IN]]
    refs = refs[2 * FRONT_IN :]
    outs = [refs[:FRONT_OUT], refs[FRONT_OUT : 2 * FRONT_OUT]]
    refs = refs[2 * FRONT_OUT :]
    scratch = [refs[:FRONT_SCRATCH], refs[FRONT_SCRATCH : 2 * FRONT_SCRATCH]]
    copies = Copies(*refs[2 * FRONT_SCRATCH :])
    streams = []
    for in_refs, out_refs, own in zip(ins, outs, scratch):
        s = Bag()
        s.x_in, s.seg_row, s.gains, s.shifts, s.bias, s.qkv, s.up_in, s.down_in, s.proj_in = in_refs
        (
            s.weight_out, s.small, s.first_out, s.messages, s.proj_full, s.up_full, s.down_full,
            s.o_out, s.lse, s.o_got,
        ) = out_refs
        (
            s.small_in, s.small_own, s.wide, s.flat, s.rows, s.mine, s.got, s.down_t, s.proj_t,
            s.query_doc, s.key_doc, s.score_keys, s.value_keys, s.x, s.up, s.down, s.proj, s.weight, s.first,
        ) = own[:19]
        s.o = own[19]
        s.heads = s.weight.shape[2] // HD
        s.features = (s.query_doc, s.key_doc)
        s.reads = [
            copies.local(src, dst)
            for src, dst in (
                (s.x_in, s.x), (s.proj_in, s.proj), (s.up_in, s.up), (s.down_in, s.down),
            )
        ]
        streams.append(s)
    meet([at.to_x, at.to_y, at.to_far] + at.to_ctx[1:])
    text, image = streams
    image.gather = Gather(copies, at, image.qkv, image.weight)
    for s in (image, text):
        spread_small(at, s.gains, s.shifts, s.bias, s.wide, s.flat, s.small_own)
    for s in (image, text):
        s.small_done = [
            copies.remote(s.small_own, s.small_in.at[i], device)
            for i, device in enumerate((at.to_x, at.to_y, at.to_far))
        ]
    image.gather.forward()
    text.gather = Gather(copies, at, text.qkv, text.weight)
    for s in (image, text):
        for copy in s.reads:
            copy.wait()
    text.down_t[...] = jnp.transpose(text.down[...])
    text.proj_t[...] = jnp.transpose(text.proj[...])
    for s in (image, text):
        document_features(s.seg_row, *s.features)

    def project(s):
        for copy in s.small_done:
            copy.wait_recv()
        s.small[...] = s.small_own[...] + s.small_in[0] + s.small_in[1] + s.small_in[2]
        s.gather.arrived()
        for step in range(s.x.shape[0] // 256):
            first_rows(s.x, s.small, s.weight, s.first, s.rows, step)
        write_messages(s.rows, s.mine, s.heads)
        s.sends = send_blocks(copies, at, s.mine, s.got)
        s.writes = [copies.local(s.weight, s.weight_out), copies.local(s.first, s.first_out)]

    def gather_rest(s):
        pieces = (s.proj_t, s.up, s.down_t) if s.heads == 4 else (s.proj, s.up, s.down)
        s.rest = [
            Gather(copies, at, piece, full)
            for piece, full in zip(pieces, (s.proj_full, s.up_full, s.down_full))
        ]

    project(image)
    text.gather.forward()
    gather_rest(text)
    project(text)
    gather_rest(image)
    for gather in text.rest:
        gather.forward()
    for copy in image.sends:
        copy.wait()
    image.writes.append(copies.local(image.got, image.messages))
    s = image
    s.o[...] = jnp.zeros_like(s.o)
    mark_keys(s.got, s.features[1], 2, s.score_keys, s.value_keys)
    attend(
        at, s.got, s.features[0], s.score_keys, s.value_keys, s.o, s.lse, image_task, 0, 12, 4, False
    )
    image.o_done = send_blocks(copies, at, image.o, image.o_got)
    image.writes.append(copies.local(image.o, image.o_out))
    image.rest[0].forward()
    for copy in text.sends:
        copy.wait()
    text.writes.append(copies.local(text.got, text.messages))
    s = text
    s.o[...] = jnp.zeros_like(s.o)
    mark_keys(s.got, s.features[1], 1, s.score_keys, s.value_keys)
    for begin, end in ((0, 4), (4, 8)):
        attend(
            at, s.got, s.features[0], s.score_keys, s.value_keys, s.o, s.lse, text_task,
            begin, end, end // 2, True,
        )
    text.o_done = send_blocks(copies, at, text.o, text.o_got)
    text.writes.append(copies.local(text.o, text.o_out))
    whole = [image.gather, text.gather, image.rest[0]] + text.rest
    for gather in whole[2:]:
        gather.arrived()
    for gather in whole:
        gather.sent()
    for gather in image.rest[1:]:
        gather.near()
    for s in (image, text):
        for copy in s.small_done:
            copy.wait_send()
        for copy in s.writes + s.o_done:
            copy.wait()


def front(streams):
    vmem, hbm = pl.BlockSpec(memory_space=pltpu.VMEM), pl.BlockSpec(memory_space=pl.ANY)
    out_shape, out_specs, scratch = [], [], []
    for x, seg, gains, shifts, bias, qkv, up, down, proj in streams:
        tokens, width = x.shape
        own = qkv.shape[2]
        messages = message_shape(own // HD, tokens)
        hidden = up.shape[1]
        small = jax.ShapeDtypeStruct((16, width), F32)
        out_shape += [
            jax.ShapeDtypeStruct((3, width, own), BF16),
            small,
            jax.ShapeDtypeStruct((width, tokens), BF16),
            jax.ShapeDtypeStruct(messages, BF16),
            jax.ShapeDtypeStruct((width, own), BF16),
            jax.ShapeDtypeStruct((width, hidden), BF16),
            jax.ShapeDtypeStruct((width, hidden), BF16),
            jax.ShapeDtypeStruct(mixed_shape(own // HD), BF16),
            jax.ShapeDtypeStruct((2 * (own // HD), 8, QB), F32),
            jax.ShapeDtypeStruct(mixed_shape(own // HD), BF16),
        ]
        out_specs += [hbm, vmem, hbm, hbm, hbm, hbm, hbm, hbm, vmem, hbm]
        scratch += [
            pltpu.VMEM((3, 16, width), F32),
            pltpu.VMEM((16, width), F32),
            pltpu.VMEM((8, width), F32),
            pltpu.VMEM((8, 3 * width), F32),
            pltpu.VMEM((tokens, 3 * own), F32),
            pltpu.VMEM(messages, BF16),
            pltpu.VMEM(messages, BF16),
            pltpu.VMEM((width // 4, hidden), BF16),
            pltpu.VMEM((width // 4, own), BF16),
            pltpu.VMEM((4 * tokens, LANES), BF16),
            pltpu.VMEM((4 * tokens, LANES), BF16),
            pltpu.VMEM((1 if own == 4 * HD else 2, 4 * tokens, LANES), BF16),
            pltpu.VMEM((1 if own == 4 * HD else 2, 4 * tokens, LANES), BF16),
            pltpu.VMEM(x.shape, BF16),
            pltpu.VMEM(up.shape, BF16),
            pltpu.VMEM(down.shape, BF16),
            pltpu.VMEM(proj.shape, BF16),
            pltpu.VMEM((3, width, own), BF16),
            pltpu.VMEM((width, tokens), BF16),
            pltpu.VMEM(mixed_shape(own // HD), BF16),
        ]
    results = pl.pallas_call(
        front_kernel,
        out_shape=out_shape,
        in_specs=[hbm, vmem, vmem, vmem, vmem, vmem, hbm, hbm, hbm] * 2,
        out_specs=out_specs,
        scratch_shapes=scratch + copy_sems(2 * (3 + 4 * 4 + 6), 2 * 14),
        compiler_params=pltpu.CompilerParams(
            collective_id=0, has_side_effects=True, vmem_limit_bytes=63 << 20
        ),
        name="front",
    )(*streams[0], *streams[1])
    return results[:FRONT_OUT], results[FRONT_OUT:]


STEP = 384


def by_columns(columns, body):
    def one(index, carry):
        body(pl.ds(pl.multiple_of(index * STEP, STEP), STEP))
        return carry

    lax.fori_loop(0, columns // STEP, one, 0)


class PlaneSum:
    def __init__(self, copies, at, src, arrivals, loads=None):
        self.copies, self.at = copies, at
        self.in_x, self.in_y, self.in_top, self.in_low = arrivals
        half, self.columns = self.in_top.shape
        self.half, rows = half, 2 * half

        def block(owner, offset, size=half):
            return src.at[pl.ds(pl.multiple_of(owner * rows + offset, 8), size), :]

        self.first = [
            copies.remote(block(at.group_far, 0), self.in_x.at[1], at.to_x),
            copies.remote(block(at.group_far, half), self.in_y.at[1], at.to_y),
            copies.remote(block(at.group_x, 0), self.in_x.at[0], at.to_x),
            copies.remote(block(at.group_y, half), self.in_y.at[0], at.to_y),
        ]
        parts = [block(at.group_y, 0), block(at.group_x, half), block(at.group, 0, rows)]
        if loads is None:
            self.loads = []
            self.pass_top, self.pass_low, self.own = parts
        else:
            self.loads = [copies.local(part, load) for part, load in zip(parts, loads)]
            self.pass_top, self.pass_low, self.own = loads

    def cross(self):
        for copy in self.loads:
            copy.wait()
        self.first[0].wait_recv()

        def top(cols):
            self.pass_top[:, cols] = (
                self.pass_top[:, cols].astype(F32) + self.in_x[1, :, cols].astype(F32)
            ).astype(BF16)

        by_columns(self.columns, top)
        self.second = [self.copies.remote(self.pass_top, self.in_top, self.at.to_y)]
        self.first[1].wait_recv()

        def low(cols):
            self.pass_low[:, cols] = (
                self.pass_low[:, cols].astype(F32) + self.in_y[1, :, cols].astype(F32)
            ).astype(BF16)

        by_columns(self.columns, low)
        self.second.append(self.copies.remote(self.pass_low, self.in_low, self.at.to_x))

    def arrived(self):
        for copy in self.first[2:] + self.second:
            copy.wait_recv()

    def halves(self, cols):
        half = self.half
        return (
            self.own[:half, cols].astype(F32)
            + self.in_x[0, :, cols].astype(F32)
            + self.in_top[:, cols].astype(F32),
            self.own[half:, cols].astype(F32)
            + self.in_y[0, :, cols].astype(F32)
            + self.in_low[:, cols].astype(F32),
        )

    def sent(self):
        for copy in self.first + self.second:
            copy.wait_send()

    @staticmethod
    def arrivals(rows, columns):
        half = rows // 2
        pair, one = pltpu.VMEM((2, half, columns), BF16), pltpu.VMEM((half, columns), BF16)
        return [pair, pair, one, one]

    @staticmethod
    def loads_scratch(rows, columns):
        half = rows // 2
        one = pltpu.VMEM((half, columns), BF16)
        return [one, one, pltpu.VMEM((rows, columns), BF16)]


class LineSum:
    def __init__(self, copies, at, values, buffers, final, begin, end):
        self.at, self.values, self.final, self.range = at, values, final, (begin, end)
        self.pair, self.outer_in, self.inner_in = buffers

        def part(ref):
            return ref.at[:, begin:end]

        self.up = copies.remote(part(self.pair), part(self.outer_in), at.to_ctx[1], False)
        self.across = copies.remote(part(self.pair), part(self.inner_in), at.to_ctx[3], False)
        self.down = copies.remote(part(final), part(final), at.to_ctx[1], False)

    def each(self, body):
        begin, end = self.range

        def one(index, carry):
            body(pl.ds(pl.multiple_of(begin + index * STEP, LANES), STEP))
            return carry

        lax.fori_loop(0, (end - begin) // STEP, one, 0)

    def gather(self):
        half = self.pair.shape[0] // 2

        @pl.when(self.at.outer)
        def _():
            def add(cols):
                top, low = self.values(cols)
                self.pair[:half, cols] = top.astype(BF16)
                self.pair[half:, cols] = low.astype(BF16)

            self.each(add)
            self.up.start()

    def join(self):
        half = self.pair.shape[0] // 2

        @pl.when(self.at.inner)
        def _():
            self.up.wait_recv()

            def add(cols):
                top, low = self.values(cols)
                self.pair[:half, cols] = (top + self.outer_in[:half, cols].astype(F32)).astype(BF16)
                self.pair[half:, cols] = (low + self.outer_in[half:, cols].astype(F32)).astype(BF16)

            self.each(add)
            self.across.start()

    def share(self):
        @pl.when(self.at.inner)
        def _():
            self.across.wait_recv()

            def add(cols):
                self.final[:, cols] = (
                    self.pair[:, cols].astype(F32) + self.inner_in[:, cols].astype(F32)
                ).astype(BF16)

            self.each(add)
            self.down.start()

    def finish(self):
        @pl.when(self.at.outer)
        def _():
            self.up.wait_send()
            self.down.wait_recv()

        @pl.when(self.at.inner)
        def _():
            self.across.wait_send()
            self.down.wait_send()

    @staticmethod
    def scratch(rows, columns):
        return [pltpu.VMEM((rows, columns), BF16)] * 3


def chunks(tokens, size=256):
    return [slice(start, start + size) for start in range(0, tokens, size)]


def as_f32(ref, index, rows=slice(None)):
    return ref[index, rows].astype(F32)


def take_halves(got, out, at, heads, start, put):
    half = out.shape[0] // 2
    for tile in range(heads // 2):
        base = 0 if tile < 2 else start
        if tile < 2:
            one, two = 2 * tile, 2 * tile + 1
        else:
            one, two = at.here_high * 2, at.here_high * 2 + 1
        rows = slice(base, base + QB)
        left, right = as_f32(got, one, rows), as_f32(got, two, rows)
        for side in range(2):
            put(tile, slice(side * half, side * half + half), lane_pair((left, side), (right, side)))


def take_mixed(got, mixed, at, heads):
    def put(tile, rows, value):
        mixed[rows, tile * LANES : (tile + 1) * LANES] = value.astype(BF16)

    take_halves(got, mixed, at, heads, QB, put)


def write_grad_o(grad, out, heads):
    for c in range(4):
        out[c, :QB] = halves_pair(grad, 0, c)
        if heads == 6:
            out[c, QB:] = halves_pair(grad, 0, 4 + c % 2)


def send_blocks(copies, at, mine, out):
    rows = mine.shape[1]
    far = rows if rows in (QB, QB + KB) else rows - QB
    done = [copies.local(mine.at[at.here], out.at[at.here])]
    for other, device, size in zip(at.ctx[1:], at.to_ctx[1:], (rows, far, far)):
        part = pl.ds(0, size)
        done.append(copies.remote(mine.at[other, part], out.at[at.here, part], device))
    return done


MIDDLE_IN, MIDDLE_OUT, MIDDLE_SCRATCH = 7, 5, 22


def middle_kernel(*refs):
    at = partners()
    ins = [refs[:MIDDLE_IN], refs[MIDDLE_IN : 2 * MIDDLE_IN]]
    refs = refs[2 * MIDDLE_IN :]
    outs = [refs[:MIDDLE_OUT], refs[MIDDLE_OUT : 2 * MIDDLE_OUT]]
    refs = refs[2 * MIDDLE_OUT :]
    scratch = [refs[:MIDDLE_SCRATCH], refs[MIDDLE_SCRATCH : 2 * MIDDLE_SCRATCH]]
    arrivals = refs[2 * MIDDLE_SCRATCH : 2 * MIDDLE_SCRATCH + 4]
    copies = Copies(*refs[2 * MIDDLE_SCRATCH + 4 :])
    streams = []
    for in_refs, out_refs, own in zip(ins, outs, scratch):
        s = Bag()
        o_in, x_in, dy_in, s.small, proj_in, up_in, down_in = in_refs
        s.y_out, s.dmid_out, s.do_out, s.rest_out, s.sums = out_refs
        (
            s.proj, s.up, s.down, s.rest, s.mixed, s.part, s.part_in, s.mid, s.first, s.first_t, s.dy_t,
            s.act, s.dz, s.grad, s.grad_in, s.do, s.do_mine, s.o, s.x, s.dy, s.y, s.dmid,
        ) = own
        s.heads = proj_in.shape[1] // HD
        s.o_done = copies.local(o_in, s.o)
        s.proj_done = copies.local(proj_in, s.proj)
        s.rows_done = [copies.local(x_in, s.x), copies.local(dy_in, s.dy)]
        s.weights = ((up_in, s.up), (down_in, s.down))
        streams.append(s)
    text, image = streams
    text.rest_done = [copies.local(src, dst) for src, dst in text.weights]
    quarter = image.up.shape[0] // 4
    near = [
        pl.ds(pl.multiple_of(owner * quarter, 8), quarter)
        for owner in (at.group, at.group_x, at.group_y)
    ]
    image.rest_done = [
        copies.local(src.at[rows, :], dst.at[rows, :])
        for src, dst in image.weights
        for rows in near
    ]
    meet([at.to_x, at.to_y] + at.to_ctx[1:] + [at.to_core])
    top = pl.ds(pl.multiple_of(at.group_y * quarter, 8), quarter // 2)
    low = pl.ds(pl.multiple_of(at.group_x * quarter + quarter // 2, 8), quarter // 2)
    image.far_done = []
    for src, dst in image.weights:
        image.far_done.append(copies.remote(src.at[top, :], dst.at[top, :], at.to_x))
        image.far_done.append(copies.remote(src.at[low, :], dst.at[low, :], at.to_y))
    text.far_done = []

    def project(s):
        s.o_done.wait()
        take_mixed(s.o, s.mixed, at, s.heads)
        s.proj_done.wait()
        for cols in chunks(s.x.shape[1]):
            s.part[:, cols] = dot(s.mixed[...], s.proj[cols, :], ((1,), (1,)))
        s.part_done = copies.remote(s.part, s.part_in, at.to_core)
        s.sums[...] = jnp.zeros_like(s.sums)
        for copy in s.rows_done:
            copy.wait()
        for rows in chunks(s.dy.shape[0]):
            s.dy_t[:, rows] = jnp.transpose(s.dy[rows, :])

    def second_norm(s):
        s.part_done.wait()
        for rows in chunks(s.x.shape[0]):
            middle = (
                s.x[rows, :].astype(F32) + s.part[rows, :] + s.part_in[rows, :] + s.small[3:4]
            )
            s.mid[rows, :] = middle
            normed, _ = normalise(middle)
            low = (normed * s.small[1:2] + s.small[4:5]).astype(BF16)
            s.first[rows, :] = low
            s.first_t[:, rows] = jnp.transpose(low)

    def feed_forward(s):
        tokens, width = s.x.shape
        hidden, own = s.up.shape[1], s.proj.shape[1]
        for copy in s.rest_done:
            copy.wait()
        for copy in s.far_done:
            copy.wait_recv()

        def tile(index, carry):
            cols = pl.ds(pl.multiple_of(index * 256, 256), 256)
            up, down = s.up[:, cols], s.down[:, cols]
            per_row = width // 256
            up_cols = pl.ds(pl.multiple_of(own + index * 256, LANES), 256)
            down_cols = pl.ds(pl.multiple_of(own + hidden + index * 256, LANES), 256)
            row = pl.ds(7 + index // per_row, 1)
            place = pl.ds(pl.multiple_of((index % per_row) * 256, 256), 256)
            bias = s.small[row, place]
            total = jnp.zeros((1, 256), F32)
            for rows in chunks(tokens):
                z = dot(s.first[rows, :], up) + bias
                sg = jax.nn.sigmoid(1.702 * z)
                zs = z * sg
                s.act[rows, cols] = zs.astype(BF16)
                grad = dot(s.dy[rows, :], down)
                low = (grad * (sg + 1.702 * zs * (1.0 - sg))).astype(BF16)
                s.dz[rows, cols] = low
                total = total + jnp.sum(low.astype(F32), axis=0, keepdims=True)
            s.sums[row, place] = total
            s.rest[:, up_cols] = dot(s.first_t[...], s.dz[:, cols]).astype(BF16)
            s.rest[:, down_cols] = dot(s.dy_t[...], s.act[:, cols]).astype(BF16)
            return carry

        lax.fori_loop(0, hidden // 256, tile, 0)
        for cols in chunks(width):
            s.grad[0, :, cols] = dot(s.dz[...], s.up[cols, :], ((1,), (1,)))
        s.grad_done = copies.remote(s.grad.at[0], s.grad_in.at[0], at.to_core)
        for cols in chunks(width):
            s.grad[1, :, cols] = dot(s.act[...], s.down[cols, :], ((1,), (1,)))
        s.y_done = copies.remote(s.grad.at[1], s.grad_in.at[1], at.to_core)

    def back(s):
        sums = s.sums
        s.grad_done.wait()
        for rows in chunks(s.x.shape[0]):
            normed, inv = normalise(s.mid[rows, :])
            second = s.grad[0, rows, :] + s.grad_in[0, rows, :]
            scaled = second * s.small[1:2]
            dy = s.dy[rows, :].astype(F32)
            dmid = dy + inv * (
                scaled
                - jnp.mean(scaled, axis=-1, keepdims=True)
                - normed * jnp.mean(scaled * normed, axis=-1, keepdims=True)
            )
            s.dmid[rows, :] = dmid
            sums[1:2] += jnp.sum(second * normed, axis=0, keepdims=True)
            sums[3:4] += jnp.sum(dmid, axis=0, keepdims=True)
            sums[4:5] += jnp.sum(second, axis=0, keepdims=True)
            sums[5:6] += jnp.sum(dy, axis=0, keepdims=True)
            low = dmid.astype(BF16)
            s.first_t[:, rows] = jnp.transpose(low)
            s.do[rows, :] = dot(low, s.proj[...])
        s.writes = [copies.local(s.dmid, s.dmid_out)]
        write_grad_o(s.do, s.do_mine, s.heads)
        s.do_done = send_blocks(copies, at, s.do_mine, s.do_out)
        s.rest[:, : s.proj.shape[1]] = dot(s.first_t[...], s.mixed[...]).astype(BF16)

    def output(s):
        s.y_done.wait()
        for rows in chunks(s.x.shape[0]):
            s.y[rows, :] = (
                s.mid[rows, :] + s.grad[1, rows, :] + s.grad_in[1, rows, :] + s.small[5:6]
            ).astype(BF16)
        s.writes.append(copies.local(s.y, s.y_out))

    project(text)
    project(image)
    second_norm(text)
    feed_forward(text)
    second_norm(image)
    back(text)
    plane = PlaneSum(copies, at, text.rest, arrivals)
    feed_forward(image)
    back(image)
    keep = copies.local(image.rest, image.rest_out)
    plane.cross()
    output(text)
    output(image)
    plane.arrived()
    half = plane.half

    def put(cols):
        text.rest_out[:half, cols], text.rest_out[half:, cols] = plane.halves(cols)

    by_columns(plane.columns, put)
    plane.sent()
    keep.wait()
    for s in streams:
        for copy in s.do_done + s.writes:
            copy.wait()
        for copy in s.far_done:
            copy.wait_send()


def middle(streams):
    vmem, hbm = pl.BlockSpec(memory_space=pltpu.VMEM), pl.BlockSpec(memory_space=pl.ANY)
    out_shape, out_specs, scratch = [], [], []
    arrivals = None
    for o, x, dy, small, proj, up, down in streams:
        tokens, width = x.shape
        hidden, own = up.shape[1], proj.shape[1]
        rest = (width, own + 2 * hidden)
        summed = arrivals is None
        if summed:
            arrivals = PlaneSum.arrivals(width // 4, rest[1])
        out_shape += [
            jax.ShapeDtypeStruct((tokens, width), BF16),
            jax.ShapeDtypeStruct((tokens, width), F32),
            jax.ShapeDtypeStruct(o.shape, BF16),
            jax.ShapeDtypeStruct((width // 4, rest[1]), F32)
            if summed
            else jax.ShapeDtypeStruct(rest, BF16),
            jax.ShapeDtypeStruct(small.shape, F32),
        ]
        out_specs += [hbm, hbm, hbm, vmem if summed else hbm, vmem]
        scratch += [
            pltpu.VMEM(proj.shape, BF16),
            pltpu.VMEM(up.shape, BF16),
            pltpu.VMEM(down.shape, BF16),
            pltpu.VMEM(rest, BF16),
            pltpu.VMEM((tokens, own), BF16),
            pltpu.VMEM((tokens, width), F32),
            pltpu.VMEM((tokens, width), F32),
            pltpu.VMEM((tokens, width), F32),
            pltpu.VMEM((tokens, width), BF16),
            pltpu.VMEM((width, tokens), BF16),
            pltpu.VMEM((width, tokens), BF16),
            pltpu.VMEM((tokens, hidden), BF16),
            pltpu.VMEM((tokens, hidden), BF16),
            pltpu.VMEM((2, tokens, width), F32),
            pltpu.VMEM((2, tokens, width), F32),
            pltpu.VMEM((tokens, own), F32),
            pltpu.VMEM(o.shape, BF16),
            pltpu.VMEM(o.shape, BF16),
            pltpu.VMEM((tokens, width), BF16),
            pltpu.VMEM((tokens, width), BF16),
            pltpu.VMEM((tokens, width), BF16),
            pltpu.VMEM((tokens, width), F32),
        ]
    results = pl.pallas_call(
        middle_kernel,
        out_shape=out_shape,
        in_specs=([hbm] * 3 + [vmem] + [hbm] * 3) * 2,
        out_specs=out_specs,
        scratch_shapes=scratch + arrivals + copy_sems(2 * 6 + 4 + 6, 2 * (4 + 3) + 8 + 1),
        compiler_params=pltpu.CompilerParams(
            collective_id=1, has_side_effects=True, vmem_limit_bytes=64 * 1024 * 1000
        ),
        name="middle",
    )(*streams[0], *streams[1])
    return results[:MIDDLE_OUT], results[MIDDLE_OUT:]


def take_dqkv(got, out, at, heads):
    width = heads * HD

    def put(which, tile, rows, value):
        start = which * width + tile * LANES
        out[rows, start : start + LANES] = value.astype(BF16)

    take_halves(got, out, at, heads, QB + 2 * KB, functools.partial(put, 0))

    def keys(position, head):
        return as_f32(got, position, key_rows(head))

    pairs = [(keys(0, 0), keys(1, 0)), (keys(2, 0), keys(3, 0))]
    if heads == 6:
        pairs.append((keys(0, 1) + keys(2, 1), keys(1, 1) + keys(3, 1)))
    for tile, (one, two) in enumerate(pairs):
        put(1, tile, slice(None), lane_pair((one, 0), (two, 0)))
        put(2, tile, slice(None), lane_pair((one, 1), (two, 1)))


LAST_IN, LAST_OUT, LAST_SCRATCH = 12, 4, 21


def last_kernel(*refs):
    at = partners()
    ins = [refs[:LAST_IN], refs[LAST_IN : 2 * LAST_IN]]
    refs = refs[2 * LAST_IN :]
    outs = [refs[:LAST_OUT], refs[LAST_OUT : 2 * LAST_OUT]]
    refs = refs[2 * LAST_OUT :]
    count = LAST_SCRATCH + 10
    scratch = [refs[:count], refs[count : 2 * count]]
    refs = refs[2 * count :]
    rest_arrivals, rest_loads = refs[:4], refs[4:7]
    copies = Copies(*refs[7:])
    streams = []
    for in_refs, out_refs, own in zip(ins, outs, scratch):
        s = Bag()
        (
            s.m_in, s.do_in, s.o_in, s.lse, s.seg_row, s.first_in, s.x_in, s.small, s.weight_in, s.dmid_in,
            s.rest, s.sums_in,
        ) = in_refs
        s.grad_rows_out, s.sums, s.rest_final, s.qkv_final = out_refs
        (
            s.m, s.do, s.o, s.query_doc, s.key_doc, s.score_keys, s.grad_rows, s.acc, s.back, s.got, s.dqkv, s.weight, s.first, s.x, s.dmid,
            s.part, s.part_in, s.g_qkv, s.sums_own, s.sums_out, s.sums_got,
        ) = own[:LAST_SCRATCH]
        s.rest_line, s.qkv_line = own[LAST_SCRATCH : LAST_SCRATCH + 3], own[LAST_SCRATCH + 3 : LAST_SCRATCH + 6]
        s.qkv_arrivals = own[LAST_SCRATCH + 6 :]
        s.heads = s.weight.shape[2] // HD
        s.features = (s.query_doc, s.key_doc)
        s.reads = [
            copies.local(src, dst) for src, dst in ((s.m_in, s.m), (s.do_in, s.do), (s.o_in, s.o))
        ]
        streams.append(s)
    text, image = streams
    meet([at.to_x, at.to_y] + at.to_ctx[1:] + [at.to_core])
    plane = PlaneSum(copies, at, image.rest, rest_arrivals, rest_loads)
    text_half = text.rest.shape[0] // 2

    def text_values(cols):
        return text.rest[:text_half, cols], text.rest[text_half:, cols]

    text_line = LineSum(
        copies, at, text_values, text.rest_line, text.rest_final, 0, text.rest.shape[1]
    )
    text_line.gather()
    for s in (image, text):
        document_features(s.seg_row, *s.features)
    for s in streams:
        s.loads = [
            copies.local(src, dst)
            for src, dst in (
                (s.weight_in, s.weight), (s.first_in, s.first), (s.x_in, s.x), (s.dmid_in, s.dmid),
            )
        ]
    for s in (image, text):
        for copy in s.reads:
            copy.wait()
    for s in (image, text):
        s.acc[...] = jnp.zeros_like(s.acc)
        s.back[...] = jnp.zeros_like(s.back)
        mark_keys(s.m, s.features[1], s.acc.shape[0], s.score_keys, None)

    def unattend_tasks(s, *task):
        unattend(
            at, s.m, s.do, s.o, s.lse, s.features[0], s.score_keys, s.acc, s.back, *task
        )

    unattend_tasks(image, image_task, 0, 8, 4, False)
    text_line.join()
    unattend_tasks(image, image_task, 8, 12, 4, False)
    key_gradients(image.acc, image.back)
    image.sends = send_blocks(copies, at, image.back, image.got)
    unattend_tasks(text, text_task, 0, 4, 2, True)
    unattend_tasks(text, text_task, 4, 8, 4, True)
    key_gradients(text.acc, text.back)
    text.sends = send_blocks(copies, at, text.back, text.got)
    plane.cross()
    text_line.share()

    def project(s):
        width = s.x.shape[1]
        own = s.heads * HD
        for copy in s.sends:
            copy.wait()
        for copy in s.loads:
            copy.wait()
        take_dqkv(s.got, s.dqkv, at, s.heads)
        for which in range(3):
            cols = slice(which * own, (which + 1) * own)
            s.g_qkv[:, cols] = dot(s.first[...], s.dqkv[:, cols]).astype(BF16)
        s.qkv_plane = PlaneSum(copies, at, s.g_qkv, s.qkv_arrivals)
        for cols in chunks(width):
            total = dot(s.dqkv[:, :own], s.weight[0, cols, :], ((1,), (1,)))
            total = total + dot(s.dqkv[:, own : 2 * own], s.weight[1, cols, :], ((1,), (1,)))
            s.part[:, cols] = total + dot(s.dqkv[:, 2 * own :], s.weight[2, cols, :], ((1,), (1,)))
        s.part_done = copies.remote(s.part, s.part_in, at.to_core)
        s.sums_own[...] = s.sums_in[...]
        s.sums_own[6:7, :own] = jnp.sum(s.dqkv[:, :own].astype(F32), axis=0, keepdims=True)
        s.sums_own[6:7, own:] = jnp.sum(s.dqkv[:, 2 * own :].astype(F32), axis=0, keepdims=True)
        s.qkv_sum = LineSum(
            copies, at, s.qkv_plane.halves, s.qkv_line, s.qkv_final, 0, 3 * own
        )

    def input_grad(s):
        s.part_done.wait()
        for rows in chunks(s.x.shape[0]):
            normed, inv = normalise(s.x[rows, :].astype(F32))
            first = s.part[rows, :] + s.part_in[rows, :]
            scaled = first * s.small[0:1]
            s.grad_rows[rows, :] = s.dmid[rows, :] + inv * (
                scaled
                - jnp.mean(scaled, axis=-1, keepdims=True)
                - normed * jnp.mean(scaled * normed, axis=-1, keepdims=True)
            )
            s.sums_own[0:1] += jnp.sum(first * normed, axis=0, keepdims=True)
            s.sums_own[2:3] += jnp.sum(first, axis=0, keepdims=True)
        s.write = copies.local(s.grad_rows, s.grad_rows_out)
        s.sums_done = [copies.remote(s.sums_own, s.sums_got.at[0], at.to_x)]

    def add_sums(s, step):
        s.sums_done[-1].wait_recv()
        before = s.sums_own if step == 0 else s.sums_out.at[step - 1]
        after = s.sums if step == 3 else s.sums_out.at[step]
        after[...] = before[...] + s.sums_got[step]
        if step < 3:
            device = (at.to_y, at.to_ctx[1], at.to_ctx[2])[step]
            s.sums_done.append(copies.remote(after, s.sums_got.at[step + 1], device))

    plane.arrived()
    third = plane.columns // (3 * STEP) * STEP
    rest_lines = [
        LineSum(copies, at, plane.halves, image.rest_line, image.rest_final, begin, end)
        for begin, end in ((0, third), (third, 2 * third), (2 * third, plane.columns))
    ]
    for line in rest_lines:
        line.gather()
    project(image)
    rest_lines[0].join()
    input_grad(image)
    image.qkv_plane.cross()
    rest_lines[1].join()
    project(text)
    rest_lines[0].share()
    image.qkv_plane.arrived()
    image.qkv_sum.gather()
    rest_lines[2].join()
    input_grad(text)
    text.qkv_plane.cross()
    rest_lines[1].share()
    image.qkv_sum.join()
    text.qkv_plane.arrived()
    text.qkv_sum.gather()
    add_sums(image, 0)
    add_sums(text, 0)
    rest_lines[2].share()
    text.qkv_sum.join()
    add_sums(image, 1)
    add_sums(text, 1)
    image.qkv_sum.share()
    text.qkv_sum.share()
    add_sums(image, 2)
    add_sums(text, 2)
    add_sums(image, 3)
    add_sums(text, 3)
    for line in [text_line] + rest_lines + [image.qkv_sum, text.qkv_sum]:
        line.finish()
    plane.sent()
    for s in streams:
        s.qkv_plane.sent()
        for copy in s.sums_done:
            copy.wait_send()
        s.write.wait()


def last(streams):
    vmem, hbm = pl.BlockSpec(memory_space=pltpu.VMEM), pl.BlockSpec(memory_space=pl.ANY)
    out_shape, scratch = [], []
    for messages, do, o, lse, seg, first, x, small, weight, dmid, rest, sums in streams:
        tokens, width = x.shape
        own = weight.shape[2]
        rest_shape, qkv_shape = (width // 4, rest.shape[1]), (width // 4, 3 * own)
        out_shape += [
            jax.ShapeDtypeStruct((tokens, width), F32),
            jax.ShapeDtypeStruct(small.shape, F32),
            jax.ShapeDtypeStruct(rest_shape, BF16),
            jax.ShapeDtypeStruct(qkv_shape, BF16),
        ]
        scratch += [
            pltpu.VMEM(messages.shape, BF16),
            pltpu.VMEM(do.shape, BF16),
            pltpu.VMEM(do.shape, BF16),
            pltpu.VMEM((4 * tokens, LANES), BF16),
            pltpu.VMEM((4 * tokens, LANES), BF16),
            pltpu.VMEM((1 if own == 4 * HD else 2, 4 * tokens, LANES), BF16),
            pltpu.VMEM((tokens, width), F32),
            pltpu.VMEM((1 if own == 4 * HD else 2, 4 * tokens, LANES), F32),
            pltpu.VMEM(messages.shape, BF16),
            pltpu.VMEM(messages.shape, BF16),
            pltpu.VMEM((tokens, 3 * own), BF16),
            pltpu.VMEM(weight.shape, BF16),
            pltpu.VMEM(first.shape, BF16),
            pltpu.VMEM((tokens, width), BF16),
            pltpu.VMEM((tokens, width), F32),
            pltpu.VMEM((tokens, width), F32),
            pltpu.VMEM((tokens, width), F32),
            pltpu.VMEM((width, 3 * own), BF16),
            pltpu.VMEM(small.shape, F32),
            pltpu.VMEM((3,) + small.shape, F32),
            pltpu.VMEM((4,) + small.shape, F32),
        ]
        scratch += LineSum.scratch(*rest_shape) + LineSum.scratch(*qkv_shape)
        scratch += PlaneSum.arrivals(*qkv_shape)
    scratch += PlaneSum.arrivals(*rest_shape) + PlaneSum.loads_scratch(*rest_shape)
    specs = [hbm, hbm, hbm, vmem, vmem, hbm, hbm, vmem, hbm, hbm, vmem, vmem]
    specs += specs[:10] + [hbm, vmem]
    results = pl.pallas_call(
        last_kernel,
        out_shape=out_shape,
        in_specs=specs,
        out_specs=[hbm, vmem, vmem, vmem] * 2,
        scratch_shapes=scratch + copy_sems(2 * (3 + 1 + 4 + 6) + 6 + 3 * 6, 2 * (1 + 7 + 1) + 3),
        compiler_params=pltpu.CompilerParams(
            collective_id=2, has_side_effects=True, vmem_limit_bytes=64 * 1024 * 1000
        ),
        name="last",
    )(*streams[0], *streams[1])
    return results[:4], results[4:]


def take_own(group, row):
    columns = row.shape[1] // 4
    return pltpu.roll(row, (4 - group) % 4 * columns, 1)[:, :columns]


def finish_kernel(*refs):
    ins = [refs[:3], refs[3:6]]
    outs = [refs[6:13], refs[13:]]
    for (sums, rest, qkv), (gains, shifts, bias, qkv_out, proj, up, down) in zip(ins, outs):
        group = lax.axis_index(FSDP)
        rows = take_own(group, sums[0:8])
        gains[...] = rows[0:2]
        shifts[...] = rows[2:6]
        line = jnp.concatenate([sums[6:7], sums[7:8], sums[8:9]], axis=1)
        bias[...] = take_own(group, jnp.broadcast_to(line, (8, line.shape[1])))[0:1]
        own = qkv.shape[1] // 3
        for which in range(3):
            qkv_out[which] = qkv[:, which * own : (which + 1) * own].astype(F32)
        hidden = up.shape[1]
        up[...] = rest[:, own : own + hidden].astype(F32)
        if down.shape[0] > down.shape[1]:
            proj[...] = jnp.transpose(rest[:, :own].astype(F32))
            down[...] = jnp.transpose(rest[:, own + hidden :].astype(F32))
        else:
            proj[...] = rest[:, :own].astype(F32)
            down[...] = rest[:, own + hidden :].astype(F32)


def finish(streams):
    out_shape = []
    for sums, rest, qkv, flip in streams:
        rows, own = qkv.shape[0], qkv.shape[1] // 3
        hidden = (rest.shape[1] - own) // 2
        shapes = [(2, rows), (4, rows), (1, 3 * rows), (3, rows, own)]
        shapes += [(own, rows), (rows, hidden), (hidden, rows)] if flip else [
            (rows, own), (rows, hidden), (rows, hidden)
        ]
        out_shape += [jax.ShapeDtypeStruct(shape, F32) for shape in shapes]
    results = pl.pallas_call(finish_kernel, out_shape=out_shape, name="finish")(
        *streams[0][:3], *streams[1][:3]
    )
    return results[:7], results[7:]


def on_device(*args):
    streams = []
    for item, causal in ((args[10:], True), (args[:10], False)):
        s = Bag()
        rows, s.seg, cotangent, s.gains, s.shifts, s.head_bias, s.qkv, proj, s.up, down = item
        s.flip, s.x, s.dy = causal, rows[0], cotangent[0]
        s.down, s.proj = (down, proj) if causal else (down.T, proj.T)
        streams.append(s)
    started = front(
        [(s.x, s.seg, s.gains, s.shifts, s.head_bias, s.qkv, s.up, s.down, s.proj) for s in streams]
    )
    for s, (weight, small, first, messages, proj, up, down, o, lse, o_got) in zip(streams, started):
        s.weight, s.small, s.first, s.messages, s.o, s.lse = weight, small, first, messages, o, lse
        s.weights, s.o_got = (proj, up, down), o_got
    done = middle([(s.o_got, s.x, s.dy, s.small, *s.weights) for s in streams])
    ended = last(
        [
            (s.messages, do, s.o, s.lse, s.seg, s.first, s.x, s.small, s.weight, dmid, rest, sums)
            for s, (y, dmid, do, rest, sums) in zip(streams, done)
        ]
    )
    final = finish([(sums, rest, qkv, s.flip) for s, (_, sums, rest, qkv) in zip(streams, ended)])
    outputs = []
    for s, (y, *_), (grad_rows, *_), (gains, shifts, bias, qkv, proj, up, down) in zip(
        streams, done, ended, final
    ):
        if not s.flip:
            proj, down = proj.T, down.T
        outputs.append((y[None], grad_rows[None], gains, shifts, bias, qkv, proj, up, down))
    return outputs[1] + outputs[0]


def layer_stats(rows):
    row_mean = jnp.mean(rows, axis=-1, keepdims=True)
    centred = rows - row_mean
    inv_std = lax.rsqrt(jnp.mean(centred * centred, axis=-1, keepdims=True) + 1e-05)
    return (centred * inv_std, inv_std)


def norm_back(grad_normed_out, normed, inv_std, gain):
    scaled = grad_normed_out * gain
    return inv_std * (
        scaled
        - jnp.mean(scaled, axis=-1, keepdims=True)
        - normed * jnp.mean(scaled * normed, axis=-1, keepdims=True)
    )


def tensor_psum(partial_rows):
    return lax.psum(partial_rows, TP)


def any_mesh_block(
    rows_in,
    seg_row,
    cotangent,
    gains,
    shifts,
    head_bias,
    qkv_weight,
    proj_weight,
    up_weight,
    down_weight,
    causal,
):
    gain_full, shift_full, bias_full, qkv_full, proj_full, up_full, down_full = (
        lax.all_gather(gains, FSDP, axis=1, tiled=True),
        lax.all_gather(shifts, FSDP, axis=1, tiled=True),
        lax.all_gather(head_bias, FSDP, axis=1, tiled=True),
        lax.all_gather(qkv_weight, FSDP, axis=1, tiled=True),
        lax.all_gather(proj_weight, FSDP, axis=1, tiled=True),
        lax.all_gather(up_weight, FSDP, axis=0, tiled=True),
        lax.all_gather(down_weight, FSDP, axis=1, tiled=True),
    )
    gain_vals = gain_full.astype(jnp.float32)
    shift_vals = shift_full.astype(jnp.float32)
    bias_vals = bias_full[0].astype(jnp.float32)
    tp_width = qkv_full.shape[2]
    local_rows = rows_in.shape[1]
    seq_length = seg_row.shape[1]
    head_local = tp_width // HD
    rows = rows_in[0].astype(jnp.float32)
    row_start = lax.axis_index(CTX) * local_rows
    seg_all = seg_row[0]
    seg_query = lax.dynamic_slice_in_dim(seg_all, row_start, local_rows)
    query_pos = row_start + jnp.arange(local_rows, dtype=jnp.int32)
    key_pos = jnp.arange(seq_length, dtype=jnp.int32)
    allowed = seg_query[:, None] == seg_all[None, :]
    if causal:
        allowed = jnp.logical_and(allowed, key_pos[None, :] <= query_pos[:, None])

    def to_heads(matrix):
        return matrix.reshape(matrix.shape[0], head_local, HD).transpose(1, 0, 2)

    def from_heads(stacked):
        return stacked.transpose(1, 0, 2).reshape(stacked.shape[1], head_local * HD)

    normed_one, inv_one = layer_stats(rows)
    first_in = (normed_one * gain_vals[0] + shift_vals[0]).astype(jnp.bfloat16)
    queries = (
        jnp.dot(first_in, qkv_full[0], preferred_element_type=jnp.float32) + bias_vals[:tp_width]
    ).astype(jnp.bfloat16)
    key_rows = jnp.dot(first_in, qkv_full[1], preferred_element_type=jnp.float32).astype(
        jnp.bfloat16
    )
    values = (
        jnp.dot(first_in, qkv_full[2], preferred_element_type=jnp.float32)
        + bias_vals[tp_width : 2 * tp_width]
    ).astype(jnp.bfloat16)
    key_all, value_all = (
        lax.all_gather(key_rows, CTX, axis=0, tiled=True),
        lax.all_gather(values, CTX, axis=0, tiled=True),
    )
    query_heads = to_heads(queries)
    key_heads = to_heads(key_all)
    value_heads = to_heads(value_all)

    def attend(head_items):
        query_h, key_h, value_h = head_items
        scores = dot(query_h, key_h, ((1,), (1,))) * 0.125
        scores = jnp.where(allowed, scores, -1e30)
        row_top = jnp.max(scores, axis=-1, keepdims=True)
        weights = jnp.exp(scores - row_top)
        row_total = jnp.sum(weights, axis=-1, keepdims=True)
        weights_low = (weights / row_total).astype(jnp.bfloat16)
        mixed_h = dot(weights_low, value_h, ((1,), (0,)))
        return (mixed_h.astype(jnp.bfloat16), row_top[:, 0] + jnp.log(row_total[:, 0]))

    mixed_heads, log_totals = lax.map(attend, (query_heads, key_heads, value_heads))
    mixed = from_heads(mixed_heads)
    middle = (
        rows
        + tensor_psum(jnp.dot(mixed, proj_full, preferred_element_type=jnp.float32))
        + shift_vals[1]
    )
    normed_two, inv_two = layer_stats(middle)
    second_in = (normed_two * gain_vals[1] + shift_vals[2]).astype(jnp.bfloat16)
    hidden = (
        jnp.dot(second_in, up_full, preferred_element_type=jnp.float32) + bias_vals[2 * tp_width :]
    )
    sigma = jax.nn.sigmoid(1.702 * hidden)
    activated = (hidden * sigma).astype(jnp.bfloat16)
    output = (
        middle
        + tensor_psum(jnp.dot(activated, down_full, preferred_element_type=jnp.float32))
        + shift_vals[3]
    )
    grad_out = cotangent[0].astype(jnp.float32)
    grad_down_bias = jnp.sum(grad_out, axis=0)
    grad_branch = grad_out.astype(jnp.bfloat16)
    grad_down = dot(activated, grad_branch, ((0,), (0,)))
    grad_act = dot(grad_branch, down_full, ((1,), (1,)))
    grad_hidden = (grad_act * (sigma + 1.702 * hidden * sigma * (1.0 - sigma))).astype(jnp.bfloat16)
    grad_up_bias = jnp.sum(grad_hidden.astype(jnp.float32), axis=0)
    grad_up = dot(second_in, grad_hidden, ((0,), (0,)))
    grad_second = tensor_psum(
        dot(grad_hidden, up_full, ((1,), (1,)))
    )
    grad_gain_two = jnp.sum(grad_second * normed_two, axis=0)
    grad_shift_two = jnp.sum(grad_second, axis=0)
    grad_middle = grad_out + norm_back(grad_second, normed_two, inv_two, gain_vals[1])
    grad_proj_bias = jnp.sum(grad_middle, axis=0)
    grad_attn = grad_middle.astype(jnp.bfloat16)
    grad_proj = dot(mixed, grad_attn, ((0,), (0,)))
    grad_mixed = dot(grad_attn, proj_full, ((1,), (1,))).astype(jnp.bfloat16)

    def attend_back(head_items):
        query_h, key_h, value_h, grad_h, log_total = head_items
        scores = dot(query_h, key_h, ((1,), (1,))) * 0.125
        weights = jnp.where(allowed, jnp.exp(scores - log_total[:, None]), 0.0)
        grad_weights = dot(grad_h, value_h, ((1,), (1,)))
        row_delta = jnp.sum(weights * grad_weights, axis=-1, keepdims=True)
        grad_scores = (weights * (grad_weights - row_delta)).astype(jnp.bfloat16)
        grad_query_h = (
            dot(grad_scores, key_h, ((1,), (0,))) * 0.125
        )
        grad_key_h = (
            dot(grad_scores, query_h, ((0,), (0,)))
            * 0.125
        )
        grad_value_h = dot(weights.astype(jnp.bfloat16), grad_h, ((0,), (0,)))
        return (grad_query_h, grad_key_h, grad_value_h)

    query_parts, key_parts, value_parts = lax.map(
        attend_back, (query_heads, key_heads, value_heads, to_heads(grad_mixed), log_totals)
    )
    key_sum, value_sum = (
        lax.psum_scatter(from_heads(key_parts), CTX, scatter_dimension=0, tiled=True),
        lax.psum_scatter(from_heads(value_parts), CTX, scatter_dimension=0, tiled=True),
    )
    grad_query = from_heads(query_parts).astype(jnp.bfloat16)
    grad_key = key_sum.astype(jnp.bfloat16)
    grad_value = value_sum.astype(jnp.bfloat16)
    grad_qkv = jnp.stack(
        [
            dot(first_in, grad_query, ((0,), (0,))),
            dot(first_in, grad_key, ((0,), (0,))),
            dot(first_in, grad_value, ((0,), (0,))),
        ]
    )
    grad_head = jnp.concatenate(
        [
            jnp.sum(grad_query.astype(jnp.float32), axis=0),
            jnp.sum(grad_value.astype(jnp.float32), axis=0),
            grad_up_bias,
        ]
    )[None, :]
    grad_first_part = dot(grad_query, qkv_full[0], ((1,), (1,)))
    grad_first_part = grad_first_part + dot(grad_key, qkv_full[1], ((1,), (1,)))
    grad_first_part = grad_first_part + dot(grad_value, qkv_full[2], ((1,), (1,)))
    grad_first = tensor_psum(grad_first_part)
    grad_gain_one = jnp.sum(grad_first * normed_one, axis=0)
    grad_shift_one = jnp.sum(grad_first, axis=0)
    grad_rows = grad_middle + norm_back(grad_first, normed_one, inv_one, gain_vals[0])
    grad_gains = jnp.stack([grad_gain_one, grad_gain_two])
    grad_shifts = jnp.stack([grad_shift_one, grad_proj_bias, grad_shift_two, grad_down_bias])
    share_gains, share_shifts, share_head, share_qkv, share_proj, share_up, share_down = (
        lax.psum_scatter(grad_gains, FSDP, scatter_dimension=1, tiled=True),
        lax.psum_scatter(grad_shifts, FSDP, scatter_dimension=1, tiled=True),
        lax.psum_scatter(grad_head, FSDP, scatter_dimension=1, tiled=True),
        lax.psum_scatter(grad_qkv, FSDP, scatter_dimension=1, tiled=True),
        lax.psum_scatter(grad_proj, FSDP, scatter_dimension=1, tiled=True),
        lax.psum_scatter(grad_up, FSDP, scatter_dimension=0, tiled=True),
        lax.psum_scatter(grad_down, FSDP, scatter_dimension=1, tiled=True),
    )
    owned = lax.psum(
        (share_gains, share_shifts, share_head, share_qkv, share_proj, share_up, share_down), CTX
    )
    return (output.astype(jnp.bfloat16)[None], grad_rows[None]) + tuple(owned)


def on_any_mesh(
    image_input,
    image_segments,
    image_cotangent,
    image_gains,
    image_shifts,
    image_head_bias,
    image_qkv_weight,
    image_proj_weight,
    image_up_weight,
    image_down_weight,
    text_input,
    text_segments,
    text_cotangent,
    text_gains,
    text_shifts,
    text_head_bias,
    text_qkv_weight,
    text_proj_weight,
    text_up_weight,
    text_down_weight,
):
    image_results = any_mesh_block(
        image_input,
        image_segments,
        image_cotangent,
        image_gains,
        image_shifts,
        image_head_bias,
        image_qkv_weight,
        image_proj_weight,
        image_up_weight,
        image_down_weight,
        False,
    )
    text_results = any_mesh_block(
        text_input,
        text_segments,
        text_cotangent,
        text_gains,
        text_shifts,
        text_head_bias,
        text_qkv_weight,
        text_proj_weight,
        text_up_weight,
        text_down_weight,
        True,
    )
    return image_results + text_results


def stream_specs():
    return (
        P(FSDP, CTX, None),
        P(FSDP, None),
        P(FSDP, CTX, None),
        P(None, FSDP),
        P(None, FSDP),
        P(TP, FSDP),
        P(None, FSDP, TP),
        P(TP, FSDP),
        P(FSDP, TP),
        P(TP, FSDP),
    )


def solution(mesh):
    one = stream_specs()
    grads = (one[0], one[0]) + one[3:]
    body = on_device
    if (mesh.shape[FSDP], mesh.shape[CTX], mesh.shape[TP]) != (4, 4, 2):
        body = on_any_mesh
    return jax.shard_map(
        body, mesh=mesh, in_specs=one + one, out_specs=grads + grads, check_vma=False
    )
```

```python
import functools

import jax
import jax.numpy as jnp
from jax import lax
from jax.experimental import pallas as pl
from jax.experimental.pallas import tpu as pltpu
from jax.sharding import PartitionSpec as P

HD = 64
LANES = 128
QB = 256
KB = 512
NEG = -1e30
F32 = jnp.float32
MESH = pl.DeviceIdType.MESH
FSDP, CTX, TP = "fsdp", "ctx", "tp"
BF16 = jnp.bfloat16


def dot(left, right, dims=((1,), (0,))):
    return lax.dot_general(left, right, (dims, ((), ())), preferred_element_type=F32)


def lane_marks():
    lane = lax.broadcasted_iota(jnp.int32, (1, LANES), 1)
    first = (lane < HD).astype(F32).astype(BF16)
    second = (lane >= HD).astype(F32).astype(BF16)
    return first, second


def document_features(row_ref, query_out, key_out):
    lane = lax.broadcasted_iota(jnp.int32, (LANES, LANES), 1) % HD
    for start in range(0, query_out.shape[0], LANES):
        row = row_ref[:, start : start + LANES].astype(F32)
        same = jnp.transpose(jnp.broadcast_to(row, (LANES, LANES))) == lane.astype(F32)
        query_out[start : start + LANES, :] = jnp.where(same, 1.0, 0.0).astype(BF16)
        key_out[start : start + LANES, :] = jnp.where(same, 0.0, NEG).astype(BF16)


def swap_halves(value):
    return pltpu.roll(value, HD, 1)


def key_range(index):
    return slice(index * KB, (index + 1) * KB)


def pick(flag, one, zero):
    return jnp.where(flag == 1, one, zero)


def query_rows(head):
    return pl.ds(pl.multiple_of(head * (QB + 2 * KB), QB), QB)


def key_rows(head):
    return pl.ds(pl.multiple_of(QB + head * KB, QB), KB)


def mark_keys(m, features, heads, score_keys, value_keys):
    first, second = lane_marks()
    for head in range(heads):
        for index in range(4):
            block = m[index, key_rows(head)]
            score_keys[head, key_range(index)] = block * first + features[key_range(index), :] * second
            if value_keys is not None:
                value_keys[head, key_range(index)] = block * second + first


def later(index, shape, axis, query_start):
    key_pos = index * KB + lax.broadcasted_iota(jnp.int32, shape, axis)
    query_pos = query_start + lax.broadcasted_iota(jnp.int32, shape, 1 - axis)
    return key_pos > query_pos


def mix_rows(query, score_keys, value_keys, head, blocks, query_start=None):
    scores = []
    for index in range(blocks):
        score = dot(query, score_keys[head, key_range(index)], ((1,), (1,)))
        if query_start is not None:
            score = jnp.where(later(index, score.shape, 1, query_start), NEG, score)
        scores.append(score)
    top = jnp.max(functools.reduce(jnp.maximum, scores), axis=1, keepdims=True)
    acc = jnp.zeros((query.shape[0], LANES), F32)
    for index, score in enumerate(scores):
        acc = acc + dot(jnp.exp(score - top).astype(BF16), value_keys[head, key_range(index)])
    return acc / swap_halves(acc), top + jnp.log(acc)


def text_task(at, task):
    return 0, task // 2, task % 2


def image_task(at, task):
    shared = 1 - (task + 8) // 12
    step = 5 - task // 2
    low, high = (at.here_low + step % 2) % 2, (at.here_high + step // 2) % 2
    return shared, pick(shared, at.here_high * 2 + task // 2, high * 2 + low), task % 2


def attend(at, m, features, score_keys, value_keys, o, lse, task_of, begin, end, blocks, causal):
    first, second = lane_marks()
    lane = lax.broadcasted_iota(jnp.int32, (QB, LANES), 1)

    def one(task, carry):
        head, source, half = task_of(at, task)
        start = (source * 2 + half) * QB
        query = m[source, query_rows(head)].astype(F32)
        query = pick(half, swap_halves(query), query).astype(BF16)
        query = query * first + features[pl.ds(pl.multiple_of(start, QB), QB), :] * second
        mixed, log_total = mix_rows(
            query, score_keys, value_keys, head, blocks, start if causal else None
        )
        lse[task] = jnp.transpose(log_total)[:8]
        mixed = pick(half, mixed, swap_halves(mixed)).astype(BF16)
        rows = pl.ds(pl.multiple_of(head * QB, QB), QB)
        o[source, rows] = jnp.where(lane // HD == half, mixed, o[source, rows])
        return carry

    lax.fori_loop(begin, end, one, 0)


def unattend(at, m, do, o, lse, features, score_keys, acc, out, task_of, begin, end, blocks, causal):
    first, second = lane_marks()
    lane = lax.broadcasted_iota(jnp.int32, (QB, LANES), 1)

    def one(task, carry):
        head, source, half = task_of(at, task)
        start = (source * 2 + half) * QB
        rows = pl.ds(pl.multiple_of(head * QB, QB), QB)
        query, grad_o = m[source, query_rows(head)].astype(F32), do[source, rows].astype(F32)
        product = jnp.transpose(grad_o * o[source, rows].astype(F32))
        delta = jnp.sum(pick(half, product[HD:], product[:HD]), axis=0, keepdims=True)
        query = pick(half, swap_halves(query), query).astype(BF16) * first
        grad_o = pick(half, grad_o, swap_halves(grad_o)).astype(BF16) * second
        marked = query + features[pl.ds(pl.multiple_of(start, QB), QB), :] * second
        row_lse = lse[task, :1]
        grad_query = jnp.zeros((QB, LANES), F32)
        for index in range(blocks):
            keys = m[index, key_rows(head)]
            score = dot(score_keys[head, key_range(index)], marked, ((1,), (1,)))
            if causal:
                score = jnp.where(later(index, score.shape, 0, start), NEG, score)
            weights = jnp.exp(score - row_lse)
            grad_weights = dot(keys, grad_o, ((1,), (1,)))
            grad_scores = (weights * (grad_weights - delta)).astype(BF16)
            acc[head, key_range(index)] += dot(grad_scores, query) + dot(weights.astype(BF16), grad_o)
            grad_query = grad_query + dot(grad_scores, keys, ((0,), (0,)))
        grad_query = grad_query * 0.125
        grad_query = pick(half, swap_halves(grad_query), grad_query).astype(BF16)
        out[source, query_rows(head)] = jnp.where(
            lane // HD == half, grad_query, out[source, query_rows(head)]
        )
        return carry

    lax.fori_loop(begin, end, one, 0)


def key_gradients(acc, out, head):
    for index in range(4):
        out[index, key_rows(head)] = acc[head, key_range(index)].astype(BF16)


class Bag:
    pass


def partners():
    at = Bag()
    group, here, core = lax.axis_index(FSDP), lax.axis_index(CTX), lax.axis_index(TP)
    at.group, at.here, at.core = group, here, core
    at.group_x = group + 1 - 2 * (group % 2)
    at.group_y = group + 2 - 4 * (group // 2)
    at.group_far = 3 - group
    at.here_low, at.here_high = here % 2, here // 2
    at.inner, at.outer = (here + 1) // 2 == 1, (here + 1) // 2 != 1
    at.ctx = (here, here + 1 - 2 * (here % 2), here + 2 - 4 * (here // 2), 3 - here)
    at.to_x, at.to_y, at.to_far = ({FSDP: g} for g in (at.group_x, at.group_y, at.group_far))
    at.to_ctx = [{CTX: c} for c in at.ctx]
    at.to_core = {TP: 1 - core}
    return at


def greet(devices):
    barrier = pltpu.get_barrier_semaphore()
    for device in devices:
        pl.semaphore_signal(barrier, inc=1, device_id=device, device_id_type=MESH)


def meet(devices):
    pl.semaphore_wait(pltpu.get_barrier_semaphore(), len(devices))


class Copies:
    def __init__(self, send_sems, recv_sems, local_sems):
        self.sems = (send_sems, recv_sems, local_sems)
        self.used = [0, 0]

    def remote(self, src, dst, device, start=True):
        index = self.used[0]
        self.used[0] += 1
        copy = pltpu.make_async_remote_copy(
            src_ref=src,
            dst_ref=dst,
            send_sem=self.sems[0].at[index],
            recv_sem=self.sems[1].at[index],
            device_id=device,
            device_id_type=MESH,
        )
        if start:
            copy.start()
        return copy

    def local(self, src, dst, start=True):
        index = self.used[1]
        self.used[1] += 1
        copy = pltpu.make_async_copy(src, dst, self.sems[2].at[index])
        if start:
            copy.start()
        return copy


def copy_sems(remote, local):
    return [
        pltpu.SemaphoreType.DMA((remote,)),
        pltpu.SemaphoreType.DMA((remote,)),
        pltpu.SemaphoreType.DMA((local,)),
    ]


class Gather:
    def __init__(self, copies, at, src, dst):
        self.copies, self.at, self.dst = copies, at, dst
        self.rows = src.shape[-2]
        own = self.part(at.group, 0, self.rows)
        self.own = copies.local(src, own)
        self.to_x = copies.remote(src, own, at.to_x)
        self.to_y = copies.remote(src, own, at.to_y)

    def part(self, owner, offset, size):
        rows = pl.ds(pl.multiple_of(owner * self.rows + offset, 8), size)
        return self.dst.at[:, rows, :] if len(self.dst.shape) == 3 else self.dst.at[rows, :]

    def near(self):
        self.own.wait()
        self.to_x.wait()
        self.to_y.wait()

    def forward(self):
        half = self.rows // 2
        self.to_x.wait_recv()
        self.to_y.wait_recv()
        top = self.part(self.at.group_y, 0, half)
        low = self.part(self.at.group_x, half, half)
        self.far_x = self.copies.remote(top, top, self.at.to_x)
        self.far_y = self.copies.remote(low, low, self.at.to_y)

    def arrived(self):
        self.own.wait()
        self.far_x.wait_recv()
        self.far_y.wait_recv()

    def sent(self):
        for copy in (self.to_x, self.to_y, self.far_x, self.far_y):
            copy.wait_send()


def normalise(rows):
    mean = jnp.mean(rows, axis=-1, keepdims=True)
    centred = rows - mean
    inv = lax.rsqrt(jnp.mean(centred * centred, axis=-1, keepdims=True) + 1e-05)
    return centred * inv, inv


def lane_pair(low, high):
    lane = lax.broadcasted_iota(jnp.int32, low[0].shape, 1)
    left = low[0] if low[1] == 0 else pltpu.roll(low[0], HD, 1)
    right = high[0] if high[1] == 1 else pltpu.roll(high[0], HD, 1)
    return jnp.where(lane < HD, left, right)


def head_tile(ref, start, index, rows=slice(None)):
    first = start + (index // 2) * LANES
    return ref[rows, first : first + LANES], index % 2


def halves_pair(ref, start, index):
    half = ref.shape[0] // 2
    return lane_pair(
        head_tile(ref, start, index, slice(0, half)), head_tile(ref, start, index, slice(half, None))
    ).astype(BF16)


def write_messages(qkv, out, heads):
    width = heads * HD

    def keys_values(index):
        return lane_pair(head_tile(qkv, width, index), head_tile(qkv, 2 * width, index)).astype(BF16)

    for c in range(4):
        out[c, query_rows(0)] = halves_pair(qkv, 0, c)
        out[c, key_rows(0)] = keys_values(c)
        if heads == 6:
            out[c, key_rows(1)] = keys_values(4 + c % 2)
            out[c, query_rows(1)] = halves_pair(qkv, 0, 4 + c % 2)


def message_shape(heads, tokens):
    return (4, (heads // 2 - 1) * (QB + tokens), LANES)


def mixed_shape(heads):
    return (4, (heads // 2 - 1) * QB, LANES)


def first_rows(x_ref, small_ref, weight_ref, first_ref, qkv_ref, step):
    width = weight_ref.shape[2]
    rows = slice(step * 256, step * 256 + 256)
    normed, _ = normalise(x_ref[rows, :].astype(F32))
    first = (normed * small_ref[0:1] + small_ref[2:3]).astype(BF16)
    first_ref[:, rows] = jnp.transpose(first)
    bias = small_ref[6:7]
    qkv_ref[rows, :width] = (dot(first, weight_ref[0]) + bias[:, :width]) * 0.125
    qkv_ref[rows, width : 2 * width] = dot(first, weight_ref[1])
    qkv_ref[rows, 2 * width :] = dot(first, weight_ref[2]) + bias[:, width : 2 * width]


def spread_small(at, gains, shifts, bias, wide, flat, out):
    width = wide.shape[1]
    columns, bias_columns = gains.shape[1], bias.shape[1]
    wide[...] = jnp.zeros_like(wide)
    flat[...] = jnp.zeros_like(flat)
    wide[0:2, :columns] = gains[...].astype(F32)
    wide[2:6, :columns] = shifts[...].astype(F32)
    flat[0:1, :bias_columns] = bias[...].astype(F32)
    out[0:8] = pltpu.roll(wide[...], at.group * columns, 1)
    line = pltpu.roll(flat[...], at.group * bias_columns, 1)
    out[8:16] = jnp.zeros((8, width), F32)
    for row in range(3):
        out[6 + row : 7 + row] = line[0:1, row * width : (row + 1) * width]


FRONT_IN, FRONT_OUT, FRONT_SCRATCH = 9, 10, 20


def front_kernel(*refs):
    at = partners()
    ins = [refs[:FRONT_IN], refs[FRONT_IN : 2 * FRONT_IN]]
    refs = refs[2 * FRONT_IN :]
    outs = [refs[:FRONT_OUT], refs[FRONT_OUT : 2 * FRONT_OUT]]
    refs = refs[2 * FRONT_OUT :]
    scratch = [refs[:FRONT_SCRATCH], refs[FRONT_SCRATCH : 2 * FRONT_SCRATCH]]
    copies = Copies(*refs[2 * FRONT_SCRATCH :])
    others = [at.to_x, at.to_y, at.to_far] + at.to_ctx[1:]
    greet(others)
    streams = []
    for in_refs, out_refs, own in zip(ins, outs, scratch):
        s = Bag()
        s.x_in, s.seg_row, s.gains, s.shifts, s.bias, s.qkv, s.up_in, s.down_in, s.proj_in = in_refs
        (
            s.weight_out, s.small, s.first_out, s.messages, s.proj_full, s.up_full, s.down_full,
            s.o_out, s.lse, s.o_got,
        ) = out_refs
        (
            s.small_in, s.small_own, s.wide, s.flat, s.rows, s.mine, s.got, s.down_t, s.proj_t,
            s.query_doc, s.key_doc, s.score_keys, s.value_keys, s.x, s.up, s.down, s.proj, s.weight, s.first,
        ) = own[:19]
        s.o = own[19]
        s.heads = s.weight.shape[2] // HD
        s.features = (s.query_doc, s.key_doc)
        s.reads = [
            copies.local(src, dst)
            for src, dst in (
                (s.x_in, s.x), (s.proj_in, s.proj), (s.up_in, s.up), (s.down_in, s.down),
            )
        ]
        streams.append(s)
    text, image = streams
    for s in (image, text):
        spread_small(at, s.gains, s.shifts, s.bias, s.wide, s.flat, s.small_own)
        document_features(s.seg_row, *s.features)
    meet(others)
    text.gather = Gather(copies, at, text.qkv, text.weight)
    for s in (text, image):
        s.small_done = [
            copies.remote(s.small_own, s.small_in.at[i], device)
            for i, device in enumerate((at.to_x, at.to_y, at.to_far))
        ]
        for copy in s.reads:
            copy.wait()
    text.down_t[...] = jnp.transpose(text.down[...])
    text.proj_t[...] = jnp.transpose(text.proj[...])
    text.gather.forward()
    image.gather = Gather(copies, at, image.qkv, image.weight)

    def project(s):
        for copy in s.small_done:
            copy.wait_recv()
        s.small[...] = s.small_own[...] + s.small_in[0] + s.small_in[1] + s.small_in[2]
        s.gather.arrived()
        for step in range(s.x.shape[0] // 256):
            first_rows(s.x, s.small, s.weight, s.first, s.rows, step)
        write_messages(s.rows, s.mine, s.heads)
        s.writes = [copies.local(s.weight, s.weight_out), copies.local(s.first, s.first_out)]

    def gather_rest(s):
        pieces = (s.proj_t, s.up, s.down_t) if s.heads == 4 else (s.proj, s.up, s.down)
        s.rest = [
            Gather(copies, at, piece, full)
            for piece, full in zip(pieces, (s.proj_full, s.up_full, s.down_full))
        ]

    project(text)
    text.sends = send_blocks(copies, at, text.mine, text.got)
    image.gather.forward()
    gather_rest(text)
    project(image)
    image.sends = send_blocks(copies, at, image.mine, image.got)
    gather_rest(image)
    s = text
    for copy in s.sends:
        copy.wait()
    s.writes.append(copies.local(s.got, s.messages))
    s.o[...] = jnp.zeros_like(s.o)
    mark_keys(s.got, s.features[1], 1, s.score_keys, s.value_keys)
    attend(
        at, s.got, s.features[0], s.score_keys, s.value_keys, s.o, s.lse, text_task, 0, 8, 4, True
    )
    for gather in s.rest:
        gather.forward()
    s = image
    for copy in s.sends:
        copy.wait()
    text.o_done = send_blocks(copies, at, text.o, text.o_got)
    s.writes.append(copies.local(s.got, s.messages))
    s.o[...] = jnp.zeros_like(s.o)
    mark_keys(s.got, s.features[1], 2, s.score_keys, s.value_keys)
    s.o_done = send_blocks(copies, at, s.o, s.o_got, start=False)

    def image_pair(index, carry):
        attend(
            at, image.got, image.features[0], image.score_keys, image.value_keys, image.o, image.lse,
            image_task, 2 * index, 2 * index + 2, 4, False,
        )
        for step, copy in enumerate(image.o_done):

            @pl.when(index == 5 - step)
            def _(copy=copy):
                copy.start()

        return carry

    lax.fori_loop(0, 6, image_pair, 0)
    s.rest[0].forward()
    for s in (text, image):
        s.writes.append(copies.local(s.o, s.o_out))
    whole = [image.gather, text.gather, image.rest[0]] + text.rest
    for gather in whole[2:]:
        gather.arrived()
    for gather in whole:
        gather.sent()
    for gather in image.rest[1:]:
        gather.near()
    for s in (image, text):
        for copy in s.small_done:
            copy.wait_send()
        for copy in s.writes + s.o_done:
            copy.wait()


def front(streams):
    vmem, hbm = pl.BlockSpec(memory_space=pltpu.VMEM), pl.BlockSpec(memory_space=pl.ANY)
    out_shape, out_specs, scratch = [], [], []
    for x, seg, gains, shifts, bias, qkv, up, down, proj in streams:
        tokens, width = x.shape
        own = qkv.shape[2]
        messages = message_shape(own // HD, tokens)
        hidden = up.shape[1]
        small = jax.ShapeDtypeStruct((16, width), F32)
        out_shape += [
            jax.ShapeDtypeStruct((3, width, own), BF16),
            small,
            jax.ShapeDtypeStruct((width, tokens), BF16),
            jax.ShapeDtypeStruct(messages, BF16),
            jax.ShapeDtypeStruct((width, own), BF16),
            jax.ShapeDtypeStruct((width, hidden), BF16),
            jax.ShapeDtypeStruct((width, hidden), BF16),
            jax.ShapeDtypeStruct(mixed_shape(own // HD), BF16),
            jax.ShapeDtypeStruct((2 * (own // HD), 8, QB), F32),
            jax.ShapeDtypeStruct(mixed_shape(own // HD), BF16),
        ]
        out_specs += [hbm, vmem, hbm, hbm, hbm, hbm, hbm, hbm, vmem, hbm]
        scratch += [
            pltpu.VMEM((3, 16, width), F32),
            pltpu.VMEM((16, width), F32),
            pltpu.VMEM((8, width), F32),
            pltpu.VMEM((8, 3 * width), F32),
            pltpu.VMEM((tokens, 3 * own), F32),
            pltpu.VMEM(messages, BF16),
            pltpu.VMEM(messages, BF16),
            pltpu.VMEM((width // 4, hidden), BF16),
            pltpu.VMEM((width // 4, own), BF16),
            pltpu.VMEM((4 * tokens, LANES), BF16),
            pltpu.VMEM((4 * tokens, LANES), BF16),
            pltpu.VMEM((1 if own == 4 * HD else 2, 4 * tokens, LANES), BF16),
            pltpu.VMEM((1 if own == 4 * HD else 2, 4 * tokens, LANES), BF16),
            pltpu.VMEM(x.shape, BF16),
            pltpu.VMEM(up.shape, BF16),
            pltpu.VMEM(down.shape, BF16),
            pltpu.VMEM(proj.shape, BF16),
            pltpu.VMEM((3, width, own), BF16),
            pltpu.VMEM((width, tokens), BF16),
            pltpu.VMEM(mixed_shape(own // HD), BF16),
        ]
    results = pl.pallas_call(
        front_kernel,
        out_shape=out_shape,
        in_specs=[hbm, vmem, vmem, vmem, vmem, vmem, hbm, hbm, hbm] * 2,
        out_specs=out_specs,
        scratch_shapes=scratch + copy_sems(2 * (3 + 4 * 4 + 6), 2 * 14),
        compiler_params=pltpu.CompilerParams(
            collective_id=0, has_side_effects=True, vmem_limit_bytes=63 << 20
        ),
        name="front",
    )(*streams[0], *streams[1])
    return results[:FRONT_OUT], results[FRONT_OUT:]


STEP = 384
TILES = 1


def by_columns(columns, body):
    def one(index, carry):
        body(pl.ds(pl.multiple_of(index * STEP, STEP), STEP))
        return carry

    lax.fori_loop(0, columns // STEP, one, 0)


class PlaneSum:
    def __init__(self, copies, at, src, arrivals, loads=None):
        self.copies, self.at = copies, at
        self.in_x, self.in_y, self.in_top, self.in_low = arrivals
        half, self.columns = self.in_top.shape
        self.half, rows = half, 2 * half

        def block(owner, offset, size=half):
            return src.at[pl.ds(pl.multiple_of(owner * rows + offset, 8), size), :]

        self.first = [
            copies.remote(block(at.group_far, 0), self.in_x.at[1], at.to_x),
            copies.remote(block(at.group_far, half), self.in_y.at[1], at.to_y),
            copies.remote(block(at.group_x, 0), self.in_x.at[0], at.to_x),
            copies.remote(block(at.group_y, half), self.in_y.at[0], at.to_y),
        ]
        parts = [block(at.group_y, 0), block(at.group_x, half), block(at.group, 0, rows)]
        if loads is None:
            self.loads = []
            self.pass_top, self.pass_low, self.own = parts
        else:
            self.loads = [copies.local(part, load) for part, load in zip(parts, loads)]
            self.pass_top, self.pass_low, self.own = loads
        self.second = [
            copies.remote(self.pass_top, self.in_top, at.to_y, False),
            copies.remote(self.pass_low, self.in_low, at.to_x, False),
        ]

    def cross(self):
        for copy in self.loads:
            copy.wait()
        self.first[0].wait_recv()

        def top(cols):
            self.pass_top[:, cols] = (
                self.pass_top[:, cols].astype(F32) + self.in_x[1, :, cols].astype(F32)
            ).astype(BF16)

        by_columns(self.columns, top)
        self.second[0].start()
        self.first[1].wait_recv()

        def low(cols):
            self.pass_low[:, cols] = (
                self.pass_low[:, cols].astype(F32) + self.in_y[1, :, cols].astype(F32)
            ).astype(BF16)

        by_columns(self.columns, low)
        self.second[1].start()

    def arrived(self):
        for copy in self.first[2:] + self.second:
            copy.wait_recv()

    def halves(self, cols):
        half = self.half
        return (
            self.own[:half, cols].astype(F32)
            + self.in_x[0, :, cols].astype(F32)
            + self.in_top[:, cols].astype(F32),
            self.own[half:, cols].astype(F32)
            + self.in_y[0, :, cols].astype(F32)
            + self.in_low[:, cols].astype(F32),
        )

    def sent(self):
        for copy in self.first + self.second:
            copy.wait_send()

    @staticmethod
    def arrivals(rows, columns):
        half = rows // 2
        pair, one = pltpu.VMEM((2, half, columns), BF16), pltpu.VMEM((half, columns), BF16)
        return [pair, pair, one, one]

    @staticmethod
    def loads_scratch(rows, columns):
        half = rows // 2
        one = pltpu.VMEM((half, columns), BF16)
        return [one, one, pltpu.VMEM((rows, columns), BF16)]


class LineSum:
    def __init__(self, copies, at, values, buffers, final, begin, end):
        self.at, self.values, self.final, self.range = at, values, final, (begin, end)
        self.pair, self.outer_in, self.inner_in = buffers

        def part(ref):
            return ref.at[:, begin:end]

        self.up = copies.remote(part(self.pair), part(self.outer_in), at.to_ctx[1], False)
        self.across = copies.remote(part(self.pair), part(self.inner_in), at.to_ctx[3], False)
        self.down = copies.remote(part(final), part(final), at.to_ctx[1], False)

    def each(self, body):
        begin, end = self.range

        def one(index, carry):
            body(pl.ds(pl.multiple_of(begin + index * STEP, LANES), STEP))
            return carry

        lax.fori_loop(0, (end - begin) // STEP, one, 0)

    def gather(self):
        half = self.pair.shape[0] // 2

        @pl.when(self.at.outer)
        def _():
            def add(cols):
                top, low = self.values(cols)
                self.pair[:half, cols] = top.astype(BF16)
                self.pair[half:, cols] = low.astype(BF16)

            self.each(add)
            self.up.start()

    def join(self):
        half = self.pair.shape[0] // 2

        @pl.when(self.at.inner)
        def _():
            self.up.wait_recv()

            def add(cols):
                top, low = self.values(cols)
                self.pair[:half, cols] = (top + self.outer_in[:half, cols].astype(F32)).astype(BF16)
                self.pair[half:, cols] = (low + self.outer_in[half:, cols].astype(F32)).astype(BF16)

            self.each(add)
            self.across.start()

    def share(self):
        @pl.when(self.at.inner)
        def _():
            self.across.wait_recv()

            def add(cols):
                self.final[:, cols] = (
                    self.pair[:, cols].astype(F32) + self.inner_in[:, cols].astype(F32)
                ).astype(BF16)

            self.each(add)
            self.down.start()

    def finish(self):
        @pl.when(self.at.outer)
        def _():
            self.up.wait_send()
            self.down.wait_recv()

        @pl.when(self.at.inner)
        def _():
            self.across.wait_send()
            self.down.wait_send()

    @staticmethod
    def scratch(rows, columns):
        return [pltpu.VMEM((rows, columns), BF16)] * 3


def chunks(tokens, size=256):
    return [slice(start, start + size) for start in range(0, tokens, size)]


def as_f32(ref, index, rows=slice(None)):
    return ref[index, rows].astype(F32)


def take_halves(got, out, at, heads, start, put):
    half = out.shape[0] // 2
    for tile in range(heads // 2):
        base = 0 if tile < 2 else start
        if tile < 2:
            one, two = 2 * tile, 2 * tile + 1
        else:
            one, two = at.here_high * 2, at.here_high * 2 + 1
        rows = slice(base, base + QB)
        left, right = as_f32(got, one, rows), as_f32(got, two, rows)
        for side in range(2):
            put(tile, slice(side * half, side * half + half), lane_pair((left, side), (right, side)))


def take_mixed(got, mixed, at, heads):
    def put(tile, rows, value):
        mixed[rows, tile * LANES : (tile + 1) * LANES] = value.astype(BF16)

    take_halves(got, mixed, at, heads, QB, put)


def write_grad_o(grad, out, heads):
    for c in range(4):
        out[c, :QB] = halves_pair(grad, 0, c)
        if heads == 6:
            out[c, QB:] = halves_pair(grad, 0, 4 + c % 2)


def send_blocks(copies, at, mine, out, begin=0, end=None, start=True):
    rows = mine.shape[1]
    end = rows if end is None else end
    far = min(end, rows if rows in (QB, QB + KB) else rows - QB)
    part = pl.ds(begin, end - begin)
    done = [copies.local(mine.at[at.here, part], out.at[at.here, part], start)]
    for other, device, last in zip(at.ctx[1:], at.to_ctx[1:], (end, far, far)):
        part = pl.ds(begin, last - begin)
        done.append(copies.remote(mine.at[other, part], out.at[at.here, part], device, start))
    return done


MIDDLE_IN, MIDDLE_OUT, MIDDLE_SCRATCH = 7, 5, 22


def middle_kernel(*refs):
    at = partners()
    ins = [refs[:MIDDLE_IN], refs[MIDDLE_IN : 2 * MIDDLE_IN]]
    refs = refs[2 * MIDDLE_IN :]
    outs = [refs[:MIDDLE_OUT], refs[MIDDLE_OUT : 2 * MIDDLE_OUT]]
    refs = refs[2 * MIDDLE_OUT :]
    scratch = [refs[:MIDDLE_SCRATCH], refs[MIDDLE_SCRATCH : 2 * MIDDLE_SCRATCH]]
    arrivals = refs[2 * MIDDLE_SCRATCH : 2 * MIDDLE_SCRATCH + 4]
    copies = Copies(*refs[2 * MIDDLE_SCRATCH + 4 :])
    others = [at.to_x, at.to_y] + at.to_ctx[1:] + [at.to_core]
    greet(others)
    streams = []
    for in_refs, out_refs, own in zip(ins, outs, scratch):
        s = Bag()
        o_in, x_in, dy_in, s.small, proj_in, up_in, down_in = in_refs
        s.y_out, s.dmid_out, s.do_out, s.rest_out, s.sums = out_refs
        (
            s.proj, s.up, s.down, s.rest, s.mixed, s.part, s.part_in, s.mid, s.first, s.first_t, s.dy_t,
            s.act, s.dz, s.grad, s.grad_in, s.do, s.do_mine, s.o, s.x, s.dy, s.y, s.dmid,
        ) = own
        s.heads = proj_in.shape[1] // HD
        s.o_done = copies.local(o_in, s.o)
        s.proj_done = copies.local(proj_in, s.proj)
        s.rows_done = [copies.local(x_in, s.x), copies.local(dy_in, s.dy)]
        s.weights = ((up_in, s.up), (down_in, s.down))
        streams.append(s)
    text, image = streams
    text.rest_done = [copies.local(src, dst) for src, dst in text.weights]
    quarter = image.up.shape[0] // 4
    near = [
        pl.ds(pl.multiple_of(owner * quarter, 8), quarter)
        for owner in (at.group, at.group_x, at.group_y)
    ]
    image.rest_done = [
        copies.local(src.at[rows, :], dst.at[rows, :])
        for src, dst in image.weights
        for rows in near
    ]
    meet(others)
    top = pl.ds(pl.multiple_of(at.group_y * quarter, 8), quarter // 2)
    low = pl.ds(pl.multiple_of(at.group_x * quarter + quarter // 2, 8), quarter // 2)
    image.far_done = []
    for src, dst in image.weights:
        image.far_done.append(copies.remote(src.at[top, :], dst.at[top, :], at.to_x))
        image.far_done.append(copies.remote(src.at[low, :], dst.at[low, :], at.to_y))
    text.far_done = []

    def project(s):
        s.o_done.wait()
        take_mixed(s.o, s.mixed, at, s.heads)
        s.proj_done.wait()
        for cols in chunks(s.x.shape[1]):
            s.part[:, cols] = dot(s.mixed[...], s.proj[cols, :], ((1,), (1,)))
        s.part_done = copies.remote(s.part, s.part_in, at.to_core)
        s.sums[...] = jnp.zeros_like(s.sums)
        for copy in s.rows_done:
            copy.wait()
        for rows in chunks(s.dy.shape[0]):
            s.dy_t[:, rows] = jnp.transpose(s.dy[rows, :])

    def second_norm(s):
        s.part_done.wait()
        for rows in chunks(s.x.shape[0]):
            middle = (
                s.x[rows, :].astype(F32) + s.part[rows, :] + s.part_in[rows, :] + s.small[3:4]
            )
            s.mid[rows, :] = middle
            normed, _ = normalise(middle)
            low = (normed * s.small[1:2] + s.small[4:5]).astype(BF16)
            s.first[rows, :] = low
            s.first_t[:, rows] = jnp.transpose(low)

    def feed_forward(s):
        tokens, width = s.x.shape
        hidden, own = s.up.shape[1], s.proj.shape[1]
        size = width // TILES
        for copy in s.rest_done:
            copy.wait()
        for copy in s.far_done:
            copy.wait_recv()

        def tile(index, carry):
            cols = pl.ds(pl.multiple_of(index * size, LANES), size)
            up, down = s.up[:, cols], s.down[:, cols]
            up_cols = pl.ds(pl.multiple_of(own + index * size, LANES), size)
            down_cols = pl.ds(pl.multiple_of(own + hidden + index * size, LANES), size)
            row = pl.ds(7 + index // (width // size), 1)
            place = pl.ds(pl.multiple_of((index % (width // size)) * size, LANES), size)
            bias = s.small[row, place]
            total = jnp.zeros((1, size), F32)
            for rows in chunks(tokens):
                z = dot(s.first[rows, :], up) + bias
                sg = jax.nn.sigmoid(1.702 * z)
                zs = z * sg
                s.act[rows, cols] = zs.astype(BF16)
                grad = dot(s.dy[rows, :], down)
                low = (grad * (sg + 1.702 * zs * (1.0 - sg))).astype(BF16)
                s.dz[rows, cols] = low
                total = total + jnp.sum(low.astype(F32), axis=0, keepdims=True)
            s.sums[row, place] = total
            s.rest[:, up_cols] = dot(s.first_t[...], s.dz[:, cols]).astype(BF16)
            s.rest[:, down_cols] = dot(s.dy_t[...], s.act[:, cols]).astype(BF16)
            return carry

        lax.fori_loop(0, hidden // size, tile, 0)
        for cols in chunks(width):
            s.grad[0, :, cols] = dot(s.dz[...], s.up[cols, :], ((1,), (1,)))
        s.grad_done = copies.remote(s.grad.at[0], s.grad_in.at[0], at.to_core)
        for cols in chunks(width):
            s.grad[1, :, cols] = dot(s.act[...], s.down[cols, :], ((1,), (1,)))
        s.y_done = copies.remote(s.grad.at[1], s.grad_in.at[1], at.to_core)

    def back(s):
        sums = s.sums
        s.grad_done.wait()
        for rows in chunks(s.x.shape[0]):
            normed, inv = normalise(s.mid[rows, :])
            second = s.grad[0, rows, :] + s.grad_in[0, rows, :]
            scaled = second * s.small[1:2]
            dy = s.dy[rows, :].astype(F32)
            dmid = dy + inv * (
                scaled
                - jnp.mean(scaled, axis=-1, keepdims=True)
                - normed * jnp.mean(scaled * normed, axis=-1, keepdims=True)
            )
            s.dmid[rows, :] = dmid
            sums[1:2] += jnp.sum(second * normed, axis=0, keepdims=True)
            sums[3:4] += jnp.sum(dmid, axis=0, keepdims=True)
            sums[4:5] += jnp.sum(second, axis=0, keepdims=True)
            sums[5:6] += jnp.sum(dy, axis=0, keepdims=True)
            low = dmid.astype(BF16)
            s.first_t[:, rows] = jnp.transpose(low)
            s.do[rows, :] = dot(low, s.proj[...])
        s.writes = [copies.local(s.dmid, s.dmid_out)]
        write_grad_o(s.do, s.do_mine, s.heads)
        s.do_done = send_blocks(copies, at, s.do_mine, s.do_out)

    def proj_grad(s):
        s.rest[:, : s.proj.shape[1]] = dot(s.first_t[...], s.mixed[...]).astype(BF16)

    def output(s):
        s.y_done.wait()
        for rows in chunks(s.x.shape[0]):
            s.y[rows, :] = (
                s.mid[rows, :] + s.grad[1, rows, :] + s.grad_in[1, rows, :] + s.small[5:6]
            ).astype(BF16)
        s.writes.append(copies.local(s.y, s.y_out))

    project(text)
    project(image)
    second_norm(text)
    feed_forward(text)
    second_norm(image)
    back(text)
    proj_grad(text)
    plane = PlaneSum(copies, at, text.rest, arrivals)
    feed_forward(image)
    back(image)
    plane.cross()
    proj_grad(image)
    keep = copies.local(image.rest, image.rest_out)
    output(text)
    output(image)
    plane.arrived()
    half = plane.half

    def put(cols):
        text.rest_out[:half, cols], text.rest_out[half:, cols] = plane.halves(cols)

    by_columns(plane.columns, put)
    plane.sent()
    keep.wait()
    for s in streams:
        for copy in s.do_done + s.writes:
            copy.wait()
        for copy in s.far_done:
            copy.wait_send()


def middle(streams):
    vmem, hbm = pl.BlockSpec(memory_space=pltpu.VMEM), pl.BlockSpec(memory_space=pl.ANY)
    out_shape, out_specs, scratch = [], [], []
    arrivals = None
    for o, x, dy, small, proj, up, down in streams:
        tokens, width = x.shape
        hidden, own = up.shape[1], proj.shape[1]
        rest = (width, own + 2 * hidden)
        summed = arrivals is None
        if summed:
            arrivals = PlaneSum.arrivals(width // 4, rest[1])
        out_shape += [
            jax.ShapeDtypeStruct((tokens, width), BF16),
            jax.ShapeDtypeStruct((tokens, width), F32),
            jax.ShapeDtypeStruct(o.shape, BF16),
            jax.ShapeDtypeStruct((width // 4, rest[1]), F32)
            if summed
            else jax.ShapeDtypeStruct(rest, BF16),
            jax.ShapeDtypeStruct(small.shape, F32),
        ]
        out_specs += [hbm, hbm, hbm, vmem if summed else hbm, vmem]
        scratch += [
            pltpu.VMEM(proj.shape, BF16),
            pltpu.VMEM(up.shape, BF16),
            pltpu.VMEM(down.shape, BF16),
            pltpu.VMEM(rest, BF16),
            pltpu.VMEM((tokens, own), BF16),
            pltpu.VMEM((tokens, width), F32),
            pltpu.VMEM((tokens, width), F32),
            pltpu.VMEM((tokens, width), F32),
            pltpu.VMEM((tokens, width), BF16),
            pltpu.VMEM((width, tokens), BF16),
            pltpu.VMEM((width, tokens), BF16),
            pltpu.VMEM((tokens, hidden), BF16),
            pltpu.VMEM((tokens, hidden), BF16),
            pltpu.VMEM((2, tokens, width), F32),
            pltpu.VMEM((2, tokens, width), F32),
            pltpu.VMEM((tokens, own), F32),
            pltpu.VMEM(o.shape, BF16),
            pltpu.VMEM(o.shape, BF16),
            pltpu.VMEM((tokens, width), BF16),
            pltpu.VMEM((tokens, width), BF16),
            pltpu.VMEM((tokens, width), BF16),
            pltpu.VMEM((tokens, width), F32),
        ]
    results = pl.pallas_call(
        middle_kernel,
        out_shape=out_shape,
        in_specs=([hbm] * 3 + [vmem] + [hbm] * 3) * 2,
        out_specs=out_specs,
        scratch_shapes=scratch + arrivals + copy_sems(2 * 6 + 4 + 6, 2 * (4 + 3) + 8 + 1),
        compiler_params=pltpu.CompilerParams(
            collective_id=1, has_side_effects=True, vmem_limit_bytes=64 * 1024 * 1000
        ),
        name="middle",
    )(*streams[0], *streams[1])
    return results[:MIDDLE_OUT], results[MIDDLE_OUT:]


def take_dqkv(got, out, at, heads):
    width = heads * HD

    def put(which, tile, rows, value):
        start = which * width + tile * LANES
        out[rows, start : start + LANES] = value.astype(BF16)

    take_halves(got, out, at, heads, QB + 2 * KB, functools.partial(put, 0))

    def keys(position, head):
        return as_f32(got, position, key_rows(head))

    pairs = [(keys(0, 0), keys(1, 0)), (keys(2, 0), keys(3, 0))]
    if heads == 6:
        pairs.append((keys(0, 1) + keys(2, 1), keys(1, 1) + keys(3, 1)))
    for tile, (one, two) in enumerate(pairs):
        put(1, tile, slice(None), lane_pair((one, 0), (two, 0)))
        put(2, tile, slice(None), lane_pair((one, 1), (two, 1)))


LAST_IN, LAST_OUT, LAST_SCRATCH = 12, 4, 22


def last_kernel(*refs):
    at = partners()
    ins = [refs[:LAST_IN], refs[LAST_IN : 2 * LAST_IN]]
    refs = refs[2 * LAST_IN :]
    outs = [refs[:LAST_OUT], refs[LAST_OUT : 2 * LAST_OUT]]
    refs = refs[2 * LAST_OUT :]
    count = LAST_SCRATCH + 10
    scratch = [refs[:count], refs[count : 2 * count]]
    refs = refs[2 * count :]
    rest_arrivals, rest_loads = refs[:4], refs[4:7]
    copies = Copies(*refs[7:])
    others = [at.to_x, at.to_y] + at.to_ctx[1:] + [at.to_core]
    greet(others)
    streams = []
    for in_refs, out_refs, own in zip(ins, outs, scratch):
        s = Bag()
        (
            s.m_in, s.do_in, s.o_in, s.lse, s.seg_row, s.first_in, s.x_in, s.small, s.weight_in, s.dmid_in,
            s.rest, s.sums_in,
        ) = in_refs
        s.grad_rows_out, s.sums, s.rest_final, s.qkv_final = out_refs
        (
            s.m, s.do, s.o, s.query_doc, s.key_doc, s.score_keys, s.grad_rows, s.acc, s.back, s.got, s.dqkv, s.weight, s.first, s.x, s.dmid,
            s.part, s.part_in, s.g_qkv, s.sums_own, s.sums_out, s.sums_got, s.sums_line,
        ) = own[:LAST_SCRATCH]
        s.rest_line, s.qkv_line = own[LAST_SCRATCH : LAST_SCRATCH + 3], own[LAST_SCRATCH + 3 : LAST_SCRATCH + 6]
        s.qkv_arrivals = own[LAST_SCRATCH + 6 :]
        s.heads = s.weight.shape[2] // HD
        s.features = (s.query_doc, s.key_doc)
        s.reads = [
            copies.local(src, dst) for src, dst in ((s.m_in, s.m), (s.do_in, s.do), (s.o_in, s.o))
        ]
        streams.append(s)
    text, image = streams
    for s in streams:
        document_features(s.seg_row, *s.features)
        s.acc[...] = jnp.zeros_like(s.acc)
        s.back[...] = jnp.zeros_like(s.back)
    meet(others)
    plane = PlaneSum(copies, at, image.rest, rest_arrivals, rest_loads)
    text_half = text.rest.shape[0] // 2

    def text_values(cols):
        return text.rest[:text_half, cols], text.rest[text_half:, cols]

    text_line = LineSum(
        copies, at, text_values, text.rest_line, text.rest_final, 0, text.rest.shape[1]
    )
    text_line.gather()
    for s in (image, text):
        for copy in s.reads:
            copy.wait()
        s.loads = [
            copies.local(src, dst)
            for src, dst in (
                (s.first_in, s.first), (s.weight_in, s.weight), (s.x_in, s.x), (s.dmid_in, s.dmid),
            )
        ]
        mark_keys(s.m, s.features[1], s.acc.shape[0], s.score_keys, None)

    def unattend_tasks(s, *task):
        unattend(
            at, s.m, s.do, s.o, s.lse, s.features[0], s.score_keys, s.acc, s.back, *task
        )

    text.sends = send_blocks(copies, at, text.back, text.got, start=False)
    split = QB + KB
    shared_sends = send_blocks(copies, at, image.back, image.got, split, None, False)
    own_sends = send_blocks(copies, at, image.back, image.got, 0, split, False)
    image.sends = shared_sends + own_sends

    def image_phase(phase, carry):
        unattend_tasks(image, image_task, phase * 4, phase * 4 + 4, 4, False)

        @pl.when(phase == 0)
        def _():
            key_gradients(image.acc, image.back, 1)
            for copy in shared_sends:
                copy.start()
            unattend_tasks(text, text_task, 0, 8, 4, True)
            key_gradients(text.acc, text.back, 0)
            for copy in text.sends:
                copy.start()

        @pl.when(phase == 1)
        def _():
            plane.cross()

        return carry

    lax.fori_loop(0, 3, image_phase, 0)
    key_gradients(image.acc, image.back, 0)
    for copy in own_sends:
        copy.start()

    def project(s):
        width = s.x.shape[1]
        own = s.heads * HD
        for copy in s.sends:
            copy.wait()
        for copy in s.loads:
            copy.wait()
        take_dqkv(s.got, s.dqkv, at, s.heads)
        for which in range(3):
            cols = slice(which * own, (which + 1) * own)
            s.g_qkv[:, cols] = dot(s.first[...], s.dqkv[:, cols]).astype(BF16)
        s.qkv_plane = PlaneSum(copies, at, s.g_qkv, s.qkv_arrivals)
        for cols in chunks(width):
            total = dot(s.dqkv[:, :own], s.weight[0, cols, :], ((1,), (1,)))
            total = total + dot(s.dqkv[:, own : 2 * own], s.weight[1, cols, :], ((1,), (1,)))
            s.part[:, cols] = total + dot(s.dqkv[:, 2 * own :], s.weight[2, cols, :], ((1,), (1,)))
        s.part_done = copies.remote(s.part, s.part_in, at.to_core)
        s.sums_own[...] = s.sums_in[...]
        s.sums_own[6:7, :own] = jnp.sum(s.dqkv[:, :own].astype(F32), axis=0, keepdims=True)
        s.sums_own[6:7, own:] = jnp.sum(s.dqkv[:, 2 * own :].astype(F32), axis=0, keepdims=True)
        cuts = (0, 3 * own) if own < STEP else (0, 2 * own, 3 * own)
        s.qkv_sums = [
            LineSum(copies, at, s.qkv_plane.halves, s.qkv_line, s.qkv_final, begin, end)
            for begin, end in zip(cuts, cuts[1:])
        ]

    def input_grad(s):
        s.part_done.wait()
        for rows in chunks(s.x.shape[0]):
            normed, inv = normalise(s.x[rows, :].astype(F32))
            first = s.part[rows, :] + s.part_in[rows, :]
            scaled = first * s.small[0:1]
            s.grad_rows[rows, :] = s.dmid[rows, :] + inv * (
                scaled
                - jnp.mean(scaled, axis=-1, keepdims=True)
                - normed * jnp.mean(scaled * normed, axis=-1, keepdims=True)
            )
            s.sums_own[0:1] += jnp.sum(first * normed, axis=0, keepdims=True)
            s.sums_own[2:3] += jnp.sum(first, axis=0, keepdims=True)
        s.write = copies.local(s.grad_rows, s.grad_rows_out)
        s.sums_done = [copies.remote(s.sums_own, s.sums_got.at[0], at.to_x)]

    def add_sums(s, step):
        s.sums_done[-1].wait_recv()
        before = s.sums_own if step == 0 else s.sums_out
        total = before[...] + s.sums_got[step]
        if step == 0:
            s.sums_out[...] = total
            s.sums_done.append(copies.remote(s.sums_out, s.sums_got.at[1], at.to_y))
        else:
            s.sums_line[at.here] = total
            mine = s.sums_line.at[at.here]
            s.sums_done += [copies.remote(mine, mine, device) for device in at.to_ctx[1:]]

    def end_sums(s):
        for copy in s.sums_done[2:]:
            copy.wait_recv()
        s.sums[...] = s.sums_line[0] + s.sums_line[1] + s.sums_line[2] + s.sums_line[3]

    cuts = [0, STEP, 4 * STEP, 7 * STEP, plane.columns]
    rest_lines = [
        LineSum(copies, at, plane.halves, image.rest_line, image.rest_final, begin, end)
        for begin, end in zip(cuts, cuts[1:])
    ]

    def by_core(one, two):
        @pl.when(at.core == 0)
        def _():
            one()
            two()

        @pl.when(at.core == 1)
        def _():
            two()
            one()

    project(text)
    plane.arrived()
    text.qkv_plane.cross()
    input_grad(text)
    for line in rest_lines:
        line.gather()
    text.qkv_plane.arrived()
    text.qkv_sums[0].gather()
    add_sums(text, 0)
    project(image)
    by_core(rest_lines[0].join, text_line.join)
    input_grad(image)
    rest_lines[1].join()
    image.qkv_plane.cross()
    add_sums(text, 1)
    add_sums(image, 0)
    by_core(rest_lines[0].share, text_line.share)
    rest_lines[2].join()
    image.qkv_plane.arrived()
    for line in image.qkv_sums:
        line.gather()
    add_sums(image, 1)
    rest_lines[1].share()
    rest_lines[3].join()
    image.qkv_sums[0].join()
    rest_lines[2].share()
    image.qkv_sums[1].join()
    text.qkv_sums[0].join()
    rest_lines[3].share()
    for line in image.qkv_sums + text.qkv_sums:
        line.share()
    for s in streams:
        end_sums(s)
    for line in [text_line] + rest_lines + image.qkv_sums + text.qkv_sums:
        line.finish()
    plane.sent()
    for s in streams:
        s.qkv_plane.sent()
        for copy in s.sums_done:
            copy.wait_send()
        s.write.wait()


def last(streams):
    vmem, hbm = pl.BlockSpec(memory_space=pltpu.VMEM), pl.BlockSpec(memory_space=pl.ANY)
    out_shape, scratch = [], []
    for messages, do, o, lse, seg, first, x, small, weight, dmid, rest, sums in streams:
        tokens, width = x.shape
        own = weight.shape[2]
        rest_shape, qkv_shape = (width // 4, rest.shape[1]), (width // 4, 3 * own)
        out_shape += [
            jax.ShapeDtypeStruct((tokens, width), F32),
            jax.ShapeDtypeStruct(small.shape, F32),
            jax.ShapeDtypeStruct(rest_shape, BF16),
            jax.ShapeDtypeStruct(qkv_shape, BF16),
        ]
        scratch += [
            pltpu.VMEM(messages.shape, BF16),
            pltpu.VMEM(do.shape, BF16),
            pltpu.VMEM(do.shape, BF16),
            pltpu.VMEM((4 * tokens, LANES), BF16),
            pltpu.VMEM((4 * tokens, LANES), BF16),
            pltpu.VMEM((1 if own == 4 * HD else 2, 4 * tokens, LANES), BF16),
            pltpu.VMEM((tokens, width), F32),
            pltpu.VMEM((1 if own == 4 * HD else 2, 4 * tokens, LANES), F32),
            pltpu.VMEM(messages.shape, BF16),
            pltpu.VMEM(messages.shape, BF16),
            pltpu.VMEM((tokens, 3 * own), BF16),
            pltpu.VMEM(weight.shape, BF16),
            pltpu.VMEM(first.shape, BF16),
            pltpu.VMEM((tokens, width), BF16),
            pltpu.VMEM((tokens, width), F32),
            pltpu.VMEM((tokens, width), F32),
            pltpu.VMEM((tokens, width), F32),
            pltpu.VMEM((width, 3 * own), BF16),
            pltpu.VMEM(small.shape, F32),
            pltpu.VMEM(small.shape, F32),
            pltpu.VMEM((2,) + small.shape, F32),
            pltpu.VMEM((4,) + small.shape, F32),
        ]
        scratch += LineSum.scratch(*rest_shape) + LineSum.scratch(*qkv_shape)
        scratch += PlaneSum.arrivals(*qkv_shape)
    scratch += PlaneSum.arrivals(*rest_shape) + PlaneSum.loads_scratch(*rest_shape)
    specs = [hbm, hbm, hbm, vmem, vmem, hbm, hbm, vmem, hbm, hbm, vmem, vmem]
    specs += specs[:10] + [hbm, vmem]
    results = pl.pallas_call(
        last_kernel,
        out_shape=out_shape,
        in_specs=specs,
        out_specs=[hbm, vmem, vmem, vmem] * 2,
        scratch_shapes=scratch + copy_sems(2 * (3 + 1 + 5 + 6) + 3 + 6 + 3 * 8, 2 * (1 + 7 + 1) + 3 + 1),
        compiler_params=pltpu.CompilerParams(
            collective_id=2, has_side_effects=True, vmem_limit_bytes=64 * 1024 * 1000
        ),
        name="last",
    )(*streams[0], *streams[1])
    return results[:4], results[4:]


def take_own(group, row):
    columns = row.shape[1] // 4
    return pltpu.roll(row, (4 - group) % 4 * columns, 1)[:, :columns]


def finish_kernel(*refs):
    ins = [refs[:5], refs[5:10]]
    outs = [refs[10:19], refs[19:28]]
    buffers, reads, writes = [refs[28:30], refs[30:32]], refs[32], refs[33]
    passes = []
    for index, (in_refs, out_refs, own) in enumerate(zip(ins, outs, buffers)):
        for place in range(2):
            step = 2 * index + place
            copy = pltpu.make_async_copy(in_refs[3 + place], own[place], reads.at[step])
            copy.start()
            passes.append(
                (copy, pltpu.make_async_copy(own[place], out_refs[7 + place], writes.at[step]))
            )
    for copy, write in passes:
        copy.wait()
        write.start()
    for (sums, rest, qkv, *_), (gains, shifts, bias, qkv_out, proj, up, down, *_) in zip(ins, outs):
        group = lax.axis_index(FSDP)
        rows = take_own(group, sums[0:8])
        gains[...] = rows[0:2]
        shifts[...] = rows[2:6]
        line = jnp.concatenate([sums[6:7], sums[7:8], sums[8:9]], axis=1)
        bias[...] = take_own(group, jnp.broadcast_to(line, (8, line.shape[1])))[0:1]
        own = qkv.shape[1] // 3
        for which in range(3):
            qkv_out[which] = qkv[:, which * own : (which + 1) * own].astype(F32)
        hidden = up.shape[1]
        up[...] = rest[:, own : own + hidden].astype(F32)
        if down.shape[0] > down.shape[1]:
            proj[...] = jnp.transpose(rest[:, :own].astype(F32))
            down[...] = jnp.transpose(rest[:, own + hidden :].astype(F32))
        else:
            proj[...] = rest[:, :own].astype(F32)
            down[...] = rest[:, own + hidden :].astype(F32)
    for _, write in passes:
        write.wait()


def finish(streams):
    vmem, hbm = pl.BlockSpec(memory_space=pltpu.VMEM), pl.BlockSpec(memory_space=pl.ANY)
    out_shape, scratch = [], []
    for sums, rest, qkv, y, grad, flip in streams:
        rows, own = qkv.shape[0], qkv.shape[1] // 3
        hidden = (rest.shape[1] - own) // 2
        shapes = [(2, rows), (4, rows), (1, 3 * rows), (3, rows, own)]
        shapes += [(own, rows), (rows, hidden), (hidden, rows)] if flip else [
            (rows, own), (rows, hidden), (rows, hidden)
        ]
        out_shape += [jax.ShapeDtypeStruct(shape, F32) for shape in shapes]
        out_shape += [jax.ShapeDtypeStruct(a.shape, a.dtype) for a in (y, grad)]
        scratch += [pltpu.VMEM(a.shape, a.dtype) for a in (y, grad)]
    results = pl.pallas_call(
        finish_kernel,
        out_shape=out_shape,
        in_specs=([vmem] * 3 + [hbm] * 2) * 2,
        out_specs=([vmem] * 7 + [hbm] * 2) * 2,
        scratch_shapes=scratch + [pltpu.SemaphoreType.DMA((4,)), pltpu.SemaphoreType.DMA((4,))],
        name="finish",
    )(*streams[0][:5], *streams[1][:5])
    return results[:9], results[9:]


def on_device(*args):
    streams = []
    for item, causal in ((args[10:], True), (args[:10], False)):
        s = Bag()
        rows, s.seg, cotangent, s.gains, s.shifts, s.head_bias, s.qkv, proj, s.up, down = item
        s.flip, s.x, s.dy = causal, rows[0], cotangent[0]
        s.down, s.proj = (down, proj) if causal else (down.T, proj.T)
        streams.append(s)
    started = front(
        [(s.x, s.seg, s.gains, s.shifts, s.head_bias, s.qkv, s.up, s.down, s.proj) for s in streams]
    )
    for s, (weight, small, first, messages, proj, up, down, o, lse, o_got) in zip(streams, started):
        s.weight, s.small, s.first, s.messages, s.o, s.lse = weight, small, first, messages, o, lse
        s.weights, s.o_got = (proj, up, down), o_got
    done = middle([(s.o_got, s.x, s.dy, s.small, *s.weights) for s in streams])
    ended = last(
        [
            (s.messages, do, s.o, s.lse, s.seg, s.first, s.x, s.small, s.weight, dmid, rest, sums)
            for s, (y, dmid, do, rest, sums) in zip(streams, done)
        ]
    )
    final = finish(
        [
            (sums, rest, qkv, y, grad, s.flip)
            for s, (y, *_), (grad, sums, rest, qkv) in zip(streams, done, ended)
        ]
    )
    outputs = []
    for s, (gains, shifts, bias, qkv, proj, up, down, y, grad_rows) in zip(streams, final):
        if not s.flip:
            proj, down = proj.T, down.T
        outputs.append((y[None], grad_rows[None], gains, shifts, bias, qkv, proj, up, down))
    return outputs[1] + outputs[0]


def layer_stats(rows):
    row_mean = jnp.mean(rows, axis=-1, keepdims=True)
    centred = rows - row_mean
    inv_std = lax.rsqrt(jnp.mean(centred * centred, axis=-1, keepdims=True) + 1e-05)
    return (centred * inv_std, inv_std)


def norm_back(grad_normed_out, normed, inv_std, gain):
    scaled = grad_normed_out * gain
    return inv_std * (
        scaled
        - jnp.mean(scaled, axis=-1, keepdims=True)
        - normed * jnp.mean(scaled * normed, axis=-1, keepdims=True)
    )


def tensor_psum(partial_rows):
    return lax.psum(partial_rows, TP)


def any_mesh_block(
    rows_in,
    seg_row,
    cotangent,
    gains,
    shifts,
    head_bias,
    qkv_weight,
    proj_weight,
    up_weight,
    down_weight,
    causal,
):
    gain_full, shift_full, bias_full, qkv_full, proj_full, up_full, down_full = (
        lax.all_gather(gains, FSDP, axis=1, tiled=True),
        lax.all_gather(shifts, FSDP, axis=1, tiled=True),
        lax.all_gather(head_bias, FSDP, axis=1, tiled=True),
        lax.all_gather(qkv_weight, FSDP, axis=1, tiled=True),
        lax.all_gather(proj_weight, FSDP, axis=1, tiled=True),
        lax.all_gather(up_weight, FSDP, axis=0, tiled=True),
        lax.all_gather(down_weight, FSDP, axis=1, tiled=True),
    )
    gain_vals = gain_full.astype(jnp.float32)
    shift_vals = shift_full.astype(jnp.float32)
    bias_vals = bias_full[0].astype(jnp.float32)
    tp_width = qkv_full.shape[2]
    local_rows = rows_in.shape[1]
    seq_length = seg_row.shape[1]
    head_local = tp_width // HD
    rows = rows_in[0].astype(jnp.float32)
    row_start = lax.axis_index(CTX) * local_rows
    seg_all = seg_row[0]
    seg_query = lax.dynamic_slice_in_dim(seg_all, row_start, local_rows)
    query_pos = row_start + jnp.arange(local_rows, dtype=jnp.int32)
    key_pos = jnp.arange(seq_length, dtype=jnp.int32)
    allowed = seg_query[:, None] == seg_all[None, :]
    if causal:
        allowed = jnp.logical_and(allowed, key_pos[None, :] <= query_pos[:, None])

    def to_heads(matrix):
        return matrix.reshape(matrix.shape[0], head_local, HD).transpose(1, 0, 2)

    def from_heads(stacked):
        return stacked.transpose(1, 0, 2).reshape(stacked.shape[1], head_local * HD)

    normed_one, inv_one = layer_stats(rows)
    first_in = (normed_one * gain_vals[0] + shift_vals[0]).astype(jnp.bfloat16)
    queries = (
        jnp.dot(first_in, qkv_full[0], preferred_element_type=jnp.float32) + bias_vals[:tp_width]
    ).astype(jnp.bfloat16)
    key_rows = jnp.dot(first_in, qkv_full[1], preferred_element_type=jnp.float32).astype(
        jnp.bfloat16
    )
    values = (
        jnp.dot(first_in, qkv_full[2], preferred_element_type=jnp.float32)
        + bias_vals[tp_width : 2 * tp_width]
    ).astype(jnp.bfloat16)
    key_all, value_all = (
        lax.all_gather(key_rows, CTX, axis=0, tiled=True),
        lax.all_gather(values, CTX, axis=0, tiled=True),
    )
    query_heads = to_heads(queries)
    key_heads = to_heads(key_all)
    value_heads = to_heads(value_all)

    def attend(head_items):
        query_h, key_h, value_h = head_items
        scores = dot(query_h, key_h, ((1,), (1,))) * 0.125
        scores = jnp.where(allowed, scores, -1e30)
        row_top = jnp.max(scores, axis=-1, keepdims=True)
        weights = jnp.exp(scores - row_top)
        row_total = jnp.sum(weights, axis=-1, keepdims=True)
        weights_low = (weights / row_total).astype(jnp.bfloat16)
        mixed_h = dot(weights_low, value_h, ((1,), (0,)))
        return (mixed_h.astype(jnp.bfloat16), row_top[:, 0] + jnp.log(row_total[:, 0]))

    mixed_heads, log_totals = lax.map(attend, (query_heads, key_heads, value_heads))
    mixed = from_heads(mixed_heads)
    middle = (
        rows
        + tensor_psum(jnp.dot(mixed, proj_full, preferred_element_type=jnp.float32))
        + shift_vals[1]
    )
    normed_two, inv_two = layer_stats(middle)
    second_in = (normed_two * gain_vals[1] + shift_vals[2]).astype(jnp.bfloat16)
    hidden = (
        jnp.dot(second_in, up_full, preferred_element_type=jnp.float32) + bias_vals[2 * tp_width :]
    )
    sigma = jax.nn.sigmoid(1.702 * hidden)
    activated = (hidden * sigma).astype(jnp.bfloat16)
    output = (
        middle
        + tensor_psum(jnp.dot(activated, down_full, preferred_element_type=jnp.float32))
        + shift_vals[3]
    )
    grad_out = cotangent[0].astype(jnp.float32)
    grad_down_bias = jnp.sum(grad_out, axis=0)
    grad_branch = grad_out.astype(jnp.bfloat16)
    grad_down = dot(activated, grad_branch, ((0,), (0,)))
    grad_act = dot(grad_branch, down_full, ((1,), (1,)))
    grad_hidden = (grad_act * (sigma + 1.702 * hidden * sigma * (1.0 - sigma))).astype(jnp.bfloat16)
    grad_up_bias = jnp.sum(grad_hidden.astype(jnp.float32), axis=0)
    grad_up = dot(second_in, grad_hidden, ((0,), (0,)))
    grad_second = tensor_psum(
        dot(grad_hidden, up_full, ((1,), (1,)))
    )
    grad_gain_two = jnp.sum(grad_second * normed_two, axis=0)
    grad_shift_two = jnp.sum(grad_second, axis=0)
    grad_middle = grad_out + norm_back(grad_second, normed_two, inv_two, gain_vals[1])
    grad_proj_bias = jnp.sum(grad_middle, axis=0)
    grad_attn = grad_middle.astype(jnp.bfloat16)
    grad_proj = dot(mixed, grad_attn, ((0,), (0,)))
    grad_mixed = dot(grad_attn, proj_full, ((1,), (1,))).astype(jnp.bfloat16)

    def attend_back(head_items):
        query_h, key_h, value_h, grad_h, log_total = head_items
        scores = dot(query_h, key_h, ((1,), (1,))) * 0.125
        weights = jnp.where(allowed, jnp.exp(scores - log_total[:, None]), 0.0)
        grad_weights = dot(grad_h, value_h, ((1,), (1,)))
        row_delta = jnp.sum(weights * grad_weights, axis=-1, keepdims=True)
        grad_scores = (weights * (grad_weights - row_delta)).astype(jnp.bfloat16)
        grad_query_h = (
            dot(grad_scores, key_h, ((1,), (0,))) * 0.125
        )
        grad_key_h = (
            dot(grad_scores, query_h, ((0,), (0,)))
            * 0.125
        )
        grad_value_h = dot(weights.astype(jnp.bfloat16), grad_h, ((0,), (0,)))
        return (grad_query_h, grad_key_h, grad_value_h)

    query_parts, key_parts, value_parts = lax.map(
        attend_back, (query_heads, key_heads, value_heads, to_heads(grad_mixed), log_totals)
    )
    key_sum, value_sum = (
        lax.psum_scatter(from_heads(key_parts), CTX, scatter_dimension=0, tiled=True),
        lax.psum_scatter(from_heads(value_parts), CTX, scatter_dimension=0, tiled=True),
    )
    grad_query = from_heads(query_parts).astype(jnp.bfloat16)
    grad_key = key_sum.astype(jnp.bfloat16)
    grad_value = value_sum.astype(jnp.bfloat16)
    grad_qkv = jnp.stack(
        [
            dot(first_in, grad_query, ((0,), (0,))),
            dot(first_in, grad_key, ((0,), (0,))),
            dot(first_in, grad_value, ((0,), (0,))),
        ]
    )
    grad_head = jnp.concatenate(
        [
            jnp.sum(grad_query.astype(jnp.float32), axis=0),
            jnp.sum(grad_value.astype(jnp.float32), axis=0),
            grad_up_bias,
        ]
    )[None, :]
    grad_first_part = dot(grad_query, qkv_full[0], ((1,), (1,)))
    grad_first_part = grad_first_part + dot(grad_key, qkv_full[1], ((1,), (1,)))
    grad_first_part = grad_first_part + dot(grad_value, qkv_full[2], ((1,), (1,)))
    grad_first = tensor_psum(grad_first_part)
    grad_gain_one = jnp.sum(grad_first * normed_one, axis=0)
    grad_shift_one = jnp.sum(grad_first, axis=0)
    grad_rows = grad_middle + norm_back(grad_first, normed_one, inv_one, gain_vals[0])
    grad_gains = jnp.stack([grad_gain_one, grad_gain_two])
    grad_shifts = jnp.stack([grad_shift_one, grad_proj_bias, grad_shift_two, grad_down_bias])
    share_gains, share_shifts, share_head, share_qkv, share_proj, share_up, share_down = (
        lax.psum_scatter(grad_gains, FSDP, scatter_dimension=1, tiled=True),
        lax.psum_scatter(grad_shifts, FSDP, scatter_dimension=1, tiled=True),
        lax.psum_scatter(grad_head, FSDP, scatter_dimension=1, tiled=True),
        lax.psum_scatter(grad_qkv, FSDP, scatter_dimension=1, tiled=True),
        lax.psum_scatter(grad_proj, FSDP, scatter_dimension=1, tiled=True),
        lax.psum_scatter(grad_up, FSDP, scatter_dimension=0, tiled=True),
        lax.psum_scatter(grad_down, FSDP, scatter_dimension=1, tiled=True),
    )
    owned = lax.psum(
        (share_gains, share_shifts, share_head, share_qkv, share_proj, share_up, share_down), CTX
    )
    return (output.astype(jnp.bfloat16)[None], grad_rows[None]) + tuple(owned)


def on_any_mesh(
    image_input,
    image_segments,
    image_cotangent,
    image_gains,
    image_shifts,
    image_head_bias,
    image_qkv_weight,
    image_proj_weight,
    image_up_weight,
    image_down_weight,
    text_input,
    text_segments,
    text_cotangent,
    text_gains,
    text_shifts,
    text_head_bias,
    text_qkv_weight,
    text_proj_weight,
    text_up_weight,
    text_down_weight,
):
    image_results = any_mesh_block(
        image_input,
        image_segments,
        image_cotangent,
        image_gains,
        image_shifts,
        image_head_bias,
        image_qkv_weight,
        image_proj_weight,
        image_up_weight,
        image_down_weight,
        False,
    )
    text_results = any_mesh_block(
        text_input,
        text_segments,
        text_cotangent,
        text_gains,
        text_shifts,
        text_head_bias,
        text_qkv_weight,
        text_proj_weight,
        text_up_weight,
        text_down_weight,
        True,
    )
    return image_results + text_results


def stream_specs():
    return (
        P(FSDP, CTX, None),
        P(FSDP, None),
        P(FSDP, CTX, None),
        P(None, FSDP),
        P(None, FSDP),
        P(TP, FSDP),
        P(None, FSDP, TP),
        P(TP, FSDP),
        P(FSDP, TP),
        P(TP, FSDP),
    )


def solution(mesh):
    one = stream_specs()
    grads = (one[0], one[0]) + one[3:]
    body = on_device
    if (mesh.shape[FSDP], mesh.shape[CTX], mesh.shape[TP]) != (4, 4, 2):
        body = on_any_mesh
    return jax.shard_map(
        body, mesh=mesh, in_specs=one + one, out_specs=grads + grads, check_vma=False
    )
```

```python
import functools

import jax
import jax.numpy as jnp
from jax import lax
from jax.experimental import pallas as pl
from jax.experimental.pallas import tpu as pltpu
from jax.sharding import PartitionSpec as P

HD = 64
LANES = 128
QB = 256
KB = 512
NEG = -1e30
F32 = jnp.float32
MESH = pl.DeviceIdType.MESH
FSDP, CTX, TP = "fsdp", "ctx", "tp"
BF16 = jnp.bfloat16


def dot(left, right, dims=((1,), (0,))):
    return lax.dot_general(left, right, (dims, ((), ())), preferred_element_type=F32)


def lane_marks():
    lane = lax.broadcasted_iota(jnp.int32, (1, LANES), 1)
    first = (lane < HD).astype(F32).astype(BF16)
    second = (lane >= HD).astype(F32).astype(BF16)
    return first, second


def document_features(row_ref, query_out, key_out):
    lane = lax.broadcasted_iota(jnp.int32, (LANES, LANES), 1) % HD
    for start in range(0, query_out.shape[0], LANES):
        row = row_ref[:, start : start + LANES].astype(F32)
        same = jnp.transpose(jnp.broadcast_to(row, (LANES, LANES))) == lane.astype(F32)
        query_out[start : start + LANES, :] = jnp.where(same, 1.0, 0.0).astype(BF16)
        key_out[start : start + LANES, :] = jnp.where(same, 0.0, NEG).astype(BF16)


def swap_halves(value):
    return pltpu.roll(value, HD, 1)


def key_range(index):
    return slice(index * KB, (index + 1) * KB)


def pick(flag, one, zero):
    return jnp.where(flag == 1, one, zero)


def query_rows(head):
    return pl.ds(pl.multiple_of(head * (QB + 2 * KB), QB), QB)


def key_rows(head):
    return pl.ds(pl.multiple_of(QB + head * KB, QB), KB)


def mark_keys(m, features, heads, score_keys, value_keys):
    first, second = lane_marks()
    for head in range(heads):
        for index in range(4):
            block = m[index, key_rows(head)]
            score_keys[head, key_range(index)] = block * first + features[key_range(index), :] * second
            if value_keys is not None:
                value_keys[head, key_range(index)] = block * second + first


def later(index, shape, axis, query_start):
    key_pos = index * KB + lax.broadcasted_iota(jnp.int32, shape, axis)
    query_pos = query_start + lax.broadcasted_iota(jnp.int32, shape, 1 - axis)
    return key_pos > query_pos


def mix_rows(query, score_keys, value_keys, head, blocks, query_start=None):
    scores = []
    for index in range(blocks):
        score = dot(query, score_keys[head, key_range(index)], ((1,), (1,)))
        if query_start is not None:
            score = jnp.where(later(index, score.shape, 1, query_start), NEG, score)
        scores.append(score)
    top = jnp.max(functools.reduce(jnp.maximum, scores), axis=1, keepdims=True)
    acc = jnp.zeros((query.shape[0], LANES), F32)
    for index, score in enumerate(scores):
        acc = acc + dot(jnp.exp(score - top).astype(BF16), value_keys[head, key_range(index)])
    return acc / swap_halves(acc), top + jnp.log(acc)


def text_task(at, task):
    return 0, task // 2, task % 2


def image_task(at, task):
    shared = 1 - (task + 8) // 12
    step = 5 - task // 2
    low, high = (at.here_low + step % 2) % 2, (at.here_high + step // 2) % 2
    return shared, pick(shared, at.here_high * 2 + task // 2, high * 2 + low), task % 2


def attend(at, m, features, score_keys, value_keys, o, lse, task_of, begin, end, blocks, causal):
    first, second = lane_marks()
    lane = lax.broadcasted_iota(jnp.int32, (QB, LANES), 1)

    def one(task, carry):
        head, source, half = task_of(at, task)
        start = (source * 2 + half) * QB
        query = m[source, query_rows(head)].astype(F32)
        query = pick(half, swap_halves(query), query).astype(BF16)
        query = query * first + features[pl.ds(pl.multiple_of(start, QB), QB), :] * second
        mixed, log_total = mix_rows(
            query, score_keys, value_keys, head, blocks, start if causal else None
        )
        lse[task] = jnp.transpose(log_total)[:8]
        mixed = pick(half, mixed, swap_halves(mixed)).astype(BF16)
        rows = pl.ds(pl.multiple_of(head * QB, QB), QB)
        o[source, rows] = jnp.where(lane // HD == half, mixed, o[source, rows])
        return carry

    lax.fori_loop(begin, end, one, 0)


def unattend(at, m, do, o, lse, features, score_keys, acc, out, task_of, begin, end, blocks, causal):
    first, second = lane_marks()
    lane = lax.broadcasted_iota(jnp.int32, (QB, LANES), 1)

    def one(task, carry):
        head, source, half = task_of(at, task)
        start = (source * 2 + half) * QB
        rows = pl.ds(pl.multiple_of(head * QB, QB), QB)
        query, grad_o = m[source, query_rows(head)].astype(F32), do[source, rows].astype(F32)
        product = jnp.transpose(grad_o * o[source, rows].astype(F32))
        delta = jnp.sum(pick(half, product[HD:], product[:HD]), axis=0, keepdims=True)
        query = pick(half, swap_halves(query), query).astype(BF16) * first
        grad_o = pick(half, grad_o, swap_halves(grad_o)).astype(BF16) * second
        marked = query + features[pl.ds(pl.multiple_of(start, QB), QB), :] * second
        row_lse = lse[task, :1]
        grad_query = jnp.zeros((QB, LANES), F32)
        for index in range(blocks):
            keys = m[index, key_rows(head)]
            score = dot(score_keys[head, key_range(index)], marked, ((1,), (1,)))
            if causal:
                score = jnp.where(later(index, score.shape, 0, start), NEG, score)
            weights = jnp.exp(score - row_lse)
            grad_weights = dot(keys, grad_o, ((1,), (1,)))
            grad_scores = (weights * (grad_weights - delta)).astype(BF16)
            acc[head, key_range(index)] += dot(grad_scores, query) + dot(weights.astype(BF16), grad_o)
            grad_query = grad_query + dot(grad_scores, keys, ((0,), (0,)))
        grad_query = grad_query * 0.125
        grad_query = pick(half, swap_halves(grad_query), grad_query).astype(BF16)
        out[source, query_rows(head)] = jnp.where(
            lane // HD == half, grad_query, out[source, query_rows(head)]
        )
        return carry

    lax.fori_loop(begin, end, one, 0)


def key_gradients(acc, out, head):
    for index in range(4):
        out[index, key_rows(head)] = acc[head, key_range(index)].astype(BF16)


class Bag:
    pass


def partners():
    at = Bag()
    group, here, core = lax.axis_index(FSDP), lax.axis_index(CTX), lax.axis_index(TP)
    at.group, at.here, at.core = group, here, core
    at.group_x = group + 1 - 2 * (group % 2)
    at.group_y = group + 2 - 4 * (group // 2)
    at.group_far = 3 - group
    at.here_low, at.here_high = here % 2, here // 2
    at.inner, at.outer = (here + 1) // 2 == 1, (here + 1) // 2 != 1
    at.ctx = (here, here + 1 - 2 * (here % 2), here + 2 - 4 * (here // 2), 3 - here)
    at.to_x, at.to_y, at.to_far = ({FSDP: g} for g in (at.group_x, at.group_y, at.group_far))
    at.to_ctx = [{CTX: c} for c in at.ctx]
    at.to_core = {TP: 1 - core}
    return at


def greet(devices):
    barrier = pltpu.get_barrier_semaphore()
    for device in devices:
        pl.semaphore_signal(barrier, inc=1, device_id=device, device_id_type=MESH)


def meet(devices):
    pl.semaphore_wait(pltpu.get_barrier_semaphore(), len(devices))


class Copies:
    def __init__(self, send_sems, recv_sems, local_sems):
        self.sems = (send_sems, recv_sems, local_sems)
        self.used = [0, 0]

    def remote(self, src, dst, device, start=True):
        index = self.used[0]
        self.used[0] += 1
        copy = pltpu.make_async_remote_copy(
            src_ref=src,
            dst_ref=dst,
            send_sem=self.sems[0].at[index],
            recv_sem=self.sems[1].at[index],
            device_id=device,
            device_id_type=MESH,
        )
        if start:
            copy.start()
        return copy

    def local(self, src, dst, start=True):
        index = self.used[1]
        self.used[1] += 1
        copy = pltpu.make_async_copy(src, dst, self.sems[2].at[index])
        if start:
            copy.start()
        return copy


def copy_sems(remote, local):
    return [
        pltpu.SemaphoreType.DMA((remote,)),
        pltpu.SemaphoreType.DMA((remote,)),
        pltpu.SemaphoreType.DMA((local,)),
    ]


class Gather:
    def __init__(self, copies, at, src, dst):
        self.copies, self.at, self.dst = copies, at, dst
        self.rows = src.shape[-2]
        own = self.part(at.group, 0, self.rows)
        self.own = copies.local(src, own)
        self.to_x = copies.remote(src, own, at.to_x)
        self.to_y = copies.remote(src, own, at.to_y)

    def part(self, owner, offset, size):
        rows = pl.ds(pl.multiple_of(owner * self.rows + offset, 8), size)
        return self.dst.at[:, rows, :] if len(self.dst.shape) == 3 else self.dst.at[rows, :]

    def near(self):
        self.own.wait()
        self.to_x.wait()
        self.to_y.wait()

    def forward(self):
        half = self.rows // 2
        self.to_x.wait_recv()
        self.to_y.wait_recv()
        top = self.part(self.at.group_y, 0, half)
        low = self.part(self.at.group_x, half, half)
        self.far_x = self.copies.remote(top, top, self.at.to_x)
        self.far_y = self.copies.remote(low, low, self.at.to_y)

    def arrived(self):
        self.own.wait()
        self.far_x.wait_recv()
        self.far_y.wait_recv()

    def sent(self):
        for copy in (self.to_x, self.to_y, self.far_x, self.far_y):
            copy.wait_send()


def normalise(rows):
    mean = jnp.mean(rows, axis=-1, keepdims=True)
    centred = rows - mean
    inv = lax.rsqrt(jnp.mean(centred * centred, axis=-1, keepdims=True) + 1e-05)
    return centred * inv, inv


def lane_pair(low, high):
    lane = lax.broadcasted_iota(jnp.int32, low[0].shape, 1)
    left = low[0] if low[1] == 0 else pltpu.roll(low[0], HD, 1)
    right = high[0] if high[1] == 1 else pltpu.roll(high[0], HD, 1)
    return jnp.where(lane < HD, left, right)


def head_tile(ref, start, index, rows=slice(None)):
    first = start + (index // 2) * LANES
    return ref[rows, first : first + LANES], index % 2


def halves_pair(ref, start, index):
    half = ref.shape[0] // 2
    return lane_pair(
        head_tile(ref, start, index, slice(0, half)), head_tile(ref, start, index, slice(half, None))
    ).astype(BF16)


def write_messages(qkv, out, heads):
    width = heads * HD

    def keys_values(index):
        return lane_pair(head_tile(qkv, width, index), head_tile(qkv, 2 * width, index)).astype(BF16)

    for c in range(4):
        out[c, query_rows(0)] = halves_pair(qkv, 0, c)
        out[c, key_rows(0)] = keys_values(c)
        if heads == 6:
            out[c, key_rows(1)] = keys_values(4 + c % 2)
            out[c, query_rows(1)] = halves_pair(qkv, 0, 4 + c % 2)


def message_shape(heads, tokens):
    return (4, (heads // 2 - 1) * (QB + tokens), LANES)


def mixed_shape(heads):
    return (4, (heads // 2 - 1) * QB, LANES)


def first_rows(x_ref, small_ref, weight_ref, first_ref, qkv_ref, step):
    width = weight_ref.shape[2]
    rows = slice(step * 256, step * 256 + 256)
    normed, _ = normalise(x_ref[rows, :].astype(F32))
    first = (normed * small_ref[0:1] + small_ref[2:3]).astype(BF16)
    first_ref[:, rows] = jnp.transpose(first)
    bias = small_ref[6:7]
    qkv_ref[rows, :width] = (dot(first, weight_ref[0]) + bias[:, :width]) * 0.125
    qkv_ref[rows, width : 2 * width] = dot(first, weight_ref[1])
    qkv_ref[rows, 2 * width :] = dot(first, weight_ref[2]) + bias[:, width : 2 * width]


def spread_small(at, gains, shifts, bias, wide, flat, out):
    width = wide.shape[1]
    columns, bias_columns = gains.shape[1], bias.shape[1]
    wide[...] = jnp.zeros_like(wide)
    flat[...] = jnp.zeros_like(flat)
    wide[0:2, :columns] = gains[...].astype(F32)
    wide[2:6, :columns] = shifts[...].astype(F32)
    flat[0:1, :bias_columns] = bias[...].astype(F32)
    out[0:8] = pltpu.roll(wide[...], at.group * columns, 1)
    line = pltpu.roll(flat[...], at.group * bias_columns, 1)
    out[8:16] = jnp.zeros((8, width), F32)
    for row in range(3):
        out[6 + row : 7 + row] = line[0:1, row * width : (row + 1) * width]


FRONT_IN, FRONT_OUT, FRONT_SCRATCH = 9, 10, 20


def front_kernel(*refs):
    at = partners()
    ins = [refs[:FRONT_IN], refs[FRONT_IN : 2 * FRONT_IN]]
    refs = refs[2 * FRONT_IN :]
    outs = [refs[:FRONT_OUT], refs[FRONT_OUT : 2 * FRONT_OUT]]
    refs = refs[2 * FRONT_OUT :]
    scratch = [refs[:FRONT_SCRATCH], refs[FRONT_SCRATCH : 2 * FRONT_SCRATCH]]
    copies = Copies(*refs[2 * FRONT_SCRATCH :])
    others = [at.to_x, at.to_y, at.to_far] + at.to_ctx[1:]
    greet(others)
    streams = []
    for in_refs, out_refs, own in zip(ins, outs, scratch):
        s = Bag()
        s.x_in, s.seg_row, s.gains, s.shifts, s.bias, s.qkv, s.up_in, s.down_in, s.proj_in = in_refs
        (
            s.weight_out, s.small, s.first_out, s.messages, s.proj_full, s.up_full, s.down_full,
            s.o_out, s.lse, s.o_got,
        ) = out_refs
        (
            s.small_in, s.small_own, s.wide, s.flat, s.rows, s.mine, s.got, s.down_t, s.proj_t,
            s.query_doc, s.key_doc, s.score_keys, s.value_keys, s.x, s.up, s.down, s.proj, s.weight, s.first,
        ) = own[:19]
        s.o = own[19]
        s.heads = s.weight.shape[2] // HD
        s.features = (s.query_doc, s.key_doc)
        s.reads = [
            copies.local(src, dst)
            for src, dst in (
                (s.x_in, s.x), (s.proj_in, s.proj), (s.up_in, s.up), (s.down_in, s.down),
            )
        ]
        streams.append(s)
    text, image = streams
    for s in (image, text):
        spread_small(at, s.gains, s.shifts, s.bias, s.wide, s.flat, s.small_own)
        document_features(s.seg_row, *s.features)
    meet(others)
    text.gather = Gather(copies, at, text.qkv, text.weight)
    for s in (text, image):
        s.small_done = [
            copies.remote(s.small_own, s.small_in.at[i], device)
            for i, device in enumerate((at.to_x, at.to_y, at.to_far))
        ]
        for copy in s.reads:
            copy.wait()
    text.down_t[...] = jnp.transpose(text.down[...])
    text.proj_t[...] = jnp.transpose(text.proj[...])
    text.gather.forward()
    image.gather = Gather(copies, at, image.qkv, image.weight)

    def project(s):
        for copy in s.small_done:
            copy.wait_recv()
        s.small[...] = s.small_own[...] + s.small_in[0] + s.small_in[1] + s.small_in[2]
        s.gather.arrived()
        for step in range(s.x.shape[0] // 256):
            first_rows(s.x, s.small, s.weight, s.first, s.rows, step)
        write_messages(s.rows, s.mine, s.heads)
        s.writes = [copies.local(s.weight, s.weight_out), copies.local(s.first, s.first_out)]

    def gather_rest(s):
        pieces = (s.proj_t, s.up, s.down_t) if s.heads == 4 else (s.proj, s.up, s.down)
        s.rest = [
            Gather(copies, at, piece, full)
            for piece, full in zip(pieces, (s.proj_full, s.up_full, s.down_full))
        ]

    project(text)
    text.sends = send_blocks(copies, at, text.mine, text.got)
    image.gather.forward()
    gather_rest(text)
    project(image)
    image.sends = send_blocks(copies, at, image.mine, image.got)
    gather_rest(image)
    s = text
    for copy in s.sends:
        copy.wait()
    s.writes.append(copies.local(s.got, s.messages))
    s.o[...] = jnp.zeros_like(s.o)
    mark_keys(s.got, s.features[1], 1, s.score_keys, s.value_keys)
    attend(
        at, s.got, s.features[0], s.score_keys, s.value_keys, s.o, s.lse, text_task, 0, 8, 4, True
    )
    for gather in s.rest:
        gather.forward()
    s = image
    for copy in s.sends:
        copy.wait()
    text.o_done = send_blocks(copies, at, text.o, text.o_got)
    s.writes.append(copies.local(s.got, s.messages))
    s.o[...] = jnp.zeros_like(s.o)
    mark_keys(s.got, s.features[1], 2, s.score_keys, s.value_keys)
    s.o_done = send_blocks(copies, at, s.o, s.o_got, start=False)

    def image_pair(index, carry):
        attend(
            at, image.got, image.features[0], image.score_keys, image.value_keys, image.o, image.lse,
            image_task, 2 * index, 2 * index + 2, 4, False,
        )
        for step, copy in enumerate(image.o_done):

            @pl.when(index == 5 - step)
            def _(copy=copy):
                copy.start()

        return carry

    lax.fori_loop(0, 6, image_pair, 0)
    s.rest[0].forward()
    for s in (text, image):
        s.writes.append(copies.local(s.o, s.o_out))
    whole = [image.gather, text.gather, image.rest[0]] + text.rest
    for gather in whole[2:]:
        gather.arrived()
    for gather in whole:
        gather.sent()
    for gather in image.rest[1:]:
        gather.near()
    for s in (image, text):
        for copy in s.small_done:
            copy.wait_send()
        for copy in s.writes + s.o_done:
            copy.wait()


def front(streams):
    vmem, hbm = pl.BlockSpec(memory_space=pltpu.VMEM), pl.BlockSpec(memory_space=pl.ANY)
    out_shape, out_specs, scratch = [], [], []
    for x, seg, gains, shifts, bias, qkv, up, down, proj in streams:
        tokens, width = x.shape
        own = qkv.shape[2]
        messages = message_shape(own // HD, tokens)
        hidden = up.shape[1]
        small = jax.ShapeDtypeStruct((16, width), F32)
        out_shape += [
            jax.ShapeDtypeStruct((3, width, own), BF16),
            small,
            jax.ShapeDtypeStruct((width, tokens), BF16),
            jax.ShapeDtypeStruct(messages, BF16),
            jax.ShapeDtypeStruct((width, own), BF16),
            jax.ShapeDtypeStruct((width, hidden), BF16),
            jax.ShapeDtypeStruct((width, hidden), BF16),
            jax.ShapeDtypeStruct(mixed_shape(own // HD), BF16),
            jax.ShapeDtypeStruct((2 * (own // HD), 8, QB), F32),
            jax.ShapeDtypeStruct(mixed_shape(own // HD), BF16),
        ]
        out_specs += [hbm, vmem, hbm, hbm, hbm, hbm, hbm, hbm, vmem, hbm]
        scratch += [
            pltpu.VMEM((3, 16, width), F32),
            pltpu.VMEM((16, width), F32),
            pltpu.VMEM((8, width), F32),
            pltpu.VMEM((8, 3 * width), F32),
            pltpu.VMEM((tokens, 3 * own), F32),
            pltpu.VMEM(messages, BF16),
            pltpu.VMEM(messages, BF16),
            pltpu.VMEM((width // 4, hidden), BF16),
            pltpu.VMEM((width // 4, own), BF16),
            pltpu.VMEM((4 * tokens, LANES), BF16),
            pltpu.VMEM((4 * tokens, LANES), BF16),
            pltpu.VMEM((1 if own == 4 * HD else 2, 4 * tokens, LANES), BF16),
            pltpu.VMEM((1 if own == 4 * HD else 2, 4 * tokens, LANES), BF16),
            pltpu.VMEM(x.shape, BF16),
            pltpu.VMEM(up.shape, BF16),
            pltpu.VMEM(down.shape, BF16),
            pltpu.VMEM(proj.shape, BF16),
            pltpu.VMEM((3, width, own), BF16),
            pltpu.VMEM((width, tokens), BF16),
            pltpu.VMEM(mixed_shape(own // HD), BF16),
        ]
    results = pl.pallas_call(
        front_kernel,
        out_shape=out_shape,
        in_specs=[hbm, vmem, vmem, vmem, vmem, vmem, hbm, hbm, hbm] * 2,
        out_specs=out_specs,
        scratch_shapes=scratch + copy_sems(2 * (3 + 4 * 4 + 6), 2 * 14),
        compiler_params=pltpu.CompilerParams(
            collective_id=0, has_side_effects=True, vmem_limit_bytes=63 << 20
        ),
        name="front",
    )(*streams[0], *streams[1])
    return results[:FRONT_OUT], results[FRONT_OUT:]


STEP = 384
TILES = 1


def by_columns(columns, body):
    def one(index, carry):
        body(pl.ds(pl.multiple_of(index * STEP, STEP), STEP))
        return carry

    lax.fori_loop(0, columns // STEP, one, 0)


class PlaneSum:
    def __init__(self, copies, at, src, arrivals, loads=None):
        self.copies, self.at = copies, at
        self.in_x, self.in_y, self.in_top, self.in_low = arrivals
        half, self.columns = self.in_top.shape
        self.half, rows = half, 2 * half

        def block(owner, offset, size=half):
            return src.at[pl.ds(pl.multiple_of(owner * rows + offset, 8), size), :]

        self.first = [
            copies.remote(block(at.group_far, 0), self.in_x.at[1], at.to_x),
            copies.remote(block(at.group_far, half), self.in_y.at[1], at.to_y),
            copies.remote(block(at.group_x, 0), self.in_x.at[0], at.to_x),
            copies.remote(block(at.group_y, half), self.in_y.at[0], at.to_y),
        ]
        parts = [block(at.group_y, 0), block(at.group_x, half), block(at.group, 0, rows)]
        if loads is None:
            self.loads = []
            self.pass_top, self.pass_low, self.own = parts
        else:
            self.loads = [copies.local(part, load) for part, load in zip(parts, loads)]
            self.pass_top, self.pass_low, self.own = loads
        self.second = [
            copies.remote(self.pass_top, self.in_top, at.to_y, False),
            copies.remote(self.pass_low, self.in_low, at.to_x, False),
        ]

    def cross(self):
        for copy in self.loads:
            copy.wait()
        self.first[0].wait_recv()

        def top(cols):
            self.pass_top[:, cols] = (
                self.pass_top[:, cols].astype(F32) + self.in_x[1, :, cols].astype(F32)
            ).astype(BF16)

        by_columns(self.columns, top)
        self.second[0].start()
        self.first[1].wait_recv()

        def low(cols):
            self.pass_low[:, cols] = (
                self.pass_low[:, cols].astype(F32) + self.in_y[1, :, cols].astype(F32)
            ).astype(BF16)

        by_columns(self.columns, low)
        self.second[1].start()

    def arrived(self):
        for copy in self.first[2:] + self.second:
            copy.wait_recv()

    def halves(self, cols):
        half = self.half
        return (
            self.own[:half, cols].astype(F32)
            + self.in_x[0, :, cols].astype(F32)
            + self.in_top[:, cols].astype(F32),
            self.own[half:, cols].astype(F32)
            + self.in_y[0, :, cols].astype(F32)
            + self.in_low[:, cols].astype(F32),
        )

    def sent(self):
        for copy in self.first + self.second:
            copy.wait_send()

    @staticmethod
    def arrivals(rows, columns):
        half = rows // 2
        pair, one = pltpu.VMEM((2, half, columns), BF16), pltpu.VMEM((half, columns), BF16)
        return [pair, pair, one, one]

    @staticmethod
    def loads_scratch(rows, columns):
        half = rows // 2
        one = pltpu.VMEM((half, columns), BF16)
        return [one, one, pltpu.VMEM((rows, columns), BF16)]


class LineSum:
    def __init__(self, copies, at, values, buffers, final, begin, end):
        self.at, self.values, self.final, self.range = at, values, final, (begin, end)
        self.pair, self.outer_in, self.inner_in = buffers

        def part(ref):
            return ref.at[:, begin:end]

        self.up = copies.remote(part(self.pair), part(self.outer_in), at.to_ctx[1], False)
        self.across = copies.remote(part(self.pair), part(self.inner_in), at.to_ctx[3], False)
        self.down = copies.remote(part(final), part(final), at.to_ctx[1], False)

    def each(self, body):
        begin, end = self.range

        def one(index, carry):
            body(pl.ds(pl.multiple_of(begin + index * STEP, LANES), STEP))
            return carry

        lax.fori_loop(0, (end - begin) // STEP, one, 0)

    def gather(self):
        half = self.pair.shape[0] // 2

        @pl.when(self.at.outer)
        def _():
            def add(cols):
                top, low = self.values(cols)
                self.pair[:half, cols] = top.astype(BF16)
                self.pair[half:, cols] = low.astype(BF16)

            self.each(add)
            self.up.start()

    def join(self):
        half = self.pair.shape[0] // 2

        @pl.when(self.at.inner)
        def _():
            self.up.wait_recv()

            def add(cols):
                top, low = self.values(cols)
                self.pair[:half, cols] = (top + self.outer_in[:half, cols].astype(F32)).astype(BF16)
                self.pair[half:, cols] = (low + self.outer_in[half:, cols].astype(F32)).astype(BF16)

            self.each(add)
            self.across.start()

    def share(self):
        @pl.when(self.at.inner)
        def _():
            self.across.wait_recv()

            def add(cols):
                self.final[:, cols] = (
                    self.pair[:, cols].astype(F32) + self.inner_in[:, cols].astype(F32)
                ).astype(BF16)

            self.each(add)
            self.down.start()

    def finish(self):
        @pl.when(self.at.outer)
        def _():
            self.up.wait_send()
            self.down.wait_recv()

        @pl.when(self.at.inner)
        def _():
            self.across.wait_send()
            self.down.wait_send()

    @staticmethod
    def scratch(rows, columns):
        return [pltpu.VMEM((rows, columns), BF16)] * 3


def chunks(tokens, size=256):
    return [slice(start, start + size) for start in range(0, tokens, size)]


def as_f32(ref, index, rows=slice(None)):
    return ref[index, rows].astype(F32)


def take_halves(got, out, at, heads, start, put):
    half = out.shape[0] // 2
    for tile in range(heads // 2):
        base = 0 if tile < 2 else start
        if tile < 2:
            one, two = 2 * tile, 2 * tile + 1
        else:
            one, two = at.here_high * 2, at.here_high * 2 + 1
        rows = slice(base, base + QB)
        left, right = as_f32(got, one, rows), as_f32(got, two, rows)
        for side in range(2):
            put(tile, slice(side * half, side * half + half), lane_pair((left, side), (right, side)))


def take_mixed(got, mixed, at, heads):
    def put(tile, rows, value):
        mixed[rows, tile * LANES : (tile + 1) * LANES] = value.astype(BF16)

    take_halves(got, mixed, at, heads, QB, put)


def write_grad_o(grad, out, heads):
    for c in range(4):
        out[c, :QB] = halves_pair(grad, 0, c)
        if heads == 6:
            out[c, QB:] = halves_pair(grad, 0, 4 + c % 2)


def send_blocks(copies, at, mine, out, begin=0, end=None, start=True):
    rows = mine.shape[1]
    end = rows if end is None else end
    far = min(end, rows if rows in (QB, QB + KB) else rows - QB)
    part = pl.ds(begin, end - begin)
    done = [copies.local(mine.at[at.here, part], out.at[at.here, part], start)]
    for other, device, last in zip(at.ctx[1:], at.to_ctx[1:], (end, far, far)):
        part = pl.ds(begin, last - begin)
        done.append(copies.remote(mine.at[other, part], out.at[at.here, part], device, start))
    return done


MIDDLE_IN, MIDDLE_OUT, MIDDLE_SCRATCH = 7, 5, 22


def middle_kernel(*refs):
    at = partners()
    ins = [refs[:MIDDLE_IN], refs[MIDDLE_IN : 2 * MIDDLE_IN]]
    refs = refs[2 * MIDDLE_IN :]
    outs = [refs[:MIDDLE_OUT], refs[MIDDLE_OUT : 2 * MIDDLE_OUT]]
    refs = refs[2 * MIDDLE_OUT :]
    scratch = [refs[:MIDDLE_SCRATCH], refs[MIDDLE_SCRATCH : 2 * MIDDLE_SCRATCH]]
    arrivals = refs[2 * MIDDLE_SCRATCH : 2 * MIDDLE_SCRATCH + 4]
    copies = Copies(*refs[2 * MIDDLE_SCRATCH + 4 :])
    others = [at.to_x, at.to_y] + at.to_ctx[1:] + [at.to_core]
    greet(others)
    streams = []
    for in_refs, out_refs, own in zip(ins, outs, scratch):
        s = Bag()
        o_in, x_in, dy_in, s.small, proj_in, up_in, down_in = in_refs
        s.y_out, s.dmid_out, s.do_out, s.rest_out, s.sums = out_refs
        (
            s.proj, s.up, s.down, s.rest, s.mixed, s.part, s.part_in, s.mid, s.first, s.first_t, s.dy_t,
            s.act, s.dz, s.grad, s.grad_in, s.do, s.do_mine, s.o, s.x, s.dy, s.y, s.dmid,
        ) = own
        s.heads = proj_in.shape[1] // HD
        s.o_done = copies.local(o_in, s.o)
        s.proj_done = copies.local(proj_in, s.proj)
        s.rows_done = [copies.local(x_in, s.x), copies.local(dy_in, s.dy)]
        s.weights = ((up_in, s.up), (down_in, s.down))
        streams.append(s)
    text, image = streams
    text.rest_done = [copies.local(src, dst) for src, dst in text.weights]
    quarter = image.up.shape[0] // 4
    near = [
        pl.ds(pl.multiple_of(owner * quarter, 8), quarter)
        for owner in (at.group, at.group_x, at.group_y)
    ]
    image.rest_done = [
        copies.local(src.at[rows, :], dst.at[rows, :])
        for src, dst in image.weights
        for rows in near
    ]
    meet(others)
    top = pl.ds(pl.multiple_of(at.group_y * quarter, 8), quarter // 2)
    low = pl.ds(pl.multiple_of(at.group_x * quarter + quarter // 2, 8), quarter // 2)
    image.far_done = []
    for src, dst in image.weights:
        image.far_done.append(copies.remote(src.at[top, :], dst.at[top, :], at.to_x))
        image.far_done.append(copies.remote(src.at[low, :], dst.at[low, :], at.to_y))
    text.far_done = []

    def project(s):
        s.o_done.wait()
        take_mixed(s.o, s.mixed, at, s.heads)
        s.proj_done.wait()
        for cols in chunks(s.x.shape[1]):
            s.part[:, cols] = dot(s.mixed[...], s.proj[cols, :], ((1,), (1,)))
        s.part_done = copies.remote(s.part, s.part_in, at.to_core)
        s.sums[...] = jnp.zeros_like(s.sums)
        for copy in s.rows_done:
            copy.wait()
        for rows in chunks(s.dy.shape[0]):
            s.dy_t[:, rows] = jnp.transpose(s.dy[rows, :])

    def second_norm(s):
        s.part_done.wait()
        for rows in chunks(s.x.shape[0]):
            middle = (
                s.x[rows, :].astype(F32) + s.part[rows, :] + s.part_in[rows, :] + s.small[3:4]
            )
            s.mid[rows, :] = middle
            normed, _ = normalise(middle)
            low = (normed * s.small[1:2] + s.small[4:5]).astype(BF16)
            s.first[rows, :] = low
            s.first_t[:, rows] = jnp.transpose(low)

    def feed_forward(s):
        tokens, width = s.x.shape
        hidden, own = s.up.shape[1], s.proj.shape[1]
        size = width // TILES
        for copy in s.rest_done:
            copy.wait()
        for copy in s.far_done:
            copy.wait_recv()

        def tile(index, carry):
            cols = pl.ds(pl.multiple_of(index * size, LANES), size)
            up, down = s.up[:, cols], s.down[:, cols]
            up_cols = pl.ds(pl.multiple_of(own + index * size, LANES), size)
            down_cols = pl.ds(pl.multiple_of(own + hidden + index * size, LANES), size)
            row = pl.ds(7 + index // (width // size), 1)
            place = pl.ds(pl.multiple_of((index % (width // size)) * size, LANES), size)
            bias = s.small[row, place]
            total = jnp.zeros((1, size), F32)
            for rows in chunks(tokens):
                z = dot(s.first[rows, :], up) + bias
                sg = jax.nn.sigmoid(1.702 * z)
                zs = z * sg
                s.act[rows, cols] = zs.astype(BF16)
                grad = dot(s.dy[rows, :], down)
                low = (grad * (sg + 1.702 * zs * (1.0 - sg))).astype(BF16)
                s.dz[rows, cols] = low
                total = total + jnp.sum(low.astype(F32), axis=0, keepdims=True)
            s.sums[row, place] = total
            s.rest[:, up_cols] = dot(s.first_t[...], s.dz[:, cols]).astype(BF16)
            s.rest[:, down_cols] = dot(s.dy_t[...], s.act[:, cols]).astype(BF16)
            return carry

        lax.fori_loop(0, hidden // size, tile, 0)
        for cols in chunks(width):
            s.grad[0, :, cols] = dot(s.dz[...], s.up[cols, :], ((1,), (1,)))
        s.grad_done = copies.remote(s.grad.at[0], s.grad_in.at[0], at.to_core)
        for cols in chunks(width):
            s.grad[1, :, cols] = dot(s.act[...], s.down[cols, :], ((1,), (1,)))
        s.y_done = copies.remote(s.grad.at[1], s.grad_in.at[1], at.to_core)

    def back(s):
        sums = s.sums
        s.grad_done.wait()
        for rows in chunks(s.x.shape[0]):
            normed, inv = normalise(s.mid[rows, :])
            second = s.grad[0, rows, :] + s.grad_in[0, rows, :]
            scaled = second * s.small[1:2]
            dy = s.dy[rows, :].astype(F32)
            dmid = dy + inv * (
                scaled
                - jnp.mean(scaled, axis=-1, keepdims=True)
                - normed * jnp.mean(scaled * normed, axis=-1, keepdims=True)
            )
            s.dmid[rows, :] = dmid
            sums[1:2] += jnp.sum(second * normed, axis=0, keepdims=True)
            sums[3:4] += jnp.sum(dmid, axis=0, keepdims=True)
            sums[4:5] += jnp.sum(second, axis=0, keepdims=True)
            sums[5:6] += jnp.sum(dy, axis=0, keepdims=True)
            low = dmid.astype(BF16)
            s.first_t[:, rows] = jnp.transpose(low)
            s.do[rows, :] = dot(low, s.proj[...])
        s.writes = [copies.local(s.dmid, s.dmid_out)]
        write_grad_o(s.do, s.do_mine, s.heads)
        s.do_done = send_blocks(copies, at, s.do_mine, s.do_out)

    def proj_grad(s):
        s.rest[:, : s.proj.shape[1]] = dot(s.first_t[...], s.mixed[...]).astype(BF16)

    def output(s):
        s.y_done.wait()
        for rows in chunks(s.x.shape[0]):
            s.y[rows, :] = (
                s.mid[rows, :] + s.grad[1, rows, :] + s.grad_in[1, rows, :] + s.small[5:6]
            ).astype(BF16)
        s.writes.append(copies.local(s.y, s.y_out))

    project(text)
    project(image)
    second_norm(text)
    feed_forward(text)
    second_norm(image)
    back(text)
    proj_grad(text)
    plane = PlaneSum(copies, at, text.rest, arrivals)
    feed_forward(image)
    back(image)
    plane.cross()
    proj_grad(image)
    keep = copies.local(image.rest, image.rest_out)
    output(text)
    output(image)
    plane.arrived()
    half = plane.half

    def put(cols):
        text.rest_out[:half, cols], text.rest_out[half:, cols] = plane.halves(cols)

    by_columns(plane.columns, put)
    plane.sent()
    keep.wait()
    for s in streams:
        for copy in s.do_done + s.writes:
            copy.wait()
        for copy in s.far_done:
            copy.wait_send()


def middle(streams):
    vmem, hbm = pl.BlockSpec(memory_space=pltpu.VMEM), pl.BlockSpec(memory_space=pl.ANY)
    out_shape, out_specs, scratch = [], [], []
    arrivals = None
    for o, x, dy, small, proj, up, down in streams:
        tokens, width = x.shape
        hidden, own = up.shape[1], proj.shape[1]
        rest = (width, own + 2 * hidden)
        summed = arrivals is None
        if summed:
            arrivals = PlaneSum.arrivals(width // 4, rest[1])
        out_shape += [
            jax.ShapeDtypeStruct((tokens, width), BF16),
            jax.ShapeDtypeStruct((tokens, width), F32),
            jax.ShapeDtypeStruct(o.shape, BF16),
            jax.ShapeDtypeStruct((width // 4, rest[1]), F32)
            if summed
            else jax.ShapeDtypeStruct(rest, BF16),
            jax.ShapeDtypeStruct(small.shape, F32),
        ]
        out_specs += [hbm, hbm, hbm, vmem if summed else hbm, vmem]
        scratch += [
            pltpu.VMEM(proj.shape, BF16),
            pltpu.VMEM(up.shape, BF16),
            pltpu.VMEM(down.shape, BF16),
            pltpu.VMEM(rest, BF16),
            pltpu.VMEM((tokens, own), BF16),
            pltpu.VMEM((tokens, width), F32),
            pltpu.VMEM((tokens, width), F32),
            pltpu.VMEM((tokens, width), F32),
            pltpu.VMEM((tokens, width), BF16),
            pltpu.VMEM((width, tokens), BF16),
            pltpu.VMEM((width, tokens), BF16),
            pltpu.VMEM((tokens, hidden), BF16),
            pltpu.VMEM((tokens, hidden), BF16),
            pltpu.VMEM((2, tokens, width), F32),
            pltpu.VMEM((2, tokens, width), F32),
            pltpu.VMEM((tokens, own), F32),
            pltpu.VMEM(o.shape, BF16),
            pltpu.VMEM(o.shape, BF16),
            pltpu.VMEM((tokens, width), BF16),
            pltpu.VMEM((tokens, width), BF16),
            pltpu.VMEM((tokens, width), BF16),
            pltpu.VMEM((tokens, width), F32),
        ]
    results = pl.pallas_call(
        middle_kernel,
        out_shape=out_shape,
        in_specs=([hbm] * 3 + [vmem] + [hbm] * 3) * 2,
        out_specs=out_specs,
        scratch_shapes=scratch + arrivals + copy_sems(2 * 6 + 4 + 6, 2 * (4 + 3) + 8 + 1),
        compiler_params=pltpu.CompilerParams(
            collective_id=1, has_side_effects=True, vmem_limit_bytes=64 * 1024 * 1000
        ),
        name="middle",
    )(*streams[0], *streams[1])
    return results[:MIDDLE_OUT], results[MIDDLE_OUT:]


def take_dqkv(got, out, at, heads):
    width = heads * HD

    def put(which, tile, rows, value):
        start = which * width + tile * LANES
        out[rows, start : start + LANES] = value.astype(BF16)

    take_halves(got, out, at, heads, QB + 2 * KB, functools.partial(put, 0))

    def keys(position, head):
        return as_f32(got, position, key_rows(head))

    pairs = [(keys(0, 0), keys(1, 0)), (keys(2, 0), keys(3, 0))]
    if heads == 6:
        pairs.append((keys(0, 1) + keys(2, 1), keys(1, 1) + keys(3, 1)))
    for tile, (one, two) in enumerate(pairs):
        put(1, tile, slice(None), lane_pair((one, 0), (two, 0)))
        put(2, tile, slice(None), lane_pair((one, 1), (two, 1)))


LAST_IN, LAST_OUT, LAST_SCRATCH = 12, 4, 22


def last_kernel(*refs):
    at = partners()
    ins = [refs[:LAST_IN], refs[LAST_IN : 2 * LAST_IN]]
    refs = refs[2 * LAST_IN :]
    outs = [refs[:LAST_OUT], refs[LAST_OUT : 2 * LAST_OUT]]
    refs = refs[2 * LAST_OUT :]
    count = LAST_SCRATCH + 10
    scratch = [refs[:count], refs[count : 2 * count]]
    refs = refs[2 * count :]
    rest_arrivals, rest_loads = refs[:4], refs[4:7]
    copies = Copies(*refs[7:])
    others = [at.to_x, at.to_y] + at.to_ctx[1:] + [at.to_core]
    greet(others)
    streams = []
    for in_refs, out_refs, own in zip(ins, outs, scratch):
        s = Bag()
        (
            s.m_in, s.do_in, s.o_in, s.lse, s.seg_row, s.first_in, s.x_in, s.small, s.weight_in, s.dmid_in,
            s.rest, s.sums_in,
        ) = in_refs
        s.grad_rows_out, s.sums, s.rest_final, s.qkv_final = out_refs
        (
            s.m, s.do, s.o, s.query_doc, s.key_doc, s.score_keys, s.grad_rows, s.acc, s.back, s.got, s.dqkv, s.weight, s.first, s.x, s.dmid,
            s.part, s.part_in, s.g_qkv, s.sums_own, s.sums_out, s.sums_got, s.sums_line,
        ) = own[:LAST_SCRATCH]
        s.rest_line, s.qkv_line = own[LAST_SCRATCH : LAST_SCRATCH + 3], own[LAST_SCRATCH + 3 : LAST_SCRATCH + 6]
        s.qkv_arrivals = own[LAST_SCRATCH + 6 :]
        s.heads = s.weight.shape[2] // HD
        s.features = (s.query_doc, s.key_doc)
        s.reads = [
            copies.local(src, dst) for src, dst in ((s.m_in, s.m), (s.do_in, s.do), (s.o_in, s.o))
        ]
        streams.append(s)
    text, image = streams
    for s in streams:
        document_features(s.seg_row, *s.features)
        s.acc[...] = jnp.zeros_like(s.acc)
        s.back[...] = jnp.zeros_like(s.back)
    meet(others)
    plane = PlaneSum(copies, at, image.rest, rest_arrivals, rest_loads)
    text_half = text.rest.shape[0] // 2

    def text_values(cols):
        return text.rest[:text_half, cols], text.rest[text_half:, cols]

    text_line = LineSum(
        copies, at, text_values, text.rest_line, text.rest_final, 0, text.rest.shape[1]
    )
    text_line.gather()
    for s in (image, text):
        for copy in s.reads:
            copy.wait()
        s.loads = [
            copies.local(src, dst)
            for src, dst in (
                (s.first_in, s.first), (s.weight_in, s.weight), (s.x_in, s.x), (s.dmid_in, s.dmid),
            )
        ]
        mark_keys(s.m, s.features[1], s.acc.shape[0], s.score_keys, None)

    def unattend_tasks(s, *task):
        unattend(
            at, s.m, s.do, s.o, s.lse, s.features[0], s.score_keys, s.acc, s.back, *task
        )

    text.sends = send_blocks(copies, at, text.back, text.got, start=False)
    split = QB + KB
    shared_sends = send_blocks(copies, at, image.back, image.got, split, None, False)
    own_sends = send_blocks(copies, at, image.back, image.got, 0, split, False)
    image.sends = shared_sends + own_sends

    def image_phase(phase, carry):
        unattend_tasks(image, image_task, phase * 4, phase * 4 + 4, 4, False)

        @pl.when(phase == 0)
        def _():
            key_gradients(image.acc, image.back, 1)
            for copy in shared_sends:
                copy.start()

        return carry

    lax.fori_loop(0, 3, image_phase, 0)
    key_gradients(image.acc, image.back, 0)
    for copy in own_sends:
        copy.start()

    text_line.join()

    def text_phase(phase, carry):
        unattend_tasks(text, text_task, phase * 4, phase * 4 + 4, 4, True)

        @pl.when(phase == 0)
        def _():
            plane.cross()

        return carry

    lax.fori_loop(0, 2, text_phase, 0)
    key_gradients(text.acc, text.back, 0)
    for copy in text.sends:
        copy.start()

    def project(s):
        width = s.x.shape[1]
        own = s.heads * HD
        for copy in s.sends:
            copy.wait()
        for copy in s.loads:
            copy.wait()
        take_dqkv(s.got, s.dqkv, at, s.heads)
        for which in range(3):
            cols = slice(which * own, (which + 1) * own)
            s.g_qkv[:, cols] = dot(s.first[...], s.dqkv[:, cols]).astype(BF16)
        s.qkv_plane = PlaneSum(copies, at, s.g_qkv, s.qkv_arrivals)
        for cols in chunks(width):
            total = dot(s.dqkv[:, :own], s.weight[0, cols, :], ((1,), (1,)))
            total = total + dot(s.dqkv[:, own : 2 * own], s.weight[1, cols, :], ((1,), (1,)))
            s.part[:, cols] = total + dot(s.dqkv[:, 2 * own :], s.weight[2, cols, :], ((1,), (1,)))
        s.part_done = copies.remote(s.part, s.part_in, at.to_core)
        s.sums_own[...] = s.sums_in[...]
        s.sums_own[6:7, :own] = jnp.sum(s.dqkv[:, :own].astype(F32), axis=0, keepdims=True)
        s.sums_own[6:7, own:] = jnp.sum(s.dqkv[:, 2 * own :].astype(F32), axis=0, keepdims=True)
        cuts = (0, 3 * own) if own < STEP else (0, 2 * own, 3 * own)
        s.qkv_sums = [
            LineSum(copies, at, s.qkv_plane.halves, s.qkv_line, s.qkv_final, begin, end)
            for begin, end in zip(cuts, cuts[1:])
        ]

    def input_grad(s):
        s.part_done.wait()
        for rows in chunks(s.x.shape[0]):
            normed, inv = normalise(s.x[rows, :].astype(F32))
            first = s.part[rows, :] + s.part_in[rows, :]
            scaled = first * s.small[0:1]
            s.grad_rows[rows, :] = s.dmid[rows, :] + inv * (
                scaled
                - jnp.mean(scaled, axis=-1, keepdims=True)
                - normed * jnp.mean(scaled * normed, axis=-1, keepdims=True)
            )
            s.sums_own[0:1] += jnp.sum(first * normed, axis=0, keepdims=True)
            s.sums_own[2:3] += jnp.sum(first, axis=0, keepdims=True)
        s.write = copies.local(s.grad_rows, s.grad_rows_out)
        s.sums_done = [copies.remote(s.sums_own, s.sums_got.at[0], at.to_x)]

    def add_sums(s, step):
        s.sums_done[-1].wait_recv()
        before = s.sums_own if step == 0 else s.sums_out
        total = before[...] + s.sums_got[step]
        if step == 0:
            s.sums_out[...] = total
            s.sums_done.append(copies.remote(s.sums_out, s.sums_got.at[1], at.to_y))
        else:
            s.sums_line[at.here] = total
            mine = s.sums_line.at[at.here]
            s.sums_done += [copies.remote(mine, mine, device) for device in at.to_ctx[1:]]

    def end_sums(s):
        for copy in s.sums_done[2:]:
            copy.wait_recv()
        s.sums[...] = s.sums_line[0] + s.sums_line[1] + s.sums_line[2] + s.sums_line[3]

    cuts = [0, STEP, 4 * STEP, 7 * STEP, plane.columns]
    rest_lines = [
        LineSum(copies, at, plane.halves, image.rest_line, image.rest_final, begin, end)
        for begin, end in zip(cuts, cuts[1:])
    ]

    project(image)
    plane.arrived()
    for line in rest_lines:
        line.gather()
    input_grad(image)
    image.qkv_plane.cross()
    text_line.share()
    add_sums(image, 0)
    rest_lines[0].join()
    rest_lines[1].join()
    project(text)
    rest_lines[2].join()
    input_grad(text)
    image.qkv_plane.arrived()
    for line in image.qkv_sums:
        line.gather()
    text.qkv_plane.cross()
    add_sums(image, 1)
    add_sums(text, 0)
    rest_lines[0].share()
    text.qkv_plane.arrived()
    text.qkv_sums[0].gather()
    add_sums(text, 1)
    rest_lines[1].share()
    rest_lines[3].join()
    image.qkv_sums[0].join()
    rest_lines[2].share()
    image.qkv_sums[1].join()
    text.qkv_sums[0].join()
    rest_lines[3].share()
    for line in image.qkv_sums + text.qkv_sums:
        line.share()
    for s in streams:
        end_sums(s)
    for line in [text_line] + rest_lines + image.qkv_sums + text.qkv_sums:
        line.finish()
    plane.sent()
    for s in streams:
        s.qkv_plane.sent()
        for copy in s.sums_done:
            copy.wait_send()
        s.write.wait()


def last(streams):
    vmem, hbm = pl.BlockSpec(memory_space=pltpu.VMEM), pl.BlockSpec(memory_space=pl.ANY)
    out_shape, scratch = [], []
    for messages, do, o, lse, seg, first, x, small, weight, dmid, rest, sums in streams:
        tokens, width = x.shape
        own = weight.shape[2]
        rest_shape, qkv_shape = (width // 4, rest.shape[1]), (width // 4, 3 * own)
        out_shape += [
            jax.ShapeDtypeStruct((tokens, width), F32),
            jax.ShapeDtypeStruct(small.shape, F32),
            jax.ShapeDtypeStruct(rest_shape, BF16),
            jax.ShapeDtypeStruct(qkv_shape, BF16),
        ]
        scratch += [
            pltpu.VMEM(messages.shape, BF16),
            pltpu.VMEM(do.shape, BF16),
            pltpu.VMEM(do.shape, BF16),
            pltpu.VMEM((4 * tokens, LANES), BF16),
            pltpu.VMEM((4 * tokens, LANES), BF16),
            pltpu.VMEM((1 if own == 4 * HD else 2, 4 * tokens, LANES), BF16),
            pltpu.VMEM((tokens, width), F32),
            pltpu.VMEM((1 if own == 4 * HD else 2, 4 * tokens, LANES), F32),
            pltpu.VMEM(messages.shape, BF16),
            pltpu.VMEM(messages.shape, BF16),
            pltpu.VMEM((tokens, 3 * own), BF16),
            pltpu.VMEM(weight.shape, BF16),
            pltpu.VMEM(first.shape, BF16),
            pltpu.VMEM((tokens, width), BF16),
            pltpu.VMEM((tokens, width), F32),
            pltpu.VMEM((tokens, width), F32),
            pltpu.VMEM((tokens, width), F32),
            pltpu.VMEM((width, 3 * own), BF16),
            pltpu.VMEM(small.shape, F32),
            pltpu.VMEM(small.shape, F32),
            pltpu.VMEM((2,) + small.shape, F32),
            pltpu.VMEM((4,) + small.shape, F32),
        ]
        scratch += LineSum.scratch(*rest_shape) + LineSum.scratch(*qkv_shape)
        scratch += PlaneSum.arrivals(*qkv_shape)
    scratch += PlaneSum.arrivals(*rest_shape) + PlaneSum.loads_scratch(*rest_shape)
    specs = [hbm, hbm, hbm, vmem, vmem, hbm, hbm, vmem, hbm, hbm, vmem, vmem]
    specs += specs[:10] + [hbm, vmem]
    results = pl.pallas_call(
        last_kernel,
        out_shape=out_shape,
        in_specs=specs,
        out_specs=[hbm, vmem, vmem, vmem] * 2,
        scratch_shapes=scratch + copy_sems(2 * (3 + 1 + 5 + 6) + 3 + 6 + 3 * 8, 2 * (1 + 7 + 1) + 3 + 1),
        compiler_params=pltpu.CompilerParams(
            collective_id=2, has_side_effects=True, vmem_limit_bytes=64 * 1024 * 1000
        ),
        name="last",
    )(*streams[0], *streams[1])
    return results[:4], results[4:]


def take_own(group, row):
    columns = row.shape[1] // 4
    return pltpu.roll(row, (4 - group) % 4 * columns, 1)[:, :columns]


FINISH_IN, FINISH_OUT = 5, 9


def finish_kernel(*refs):
    ins = [refs[:FINISH_IN], refs[FINISH_IN : 2 * FINISH_IN]]
    refs = refs[2 * FINISH_IN :]
    outs = [refs[:FINISH_OUT], refs[FINISH_OUT : 2 * FINISH_OUT]]
    refs = refs[2 * FINISH_OUT :]
    count = FINISH_IN + FINISH_OUT - 2
    scratch = [refs[:count], refs[count : 2 * count]]
    reads, writes = refs[2 * count :]
    streams, written = [], []

    def write(src, dst):
        copy = pltpu.make_async_copy(src, dst, writes.at[len(written)])
        copy.start()
        written.append(copy)

    for which, (in_refs, own) in enumerate(zip(ins, scratch)):
        streams.append([])
        for index in range(FINISH_IN):
            copy = pltpu.make_async_copy(
                in_refs[index], own[index], reads.at[which * FINISH_IN + index]
            )
            copy.start()
            streams[which].append(copy)
    for copies, out, own in reversed(list(zip(streams, outs, scratch))):
        sums, rest, qkv, y, grad, gains, shifts, bias, qkv_out, proj, up, down = own
        copies[1].wait()
        width = qkv.shape[1] // 3
        hidden = up.shape[1]
        up[...] = rest[:, width : width + hidden].astype(F32)
        write(up, out[5])
        if down.shape[0] > down.shape[1]:
            down[...] = jnp.transpose(rest[:, width + hidden :].astype(F32))
            proj[...] = jnp.transpose(rest[:, :width].astype(F32))
        else:
            down[...] = rest[:, width + hidden :].astype(F32)
            proj[...] = rest[:, :width].astype(F32)
        write(down, out[6])
        write(proj, out[4])
        copies[2].wait()
        for index in range(3):
            qkv_out[index] = qkv[:, index * width : (index + 1) * width].astype(F32)
        write(qkv_out, out[3])
        copies[3].wait()
        write(y, out[7])
        copies[4].wait()
        write(grad, out[8])
        copies[0].wait()
        group = lax.axis_index(FSDP)
        rows = take_own(group, sums[0:8])
        gains[...] = rows[0:2]
        shifts[...] = rows[2:6]
        line = jnp.concatenate([sums[6:7], sums[7:8], sums[8:9]], axis=1)
        bias[...] = take_own(group, jnp.broadcast_to(line, (8, line.shape[1])))[0:1]
        write(gains, out[0])
        write(shifts, out[1])
        write(bias, out[2])
    for copy in written:
        copy.wait()


def finish(streams):
    hbm = pl.BlockSpec(memory_space=pl.ANY)
    out_shape, scratch = [], []
    for sums, rest, qkv, y, grad, flip in streams:
        rows, own = qkv.shape[0], qkv.shape[1] // 3
        hidden = (rest.shape[1] - own) // 2
        shapes = [(2, rows), (4, rows), (1, 3 * rows), (3, rows, own)]
        shapes += [(own, rows), (rows, hidden), (hidden, rows)] if flip else [
            (rows, own), (rows, hidden), (rows, hidden)
        ]
        out_shape += [jax.ShapeDtypeStruct(shape, F32) for shape in shapes]
        out_shape += [jax.ShapeDtypeStruct(a.shape, a.dtype) for a in (y, grad)]
        scratch += [pltpu.VMEM(a.shape, a.dtype) for a in (sums, rest, qkv, y, grad)]
        scratch += [pltpu.VMEM(shape, F32) for shape in shapes]
    results = pl.pallas_call(
        finish_kernel,
        out_shape=out_shape,
        in_specs=[hbm] * (2 * FINISH_IN),
        out_specs=[hbm] * (2 * FINISH_OUT),
        scratch_shapes=scratch
        + [
            pltpu.SemaphoreType.DMA((2 * FINISH_IN,)),
            pltpu.SemaphoreType.DMA((2 * FINISH_OUT,)),
        ],
        compiler_params=pltpu.CompilerParams(vmem_limit_bytes=64 * 1024 * 1000),
        name="finish",
    )(*streams[0][:FINISH_IN], *streams[1][:FINISH_IN])
    return results[:FINISH_OUT], results[FINISH_OUT:]


def on_device(*args):
    streams = []
    for item, causal in ((args[10:], True), (args[:10], False)):
        s = Bag()
        rows, s.seg, cotangent, s.gains, s.shifts, s.head_bias, s.qkv, proj, s.up, down = item
        s.flip, s.x, s.dy = causal, rows[0], cotangent[0]
        s.down, s.proj = (down, proj) if causal else (down.T, proj.T)
        streams.append(s)
    started = front(
        [(s.x, s.seg, s.gains, s.shifts, s.head_bias, s.qkv, s.up, s.down, s.proj) for s in streams]
    )
    for s, (weight, small, first, messages, proj, up, down, o, lse, o_got) in zip(streams, started):
        s.weight, s.small, s.first, s.messages, s.o, s.lse = weight, small, first, messages, o, lse
        s.weights, s.o_got = (proj, up, down), o_got
    done = middle([(s.o_got, s.x, s.dy, s.small, *s.weights) for s in streams])
    ended = last(
        [
            (s.messages, do, s.o, s.lse, s.seg, s.first, s.x, s.small, s.weight, dmid, rest, sums)
            for s, (y, dmid, do, rest, sums) in zip(streams, done)
        ]
    )
    final = finish(
        [
            (sums, rest, qkv, y, grad, s.flip)
            for s, (y, *_), (grad, sums, rest, qkv) in zip(streams, done, ended)
        ]
    )
    outputs = []
    for s, (gains, shifts, bias, qkv, proj, up, down, y, grad_rows) in zip(streams, final):
        if not s.flip:
            proj, down = proj.T, down.T
        outputs.append((y[None], grad_rows[None], gains, shifts, bias, qkv, proj, up, down))
    return outputs[1] + outputs[0]


def layer_stats(rows):
    row_mean = jnp.mean(rows, axis=-1, keepdims=True)
    centred = rows - row_mean
    inv_std = lax.rsqrt(jnp.mean(centred * centred, axis=-1, keepdims=True) + 1e-05)
    return (centred * inv_std, inv_std)


def norm_back(grad_normed_out, normed, inv_std, gain):
    scaled = grad_normed_out * gain
    return inv_std * (
        scaled
        - jnp.mean(scaled, axis=-1, keepdims=True)
        - normed * jnp.mean(scaled * normed, axis=-1, keepdims=True)
    )


def tensor_psum(partial_rows):
    return lax.psum(partial_rows, TP)


def any_mesh_block(
    rows_in,
    seg_row,
    cotangent,
    gains,
    shifts,
    head_bias,
    qkv_weight,
    proj_weight,
    up_weight,
    down_weight,
    causal,
):
    gain_full, shift_full, bias_full, qkv_full, proj_full, up_full, down_full = (
        lax.all_gather(gains, FSDP, axis=1, tiled=True),
        lax.all_gather(shifts, FSDP, axis=1, tiled=True),
        lax.all_gather(head_bias, FSDP, axis=1, tiled=True),
        lax.all_gather(qkv_weight, FSDP, axis=1, tiled=True),
        lax.all_gather(proj_weight, FSDP, axis=1, tiled=True),
        lax.all_gather(up_weight, FSDP, axis=0, tiled=True),
        lax.all_gather(down_weight, FSDP, axis=1, tiled=True),
    )
    gain_vals = gain_full.astype(jnp.float32)
    shift_vals = shift_full.astype(jnp.float32)
    bias_vals = bias_full[0].astype(jnp.float32)
    tp_width = qkv_full.shape[2]
    local_rows = rows_in.shape[1]
    seq_length = seg_row.shape[1]
    head_local = tp_width // HD
    rows = rows_in[0].astype(jnp.float32)
    row_start = lax.axis_index(CTX) * local_rows
    seg_all = seg_row[0]
    seg_query = lax.dynamic_slice_in_dim(seg_all, row_start, local_rows)
    query_pos = row_start + jnp.arange(local_rows, dtype=jnp.int32)
    key_pos = jnp.arange(seq_length, dtype=jnp.int32)
    allowed = seg_query[:, None] == seg_all[None, :]
    if causal:
        allowed = jnp.logical_and(allowed, key_pos[None, :] <= query_pos[:, None])

    def to_heads(matrix):
        return matrix.reshape(matrix.shape[0], head_local, HD).transpose(1, 0, 2)

    def from_heads(stacked):
        return stacked.transpose(1, 0, 2).reshape(stacked.shape[1], head_local * HD)

    normed_one, inv_one = layer_stats(rows)
    first_in = (normed_one * gain_vals[0] + shift_vals[0]).astype(jnp.bfloat16)
    queries = (
        jnp.dot(first_in, qkv_full[0], preferred_element_type=jnp.float32) + bias_vals[:tp_width]
    ).astype(jnp.bfloat16)
    key_rows = jnp.dot(first_in, qkv_full[1], preferred_element_type=jnp.float32).astype(
        jnp.bfloat16
    )
    values = (
        jnp.dot(first_in, qkv_full[2], preferred_element_type=jnp.float32)
        + bias_vals[tp_width : 2 * tp_width]
    ).astype(jnp.bfloat16)
    key_all, value_all = (
        lax.all_gather(key_rows, CTX, axis=0, tiled=True),
        lax.all_gather(values, CTX, axis=0, tiled=True),
    )
    query_heads = to_heads(queries)
    key_heads = to_heads(key_all)
    value_heads = to_heads(value_all)

    def attend(head_items):
        query_h, key_h, value_h = head_items
        scores = dot(query_h, key_h, ((1,), (1,))) * 0.125
        scores = jnp.where(allowed, scores, -1e30)
        row_top = jnp.max(scores, axis=-1, keepdims=True)
        weights = jnp.exp(scores - row_top)
        row_total = jnp.sum(weights, axis=-1, keepdims=True)
        weights_low = (weights / row_total).astype(jnp.bfloat16)
        mixed_h = dot(weights_low, value_h, ((1,), (0,)))
        return (mixed_h.astype(jnp.bfloat16), row_top[:, 0] + jnp.log(row_total[:, 0]))

    mixed_heads, log_totals = lax.map(attend, (query_heads, key_heads, value_heads))
    mixed = from_heads(mixed_heads)
    middle = (
        rows
        + tensor_psum(jnp.dot(mixed, proj_full, preferred_element_type=jnp.float32))
        + shift_vals[1]
    )
    normed_two, inv_two = layer_stats(middle)
    second_in = (normed_two * gain_vals[1] + shift_vals[2]).astype(jnp.bfloat16)
    hidden = (
        jnp.dot(second_in, up_full, preferred_element_type=jnp.float32) + bias_vals[2 * tp_width :]
    )
    sigma = jax.nn.sigmoid(1.702 * hidden)
    activated = (hidden * sigma).astype(jnp.bfloat16)
    output = (
        middle
        + tensor_psum(jnp.dot(activated, down_full, preferred_element_type=jnp.float32))
        + shift_vals[3]
    )
    grad_out = cotangent[0].astype(jnp.float32)
    grad_down_bias = jnp.sum(grad_out, axis=0)
    grad_branch = grad_out.astype(jnp.bfloat16)
    grad_down = dot(activated, grad_branch, ((0,), (0,)))
    grad_act = dot(grad_branch, down_full, ((1,), (1,)))
    grad_hidden = (grad_act * (sigma + 1.702 * hidden * sigma * (1.0 - sigma))).astype(jnp.bfloat16)
    grad_up_bias = jnp.sum(grad_hidden.astype(jnp.float32), axis=0)
    grad_up = dot(second_in, grad_hidden, ((0,), (0,)))
    grad_second = tensor_psum(
        dot(grad_hidden, up_full, ((1,), (1,)))
    )
    grad_gain_two = jnp.sum(grad_second * normed_two, axis=0)
    grad_shift_two = jnp.sum(grad_second, axis=0)
    grad_middle = grad_out + norm_back(grad_second, normed_two, inv_two, gain_vals[1])
    grad_proj_bias = jnp.sum(grad_middle, axis=0)
    grad_attn = grad_middle.astype(jnp.bfloat16)
    grad_proj = dot(mixed, grad_attn, ((0,), (0,)))
    grad_mixed = dot(grad_attn, proj_full, ((1,), (1,))).astype(jnp.bfloat16)

    def attend_back(head_items):
        query_h, key_h, value_h, grad_h, log_total = head_items
        scores = dot(query_h, key_h, ((1,), (1,))) * 0.125
        weights = jnp.where(allowed, jnp.exp(scores - log_total[:, None]), 0.0)
        grad_weights = dot(grad_h, value_h, ((1,), (1,)))
        row_delta = jnp.sum(weights * grad_weights, axis=-1, keepdims=True)
        grad_scores = (weights * (grad_weights - row_delta)).astype(jnp.bfloat16)
        grad_query_h = (
            dot(grad_scores, key_h, ((1,), (0,))) * 0.125
        )
        grad_key_h = (
            dot(grad_scores, query_h, ((0,), (0,)))
            * 0.125
        )
        grad_value_h = dot(weights.astype(jnp.bfloat16), grad_h, ((0,), (0,)))
        return (grad_query_h, grad_key_h, grad_value_h)

    query_parts, key_parts, value_parts = lax.map(
        attend_back, (query_heads, key_heads, value_heads, to_heads(grad_mixed), log_totals)
    )
    key_sum, value_sum = (
        lax.psum_scatter(from_heads(key_parts), CTX, scatter_dimension=0, tiled=True),
        lax.psum_scatter(from_heads(value_parts), CTX, scatter_dimension=0, tiled=True),
    )
    grad_query = from_heads(query_parts).astype(jnp.bfloat16)
    grad_key = key_sum.astype(jnp.bfloat16)
    grad_value = value_sum.astype(jnp.bfloat16)
    grad_qkv = jnp.stack(
        [
            dot(first_in, grad_query, ((0,), (0,))),
            dot(first_in, grad_key, ((0,), (0,))),
            dot(first_in, grad_value, ((0,), (0,))),
        ]
    )
    grad_head = jnp.concatenate(
        [
            jnp.sum(grad_query.astype(jnp.float32), axis=0),
            jnp.sum(grad_value.astype(jnp.float32), axis=0),
            grad_up_bias,
        ]
    )[None, :]
    grad_first_part = dot(grad_query, qkv_full[0], ((1,), (1,)))
    grad_first_part = grad_first_part + dot(grad_key, qkv_full[1], ((1,), (1,)))
    grad_first_part = grad_first_part + dot(grad_value, qkv_full[2], ((1,), (1,)))
    grad_first = tensor_psum(grad_first_part)
    grad_gain_one = jnp.sum(grad_first * normed_one, axis=0)
    grad_shift_one = jnp.sum(grad_first, axis=0)
    grad_rows = grad_middle + norm_back(grad_first, normed_one, inv_one, gain_vals[0])
    grad_gains = jnp.stack([grad_gain_one, grad_gain_two])
    grad_shifts = jnp.stack([grad_shift_one, grad_proj_bias, grad_shift_two, grad_down_bias])
    share_gains, share_shifts, share_head, share_qkv, share_proj, share_up, share_down = (
        lax.psum_scatter(grad_gains, FSDP, scatter_dimension=1, tiled=True),
        lax.psum_scatter(grad_shifts, FSDP, scatter_dimension=1, tiled=True),
        lax.psum_scatter(grad_head, FSDP, scatter_dimension=1, tiled=True),
        lax.psum_scatter(grad_qkv, FSDP, scatter_dimension=1, tiled=True),
        lax.psum_scatter(grad_proj, FSDP, scatter_dimension=1, tiled=True),
        lax.psum_scatter(grad_up, FSDP, scatter_dimension=0, tiled=True),
        lax.psum_scatter(grad_down, FSDP, scatter_dimension=1, tiled=True),
    )
    owned = lax.psum(
        (share_gains, share_shifts, share_head, share_qkv, share_proj, share_up, share_down), CTX
    )
    return (output.astype(jnp.bfloat16)[None], grad_rows[None]) + tuple(owned)


def on_any_mesh(
    image_input,
    image_segments,
    image_cotangent,
    image_gains,
    image_shifts,
    image_head_bias,
    image_qkv_weight,
    image_proj_weight,
    image_up_weight,
    image_down_weight,
    text_input,
    text_segments,
    text_cotangent,
    text_gains,
    text_shifts,
    text_head_bias,
    text_qkv_weight,
    text_proj_weight,
    text_up_weight,
    text_down_weight,
):
    image_results = any_mesh_block(
        image_input,
        image_segments,
        image_cotangent,
        image_gains,
        image_shifts,
        image_head_bias,
        image_qkv_weight,
        image_proj_weight,
        image_up_weight,
        image_down_weight,
        False,
    )
    text_results = any_mesh_block(
        text_input,
        text_segments,
        text_cotangent,
        text_gains,
        text_shifts,
        text_head_bias,
        text_qkv_weight,
        text_proj_weight,
        text_up_weight,
        text_down_weight,
        True,
    )
    return image_results + text_results


def stream_specs():
    return (
        P(FSDP, CTX, None),
        P(FSDP, None),
        P(FSDP, CTX, None),
        P(None, FSDP),
        P(None, FSDP),
        P(TP, FSDP),
        P(None, FSDP, TP),
        P(TP, FSDP),
        P(FSDP, TP),
        P(TP, FSDP),
    )


def solution(mesh):
    one = stream_specs()
    grads = (one[0], one[0]) + one[3:]
    body = on_device
    if (mesh.shape[FSDP], mesh.shape[CTX], mesh.shape[TP]) != (4, 4, 2):
        body = on_any_mesh
    return jax.shard_map(
        body, mesh=mesh, in_specs=one + one, out_specs=grads + grads, check_vma=False
    )
```

```python
import functools

import jax
import jax.numpy as jnp
from jax import lax
from jax.experimental import pallas as pl
from jax.experimental.pallas import tpu as pltpu
from jax.sharding import PartitionSpec as P

HD = 64
LANES = 128
QB = 256
KB = 512
NEG = -1e30
F32 = jnp.float32
MESH = pl.DeviceIdType.MESH
FSDP, CTX, TP = "fsdp", "ctx", "tp"
BF16 = jnp.bfloat16


def dot(left, right, dims=((1,), (0,))):
    return lax.dot_general(left, right, (dims, ((), ())), preferred_element_type=F32)


def lane_marks():
    lane = lax.broadcasted_iota(jnp.int32, (1, LANES), 1)
    first = (lane < HD).astype(F32).astype(BF16)
    second = (lane >= HD).astype(F32).astype(BF16)
    return first, second


def document_features(row_ref, query_out, key_out):
    lane = lax.broadcasted_iota(jnp.int32, (LANES, LANES), 1) % HD
    for start in range(0, query_out.shape[0], LANES):
        row = row_ref[:, start : start + LANES].astype(F32)
        same = jnp.transpose(jnp.broadcast_to(row, (LANES, LANES))) == lane.astype(F32)
        query_out[start : start + LANES, :] = jnp.where(same, 1.0, 0.0).astype(BF16)
        key_out[start : start + LANES, :] = jnp.where(same, 0.0, NEG).astype(BF16)


def swap_halves(value):
    return pltpu.roll(value, HD, 1)


def key_range(index):
    return slice(index * KB, (index + 1) * KB)


def pick(flag, one, zero):
    return jnp.where(flag == 1, one, zero)


def query_rows(head):
    return pl.ds(pl.multiple_of(head * (QB + 2 * KB), QB), QB)


def key_rows(head):
    return pl.ds(pl.multiple_of(QB + head * KB, QB), KB)


def mark_keys(m, features, heads, score_keys, value_keys):
    first, second = lane_marks()
    for head in range(heads):
        for index in range(4):
            block = m[index, key_rows(head)]
            score_keys[head, key_range(index)] = block * first + features[key_range(index), :] * second
            if value_keys is not None:
                value_keys[head, key_range(index)] = block * second + first


def later(index, shape, axis, query_start):
    key_pos = index * KB + lax.broadcasted_iota(jnp.int32, shape, axis)
    query_pos = query_start + lax.broadcasted_iota(jnp.int32, shape, 1 - axis)
    return key_pos > query_pos


def mix_rows(query, score_keys, value_keys, head, blocks, query_start=None):
    scores = []
    for index in range(blocks):
        score = dot(query, score_keys[head, key_range(index)], ((1,), (1,)))
        if query_start is not None:
            score = jnp.where(later(index, score.shape, 1, query_start), NEG, score)
        scores.append(score)
    top = jnp.max(functools.reduce(jnp.maximum, scores), axis=1, keepdims=True)
    acc = jnp.zeros((query.shape[0], LANES), F32)
    for index, score in enumerate(scores):
        acc = acc + dot(jnp.exp(score - top).astype(BF16), value_keys[head, key_range(index)])
    return acc / swap_halves(acc), top + jnp.log(acc)


def text_task(at, task):
    return 0, task // 2, task % 2


def image_task(at, task):
    shared = 1 - (task + 8) // 12
    step = 5 - task // 2
    low, high = (at.here_low + step % 2) % 2, (at.here_high + step // 2) % 2
    return shared, pick(shared, at.here_high * 2 + task // 2, high * 2 + low), task % 2


def attend(at, m, features, score_keys, value_keys, o, lse, task_of, begin, end, blocks, causal):
    first, second = lane_marks()
    lane = lax.broadcasted_iota(jnp.int32, (QB, LANES), 1)

    def one(task, carry):
        head, source, half = task_of(at, task)
        start = (source * 2 + half) * QB
        query = m[source, query_rows(head)].astype(F32)
        query = pick(half, swap_halves(query), query).astype(BF16)
        query = query * first + features[pl.ds(pl.multiple_of(start, QB), QB), :] * second
        mixed, log_total = mix_rows(
            query, score_keys, value_keys, head, blocks, start if causal else None
        )
        lse[task] = jnp.transpose(log_total)[:8]
        mixed = pick(half, mixed, swap_halves(mixed)).astype(BF16)
        rows = pl.ds(pl.multiple_of(head * QB, QB), QB)
        o[source, rows] = jnp.where(lane // HD == half, mixed, o[source, rows])
        return carry

    lax.fori_loop(begin, end, one, 0)


def unattend(at, m, do, o, lse, features, score_keys, acc, out, task_of, begin, end, blocks, causal):
    first, second = lane_marks()
    lane = lax.broadcasted_iota(jnp.int32, (QB, LANES), 1)

    def one(task, carry):
        head, source, half = task_of(at, task)
        start = (source * 2 + half) * QB
        rows = pl.ds(pl.multiple_of(head * QB, QB), QB)
        query, grad_o = m[source, query_rows(head)].astype(F32), do[source, rows].astype(F32)
        product = jnp.transpose(grad_o * o[source, rows].astype(F32))
        delta = jnp.sum(pick(half, product[HD:], product[:HD]), axis=0, keepdims=True)
        query = pick(half, swap_halves(query), query).astype(BF16) * first
        grad_o = pick(half, grad_o, swap_halves(grad_o)).astype(BF16) * second
        marked = query + features[pl.ds(pl.multiple_of(start, QB), QB), :] * second
        row_lse = lse[task, :1]
        grad_query = jnp.zeros((QB, LANES), F32)
        for index in range(blocks):
            keys = m[index, key_rows(head)]
            score = dot(score_keys[head, key_range(index)], marked, ((1,), (1,)))
            if causal:
                score = jnp.where(later(index, score.shape, 0, start), NEG, score)
            weights = jnp.exp(score - row_lse)
            grad_weights = dot(keys, grad_o, ((1,), (1,)))
            grad_scores = (weights * (grad_weights - delta)).astype(BF16)
            acc[head, key_range(index)] += dot(grad_scores, query) + dot(weights.astype(BF16), grad_o)
            grad_query = grad_query + dot(grad_scores, keys, ((0,), (0,)))
        grad_query = grad_query * 0.125
        grad_query = pick(half, swap_halves(grad_query), grad_query).astype(BF16)
        out[source, query_rows(head)] = jnp.where(
            lane // HD == half, grad_query, out[source, query_rows(head)]
        )
        return carry

    lax.fori_loop(begin, end, one, 0)


def key_gradients(acc, out, head):
    for index in range(4):
        out[index, key_rows(head)] = acc[head, key_range(index)].astype(BF16)


class Bag:
    pass


def partners():
    at = Bag()
    group, here, core = lax.axis_index(FSDP), lax.axis_index(CTX), lax.axis_index(TP)
    at.group, at.here, at.core = group, here, core
    at.group_x = group + 1 - 2 * (group % 2)
    at.group_y = group + 2 - 4 * (group // 2)
    at.group_far = 3 - group
    at.here_low, at.here_high = here % 2, here // 2
    at.inner, at.outer = (here + 1) // 2 == 1, (here + 1) // 2 != 1
    at.ctx = (here, here + 1 - 2 * (here % 2), here + 2 - 4 * (here // 2), 3 - here)
    at.to_x, at.to_y, at.to_far = ({FSDP: g} for g in (at.group_x, at.group_y, at.group_far))
    at.to_ctx = [{CTX: c} for c in at.ctx]
    at.to_core = {TP: 1 - core}
    return at


def greet(devices):
    barrier = pltpu.get_barrier_semaphore()
    for device in devices:
        pl.semaphore_signal(barrier, inc=1, device_id=device, device_id_type=MESH)


def meet(devices):
    pl.semaphore_wait(pltpu.get_barrier_semaphore(), len(devices))


class Copies:
    def __init__(self, send_sems, recv_sems, local_sems):
        self.sems = (send_sems, recv_sems, local_sems)
        self.used = [0, 0]

    def remote(self, src, dst, device, start=True):
        index = self.used[0]
        self.used[0] += 1
        copy = pltpu.make_async_remote_copy(
            src_ref=src,
            dst_ref=dst,
            send_sem=self.sems[0].at[index],
            recv_sem=self.sems[1].at[index],
            device_id=device,
            device_id_type=MESH,
        )
        if start:
            copy.start()
        return copy

    def local(self, src, dst, start=True):
        index = self.used[1]
        self.used[1] += 1
        copy = pltpu.make_async_copy(src, dst, self.sems[2].at[index])
        if start:
            copy.start()
        return copy


def copy_sems(remote, local):
    return [
        pltpu.SemaphoreType.DMA((remote,)),
        pltpu.SemaphoreType.DMA((remote,)),
        pltpu.SemaphoreType.DMA((local,)),
    ]


class Gather:
    def __init__(self, copies, at, src, dst):
        self.copies, self.at, self.dst = copies, at, dst
        self.rows = src.shape[-2]
        own = self.part(at.group, 0, self.rows)
        self.own = copies.local(src, own)
        self.to_x = copies.remote(src, own, at.to_x)
        self.to_y = copies.remote(src, own, at.to_y)

    def part(self, owner, offset, size):
        rows = pl.ds(pl.multiple_of(owner * self.rows + offset, 8), size)
        return self.dst.at[:, rows, :] if len(self.dst.shape) == 3 else self.dst.at[rows, :]

    def near(self):
        self.own.wait()
        self.to_x.wait()
        self.to_y.wait()

    def forward(self):
        half = self.rows // 2
        self.to_x.wait_recv()
        self.to_y.wait_recv()
        top = self.part(self.at.group_y, 0, half)
        low = self.part(self.at.group_x, half, half)
        self.far_x = self.copies.remote(top, top, self.at.to_x)
        self.far_y = self.copies.remote(low, low, self.at.to_y)

    def arrived(self):
        self.own.wait()
        self.far_x.wait_recv()
        self.far_y.wait_recv()

    def sent(self):
        for copy in (self.to_x, self.to_y, self.far_x, self.far_y):
            copy.wait_send()


def normalise(rows):
    mean = jnp.mean(rows, axis=-1, keepdims=True)
    centred = rows - mean
    inv = lax.rsqrt(jnp.mean(centred * centred, axis=-1, keepdims=True) + 1e-05)
    return centred * inv, inv


def lane_pair(low, high):
    lane = lax.broadcasted_iota(jnp.int32, low[0].shape, 1)
    left = low[0] if low[1] == 0 else pltpu.roll(low[0], HD, 1)
    right = high[0] if high[1] == 1 else pltpu.roll(high[0], HD, 1)
    return jnp.where(lane < HD, left, right)


def head_tile(ref, start, index, rows=slice(None)):
    first = start + (index // 2) * LANES
    return ref[rows, first : first + LANES], index % 2


def halves_pair(ref, start, index):
    half = ref.shape[0] // 2
    return lane_pair(
        head_tile(ref, start, index, slice(0, half)), head_tile(ref, start, index, slice(half, None))
    ).astype(BF16)


def write_messages(qkv, out, heads):
    width = heads * HD

    def keys_values(index):
        return lane_pair(head_tile(qkv, width, index), head_tile(qkv, 2 * width, index)).astype(BF16)

    for c in range(4):
        out[c, query_rows(0)] = halves_pair(qkv, 0, c)
        out[c, key_rows(0)] = keys_values(c)
        if heads == 6:
            out[c, key_rows(1)] = keys_values(4 + c % 2)
            out[c, query_rows(1)] = halves_pair(qkv, 0, 4 + c % 2)


def message_shape(heads, tokens):
    return (4, (heads // 2 - 1) * (QB + tokens), LANES)


def mixed_shape(heads):
    return (4, (heads // 2 - 1) * QB, LANES)


def first_rows(x_ref, small_ref, normal_ref, first_ref, rows):
    normed, _ = normalise(x_ref[rows, :].astype(F32))
    first = (normed * small_ref[0:1] + small_ref[2:3]).astype(BF16)
    normal_ref[rows, :] = first
    first_ref[:, rows] = jnp.transpose(first)


def project_rows(normal_ref, small_ref, weight_ref, qkv_ref, rows):
    width = weight_ref.shape[2]
    first = normal_ref[rows, :]
    bias = small_ref[6:7]
    qkv_ref[rows, :width] = (dot(first, weight_ref[0]) + bias[:, :width]) * 0.125
    qkv_ref[rows, width : 2 * width] = dot(first, weight_ref[1])
    qkv_ref[rows, 2 * width :] = dot(first, weight_ref[2]) + bias[:, width : 2 * width]


def spread_small(at, gains, shifts, bias, wide, flat, out):
    width = wide.shape[1]
    columns, bias_columns = gains.shape[1], bias.shape[1]
    wide[...] = jnp.zeros_like(wide)
    flat[...] = jnp.zeros_like(flat)
    wide[0:2, :columns] = gains[...].astype(F32)
    wide[2:6, :columns] = shifts[...].astype(F32)
    flat[0:1, :bias_columns] = bias[...].astype(F32)
    out[0:8] = pltpu.roll(wide[...], at.group * columns, 1)
    line = pltpu.roll(flat[...], at.group * bias_columns, 1)
    out[8:16] = jnp.zeros((8, width), F32)
    for row in range(3):
        out[6 + row : 7 + row] = line[0:1, row * width : (row + 1) * width]


FRONT_IN, FRONT_OUT, FRONT_SCRATCH = 9, 10, 21


def front_kernel(*refs):
    at = partners()
    ins = [refs[:FRONT_IN], refs[FRONT_IN : 2 * FRONT_IN]]
    refs = refs[2 * FRONT_IN :]
    outs = [refs[:FRONT_OUT], refs[FRONT_OUT : 2 * FRONT_OUT]]
    refs = refs[2 * FRONT_OUT :]
    scratch = [refs[:FRONT_SCRATCH], refs[FRONT_SCRATCH : 2 * FRONT_SCRATCH]]
    copies = Copies(*refs[2 * FRONT_SCRATCH :])
    others = [at.to_x, at.to_y, at.to_far] + at.to_ctx[1:]
    greet(others)
    streams = []
    for in_refs, out_refs, own in zip(ins, outs, scratch):
        s = Bag()
        s.x_in, s.seg_row, s.gains, s.shifts, s.bias, s.qkv, s.up_in, s.down_in, s.proj_in = in_refs
        (
            s.weight_out, s.small, s.first_out, s.messages, s.proj_full, s.up_full, s.down_full,
            s.o_out, s.lse, s.o_got,
        ) = out_refs
        (
            s.small_in, s.small_own, s.wide, s.flat, s.rows, s.mine, s.got, s.down_t, s.proj_t,
            s.query_doc, s.key_doc, s.score_keys, s.value_keys, s.x, s.up, s.down, s.proj, s.weight, s.first,
        ) = own[:19]
        s.o, s.normal = own[19:]
        s.heads = s.weight.shape[2] // HD
        s.features = (s.query_doc, s.key_doc)
        s.reads = [
            copies.local(src, dst)
            for src, dst in (
                (s.x_in, s.x), (s.proj_in, s.proj), (s.up_in, s.up), (s.down_in, s.down),
            )
        ]
        streams.append(s)
    text, image = streams
    for s in (image, text):
        spread_small(at, s.gains, s.shifts, s.bias, s.wide, s.flat, s.small_own)
        document_features(s.seg_row, *s.features)
    meet(others)
    text.gather = Gather(copies, at, text.qkv, text.weight)
    for s in (text, image):
        s.small_done = [
            copies.remote(s.small_own, s.small_in.at[i], device)
            for i, device in enumerate((at.to_x, at.to_y, at.to_far))
        ]
        for copy in s.reads:
            copy.wait()
    text.down_t[...] = jnp.transpose(text.down[...])
    text.proj_t[...] = jnp.transpose(text.proj[...])
    text.gather.forward()
    image.gather = Gather(copies, at, image.qkv, image.weight)

    def project(s):
        for copy in s.small_done:
            copy.wait_recv()
        s.small[...] = s.small_own[...] + s.small_in[0] + s.small_in[1] + s.small_in[2]
        for rows in chunks(s.x.shape[0]):
            first_rows(s.x, s.small, s.normal, s.first, rows)
        s.gather.arrived()
        for rows in chunks(s.x.shape[0]):
            project_rows(s.normal, s.small, s.weight, s.rows, rows)
        write_messages(s.rows, s.mine, s.heads)
        s.writes = [copies.local(s.weight, s.weight_out), copies.local(s.first, s.first_out)]

    def gather_rest(s):
        pieces = (s.proj_t, s.up, s.down_t) if s.heads == 4 else (s.proj, s.up, s.down)
        s.rest = [
            Gather(copies, at, piece, full)
            for piece, full in zip(pieces, (s.proj_full, s.up_full, s.down_full))
        ]

    project(text)
    text.sends = send_blocks(copies, at, text.mine, text.got)
    image.gather.forward()
    gather_rest(text)
    project(image)
    image.sends = send_blocks(copies, at, image.mine, image.got)
    gather_rest(image)
    s = text
    for copy in s.sends:
        copy.wait()
    s.writes.append(copies.local(s.got, s.messages))
    s.o[...] = jnp.zeros_like(s.o)
    mark_keys(s.got, s.features[1], 1, s.score_keys, s.value_keys)
    attend(
        at, s.got, s.features[0], s.score_keys, s.value_keys, s.o, s.lse, text_task, 0, 8, 4, True
    )
    for gather in s.rest:
        gather.forward()
    s = image
    for copy in s.sends:
        copy.wait()
    text.o_done = send_blocks(copies, at, text.o, text.o_got)
    s.writes.append(copies.local(s.got, s.messages))
    s.o[...] = jnp.zeros_like(s.o)
    mark_keys(s.got, s.features[1], 2, s.score_keys, s.value_keys)
    s.o_done = send_blocks(copies, at, s.o, s.o_got, start=False)

    def image_pair(index, carry):
        attend(
            at, image.got, image.features[0], image.score_keys, image.value_keys, image.o, image.lse,
            image_task, 2 * index, 2 * index + 2, 4, False,
        )
        for step, copy in enumerate(image.o_done):

            @pl.when(index == 5 - step)
            def _(copy=copy):
                copy.start()

        return carry

    lax.fori_loop(0, 6, image_pair, 0)
    s.rest[0].forward()
    for s in (text, image):
        s.writes.append(copies.local(s.o, s.o_out))
    whole = [image.gather, text.gather, image.rest[0]] + text.rest
    for gather in whole[2:]:
        gather.arrived()
    for gather in whole:
        gather.sent()
    for gather in image.rest[1:]:
        gather.near()
    for s in (image, text):
        for copy in s.small_done:
            copy.wait_send()
        for copy in s.writes + s.o_done:
            copy.wait()


def front(streams):
    vmem, hbm = pl.BlockSpec(memory_space=pltpu.VMEM), pl.BlockSpec(memory_space=pl.ANY)
    out_shape, out_specs, scratch = [], [], []
    for x, seg, gains, shifts, bias, qkv, up, down, proj in streams:
        tokens, width = x.shape
        own = qkv.shape[2]
        messages = message_shape(own // HD, tokens)
        hidden = up.shape[1]
        small = jax.ShapeDtypeStruct((16, width), F32)
        out_shape += [
            jax.ShapeDtypeStruct((3, width, own), BF16),
            small,
            jax.ShapeDtypeStruct((width, tokens), BF16),
            jax.ShapeDtypeStruct(messages, BF16),
            jax.ShapeDtypeStruct((width, own), BF16),
            jax.ShapeDtypeStruct((width, hidden), BF16),
            jax.ShapeDtypeStruct((width, hidden), BF16),
            jax.ShapeDtypeStruct(mixed_shape(own // HD), BF16),
            jax.ShapeDtypeStruct((2 * (own // HD), 8, QB), F32),
            jax.ShapeDtypeStruct(mixed_shape(own // HD), BF16),
        ]
        out_specs += [hbm, vmem, hbm, hbm, hbm, hbm, hbm, hbm, vmem, hbm]
        scratch += [
            pltpu.VMEM((3, 16, width), F32),
            pltpu.VMEM((16, width), F32),
            pltpu.VMEM((8, width), F32),
            pltpu.VMEM((8, 3 * width), F32),
            pltpu.VMEM((tokens, 3 * own), F32),
            pltpu.VMEM(messages, BF16),
            pltpu.VMEM(messages, BF16),
            pltpu.VMEM((width // 4, hidden), BF16),
            pltpu.VMEM((width // 4, own), BF16),
            pltpu.VMEM((4 * tokens, LANES), BF16),
            pltpu.VMEM((4 * tokens, LANES), BF16),
            pltpu.VMEM((1 if own == 4 * HD else 2, 4 * tokens, LANES), BF16),
            pltpu.VMEM((1 if own == 4 * HD else 2, 4 * tokens, LANES), BF16),
            pltpu.VMEM(x.shape, BF16),
            pltpu.VMEM(up.shape, BF16),
            pltpu.VMEM(down.shape, BF16),
            pltpu.VMEM(proj.shape, BF16),
            pltpu.VMEM((3, width, own), BF16),
            pltpu.VMEM((width, tokens), BF16),
            pltpu.VMEM(mixed_shape(own // HD), BF16),
            pltpu.VMEM((tokens, width), BF16),
        ]
    results = pl.pallas_call(
        front_kernel,
        out_shape=out_shape,
        in_specs=[hbm, vmem, vmem, vmem, vmem, vmem, hbm, hbm, hbm] * 2,
        out_specs=out_specs,
        scratch_shapes=scratch + copy_sems(2 * (3 + 4 * 4 + 6), 2 * 14),
        compiler_params=pltpu.CompilerParams(
            collective_id=0, has_side_effects=True, vmem_limit_bytes=63 << 20
        ),
        name="front",
    )(*streams[0], *streams[1])
    return results[:FRONT_OUT], results[FRONT_OUT:]


STEP = 384
TILES = 1


def by_columns(columns, body):
    def one(index, carry):
        body(pl.ds(pl.multiple_of(index * STEP, STEP), STEP))
        return carry

    lax.fori_loop(0, columns // STEP, one, 0)


class PlaneSum:
    def __init__(self, copies, at, src, arrivals, loads=None):
        self.copies, self.at = copies, at
        self.in_x, self.in_y, self.in_top, self.in_low = arrivals
        half, self.columns = self.in_top.shape
        self.half, rows = half, 2 * half

        def block(owner, offset, size=half):
            return src.at[pl.ds(pl.multiple_of(owner * rows + offset, 8), size), :]

        self.first = [
            copies.remote(block(at.group_far, 0), self.in_x.at[1], at.to_x),
            copies.remote(block(at.group_far, half), self.in_y.at[1], at.to_y),
            copies.remote(block(at.group_x, 0), self.in_x.at[0], at.to_x),
            copies.remote(block(at.group_y, half), self.in_y.at[0], at.to_y),
        ]
        parts = [block(at.group_y, 0), block(at.group_x, half), block(at.group, 0, rows)]
        if loads is None:
            self.loads = []
            self.pass_top, self.pass_low, self.own = parts
        else:
            self.loads = [copies.local(part, load) for part, load in zip(parts, loads)]
            self.pass_top, self.pass_low, self.own = loads
        self.second = [
            copies.remote(self.pass_top, self.in_top, at.to_y, False),
            copies.remote(self.pass_low, self.in_low, at.to_x, False),
        ]

    def cross(self):
        for copy in self.loads:
            copy.wait()
        self.first[0].wait_recv()

        def top(cols):
            self.pass_top[:, cols] = (
                self.pass_top[:, cols].astype(F32) + self.in_x[1, :, cols].astype(F32)
            ).astype(BF16)

        by_columns(self.columns, top)
        self.second[0].start()
        self.first[1].wait_recv()

        def low(cols):
            self.pass_low[:, cols] = (
                self.pass_low[:, cols].astype(F32) + self.in_y[1, :, cols].astype(F32)
            ).astype(BF16)

        by_columns(self.columns, low)
        self.second[1].start()

    def arrived(self):
        for copy in self.first[2:] + self.second:
            copy.wait_recv()

    def halves(self, cols):
        half = self.half
        return (
            self.own[:half, cols].astype(F32)
            + self.in_x[0, :, cols].astype(F32)
            + self.in_top[:, cols].astype(F32),
            self.own[half:, cols].astype(F32)
            + self.in_y[0, :, cols].astype(F32)
            + self.in_low[:, cols].astype(F32),
        )

    def sent(self):
        for copy in self.first + self.second:
            copy.wait_send()

    @staticmethod
    def arrivals(rows, columns):
        half = rows // 2
        pair, one = pltpu.VMEM((2, half, columns), BF16), pltpu.VMEM((half, columns), BF16)
        return [pair, pair, one, one]

    @staticmethod
    def loads_scratch(rows, columns):
        half = rows // 2
        one = pltpu.VMEM((half, columns), BF16)
        return [one, one, pltpu.VMEM((rows, columns), BF16)]


class LineSum:
    def __init__(self, copies, at, values, buffers, final, begin, end):
        self.at, self.values, self.final, self.range = at, values, final, (begin, end)
        self.pair, self.outer_in, self.inner_in = buffers

        def part(ref):
            return ref.at[:, begin:end]

        self.up = copies.remote(part(self.pair), part(self.outer_in), at.to_ctx[1], False)
        self.across = copies.remote(part(self.pair), part(self.inner_in), at.to_ctx[3], False)
        self.down = copies.remote(part(final), part(final), at.to_ctx[1], False)

    def each(self, body):
        begin, end = self.range

        def one(index, carry):
            body(pl.ds(pl.multiple_of(begin + index * STEP, LANES), STEP))
            return carry

        lax.fori_loop(0, (end - begin) // STEP, one, 0)

    def gather(self):
        half = self.pair.shape[0] // 2

        @pl.when(self.at.outer)
        def _():
            def add(cols):
                top, low = self.values(cols)
                self.pair[:half, cols] = top.astype(BF16)
                self.pair[half:, cols] = low.astype(BF16)

            self.each(add)
            self.up.start()

    def join(self):
        half = self.pair.shape[0] // 2

        @pl.when(self.at.inner)
        def _():
            self.up.wait_recv()

            def add(cols):
                top, low = self.values(cols)
                self.pair[:half, cols] = (top + self.outer_in[:half, cols].astype(F32)).astype(BF16)
                self.pair[half:, cols] = (low + self.outer_in[half:, cols].astype(F32)).astype(BF16)

            self.each(add)
            self.across.start()

    def share(self):
        @pl.when(self.at.inner)
        def _():
            self.across.wait_recv()

            def add(cols):
                self.final[:, cols] = (
                    self.pair[:, cols].astype(F32) + self.inner_in[:, cols].astype(F32)
                ).astype(BF16)

            self.each(add)
            self.down.start()

    def finish(self):
        @pl.when(self.at.outer)
        def _():
            self.up.wait_send()
            self.down.wait_recv()

        @pl.when(self.at.inner)
        def _():
            self.across.wait_send()
            self.down.wait_send()

    @staticmethod
    def scratch(rows, columns):
        return [pltpu.VMEM((rows, columns), BF16)] * 3


def chunks(tokens, size=256):
    return [slice(start, start + size) for start in range(0, tokens, size)]


def as_f32(ref, index, rows=slice(None)):
    return ref[index, rows].astype(F32)


def take_halves(got, out, at, heads, start, put):
    half = out.shape[0] // 2
    for tile in range(heads // 2):
        base = 0 if tile < 2 else start
        if tile < 2:
            one, two = 2 * tile, 2 * tile + 1
        else:
            one, two = at.here_high * 2, at.here_high * 2 + 1
        rows = slice(base, base + QB)
        left, right = as_f32(got, one, rows), as_f32(got, two, rows)
        for side in range(2):
            put(tile, slice(side * half, side * half + half), lane_pair((left, side), (right, side)))


def take_mixed(got, mixed, at, heads):
    def put(tile, rows, value):
        mixed[rows, tile * LANES : (tile + 1) * LANES] = value.astype(BF16)

    take_halves(got, mixed, at, heads, QB, put)


def write_grad_o(grad, out, heads):
    for c in range(4):
        out[c, :QB] = halves_pair(grad, 0, c)
        if heads == 6:
            out[c, QB:] = halves_pair(grad, 0, 4 + c % 2)


def send_blocks(copies, at, mine, out, begin=0, end=None, start=True):
    rows = mine.shape[1]
    end = rows if end is None else end
    far = min(end, rows if rows in (QB, QB + KB) else rows - QB)
    part = pl.ds(begin, end - begin)
    done = [copies.local(mine.at[at.here, part], out.at[at.here, part], start)]
    for other, device, last in zip(at.ctx[1:], at.to_ctx[1:], (end, far, far)):
        part = pl.ds(begin, last - begin)
        done.append(copies.remote(mine.at[other, part], out.at[at.here, part], device, start))
    return done


MIDDLE_IN, MIDDLE_OUT, MIDDLE_SCRATCH = 7, 5, 22


def middle_kernel(*refs):
    at = partners()
    ins = [refs[:MIDDLE_IN], refs[MIDDLE_IN : 2 * MIDDLE_IN]]
    refs = refs[2 * MIDDLE_IN :]
    outs = [refs[:MIDDLE_OUT], refs[MIDDLE_OUT : 2 * MIDDLE_OUT]]
    refs = refs[2 * MIDDLE_OUT :]
    scratch = [refs[:MIDDLE_SCRATCH], refs[MIDDLE_SCRATCH : 2 * MIDDLE_SCRATCH]]
    arrivals = refs[2 * MIDDLE_SCRATCH : 2 * MIDDLE_SCRATCH + 4]
    copies = Copies(*refs[2 * MIDDLE_SCRATCH + 4 :])
    others = [at.to_x, at.to_y] + at.to_ctx[1:] + [at.to_core]
    greet(others)
    streams = []
    for in_refs, out_refs, own in zip(ins, outs, scratch):
        s = Bag()
        o_in, x_in, dy_in, s.small, proj_in, up_in, down_in = in_refs
        s.y_out, s.dmid_out, s.do_out, s.rest_out, s.sums = out_refs
        (
            s.proj, s.up, s.down, s.rest, s.mixed, s.part, s.part_in, s.mid, s.first, s.first_t, s.dy_t,
            s.act, s.dz, s.grad, s.grad_in, s.do, s.do_mine, s.o, s.x, s.dy, s.y, s.dmid,
        ) = own
        s.heads = proj_in.shape[1] // HD
        s.o_done = copies.local(o_in, s.o)
        s.proj_done = copies.local(proj_in, s.proj)
        s.rows_done = [copies.local(x_in, s.x), copies.local(dy_in, s.dy)]
        s.weights = ((up_in, s.up), (down_in, s.down))
        streams.append(s)
    text, image = streams
    text.rest_done = [copies.local(src, dst) for src, dst in text.weights]
    quarter = image.up.shape[0] // 4
    near = [
        pl.ds(pl.multiple_of(owner * quarter, 8), quarter)
        for owner in (at.group, at.group_x, at.group_y)
    ]
    image.rest_done = [
        copies.local(src.at[rows, :], dst.at[rows, :])
        for src, dst in image.weights
        for rows in near
    ]
    meet(others)
    top = pl.ds(pl.multiple_of(at.group_y * quarter, 8), quarter // 2)
    low = pl.ds(pl.multiple_of(at.group_x * quarter + quarter // 2, 8), quarter // 2)
    image.far_done = []
    for src, dst in image.weights:
        image.far_done.append(copies.remote(src.at[top, :], dst.at[top, :], at.to_x))
        image.far_done.append(copies.remote(src.at[low, :], dst.at[low, :], at.to_y))
    text.far_done = []

    def project(s):
        s.o_done.wait()
        take_mixed(s.o, s.mixed, at, s.heads)
        s.proj_done.wait()
        for cols in chunks(s.x.shape[1]):
            s.part[:, cols] = dot(s.mixed[...], s.proj[cols, :], ((1,), (1,)))
        s.part_done = copies.remote(s.part, s.part_in, at.to_core)
        s.sums[...] = jnp.zeros_like(s.sums)
        for copy in s.rows_done:
            copy.wait()
        for rows in chunks(s.dy.shape[0]):
            s.dy_t[:, rows] = jnp.transpose(s.dy[rows, :])

    def second_norm(s):
        s.part_done.wait()
        for rows in chunks(s.x.shape[0]):
            middle = (
                s.x[rows, :].astype(F32) + s.part[rows, :] + s.part_in[rows, :] + s.small[3:4]
            )
            s.mid[rows, :] = middle
            normed, _ = normalise(middle)
            low = (normed * s.small[1:2] + s.small[4:5]).astype(BF16)
            s.first[rows, :] = low
            s.first_t[:, rows] = jnp.transpose(low)

    def feed_forward(s):
        tokens, width = s.x.shape
        hidden, own = s.up.shape[1], s.proj.shape[1]
        size = width // TILES
        for copy in s.rest_done:
            copy.wait()
        for copy in s.far_done:
            copy.wait_recv()

        def tile(index, carry):
            cols = pl.ds(pl.multiple_of(index * size, LANES), size)
            up, down = s.up[:, cols], s.down[:, cols]
            up_cols = pl.ds(pl.multiple_of(own + index * size, LANES), size)
            down_cols = pl.ds(pl.multiple_of(own + hidden + index * size, LANES), size)
            row = pl.ds(7 + index // (width // size), 1)
            place = pl.ds(pl.multiple_of((index % (width // size)) * size, LANES), size)
            bias = s.small[row, place]
            total = jnp.zeros((1, size), F32)
            for rows in chunks(tokens):
                z = dot(s.first[rows, :], up) + bias
                sg = jax.nn.sigmoid(1.702 * z)
                zs = z * sg
                s.act[rows, cols] = zs.astype(BF16)
                grad = dot(s.dy[rows, :], down)
                low = (grad * (sg + 1.702 * zs * (1.0 - sg))).astype(BF16)
                s.dz[rows, cols] = low
                total = total + jnp.sum(low.astype(F32), axis=0, keepdims=True)
            s.sums[row, place] = total
            s.rest[:, up_cols] = dot(s.first_t[...], s.dz[:, cols]).astype(BF16)
            s.rest[:, down_cols] = dot(s.dy_t[...], s.act[:, cols]).astype(BF16)
            return carry

        lax.fori_loop(0, hidden // size, tile, 0)
        for cols in chunks(width):
            s.grad[0, :, cols] = dot(s.dz[...], s.up[cols, :], ((1,), (1,)))
        s.grad_done = copies.remote(s.grad.at[0], s.grad_in.at[0], at.to_core)
        for cols in chunks(width):
            s.grad[1, :, cols] = dot(s.act[...], s.down[cols, :], ((1,), (1,)))
        s.y_done = copies.remote(s.grad.at[1], s.grad_in.at[1], at.to_core)

    def back(s):
        sums = s.sums
        s.grad_done.wait()
        for rows in chunks(s.x.shape[0]):
            normed, inv = normalise(s.mid[rows, :])
            second = s.grad[0, rows, :] + s.grad_in[0, rows, :]
            scaled = second * s.small[1:2]
            dy = s.dy[rows, :].astype(F32)
            dmid = dy + inv * (
                scaled
                - jnp.mean(scaled, axis=-1, keepdims=True)
                - normed * jnp.mean(scaled * normed, axis=-1, keepdims=True)
            )
            s.dmid[rows, :] = dmid
            sums[1:2] += jnp.sum(second * normed, axis=0, keepdims=True)
            sums[3:4] += jnp.sum(dmid, axis=0, keepdims=True)
            sums[4:5] += jnp.sum(second, axis=0, keepdims=True)
            sums[5:6] += jnp.sum(dy, axis=0, keepdims=True)
            low = dmid.astype(BF16)
            s.first_t[:, rows] = jnp.transpose(low)
            s.do[rows, :] = dot(low, s.proj[...])
        s.writes = [copies.local(s.dmid, s.dmid_out)]
        write_grad_o(s.do, s.do_mine, s.heads)
        s.do_done = send_blocks(copies, at, s.do_mine, s.do_out)

    def proj_grad(s):
        s.rest[:, : s.proj.shape[1]] = dot(s.first_t[...], s.mixed[...]).astype(BF16)

    def output(s):
        s.y_done.wait()
        for rows in chunks(s.x.shape[0]):
            s.y[rows, :] = (
                s.mid[rows, :] + s.grad[1, rows, :] + s.grad_in[1, rows, :] + s.small[5:6]
            ).astype(BF16)
        s.writes.append(copies.local(s.y, s.y_out))

    project(text)
    project(image)
    second_norm(text)
    feed_forward(text)
    second_norm(image)
    back(text)
    proj_grad(text)
    plane = PlaneSum(copies, at, text.rest, arrivals)
    feed_forward(image)
    plane.cross()
    back(image)
    proj_grad(image)
    keep = copies.local(image.rest, image.rest_out)
    output(text)
    output(image)
    plane.arrived()
    half = plane.half

    def put(cols):
        text.rest_out[:half, cols], text.rest_out[half:, cols] = plane.halves(cols)

    by_columns(plane.columns, put)
    plane.sent()
    keep.wait()
    for s in streams:
        for copy in s.do_done + s.writes:
            copy.wait()
        for copy in s.far_done:
            copy.wait_send()


def middle(streams):
    vmem, hbm = pl.BlockSpec(memory_space=pltpu.VMEM), pl.BlockSpec(memory_space=pl.ANY)
    out_shape, out_specs, scratch = [], [], []
    arrivals = None
    for o, x, dy, small, proj, up, down in streams:
        tokens, width = x.shape
        hidden, own = up.shape[1], proj.shape[1]
        rest = (width, own + 2 * hidden)
        summed = arrivals is None
        if summed:
            arrivals = PlaneSum.arrivals(width // 4, rest[1])
        out_shape += [
            jax.ShapeDtypeStruct((tokens, width), BF16),
            jax.ShapeDtypeStruct((tokens, width), F32),
            jax.ShapeDtypeStruct(o.shape, BF16),
            jax.ShapeDtypeStruct((width // 4, rest[1]), F32)
            if summed
            else jax.ShapeDtypeStruct(rest, BF16),
            jax.ShapeDtypeStruct(small.shape, F32),
        ]
        out_specs += [hbm, hbm, hbm, vmem if summed else hbm, vmem]
        scratch += [
            pltpu.VMEM(proj.shape, BF16),
            pltpu.VMEM(up.shape, BF16),
            pltpu.VMEM(down.shape, BF16),
            pltpu.VMEM(rest, BF16),
            pltpu.VMEM((tokens, own), BF16),
            pltpu.VMEM((tokens, width), F32),
            pltpu.VMEM((tokens, width), F32),
            pltpu.VMEM((tokens, width), F32),
            pltpu.VMEM((tokens, width), BF16),
            pltpu.VMEM((width, tokens), BF16),
            pltpu.VMEM((width, tokens), BF16),
            pltpu.VMEM((tokens, hidden), BF16),
            pltpu.VMEM((tokens, hidden), BF16),
            pltpu.VMEM((2, tokens, width), F32),
            pltpu.VMEM((2, tokens, width), F32),
            pltpu.VMEM((tokens, own), F32),
            pltpu.VMEM(o.shape, BF16),
            pltpu.VMEM(o.shape, BF16),
            pltpu.VMEM((tokens, width), BF16),
            pltpu.VMEM((tokens, width), BF16),
            pltpu.VMEM((tokens, width), BF16),
            pltpu.VMEM((tokens, width), F32),
        ]
    results = pl.pallas_call(
        middle_kernel,
        out_shape=out_shape,
        in_specs=([hbm] * 3 + [vmem] + [hbm] * 3) * 2,
        out_specs=out_specs,
        scratch_shapes=scratch + arrivals + copy_sems(2 * 6 + 4 + 6, 2 * (4 + 3) + 8 + 1),
        compiler_params=pltpu.CompilerParams(
            collective_id=1, has_side_effects=True, vmem_limit_bytes=64 * 1024 * 1000
        ),
        name="middle",
    )(*streams[0], *streams[1])
    return results[:MIDDLE_OUT], results[MIDDLE_OUT:]


def take_dqkv(got, out, at, heads):
    width = heads * HD

    def put(which, tile, rows, value):
        start = which * width + tile * LANES
        out[rows, start : start + LANES] = value.astype(BF16)

    take_halves(got, out, at, heads, QB + 2 * KB, functools.partial(put, 0))

    def keys(position, head):
        return as_f32(got, position, key_rows(head))

    pairs = [(keys(0, 0), keys(1, 0)), (keys(2, 0), keys(3, 0))]
    if heads == 6:
        pairs.append((keys(0, 1) + keys(2, 1), keys(1, 1) + keys(3, 1)))
    for tile, (one, two) in enumerate(pairs):
        put(1, tile, slice(None), lane_pair((one, 0), (two, 0)))
        put(2, tile, slice(None), lane_pair((one, 1), (two, 1)))


LAST_IN, LAST_OUT, LAST_SCRATCH = 12, 4, 22


def last_kernel(*refs):
    at = partners()
    ins = [refs[:LAST_IN], refs[LAST_IN : 2 * LAST_IN]]
    refs = refs[2 * LAST_IN :]
    outs = [refs[:LAST_OUT], refs[LAST_OUT : 2 * LAST_OUT]]
    refs = refs[2 * LAST_OUT :]
    count = LAST_SCRATCH + 10
    scratch = [refs[:count], refs[count : 2 * count]]
    refs = refs[2 * count :]
    rest_arrivals, rest_loads = refs[:4], refs[4:7]
    copies = Copies(*refs[7:])
    others = [at.to_x, at.to_y] + at.to_ctx[1:] + [at.to_core]
    greet(others)
    streams = []
    for in_refs, out_refs, own in zip(ins, outs, scratch):
        s = Bag()
        (
            s.m_in, s.do_in, s.o_in, s.lse, s.seg_row, s.first_in, s.x_in, s.small, s.weight_in, s.dmid_in,
            s.rest, s.sums_in,
        ) = in_refs
        s.grad_rows_out, s.sums, s.rest_final, s.qkv_final = out_refs
        (
            s.m, s.do, s.o, s.query_doc, s.key_doc, s.score_keys, s.grad_rows, s.acc, s.back, s.got, s.dqkv, s.weight, s.first, s.x, s.dmid,
            s.part, s.part_in, s.g_qkv, s.sums_own, s.sums_out, s.sums_got, s.sums_line,
        ) = own[:LAST_SCRATCH]
        s.rest_line, s.qkv_line = own[LAST_SCRATCH : LAST_SCRATCH + 3], own[LAST_SCRATCH + 3 : LAST_SCRATCH + 6]
        s.qkv_arrivals = own[LAST_SCRATCH + 6 :]
        s.heads = s.weight.shape[2] // HD
        s.features = (s.query_doc, s.key_doc)
        s.reads = [
            copies.local(src, dst) for src, dst in ((s.m_in, s.m), (s.do_in, s.do), (s.o_in, s.o))
        ]
        streams.append(s)
    text, image = streams
    for s in streams:
        document_features(s.seg_row, *s.features)
        s.acc[...] = jnp.zeros_like(s.acc)
        s.back[...] = jnp.zeros_like(s.back)
    meet(others)
    plane = PlaneSum(copies, at, image.rest, rest_arrivals, rest_loads)
    text_half = text.rest.shape[0] // 2

    def text_values(cols):
        return text.rest[:text_half, cols], text.rest[text_half:, cols]

    text_line = LineSum(
        copies, at, text_values, text.rest_line, text.rest_final, 0, text.rest.shape[1]
    )
    text_line.gather()
    for s in (image, text):
        for copy in s.reads:
            copy.wait()
        s.loads = [
            copies.local(src, dst)
            for src, dst in (
                (s.first_in, s.first), (s.weight_in, s.weight), (s.x_in, s.x), (s.dmid_in, s.dmid),
            )
        ]
        mark_keys(s.m, s.features[1], s.acc.shape[0], s.score_keys, None)

    def unattend_tasks(s, *task):
        unattend(
            at, s.m, s.do, s.o, s.lse, s.features[0], s.score_keys, s.acc, s.back, *task
        )

    text.sends = send_blocks(copies, at, text.back, text.got, start=False)
    split = QB + KB
    shared_sends = send_blocks(copies, at, image.back, image.got, split, None, False)
    own_sends = send_blocks(copies, at, image.back, image.got, 0, split, False)
    image.sends = shared_sends + own_sends

    def image_phase(phase, carry):
        unattend_tasks(image, image_task, phase * 4, phase * 4 + 4, 4, False)

        @pl.when(phase == 0)
        def _():
            key_gradients(image.acc, image.back, 1)
            for copy in shared_sends:
                copy.start()

        return carry

    lax.fori_loop(0, 3, image_phase, 0)
    key_gradients(image.acc, image.back, 0)
    for copy in own_sends:
        copy.start()

    text_line.join()

    def text_phase(phase, carry):
        unattend_tasks(text, text_task, phase * 4, phase * 4 + 4, 4, True)

        @pl.when(phase == 0)
        def _():
            plane.cross()

        return carry

    lax.fori_loop(0, 2, text_phase, 0)
    key_gradients(text.acc, text.back, 0)
    for copy in text.sends:
        copy.start()

    def project(s):
        width = s.x.shape[1]
        own = s.heads * HD
        for copy in s.sends:
            copy.wait()
        for copy in s.loads:
            copy.wait()
        take_dqkv(s.got, s.dqkv, at, s.heads)
        for which in range(3):
            cols = slice(which * own, (which + 1) * own)
            s.g_qkv[:, cols] = dot(s.first[...], s.dqkv[:, cols]).astype(BF16)
        s.qkv_plane = PlaneSum(copies, at, s.g_qkv, s.qkv_arrivals)
        for cols in chunks(width):
            total = dot(s.dqkv[:, :own], s.weight[0, cols, :], ((1,), (1,)))
            total = total + dot(s.dqkv[:, own : 2 * own], s.weight[1, cols, :], ((1,), (1,)))
            s.part[:, cols] = total + dot(s.dqkv[:, 2 * own :], s.weight[2, cols, :], ((1,), (1,)))
        s.part_done = copies.remote(s.part, s.part_in, at.to_core)
        s.sums_own[...] = s.sums_in[...]
        s.sums_own[6:7, :own] = jnp.sum(s.dqkv[:, :own].astype(F32), axis=0, keepdims=True)
        s.sums_own[6:7, own:] = jnp.sum(s.dqkv[:, 2 * own :].astype(F32), axis=0, keepdims=True)
        cuts = (0, 3 * own) if own < STEP else (0, 2 * own, 3 * own)
        s.qkv_sums = [
            LineSum(copies, at, s.qkv_plane.halves, s.qkv_line, s.qkv_final, begin, end)
            for begin, end in zip(cuts, cuts[1:])
        ]

    def input_grad(s):
        s.part_done.wait()
        for rows in chunks(s.x.shape[0]):
            normed, inv = normalise(s.x[rows, :].astype(F32))
            first = s.part[rows, :] + s.part_in[rows, :]
            scaled = first * s.small[0:1]
            s.grad_rows[rows, :] = s.dmid[rows, :] + inv * (
                scaled
                - jnp.mean(scaled, axis=-1, keepdims=True)
                - normed * jnp.mean(scaled * normed, axis=-1, keepdims=True)
            )
            s.sums_own[0:1] += jnp.sum(first * normed, axis=0, keepdims=True)
            s.sums_own[2:3] += jnp.sum(first, axis=0, keepdims=True)
        s.write = copies.local(s.grad_rows, s.grad_rows_out)
        s.sums_done = [copies.remote(s.sums_own, s.sums_got.at[0], at.to_x)]

    def add_sums(s, step):
        s.sums_done[-1].wait_recv()
        before = s.sums_own if step == 0 else s.sums_out
        total = before[...] + s.sums_got[step]
        if step == 0:
            s.sums_out[...] = total
            s.sums_done.append(copies.remote(s.sums_out, s.sums_got.at[1], at.to_y))
        else:
            s.sums_line[at.here] = total
            mine = s.sums_line.at[at.here]
            s.sums_done += [copies.remote(mine, mine, device) for device in at.to_ctx[1:]]

    def end_sums(s):
        for copy in s.sums_done[2:]:
            copy.wait_recv()
        s.sums[...] = s.sums_line[0] + s.sums_line[1] + s.sums_line[2] + s.sums_line[3]

    cuts = [0, STEP, 4 * STEP, 7 * STEP, plane.columns]
    rest_lines = [
        LineSum(copies, at, plane.halves, image.rest_line, image.rest_final, begin, end)
        for begin, end in zip(cuts, cuts[1:])
    ]

    project(image)
    plane.arrived()
    for line in rest_lines:
        line.gather()
    input_grad(image)
    image.qkv_plane.cross()
    text_line.share()
    add_sums(image, 0)
    rest_lines[0].join()
    rest_lines[1].join()
    project(text)
    rest_lines[2].join()
    input_grad(text)
    image.qkv_plane.arrived()
    for line in image.qkv_sums:
        line.gather()
    text.qkv_plane.cross()
    add_sums(image, 1)
    add_sums(text, 0)
    rest_lines[0].share()
    text.qkv_plane.arrived()
    text.qkv_sums[0].gather()
    add_sums(text, 1)
    rest_lines[1].share()
    rest_lines[3].join()
    image.qkv_sums[0].join()
    rest_lines[2].share()
    image.qkv_sums[1].join()
    text.qkv_sums[0].join()
    rest_lines[3].share()
    for line in image.qkv_sums + text.qkv_sums:
        line.share()
    for s in streams:
        end_sums(s)
    for line in [text_line] + rest_lines + image.qkv_sums + text.qkv_sums:
        line.finish()
    plane.sent()
    for s in streams:
        s.qkv_plane.sent()
        for copy in s.sums_done:
            copy.wait_send()
        s.write.wait()


def last(streams):
    vmem, hbm = pl.BlockSpec(memory_space=pltpu.VMEM), pl.BlockSpec(memory_space=pl.ANY)
    out_shape, scratch = [], []
    for messages, do, o, lse, seg, first, x, small, weight, dmid, rest, sums in streams:
        tokens, width = x.shape
        own = weight.shape[2]
        rest_shape, qkv_shape = (width // 4, rest.shape[1]), (width // 4, 3 * own)
        out_shape += [
            jax.ShapeDtypeStruct((tokens, width), F32),
            jax.ShapeDtypeStruct(small.shape, F32),
            jax.ShapeDtypeStruct(rest_shape, BF16),
            jax.ShapeDtypeStruct(qkv_shape, BF16),
        ]
        scratch += [
            pltpu.VMEM(messages.shape, BF16),
            pltpu.VMEM(do.shape, BF16),
            pltpu.VMEM(do.shape, BF16),
            pltpu.VMEM((4 * tokens, LANES), BF16),
            pltpu.VMEM((4 * tokens, LANES), BF16),
            pltpu.VMEM((1 if own == 4 * HD else 2, 4 * tokens, LANES), BF16),
            pltpu.VMEM((tokens, width), F32),
            pltpu.VMEM((1 if own == 4 * HD else 2, 4 * tokens, LANES), F32),
            pltpu.VMEM(messages.shape, BF16),
            pltpu.VMEM(messages.shape, BF16),
            pltpu.VMEM((tokens, 3 * own), BF16),
            pltpu.VMEM(weight.shape, BF16),
            pltpu.VMEM(first.shape, BF16),
            pltpu.VMEM((tokens, width), BF16),
            pltpu.VMEM((tokens, width), F32),
            pltpu.VMEM((tokens, width), F32),
            pltpu.VMEM((tokens, width), F32),
            pltpu.VMEM((width, 3 * own), BF16),
            pltpu.VMEM(small.shape, F32),
            pltpu.VMEM(small.shape, F32),
            pltpu.VMEM((2,) + small.shape, F32),
            pltpu.VMEM((4,) + small.shape, F32),
        ]
        scratch += LineSum.scratch(*rest_shape) + LineSum.scratch(*qkv_shape)
        scratch += PlaneSum.arrivals(*qkv_shape)
    scratch += PlaneSum.arrivals(*rest_shape) + PlaneSum.loads_scratch(*rest_shape)
    specs = [hbm, hbm, hbm, vmem, vmem, hbm, hbm, vmem, hbm, hbm, vmem, vmem]
    specs += specs[:10] + [hbm, vmem]
    results = pl.pallas_call(
        last_kernel,
        out_shape=out_shape,
        in_specs=specs,
        out_specs=[hbm, vmem, vmem, vmem] * 2,
        scratch_shapes=scratch + copy_sems(2 * (3 + 1 + 5 + 6) + 3 + 6 + 3 * 8, 2 * (1 + 7 + 1) + 3 + 1),
        compiler_params=pltpu.CompilerParams(
            collective_id=2, has_side_effects=True, vmem_limit_bytes=64 * 1024 * 1000
        ),
        name="last",
    )(*streams[0], *streams[1])
    return results[:4], results[4:]


def take_own(group, row):
    columns = row.shape[1] // 4
    return pltpu.roll(row, (4 - group) % 4 * columns, 1)[:, :columns]


FINISH_IN, FINISH_OUT = 5, 9


def finish_kernel(*refs):
    ins = [refs[:FINISH_IN], refs[FINISH_IN : 2 * FINISH_IN]]
    refs = refs[2 * FINISH_IN :]
    outs = [refs[:FINISH_OUT], refs[FINISH_OUT : 2 * FINISH_OUT]]
    refs = refs[2 * FINISH_OUT :]
    count = FINISH_IN + FINISH_OUT - 2
    scratch = [refs[:count], refs[count : 2 * count]]
    reads, writes = refs[2 * count :]
    streams, written = [], []

    def write(src, dst):
        copy = pltpu.make_async_copy(src, dst, writes.at[len(written)])
        copy.start()
        written.append(copy)

    for which, (in_refs, own) in enumerate(zip(ins, scratch)):
        streams.append([])
        for index in range(FINISH_IN):
            copy = pltpu.make_async_copy(
                in_refs[index], own[index], reads.at[which * FINISH_IN + index]
            )
            copy.start()
            streams[which].append(copy)
    for copies, out, own in reversed(list(zip(streams, outs, scratch))):
        sums, rest, qkv, y, grad, gains, shifts, bias, qkv_out, proj, up, down = own
        copies[1].wait()
        width = qkv.shape[1] // 3
        hidden = up.shape[1]
        up[...] = rest[:, width : width + hidden].astype(F32)
        write(up, out[5])
        if down.shape[0] > down.shape[1]:
            down[...] = jnp.transpose(rest[:, width + hidden :].astype(F32))
            proj[...] = jnp.transpose(rest[:, :width].astype(F32))
        else:
            down[...] = rest[:, width + hidden :].astype(F32)
            proj[...] = rest[:, :width].astype(F32)
        write(down, out[6])
        write(proj, out[4])
        copies[2].wait()
        for index in range(3):
            qkv_out[index] = qkv[:, index * width : (index + 1) * width].astype(F32)
        write(qkv_out, out[3])
        copies[3].wait()
        write(y, out[7])
        copies[4].wait()
        write(grad, out[8])
        copies[0].wait()
        group = lax.axis_index(FSDP)
        rows = take_own(group, sums[0:8])
        gains[...] = rows[0:2]
        shifts[...] = rows[2:6]
        line = jnp.concatenate([sums[6:7], sums[7:8], sums[8:9]], axis=1)
        bias[...] = take_own(group, jnp.broadcast_to(line, (8, line.shape[1])))[0:1]
        write(gains, out[0])
        write(shifts, out[1])
        write(bias, out[2])
    for copy in written:
        copy.wait()


def finish(streams):
    hbm = pl.BlockSpec(memory_space=pl.ANY)
    out_shape, scratch = [], []
    for sums, rest, qkv, y, grad, flip in streams:
        rows, own = qkv.shape[0], qkv.shape[1] // 3
        hidden = (rest.shape[1] - own) // 2
        shapes = [(2, rows), (4, rows), (1, 3 * rows), (3, rows, own)]
        shapes += [(own, rows), (rows, hidden), (hidden, rows)] if flip else [
            (rows, own), (rows, hidden), (rows, hidden)
        ]
        out_shape += [jax.ShapeDtypeStruct(shape, F32) for shape in shapes]
        out_shape += [jax.ShapeDtypeStruct(a.shape, a.dtype) for a in (y, grad)]
        scratch += [pltpu.VMEM(a.shape, a.dtype) for a in (sums, rest, qkv, y, grad)]
        scratch += [pltpu.VMEM(shape, F32) for shape in shapes]
    results = pl.pallas_call(
        finish_kernel,
        out_shape=out_shape,
        in_specs=[hbm] * (2 * FINISH_IN),
        out_specs=[hbm] * (2 * FINISH_OUT),
        scratch_shapes=scratch
        + [
            pltpu.SemaphoreType.DMA((2 * FINISH_IN,)),
            pltpu.SemaphoreType.DMA((2 * FINISH_OUT,)),
        ],
        compiler_params=pltpu.CompilerParams(vmem_limit_bytes=64 * 1024 * 1000),
        name="finish",
    )(*streams[0][:FINISH_IN], *streams[1][:FINISH_IN])
    return results[:FINISH_OUT], results[FINISH_OUT:]


def on_device(*args):
    streams = []
    for item, causal in ((args[10:], True), (args[:10], False)):
        s = Bag()
        rows, s.seg, cotangent, s.gains, s.shifts, s.head_bias, s.qkv, proj, s.up, down = item
        s.flip, s.x, s.dy = causal, rows[0], cotangent[0]
        s.down, s.proj = (down, proj) if causal else (down.T, proj.T)
        streams.append(s)
    started = front(
        [(s.x, s.seg, s.gains, s.shifts, s.head_bias, s.qkv, s.up, s.down, s.proj) for s in streams]
    )
    for s, (weight, small, first, messages, proj, up, down, o, lse, o_got) in zip(streams, started):
        s.weight, s.small, s.first, s.messages, s.o, s.lse = weight, small, first, messages, o, lse
        s.weights, s.o_got = (proj, up, down), o_got
    done = middle([(s.o_got, s.x, s.dy, s.small, *s.weights) for s in streams])
    ended = last(
        [
            (s.messages, do, s.o, s.lse, s.seg, s.first, s.x, s.small, s.weight, dmid, rest, sums)
            for s, (y, dmid, do, rest, sums) in zip(streams, done)
        ]
    )
    final = finish(
        [
            (sums, rest, qkv, y, grad, s.flip)
            for s, (y, *_), (grad, sums, rest, qkv) in zip(streams, done, ended)
        ]
    )
    outputs = []
    for s, (gains, shifts, bias, qkv, proj, up, down, y, grad_rows) in zip(streams, final):
        if not s.flip:
            proj, down = proj.T, down.T
        outputs.append((y[None], grad_rows[None], gains, shifts, bias, qkv, proj, up, down))
    return outputs[1] + outputs[0]


def layer_stats(rows):
    row_mean = jnp.mean(rows, axis=-1, keepdims=True)
    centred = rows - row_mean
    inv_std = lax.rsqrt(jnp.mean(centred * centred, axis=-1, keepdims=True) + 1e-05)
    return (centred * inv_std, inv_std)


def norm_back(grad_normed_out, normed, inv_std, gain):
    scaled = grad_normed_out * gain
    return inv_std * (
        scaled
        - jnp.mean(scaled, axis=-1, keepdims=True)
        - normed * jnp.mean(scaled * normed, axis=-1, keepdims=True)
    )


def tensor_psum(partial_rows):
    return lax.psum(partial_rows, TP)


def any_mesh_block(
    rows_in,
    seg_row,
    cotangent,
    gains,
    shifts,
    head_bias,
    qkv_weight,
    proj_weight,
    up_weight,
    down_weight,
    causal,
):
    gain_full, shift_full, bias_full, qkv_full, proj_full, up_full, down_full = (
        lax.all_gather(gains, FSDP, axis=1, tiled=True),
        lax.all_gather(shifts, FSDP, axis=1, tiled=True),
        lax.all_gather(head_bias, FSDP, axis=1, tiled=True),
        lax.all_gather(qkv_weight, FSDP, axis=1, tiled=True),
        lax.all_gather(proj_weight, FSDP, axis=1, tiled=True),
        lax.all_gather(up_weight, FSDP, axis=0, tiled=True),
        lax.all_gather(down_weight, FSDP, axis=1, tiled=True),
    )
    gain_vals = gain_full.astype(jnp.float32)
    shift_vals = shift_full.astype(jnp.float32)
    bias_vals = bias_full[0].astype(jnp.float32)
    tp_width = qkv_full.shape[2]
    local_rows = rows_in.shape[1]
    seq_length = seg_row.shape[1]
    head_local = tp_width // HD
    rows = rows_in[0].astype(jnp.float32)
    row_start = lax.axis_index(CTX) * local_rows
    seg_all = seg_row[0]
    seg_query = lax.dynamic_slice_in_dim(seg_all, row_start, local_rows)
    query_pos = row_start + jnp.arange(local_rows, dtype=jnp.int32)
    key_pos = jnp.arange(seq_length, dtype=jnp.int32)
    allowed = seg_query[:, None] == seg_all[None, :]
    if causal:
        allowed = jnp.logical_and(allowed, key_pos[None, :] <= query_pos[:, None])

    def to_heads(matrix):
        return matrix.reshape(matrix.shape[0], head_local, HD).transpose(1, 0, 2)

    def from_heads(stacked):
        return stacked.transpose(1, 0, 2).reshape(stacked.shape[1], head_local * HD)

    normed_one, inv_one = layer_stats(rows)
    first_in = (normed_one * gain_vals[0] + shift_vals[0]).astype(jnp.bfloat16)
    queries = (
        jnp.dot(first_in, qkv_full[0], preferred_element_type=jnp.float32) + bias_vals[:tp_width]
    ).astype(jnp.bfloat16)
    key_rows = jnp.dot(first_in, qkv_full[1], preferred_element_type=jnp.float32).astype(
        jnp.bfloat16
    )
    values = (
        jnp.dot(first_in, qkv_full[2], preferred_element_type=jnp.float32)
        + bias_vals[tp_width : 2 * tp_width]
    ).astype(jnp.bfloat16)
    key_all, value_all = (
        lax.all_gather(key_rows, CTX, axis=0, tiled=True),
        lax.all_gather(values, CTX, axis=0, tiled=True),
    )
    query_heads = to_heads(queries)
    key_heads = to_heads(key_all)
    value_heads = to_heads(value_all)

    def attend(head_items):
        query_h, key_h, value_h = head_items
        scores = dot(query_h, key_h, ((1,), (1,))) * 0.125
        scores = jnp.where(allowed, scores, -1e30)
        row_top = jnp.max(scores, axis=-1, keepdims=True)
        weights = jnp.exp(scores - row_top)
        row_total = jnp.sum(weights, axis=-1, keepdims=True)
        weights_low = (weights / row_total).astype(jnp.bfloat16)
        mixed_h = dot(weights_low, value_h, ((1,), (0,)))
        return (mixed_h.astype(jnp.bfloat16), row_top[:, 0] + jnp.log(row_total[:, 0]))

    mixed_heads, log_totals = lax.map(attend, (query_heads, key_heads, value_heads))
    mixed = from_heads(mixed_heads)
    middle = (
        rows
        + tensor_psum(jnp.dot(mixed, proj_full, preferred_element_type=jnp.float32))
        + shift_vals[1]
    )
    normed_two, inv_two = layer_stats(middle)
    second_in = (normed_two * gain_vals[1] + shift_vals[2]).astype(jnp.bfloat16)
    hidden = (
        jnp.dot(second_in, up_full, preferred_element_type=jnp.float32) + bias_vals[2 * tp_width :]
    )
    sigma = jax.nn.sigmoid(1.702 * hidden)
    activated = (hidden * sigma).astype(jnp.bfloat16)
    output = (
        middle
        + tensor_psum(jnp.dot(activated, down_full, preferred_element_type=jnp.float32))
        + shift_vals[3]
    )
    grad_out = cotangent[0].astype(jnp.float32)
    grad_down_bias = jnp.sum(grad_out, axis=0)
    grad_branch = grad_out.astype(jnp.bfloat16)
    grad_down = dot(activated, grad_branch, ((0,), (0,)))
    grad_act = dot(grad_branch, down_full, ((1,), (1,)))
    grad_hidden = (grad_act * (sigma + 1.702 * hidden * sigma * (1.0 - sigma))).astype(jnp.bfloat16)
    grad_up_bias = jnp.sum(grad_hidden.astype(jnp.float32), axis=0)
    grad_up = dot(second_in, grad_hidden, ((0,), (0,)))
    grad_second = tensor_psum(
        dot(grad_hidden, up_full, ((1,), (1,)))
    )
    grad_gain_two = jnp.sum(grad_second * normed_two, axis=0)
    grad_shift_two = jnp.sum(grad_second, axis=0)
    grad_middle = grad_out + norm_back(grad_second, normed_two, inv_two, gain_vals[1])
    grad_proj_bias = jnp.sum(grad_middle, axis=0)
    grad_attn = grad_middle.astype(jnp.bfloat16)
    grad_proj = dot(mixed, grad_attn, ((0,), (0,)))
    grad_mixed = dot(grad_attn, proj_full, ((1,), (1,))).astype(jnp.bfloat16)

    def attend_back(head_items):
        query_h, key_h, value_h, grad_h, log_total = head_items
        scores = dot(query_h, key_h, ((1,), (1,))) * 0.125
        weights = jnp.where(allowed, jnp.exp(scores - log_total[:, None]), 0.0)
        grad_weights = dot(grad_h, value_h, ((1,), (1,)))
        row_delta = jnp.sum(weights * grad_weights, axis=-1, keepdims=True)
        grad_scores = (weights * (grad_weights - row_delta)).astype(jnp.bfloat16)
        grad_query_h = (
            dot(grad_scores, key_h, ((1,), (0,))) * 0.125
        )
        grad_key_h = (
            dot(grad_scores, query_h, ((0,), (0,)))
            * 0.125
        )
        grad_value_h = dot(weights.astype(jnp.bfloat16), grad_h, ((0,), (0,)))
        return (grad_query_h, grad_key_h, grad_value_h)

    query_parts, key_parts, value_parts = lax.map(
        attend_back, (query_heads, key_heads, value_heads, to_heads(grad_mixed), log_totals)
    )
    key_sum, value_sum = (
        lax.psum_scatter(from_heads(key_parts), CTX, scatter_dimension=0, tiled=True),
        lax.psum_scatter(from_heads(value_parts), CTX, scatter_dimension=0, tiled=True),
    )
    grad_query = from_heads(query_parts).astype(jnp.bfloat16)
    grad_key = key_sum.astype(jnp.bfloat16)
    grad_value = value_sum.astype(jnp.bfloat16)
    grad_qkv = jnp.stack(
        [
            dot(first_in, grad_query, ((0,), (0,))),
            dot(first_in, grad_key, ((0,), (0,))),
            dot(first_in, grad_value, ((0,), (0,))),
        ]
    )
    grad_head = jnp.concatenate(
        [
            jnp.sum(grad_query.astype(jnp.float32), axis=0),
            jnp.sum(grad_value.astype(jnp.float32), axis=0),
            grad_up_bias,
        ]
    )[None, :]
    grad_first_part = dot(grad_query, qkv_full[0], ((1,), (1,)))
    grad_first_part = grad_first_part + dot(grad_key, qkv_full[1], ((1,), (1,)))
    grad_first_part = grad_first_part + dot(grad_value, qkv_full[2], ((1,), (1,)))
    grad_first = tensor_psum(grad_first_part)
    grad_gain_one = jnp.sum(grad_first * normed_one, axis=0)
    grad_shift_one = jnp.sum(grad_first, axis=0)
    grad_rows = grad_middle + norm_back(grad_first, normed_one, inv_one, gain_vals[0])
    grad_gains = jnp.stack([grad_gain_one, grad_gain_two])
    grad_shifts = jnp.stack([grad_shift_one, grad_proj_bias, grad_shift_two, grad_down_bias])
    share_gains, share_shifts, share_head, share_qkv, share_proj, share_up, share_down = (
        lax.psum_scatter(grad_gains, FSDP, scatter_dimension=1, tiled=True),
        lax.psum_scatter(grad_shifts, FSDP, scatter_dimension=1, tiled=True),
        lax.psum_scatter(grad_head, FSDP, scatter_dimension=1, tiled=True),
        lax.psum_scatter(grad_qkv, FSDP, scatter_dimension=1, tiled=True),
        lax.psum_scatter(grad_proj, FSDP, scatter_dimension=1, tiled=True),
        lax.psum_scatter(grad_up, FSDP, scatter_dimension=0, tiled=True),
        lax.psum_scatter(grad_down, FSDP, scatter_dimension=1, tiled=True),
    )
    owned = lax.psum(
        (share_gains, share_shifts, share_head, share_qkv, share_proj, share_up, share_down), CTX
    )
    return (output.astype(jnp.bfloat16)[None], grad_rows[None]) + tuple(owned)


def on_any_mesh(
    image_input,
    image_segments,
    image_cotangent,
    image_gains,
    image_shifts,
    image_head_bias,
    image_qkv_weight,
    image_proj_weight,
    image_up_weight,
    image_down_weight,
    text_input,
    text_segments,
    text_cotangent,
    text_gains,
    text_shifts,
    text_head_bias,
    text_qkv_weight,
    text_proj_weight,
    text_up_weight,
    text_down_weight,
):
    image_results = any_mesh_block(
        image_input,
        image_segments,
        image_cotangent,
        image_gains,
        image_shifts,
        image_head_bias,
        image_qkv_weight,
        image_proj_weight,
        image_up_weight,
        image_down_weight,
        False,
    )
    text_results = any_mesh_block(
        text_input,
        text_segments,
        text_cotangent,
        text_gains,
        text_shifts,
        text_head_bias,
        text_qkv_weight,
        text_proj_weight,
        text_up_weight,
        text_down_weight,
        True,
    )
    return image_results + text_results


def stream_specs():
    return (
        P(FSDP, CTX, None),
        P(FSDP, None),
        P(FSDP, CTX, None),
        P(None, FSDP),
        P(None, FSDP),
        P(TP, FSDP),
        P(None, FSDP, TP),
        P(TP, FSDP),
        P(FSDP, TP),
        P(TP, FSDP),
    )


def solution(mesh):
    one = stream_specs()
    grads = (one[0], one[0]) + one[3:]
    body = on_device
    if (mesh.shape[FSDP], mesh.shape[CTX], mesh.shape[TP]) != (4, 4, 2):
        body = on_any_mesh
    return jax.shard_map(
        body, mesh=mesh, in_specs=one + one, out_specs=grads + grads, check_vma=False
    )
```

```python
import functools

import jax
import jax.numpy as jnp
from jax import lax
from jax.experimental import pallas as pl
from jax.experimental.pallas import tpu as pltpu
from jax.sharding import PartitionSpec as P

HD = 64
LANES = 128
QB = 256
KB = 512
NEG = -1e30
F32 = jnp.float32
MESH = pl.DeviceIdType.MESH
FSDP, CTX, TP = "fsdp", "ctx", "tp"
BF16 = jnp.bfloat16


def dot(left, right, dims=((1,), (0,))):
    return lax.dot_general(left, right, (dims, ((), ())), preferred_element_type=F32)


def lane_marks():
    lane = lax.broadcasted_iota(jnp.int32, (1, LANES), 1)
    first = (lane < HD).astype(F32).astype(BF16)
    second = (lane >= HD).astype(F32).astype(BF16)
    return first, second


def document_features(row_ref, query_out, key_out):
    lane = lax.broadcasted_iota(jnp.int32, (LANES, LANES), 1) % HD
    for start in range(0, query_out.shape[0], LANES):
        row = row_ref[:, start : start + LANES].astype(F32)
        same = jnp.transpose(jnp.broadcast_to(row, (LANES, LANES))) == lane.astype(F32)
        query_out[start : start + LANES, :] = jnp.where(same, 1.0, 0.0).astype(BF16)
        key_out[start : start + LANES, :] = jnp.where(same, 0.0, NEG).astype(BF16)


def swap_halves(value):
    return pltpu.roll(value, HD, 1)


def key_range(index):
    return slice(index * KB, (index + 1) * KB)


def pick(flag, one, zero):
    return jnp.where(flag == 1, one, zero)


def query_rows(head):
    return pl.ds(pl.multiple_of(head * (QB + 2 * KB), QB), QB)


def key_rows(head):
    return pl.ds(pl.multiple_of(QB + head * KB, QB), KB)


def mark_keys(m, features, heads, score_keys, value_keys):
    first, second = lane_marks()
    for head in range(heads):
        for index in range(4):
            block = m[index, key_rows(head)]
            score_keys[head, key_range(index)] = block * first + features[key_range(index), :] * second
            if value_keys is not None:
                value_keys[head, key_range(index)] = block * second + first


def later(index, shape, axis, query_start):
    key_pos = index * KB + lax.broadcasted_iota(jnp.int32, shape, axis)
    query_pos = query_start + lax.broadcasted_iota(jnp.int32, shape, 1 - axis)
    return key_pos > query_pos


def mix_rows(query, score_keys, value_keys, head, blocks, query_start=None):
    scores = []
    for index in range(blocks):
        score = dot(query, score_keys[head, key_range(index)], ((1,), (1,)))
        if query_start is not None:
            score = jnp.where(later(index, score.shape, 1, query_start), NEG, score)
        scores.append(score)
    top = jnp.max(functools.reduce(jnp.maximum, scores), axis=1, keepdims=True)
    acc = jnp.zeros((query.shape[0], LANES), F32)
    for index, score in enumerate(scores):
        acc = acc + dot(jnp.exp(score - top).astype(BF16), value_keys[head, key_range(index)])
    return acc / swap_halves(acc), top + jnp.log(acc)


def text_task(at, task):
    return 0, task // 2, task % 2


def image_task(at, task):
    shared = 1 - (task + 8) // 12
    step = 5 - task // 2
    low, high = (at.here_low + step % 2) % 2, (at.here_high + step // 2) % 2
    return shared, pick(shared, at.here_high * 2 + task // 2, high * 2 + low), task % 2


def attend(at, m, features, score_keys, value_keys, o, lse, task_of, begin, end, blocks, causal):
    first, second = lane_marks()
    lane = lax.broadcasted_iota(jnp.int32, (QB, LANES), 1)

    def one(task, carry):
        head, source, half = task_of(at, task)
        start = (source * 2 + half) * QB
        query = m[source, query_rows(head)].astype(F32)
        query = pick(half, swap_halves(query), query).astype(BF16)
        query = query * first + features[pl.ds(pl.multiple_of(start, QB), QB), :] * second
        mixed, log_total = mix_rows(
            query, score_keys, value_keys, head, blocks, start if causal else None
        )
        lse[task] = jnp.transpose(log_total)[:8]
        mixed = pick(half, mixed, swap_halves(mixed)).astype(BF16)
        rows = pl.ds(pl.multiple_of(head * QB, QB), QB)
        o[source, rows] = jnp.where(lane // HD == half, mixed, o[source, rows])
        return carry

    lax.fori_loop(begin, end, one, 0)


def unattend(at, m, do, o, lse, features, score_keys, acc, out, task_of, begin, end, blocks, causal):
    first, second = lane_marks()
    lane = lax.broadcasted_iota(jnp.int32, (QB, LANES), 1)

    def one(task, carry):
        head, source, half = task_of(at, task)
        start = (source * 2 + half) * QB
        rows = pl.ds(pl.multiple_of(head * QB, QB), QB)
        query, grad_o = m[source, query_rows(head)].astype(F32), do[source, rows].astype(F32)
        product = jnp.transpose(grad_o * o[source, rows].astype(F32))
        delta = jnp.sum(pick(half, product[HD:], product[:HD]), axis=0, keepdims=True)
        query = pick(half, swap_halves(query), query).astype(BF16) * first
        grad_o = pick(half, grad_o, swap_halves(grad_o)).astype(BF16) * second
        marked = query + features[pl.ds(pl.multiple_of(start, QB), QB), :] * second
        row_lse = lse[task, :1]
        grad_query = jnp.zeros((QB, LANES), F32)
        for index in range(blocks):
            keys = m[index, key_rows(head)]
            score = dot(score_keys[head, key_range(index)], marked, ((1,), (1,)))
            if causal:
                score = jnp.where(later(index, score.shape, 0, start), NEG, score)
            weights = jnp.exp(score - row_lse)
            grad_weights = dot(keys, grad_o, ((1,), (1,)))
            grad_scores = (weights * (grad_weights - delta)).astype(BF16)
            acc[head, key_range(index)] += dot(grad_scores, query) + dot(weights.astype(BF16), grad_o)
            grad_query = grad_query + dot(grad_scores, keys, ((0,), (0,)))
        grad_query = grad_query * 0.125
        grad_query = pick(half, swap_halves(grad_query), grad_query).astype(BF16)
        out[source, query_rows(head)] = jnp.where(
            lane // HD == half, grad_query, out[source, query_rows(head)]
        )
        return carry

    lax.fori_loop(begin, end, one, 0)


def key_gradients(acc, out, head):
    for index in range(4):
        out[index, key_rows(head)] = acc[head, key_range(index)].astype(BF16)


class Bag:
    pass


def partners():
    at = Bag()
    group, here, core = lax.axis_index(FSDP), lax.axis_index(CTX), lax.axis_index(TP)
    at.group, at.here, at.core = group, here, core
    at.group_x = group + 1 - 2 * (group % 2)
    at.group_y = group + 2 - 4 * (group // 2)
    at.group_far = 3 - group
    at.here_low, at.here_high = here % 2, here // 2
    at.inner, at.outer = (here + 1) // 2 == 1, (here + 1) // 2 != 1
    at.ctx = (here, here + 1 - 2 * (here % 2), here + 2 - 4 * (here // 2), 3 - here)
    at.to_x, at.to_y, at.to_far = ({FSDP: g} for g in (at.group_x, at.group_y, at.group_far))
    at.to_ctx = [{CTX: c} for c in at.ctx]
    at.to_core = {TP: 1 - core}
    return at


def greet(devices):
    barrier = pltpu.get_barrier_semaphore()
    for device in devices:
        pl.semaphore_signal(barrier, inc=1, device_id=device, device_id_type=MESH)


def meet(devices):
    pl.semaphore_wait(pltpu.get_barrier_semaphore(), len(devices))


class Copies:
    def __init__(self, send_sems, recv_sems, local_sems):
        self.sems = (send_sems, recv_sems, local_sems)
        self.used = [0, 0]

    def remote(self, src, dst, device, start=True):
        index = self.used[0]
        self.used[0] += 1
        copy = pltpu.make_async_remote_copy(
            src_ref=src,
            dst_ref=dst,
            send_sem=self.sems[0].at[index],
            recv_sem=self.sems[1].at[index],
            device_id=device,
            device_id_type=MESH,
        )
        if start:
            copy.start()
        return copy

    def local(self, src, dst, start=True):
        index = self.used[1]
        self.used[1] += 1
        copy = pltpu.make_async_copy(src, dst, self.sems[2].at[index])
        if start:
            copy.start()
        return copy


def copy_sems(remote, local):
    return [
        pltpu.SemaphoreType.DMA((remote,)),
        pltpu.SemaphoreType.DMA((remote,)),
        pltpu.SemaphoreType.DMA((local,)),
    ]


class Gather:
    def __init__(self, copies, at, src, dst):
        self.copies, self.at, self.dst = copies, at, dst
        self.rows = src.shape[-2]
        own = self.part(at.group, 0, self.rows)
        self.own = copies.local(src, own)
        self.to_x = copies.remote(src, own, at.to_x)
        self.to_y = copies.remote(src, own, at.to_y)

    def part(self, owner, offset, size):
        rows = pl.ds(pl.multiple_of(owner * self.rows + offset, 8), size)
        return self.dst.at[:, rows, :] if len(self.dst.shape) == 3 else self.dst.at[rows, :]

    def near(self):
        self.own.wait()
        self.to_x.wait()
        self.to_y.wait()

    def forward(self):
        half = self.rows // 2
        self.to_x.wait_recv()
        self.to_y.wait_recv()
        top = self.part(self.at.group_y, 0, half)
        low = self.part(self.at.group_x, half, half)
        self.far_x = self.copies.remote(top, top, self.at.to_x)
        self.far_y = self.copies.remote(low, low, self.at.to_y)

    def arrived(self):
        self.own.wait()
        self.far_x.wait_recv()
        self.far_y.wait_recv()

    def sent(self):
        for copy in (self.to_x, self.to_y, self.far_x, self.far_y):
            copy.wait_send()


def normalise(rows):
    mean = jnp.mean(rows, axis=-1, keepdims=True)
    centred = rows - mean
    inv = lax.rsqrt(jnp.mean(centred * centred, axis=-1, keepdims=True) + 1e-05)
    return centred * inv, inv


def lane_pair(low, high):
    lane = lax.broadcasted_iota(jnp.int32, low[0].shape, 1)
    left = low[0] if low[1] == 0 else pltpu.roll(low[0], HD, 1)
    right = high[0] if high[1] == 1 else pltpu.roll(high[0], HD, 1)
    return jnp.where(lane < HD, left, right)


def head_tile(ref, start, index, rows=slice(None)):
    first = start + (index // 2) * LANES
    return ref[rows, first : first + LANES], index % 2


def halves_pair(ref, start, index):
    half = ref.shape[0] // 2
    return lane_pair(
        head_tile(ref, start, index, slice(0, half)), head_tile(ref, start, index, slice(half, None))
    ).astype(BF16)


def write_messages(qkv, out, heads):
    width = heads * HD

    def keys_values(index):
        return lane_pair(head_tile(qkv, width, index), head_tile(qkv, 2 * width, index)).astype(BF16)

    for c in range(4):
        out[c, query_rows(0)] = halves_pair(qkv, 0, c)
        out[c, key_rows(0)] = keys_values(c)
        if heads == 6:
            out[c, key_rows(1)] = keys_values(4 + c % 2)
            out[c, query_rows(1)] = halves_pair(qkv, 0, 4 + c % 2)


def message_shape(heads, tokens):
    return (4, (heads // 2 - 1) * (QB + tokens), LANES)


def mixed_shape(heads):
    return (4, (heads // 2 - 1) * QB, LANES)


def first_rows(x_ref, small_ref, normal_ref, first_ref, rows):
    normed, _ = normalise(x_ref[rows, :].astype(F32))
    first = (normed * small_ref[0:1] + small_ref[2:3]).astype(BF16)
    normal_ref[rows, :] = first
    first_ref[:, rows] = jnp.transpose(first)


def project_rows(normal_ref, small_ref, weight_ref, qkv_ref, rows):
    width = weight_ref.shape[2]
    first = normal_ref[rows, :]
    bias = small_ref[6:7]
    qkv_ref[rows, :width] = (dot(first, weight_ref[0]) + bias[:, :width]) * 0.125
    qkv_ref[rows, width : 2 * width] = dot(first, weight_ref[1])
    qkv_ref[rows, 2 * width :] = dot(first, weight_ref[2]) + bias[:, width : 2 * width]


def spread_small(at, gains, shifts, bias, wide, flat, out):
    width = wide.shape[1]
    columns, bias_columns = gains.shape[1], bias.shape[1]
    wide[...] = jnp.zeros_like(wide)
    flat[...] = jnp.zeros_like(flat)
    wide[0:2, :columns] = gains[...].astype(F32)
    wide[2:6, :columns] = shifts[...].astype(F32)
    flat[0:1, :bias_columns] = bias[...].astype(F32)
    out[0:8] = pltpu.roll(wide[...], at.group * columns, 1)
    line = pltpu.roll(flat[...], at.group * bias_columns, 1)
    out[8:16] = jnp.zeros((8, width), F32)
    for row in range(3):
        out[6 + row : 7 + row] = line[0:1, row * width : (row + 1) * width]


FRONT_IN, FRONT_OUT, FRONT_SCRATCH = 9, 10, 21


def front_kernel(*refs):
    at = partners()
    ins = [refs[:FRONT_IN], refs[FRONT_IN : 2 * FRONT_IN]]
    refs = refs[2 * FRONT_IN :]
    outs = [refs[:FRONT_OUT], refs[FRONT_OUT : 2 * FRONT_OUT]]
    refs = refs[2 * FRONT_OUT :]
    scratch = [refs[:FRONT_SCRATCH], refs[FRONT_SCRATCH : 2 * FRONT_SCRATCH]]
    copies = Copies(*refs[2 * FRONT_SCRATCH :])
    others = [at.to_x, at.to_y, at.to_far] + at.to_ctx[1:]
    greet(others)
    streams = []
    for in_refs, out_refs, own in zip(ins, outs, scratch):
        s = Bag()
        s.x_in, s.seg_row, s.gains, s.shifts, s.bias, s.qkv, s.up_in, s.down_in, s.proj_in = in_refs
        (
            s.weight_out, s.small, s.first_out, s.messages, s.proj_full, s.up_full, s.down_full,
            s.o_out, s.lse, s.o_got,
        ) = out_refs
        (
            s.small_in, s.small_own, s.wide, s.flat, s.rows, s.mine, s.got, s.down_t, s.proj_t,
            s.query_doc, s.key_doc, s.score_keys, s.value_keys, s.x, s.up, s.down, s.proj, s.weight, s.first,
        ) = own[:19]
        s.o, s.normal = own[19:]
        s.heads = s.weight.shape[2] // HD
        s.features = (s.query_doc, s.key_doc)
        s.reads = [
            copies.local(src, dst)
            for src, dst in (
                (s.x_in, s.x), (s.proj_in, s.proj), (s.up_in, s.up), (s.down_in, s.down),
            )
        ]
        streams.append(s)
    text, image = streams
    for s in (image, text):
        spread_small(at, s.gains, s.shifts, s.bias, s.wide, s.flat, s.small_own)
        document_features(s.seg_row, *s.features)
    meet(others)
    text.gather = Gather(copies, at, text.qkv, text.weight)
    for s in (text, image):
        s.small_done = [
            copies.remote(s.small_own, s.small_in.at[i], device)
            for i, device in enumerate((at.to_x, at.to_y, at.to_far))
        ]
        for copy in s.reads:
            copy.wait()
    text.down_t[...] = jnp.transpose(text.down[...])
    text.proj_t[...] = jnp.transpose(text.proj[...])
    text.gather.forward()
    image.gather = Gather(copies, at, image.qkv, image.weight)

    def project(s):
        for copy in s.small_done:
            copy.wait_recv()
        s.small[...] = s.small_own[...] + s.small_in[0] + s.small_in[1] + s.small_in[2]
        for rows in chunks(s.x.shape[0]):
            first_rows(s.x, s.small, s.normal, s.first, rows)
        s.gather.arrived()
        for rows in chunks(s.x.shape[0]):
            project_rows(s.normal, s.small, s.weight, s.rows, rows)
        write_messages(s.rows, s.mine, s.heads)
        s.writes = [copies.local(s.weight, s.weight_out), copies.local(s.first, s.first_out)]

    def gather_rest(s):
        pieces = (s.proj_t, s.up, s.down_t) if s.heads == 4 else (s.proj, s.up, s.down)
        s.rest = [
            Gather(copies, at, piece, full)
            for piece, full in zip(pieces, (s.proj_full, s.up_full, s.down_full))
        ]

    project(text)
    text.sends = send_blocks(copies, at, text.mine, text.got)
    image.gather.forward()
    gather_rest(text)
    project(image)
    image.sends = send_blocks(copies, at, image.mine, image.got)
    gather_rest(image)
    s = text
    for copy in s.sends:
        copy.wait()
    s.writes.append(copies.local(s.got, s.messages))
    s.o[...] = jnp.zeros_like(s.o)
    mark_keys(s.got, s.features[1], 1, s.score_keys, s.value_keys)
    attend(
        at, s.got, s.features[0], s.score_keys, s.value_keys, s.o, s.lse, text_task, 0, 8, 4, True
    )
    for gather in s.rest:
        gather.forward()
    s = image
    for copy in s.sends:
        copy.wait()
    text.o_done = send_blocks(copies, at, text.o, text.o_got)
    s.writes.append(copies.local(s.got, s.messages))
    s.o[...] = jnp.zeros_like(s.o)
    mark_keys(s.got, s.features[1], 2, s.score_keys, s.value_keys)
    s.o_done = send_blocks(copies, at, s.o, s.o_got, start=False)

    def image_pair(index, carry):
        attend(
            at, image.got, image.features[0], image.score_keys, image.value_keys, image.o, image.lse,
            image_task, 2 * index, 2 * index + 2, 4, False,
        )
        for step, copy in enumerate(image.o_done):

            @pl.when(index == 5 - step)
            def _(copy=copy):
                copy.start()

        return carry

    lax.fori_loop(0, 6, image_pair, 0)
    s.rest[0].forward()
    for s in (text, image):
        s.writes.append(copies.local(s.o, s.o_out))
    whole = [image.gather, text.gather, image.rest[0]] + text.rest
    for gather in whole[2:]:
        gather.arrived()
    for gather in whole:
        gather.sent()
    for gather in image.rest[1:]:
        gather.near()
    for s in (image, text):
        for copy in s.small_done:
            copy.wait_send()
        for copy in s.writes + s.o_done:
            copy.wait()


def front(streams):
    vmem, hbm = pl.BlockSpec(memory_space=pltpu.VMEM), pl.BlockSpec(memory_space=pl.ANY)
    out_shape, out_specs, scratch = [], [], []
    for x, seg, gains, shifts, bias, qkv, up, down, proj in streams:
        tokens, width = x.shape
        own = qkv.shape[2]
        messages = message_shape(own // HD, tokens)
        hidden = up.shape[1]
        small = jax.ShapeDtypeStruct((16, width), F32)
        out_shape += [
            jax.ShapeDtypeStruct((3, width, own), BF16),
            small,
            jax.ShapeDtypeStruct((width, tokens), BF16),
            jax.ShapeDtypeStruct(messages, BF16),
            jax.ShapeDtypeStruct((width, own), BF16),
            jax.ShapeDtypeStruct((width, hidden), BF16),
            jax.ShapeDtypeStruct((width, hidden), BF16),
            jax.ShapeDtypeStruct(mixed_shape(own // HD), BF16),
            jax.ShapeDtypeStruct((2 * (own // HD), 8, QB), F32),
            jax.ShapeDtypeStruct(mixed_shape(own // HD), BF16),
        ]
        out_specs += [hbm, vmem, hbm, hbm, hbm, hbm, hbm, hbm, vmem, hbm]
        scratch += [
            pltpu.VMEM((3, 16, width), F32),
            pltpu.VMEM((16, width), F32),
            pltpu.VMEM((8, width), F32),
            pltpu.VMEM((8, 3 * width), F32),
            pltpu.VMEM((tokens, 3 * own), F32),
            pltpu.VMEM(messages, BF16),
            pltpu.VMEM(messages, BF16),
            pltpu.VMEM((width // 4, hidden), BF16),
            pltpu.VMEM((width // 4, own), BF16),
            pltpu.VMEM((4 * tokens, LANES), BF16),
            pltpu.VMEM((4 * tokens, LANES), BF16),
            pltpu.VMEM((1 if own == 4 * HD else 2, 4 * tokens, LANES), BF16),
            pltpu.VMEM((1 if own == 4 * HD else 2, 4 * tokens, LANES), BF16),
            pltpu.VMEM(x.shape, BF16),
            pltpu.VMEM(up.shape, BF16),
            pltpu.VMEM(down.shape, BF16),
            pltpu.VMEM(proj.shape, BF16),
            pltpu.VMEM((3, width, own), BF16),
            pltpu.VMEM((width, tokens), BF16),
            pltpu.VMEM(mixed_shape(own // HD), BF16),
            pltpu.VMEM((tokens, width), BF16),
        ]
    results = pl.pallas_call(
        front_kernel,
        out_shape=out_shape,
        in_specs=[hbm, vmem, vmem, vmem, vmem, vmem, hbm, hbm, hbm] * 2,
        out_specs=out_specs,
        scratch_shapes=scratch + copy_sems(2 * (3 + 4 * 4 + 6), 2 * 14),
        compiler_params=pltpu.CompilerParams(
            collective_id=0, has_side_effects=True, vmem_limit_bytes=63 << 20
        ),
        name="front",
    )(*streams[0], *streams[1])
    return results[:FRONT_OUT], results[FRONT_OUT:]


STEP = 384
TILES = 1


def by_columns(columns, body):
    def one(index, carry):
        body(pl.ds(pl.multiple_of(index * STEP, STEP), STEP))
        return carry

    lax.fori_loop(0, columns // STEP, one, 0)


class PlaneSum:
    def __init__(self, copies, at, src, arrivals, loads=None):
        self.copies, self.at = copies, at
        self.in_x, self.in_y, self.in_top, self.in_low = arrivals
        half, self.columns = self.in_top.shape
        self.half, rows = half, 2 * half

        def block(owner, offset, size=half):
            return src.at[pl.ds(pl.multiple_of(owner * rows + offset, 8), size), :]

        self.first = [
            copies.remote(block(at.group_far, 0), self.in_x.at[1], at.to_x),
            copies.remote(block(at.group_far, half), self.in_y.at[1], at.to_y),
            copies.remote(block(at.group_x, 0), self.in_x.at[0], at.to_x),
            copies.remote(block(at.group_y, half), self.in_y.at[0], at.to_y),
        ]
        parts = [block(at.group_y, 0), block(at.group_x, half), block(at.group, 0, rows)]
        if loads is None:
            self.loads = []
            self.pass_top, self.pass_low, self.own = parts
        else:
            self.loads = [copies.local(part, load) for part, load in zip(parts, loads)]
            self.pass_top, self.pass_low, self.own = loads
        self.second = [
            copies.remote(self.pass_top, self.in_top, at.to_y, False),
            copies.remote(self.pass_low, self.in_low, at.to_x, False),
        ]

    def cross(self):
        for copy in self.loads:
            copy.wait()
        self.first[0].wait_recv()

        def top(cols):
            self.pass_top[:, cols] = (
                self.pass_top[:, cols].astype(F32) + self.in_x[1, :, cols].astype(F32)
            ).astype(BF16)

        by_columns(self.columns, top)
        self.second[0].start()
        self.first[1].wait_recv()

        def low(cols):
            self.pass_low[:, cols] = (
                self.pass_low[:, cols].astype(F32) + self.in_y[1, :, cols].astype(F32)
            ).astype(BF16)

        by_columns(self.columns, low)
        self.second[1].start()

    def arrived(self):
        for copy in self.first[2:] + self.second:
            copy.wait_recv()

    def halves(self, cols):
        half = self.half
        return (
            self.own[:half, cols].astype(F32)
            + self.in_x[0, :, cols].astype(F32)
            + self.in_top[:, cols].astype(F32),
            self.own[half:, cols].astype(F32)
            + self.in_y[0, :, cols].astype(F32)
            + self.in_low[:, cols].astype(F32),
        )

    def sent(self):
        for copy in self.first + self.second:
            copy.wait_send()

    @staticmethod
    def arrivals(rows, columns):
        half = rows // 2
        pair, one = pltpu.VMEM((2, half, columns), BF16), pltpu.VMEM((half, columns), BF16)
        return [pair, pair, one, one]

    @staticmethod
    def loads_scratch(rows, columns):
        half = rows // 2
        one = pltpu.VMEM((half, columns), BF16)
        return [one, one, pltpu.VMEM((rows, columns), BF16)]


class LineSum:
    def __init__(self, copies, at, values, buffers, final, begin, end):
        self.at, self.values, self.final, self.range = at, values, final, (begin, end)
        self.pair, self.outer_in, self.inner_in = buffers

        def part(ref):
            return ref.at[:, begin:end]

        self.up = copies.remote(part(self.pair), part(self.outer_in), at.to_ctx[1], False)
        self.across = copies.remote(part(self.pair), part(self.inner_in), at.to_ctx[3], False)
        self.down = copies.remote(part(final), part(final), at.to_ctx[1], False)

    def each(self, body):
        begin, end = self.range

        def one(index, carry):
            body(pl.ds(pl.multiple_of(begin + index * STEP, LANES), STEP))
            return carry

        lax.fori_loop(0, (end - begin) // STEP, one, 0)

    def gather(self):
        half = self.pair.shape[0] // 2

        @pl.when(self.at.outer)
        def _():
            def add(cols):
                top, low = self.values(cols)
                self.pair[:half, cols] = top.astype(BF16)
                self.pair[half:, cols] = low.astype(BF16)

            self.each(add)
            self.up.start()

    def join(self):
        half = self.pair.shape[0] // 2

        @pl.when(self.at.inner)
        def _():
            self.up.wait_recv()

            def add(cols):
                top, low = self.values(cols)
                self.pair[:half, cols] = (top + self.outer_in[:half, cols].astype(F32)).astype(BF16)
                self.pair[half:, cols] = (low + self.outer_in[half:, cols].astype(F32)).astype(BF16)

            self.each(add)
            self.across.start()

    def share(self):
        @pl.when(self.at.inner)
        def _():
            self.across.wait_recv()

            def add(cols):
                self.final[:, cols] = (
                    self.pair[:, cols].astype(F32) + self.inner_in[:, cols].astype(F32)
                ).astype(BF16)

            self.each(add)
            self.down.start()

    def finish(self):
        @pl.when(self.at.outer)
        def _():
            self.up.wait_send()
            self.down.wait_recv()

        @pl.when(self.at.inner)
        def _():
            self.across.wait_send()
            self.down.wait_send()

    @staticmethod
    def scratch(rows, columns):
        return [pltpu.VMEM((rows, columns), BF16)] * 3


def chunks(tokens, size=256):
    return [slice(start, start + size) for start in range(0, tokens, size)]


def as_f32(ref, index, rows=slice(None)):
    return ref[index, rows].astype(F32)


def take_halves(got, out, at, heads, start, put):
    half = out.shape[0] // 2
    for tile in range(heads // 2):
        base = 0 if tile < 2 else start
        if tile < 2:
            one, two = 2 * tile, 2 * tile + 1
        else:
            one, two = at.here_high * 2, at.here_high * 2 + 1
        rows = slice(base, base + QB)
        left, right = as_f32(got, one, rows), as_f32(got, two, rows)
        for side in range(2):
            put(tile, slice(side * half, side * half + half), lane_pair((left, side), (right, side)))


def take_mixed(got, mixed, at, heads):
    def put(tile, rows, value):
        mixed[rows, tile * LANES : (tile + 1) * LANES] = value.astype(BF16)

    take_halves(got, mixed, at, heads, QB, put)


def write_grad_o(grad, out, heads):
    for c in range(4):
        out[c, :QB] = halves_pair(grad, 0, c)
        if heads == 6:
            out[c, QB:] = halves_pair(grad, 0, 4 + c % 2)


def send_blocks(copies, at, mine, out, begin=0, end=None, start=True):
    rows = mine.shape[1]
    end = rows if end is None else end
    far = min(end, rows if rows in (QB, QB + KB) else rows - QB)
    part = pl.ds(begin, end - begin)
    done = [copies.local(mine.at[at.here, part], out.at[at.here, part], start)]
    for other, device, last in zip(at.ctx[1:], at.to_ctx[1:], (end, far, far)):
        part = pl.ds(begin, last - begin)
        done.append(copies.remote(mine.at[other, part], out.at[at.here, part], device, start))
    return done


MIDDLE_IN, MIDDLE_OUT, MIDDLE_SCRATCH = 7, 5, 22


def middle_kernel(*refs):
    at = partners()
    ins = [refs[:MIDDLE_IN], refs[MIDDLE_IN : 2 * MIDDLE_IN]]
    refs = refs[2 * MIDDLE_IN :]
    outs = [refs[:MIDDLE_OUT], refs[MIDDLE_OUT : 2 * MIDDLE_OUT]]
    refs = refs[2 * MIDDLE_OUT :]
    scratch = [refs[:MIDDLE_SCRATCH], refs[MIDDLE_SCRATCH : 2 * MIDDLE_SCRATCH]]
    arrivals = refs[2 * MIDDLE_SCRATCH : 2 * MIDDLE_SCRATCH + 4]
    near = refs[2 * MIDDLE_SCRATCH + 4]
    copies = Copies(*refs[2 * MIDDLE_SCRATCH + 5 :])
    others = [at.to_x, at.to_y] + at.to_ctx[1:] + [at.to_core]
    greet(others)
    streams = []
    for in_refs, out_refs, own in zip(ins, outs, scratch):
        s = Bag()
        o_in, x_in, dy_in, s.small, proj_in, up_in, down_in = in_refs
        s.y_out, s.dmid_out, s.do_out, s.rest_out, s.sums = out_refs
        (
            s.proj, s.up, s.down, s.rest, s.mixed, s.part, s.part_in, s.mid, s.first, s.first_t, s.dy_t,
            s.act, s.dz, s.grad, s.grad_in, s.do, s.do_mine, s.o, s.x, s.dy, s.y, s.dmid,
        ) = own
        s.heads = proj_in.shape[1] // HD
        s.o_done = copies.local(o_in, s.o)
        s.proj_done = copies.local(proj_in, s.proj)
        s.rows_done = [copies.local(x_in, s.x), copies.local(dy_in, s.dy)]
        s.weights = ((up_in, s.up), (down_in, s.down))
        streams.append(s)
    text, image = streams
    text.rest_done = [copies.local(src, dst) for src, dst in text.weights]
    quarter = image.up.shape[0] // 4
    close = [
        pl.ds(pl.multiple_of(owner * quarter, 8), quarter)
        for owner in (at.group, at.group_x, at.group_y)
    ]
    image.rest_done = [
        copies.local(src.at[rows, :], dst.at[rows, :])
        for src, dst in image.weights
        for rows in close
    ]
    meet(others)
    top = pl.ds(pl.multiple_of(at.group_y * quarter, 8), quarter // 2)
    low = pl.ds(pl.multiple_of(at.group_x * quarter + quarter // 2, 8), quarter // 2)
    image.far_done = []
    for src, dst in image.weights:
        image.far_done.append(copies.remote(src.at[top, :], dst.at[top, :], at.to_x))
        image.far_done.append(copies.remote(src.at[low, :], dst.at[low, :], at.to_y))
    text.far_done = []

    def project(s):
        s.o_done.wait()
        take_mixed(s.o, s.mixed, at, s.heads)
        s.proj_done.wait()
        for cols in chunks(s.x.shape[1]):
            s.part[:, cols] = dot(s.mixed[...], s.proj[cols, :], ((1,), (1,)))
        s.part_done = copies.remote(s.part, s.part_in, at.to_core)
        s.sums[...] = jnp.zeros_like(s.sums)
        for copy in s.rows_done:
            copy.wait()
        for rows in chunks(s.dy.shape[0]):
            s.dy_t[:, rows] = jnp.transpose(s.dy[rows, :])

    def second_norm(s):
        s.part_done.wait()
        for rows in chunks(s.x.shape[0]):
            middle = (
                s.x[rows, :].astype(F32) + s.part[rows, :] + s.part_in[rows, :] + s.small[3:4]
            )
            s.mid[rows, :] = middle
            normed, _ = normalise(middle)
            low = (normed * s.small[1:2] + s.small[4:5]).astype(BF16)
            s.first[rows, :] = low
            s.first_t[:, rows] = jnp.transpose(low)

    def feed_forward(s):
        tokens, width = s.x.shape
        hidden, own = s.up.shape[1], s.proj.shape[1]
        size = width // TILES
        for copy in s.rest_done:
            copy.wait()
        for copy in s.far_done:
            copy.wait_recv()

        def tile(index, carry):
            cols = pl.ds(pl.multiple_of(index * size, LANES), size)
            up, down = s.up[:, cols], s.down[:, cols]
            up_cols = pl.ds(pl.multiple_of(own + index * size, LANES), size)
            down_cols = pl.ds(pl.multiple_of(own + hidden + index * size, LANES), size)
            row = pl.ds(7 + index // (width // size), 1)
            place = pl.ds(pl.multiple_of((index % (width // size)) * size, LANES), size)
            bias = s.small[row, place]
            total = jnp.zeros((1, size), F32)
            for rows in chunks(tokens):
                z = dot(s.first[rows, :], up) + bias
                sg = jax.nn.sigmoid(1.702 * z)
                zs = z * sg
                s.act[rows, cols] = zs.astype(BF16)
                grad = dot(s.dy[rows, :], down)
                low = (grad * (sg + 1.702 * zs * (1.0 - sg))).astype(BF16)
                s.dz[rows, cols] = low
                total = total + jnp.sum(low.astype(F32), axis=0, keepdims=True)
            s.sums[row, place] = total
            s.rest[:, up_cols] = dot(s.first_t[...], s.dz[:, cols]).astype(BF16)
            s.rest[:, down_cols] = dot(s.dy_t[...], s.act[:, cols]).astype(BF16)
            return carry

        lax.fori_loop(0, hidden // size, tile, 0)
        for cols in chunks(width):
            s.grad[0, :, cols] = dot(s.dz[...], s.up[cols, :], ((1,), (1,)))
        s.grad_done = copies.remote(s.grad.at[0], s.grad_in.at[0], at.to_core)
        for cols in chunks(width):
            s.grad[1, :, cols] = dot(s.act[...], s.down[cols, :], ((1,), (1,)))
        s.y_done = copies.remote(s.grad.at[1], s.grad_in.at[1], at.to_core)

    def back(s):
        sums = s.sums
        s.grad_done.wait()
        for rows in chunks(s.x.shape[0]):
            normed, inv = normalise(s.mid[rows, :])
            second = s.grad[0, rows, :] + s.grad_in[0, rows, :]
            scaled = second * s.small[1:2]
            dy = s.dy[rows, :].astype(F32)
            dmid = dy + inv * (
                scaled
                - jnp.mean(scaled, axis=-1, keepdims=True)
                - normed * jnp.mean(scaled * normed, axis=-1, keepdims=True)
            )
            s.dmid[rows, :] = dmid
            sums[1:2] += jnp.sum(second * normed, axis=0, keepdims=True)
            sums[3:4] += jnp.sum(dmid, axis=0, keepdims=True)
            sums[4:5] += jnp.sum(second, axis=0, keepdims=True)
            sums[5:6] += jnp.sum(dy, axis=0, keepdims=True)
            low = dmid.astype(BF16)
            s.first_t[:, rows] = jnp.transpose(low)
            s.do[rows, :] = dot(low, s.proj[...])
        s.writes = [copies.local(s.dmid, s.dmid_out)]
        write_grad_o(s.do, s.do_mine, s.heads)
        s.do_done = send_blocks(copies, at, s.do_mine, s.do_out)

    def proj_grad(s):
        s.rest[:, : s.proj.shape[1]] = dot(s.first_t[...], s.mixed[...]).astype(BF16)

    def output(s):
        s.y_done.wait()
        for rows in chunks(s.x.shape[0]):
            s.y[rows, :] = (
                s.mid[rows, :] + s.grad[1, rows, :] + s.grad_in[1, rows, :] + s.small[5:6]
            ).astype(BF16)
        s.writes.append(copies.local(s.y, s.y_out))

    project(text)
    project(image)
    second_norm(text)
    feed_forward(text)
    second_norm(image)
    back(text)
    proj_grad(text)
    plane = PlaneSum(copies, at, text.rest, arrivals)
    feed_forward(image)
    plane.cross()
    back(image)
    proj_grad(image)
    keep = copies.local(image.rest, image.rest_out)
    output(text)
    output(image)
    plane.arrived()
    half = plane.half

    def put(cols):
        near[:half, cols], near[half:, cols] = plane.halves(cols)

    by_columns(plane.columns, put)
    near_done = copies.local(near, text.rest_out)
    plane.sent()
    keep.wait()
    near_done.wait()
    for s in streams:
        for copy in s.do_done + s.writes:
            copy.wait()
        for copy in s.far_done:
            copy.wait_send()


def middle(streams):
    vmem, hbm = pl.BlockSpec(memory_space=pltpu.VMEM), pl.BlockSpec(memory_space=pl.ANY)
    out_shape, out_specs, scratch = [], [], []
    arrivals = None
    for o, x, dy, small, proj, up, down in streams:
        tokens, width = x.shape
        hidden, own = up.shape[1], proj.shape[1]
        rest = (width, own + 2 * hidden)
        summed = arrivals is None
        if summed:
            arrivals = PlaneSum.arrivals(width // 4, rest[1])
            arrivals.append(pltpu.VMEM((width // 4, rest[1]), F32))
        out_shape += [
            jax.ShapeDtypeStruct((tokens, width), BF16),
            jax.ShapeDtypeStruct((tokens, width), F32),
            jax.ShapeDtypeStruct(o.shape, BF16),
            jax.ShapeDtypeStruct((width // 4, rest[1]), F32)
            if summed
            else jax.ShapeDtypeStruct(rest, BF16),
            jax.ShapeDtypeStruct(small.shape, F32),
        ]
        out_specs += [hbm, hbm, hbm, hbm, vmem]
        scratch += [
            pltpu.VMEM(proj.shape, BF16),
            pltpu.VMEM(up.shape, BF16),
            pltpu.VMEM(down.shape, BF16),
            pltpu.VMEM(rest, BF16),
            pltpu.VMEM((tokens, own), BF16),
            pltpu.VMEM((tokens, width), F32),
            pltpu.VMEM((tokens, width), F32),
            pltpu.VMEM((tokens, width), F32),
            pltpu.VMEM((tokens, width), BF16),
            pltpu.VMEM((width, tokens), BF16),
            pltpu.VMEM((width, tokens), BF16),
            pltpu.VMEM((tokens, hidden), BF16),
            pltpu.VMEM((tokens, hidden), BF16),
            pltpu.VMEM((2, tokens, width), F32),
            pltpu.VMEM((2, tokens, width), F32),
            pltpu.VMEM((tokens, own), F32),
            pltpu.VMEM(o.shape, BF16),
            pltpu.VMEM(o.shape, BF16),
            pltpu.VMEM((tokens, width), BF16),
            pltpu.VMEM((tokens, width), BF16),
            pltpu.VMEM((tokens, width), BF16),
            pltpu.VMEM((tokens, width), F32),
        ]
    results = pl.pallas_call(
        middle_kernel,
        out_shape=out_shape,
        in_specs=([hbm] * 3 + [vmem] + [hbm] * 3) * 2,
        out_specs=out_specs,
        scratch_shapes=scratch + arrivals + copy_sems(2 * 6 + 4 + 6, 2 * (4 + 3) + 8 + 2),
        compiler_params=pltpu.CompilerParams(
            collective_id=1, has_side_effects=True, vmem_limit_bytes=64 * 1024 * 1000
        ),
        name="middle",
    )(*streams[0], *streams[1])
    return results[:MIDDLE_OUT], results[MIDDLE_OUT:]


def take_dqkv(got, out, at, heads):
    width = heads * HD

    def put(which, tile, rows, value):
        start = which * width + tile * LANES
        out[rows, start : start + LANES] = value.astype(BF16)

    take_halves(got, out, at, heads, QB + 2 * KB, functools.partial(put, 0))

    def keys(position, head):
        return as_f32(got, position, key_rows(head))

    pairs = [(keys(0, 0), keys(1, 0)), (keys(2, 0), keys(3, 0))]
    if heads == 6:
        pairs.append((keys(0, 1) + keys(2, 1), keys(1, 1) + keys(3, 1)))
    for tile, (one, two) in enumerate(pairs):
        put(1, tile, slice(None), lane_pair((one, 0), (two, 0)))
        put(2, tile, slice(None), lane_pair((one, 1), (two, 1)))


LAST_IN, LAST_OUT, LAST_SCRATCH = 12, 4, 22


def last_kernel(*refs):
    at = partners()
    ins = [refs[:LAST_IN], refs[LAST_IN : 2 * LAST_IN]]
    refs = refs[2 * LAST_IN :]
    outs = [refs[:LAST_OUT], refs[LAST_OUT : 2 * LAST_OUT]]
    refs = refs[2 * LAST_OUT :]
    count = LAST_SCRATCH + 10
    scratch = [refs[:count], refs[count : 2 * count]]
    refs = refs[2 * count :]
    rest_arrivals, rest_loads, text_near = refs[:4], refs[4:7], refs[7]
    copies = Copies(*refs[8:])
    others = [at.to_x, at.to_y] + at.to_ctx[1:] + [at.to_core]
    greet(others)
    streams = []
    for in_refs, out_refs, own in zip(ins, outs, scratch):
        s = Bag()
        (
            s.m_in, s.do_in, s.o_in, s.lse, s.seg_row, s.first_in, s.x_in, s.small, s.weight_in, s.dmid_in,
            s.rest, s.sums_in,
        ) = in_refs
        s.grad_rows_out, s.sums, s.rest_final, s.qkv_final = out_refs
        (
            s.m, s.do, s.o, s.query_doc, s.key_doc, s.score_keys, s.grad_rows, s.acc, s.back, s.got, s.dqkv, s.weight, s.first, s.x, s.dmid,
            s.part, s.part_in, s.g_qkv, s.sums_own, s.sums_out, s.sums_got, s.sums_line,
        ) = own[:LAST_SCRATCH]
        s.rest_line, s.qkv_line = own[LAST_SCRATCH : LAST_SCRATCH + 3], own[LAST_SCRATCH + 3 : LAST_SCRATCH + 6]
        s.qkv_arrivals = own[LAST_SCRATCH + 6 :]
        s.heads = s.weight.shape[2] // HD
        s.features = (s.query_doc, s.key_doc)
        s.reads = [
            copies.local(src, dst) for src, dst in ((s.m_in, s.m), (s.do_in, s.do), (s.o_in, s.o))
        ]
        streams.append(s)
    text, image = streams

    def prepare(s):
        document_features(s.seg_row, *s.features)
        s.acc[...] = jnp.zeros_like(s.acc)
        s.back[...] = jnp.zeros_like(s.back)

    rest_done = copies.local(text.rest, text_near)
    prepare(image)
    meet(others)
    plane = PlaneSum(copies, at, image.rest, rest_arrivals, rest_loads)
    text_half = text_near.shape[0] // 2

    def text_values(cols):
        return text_near[:text_half, cols], text_near[text_half:, cols]

    text_line = LineSum(
        copies, at, text_values, text.rest_line, text.rest_final, 0, text.rest.shape[1]
    )
    rest_done.wait()
    text_line.gather()
    for s in (image, text):
        for copy in s.reads:
            copy.wait()
        s.loads = [
            copies.local(src, dst)
            for src, dst in (
                (s.first_in, s.first), (s.weight_in, s.weight), (s.x_in, s.x), (s.dmid_in, s.dmid),
            )
        ]
    mark_keys(image.m, image.features[1], 2, image.score_keys, None)

    def unattend_tasks(s, *task):
        unattend(
            at, s.m, s.do, s.o, s.lse, s.features[0], s.score_keys, s.acc, s.back, *task
        )

    text.sends = send_blocks(copies, at, text.back, text.got, start=False)
    split = QB + KB
    shared_sends = send_blocks(copies, at, image.back, image.got, split, None, False)
    own_sends = send_blocks(copies, at, image.back, image.got, 0, split, False)
    image.sends = shared_sends + own_sends

    def image_phase(phase, carry):
        unattend_tasks(image, image_task, phase * 4, phase * 4 + 4, 4, False)

        @pl.when(phase == 0)
        def _():
            key_gradients(image.acc, image.back, 1)
            for copy in shared_sends:
                copy.start()

        return carry

    lax.fori_loop(0, 3, image_phase, 0)
    key_gradients(image.acc, image.back, 0)
    for copy in own_sends:
        copy.start()

    text_line.join()
    prepare(text)
    mark_keys(text.m, text.features[1], 1, text.score_keys, None)

    def text_phase(phase, carry):
        unattend_tasks(text, text_task, phase * 4, phase * 4 + 4, 4, True)

        @pl.when(phase == 0)
        def _():
            plane.cross()

        return carry

    lax.fori_loop(0, 2, text_phase, 0)
    key_gradients(text.acc, text.back, 0)
    for copy in text.sends:
        copy.start()

    def project(s):
        width = s.x.shape[1]
        own = s.heads * HD
        for copy in s.sends:
            copy.wait()
        for copy in s.loads:
            copy.wait()
        take_dqkv(s.got, s.dqkv, at, s.heads)
        for which in range(3):
            cols = slice(which * own, (which + 1) * own)
            s.g_qkv[:, cols] = dot(s.first[...], s.dqkv[:, cols]).astype(BF16)
        s.qkv_plane = PlaneSum(copies, at, s.g_qkv, s.qkv_arrivals)
        for cols in chunks(width):
            total = dot(s.dqkv[:, :own], s.weight[0, cols, :], ((1,), (1,)))
            total = total + dot(s.dqkv[:, own : 2 * own], s.weight[1, cols, :], ((1,), (1,)))
            s.part[:, cols] = total + dot(s.dqkv[:, 2 * own :], s.weight[2, cols, :], ((1,), (1,)))
        s.part_done = copies.remote(s.part, s.part_in, at.to_core)
        s.sums_own[...] = s.sums_in[...]
        s.sums_own[6:7, :own] = jnp.sum(s.dqkv[:, :own].astype(F32), axis=0, keepdims=True)
        s.sums_own[6:7, own:] = jnp.sum(s.dqkv[:, 2 * own :].astype(F32), axis=0, keepdims=True)
        cuts = (0, 3 * own) if own < STEP else (0, 2 * own, 3 * own)
        s.qkv_sums = [
            LineSum(copies, at, s.qkv_plane.halves, s.qkv_line, s.qkv_final, begin, end)
            for begin, end in zip(cuts, cuts[1:])
        ]

    def input_grad(s):
        s.part_done.wait()
        for rows in chunks(s.x.shape[0]):
            normed, inv = normalise(s.x[rows, :].astype(F32))
            first = s.part[rows, :] + s.part_in[rows, :]
            scaled = first * s.small[0:1]
            s.grad_rows[rows, :] = s.dmid[rows, :] + inv * (
                scaled
                - jnp.mean(scaled, axis=-1, keepdims=True)
                - normed * jnp.mean(scaled * normed, axis=-1, keepdims=True)
            )
            s.sums_own[0:1] += jnp.sum(first * normed, axis=0, keepdims=True)
            s.sums_own[2:3] += jnp.sum(first, axis=0, keepdims=True)
        s.write = copies.local(s.grad_rows, s.grad_rows_out)
        s.sums_done = [copies.remote(s.sums_own, s.sums_got.at[0], at.to_x)]

    def add_sums(s, step):
        s.sums_done[-1].wait_recv()
        before = s.sums_own if step == 0 else s.sums_out
        total = before[...] + s.sums_got[step]
        if step == 0:
            s.sums_out[...] = total
            s.sums_done.append(copies.remote(s.sums_out, s.sums_got.at[1], at.to_y))
        else:
            s.sums_line[at.here] = total
            mine = s.sums_line.at[at.here]
            s.sums_done += [copies.remote(mine, mine, device) for device in at.to_ctx[1:]]

    def end_sums(s):
        for copy in s.sums_done[2:]:
            copy.wait_recv()
        s.sums[...] = s.sums_line[0] + s.sums_line[1] + s.sums_line[2] + s.sums_line[3]

    cuts = [0, STEP, 4 * STEP, 7 * STEP, plane.columns]
    rest_lines = [
        LineSum(copies, at, plane.halves, image.rest_line, image.rest_final, begin, end)
        for begin, end in zip(cuts, cuts[1:])
    ]

    project(image)
    plane.arrived()
    for line in rest_lines:
        line.gather()
    input_grad(image)
    image.qkv_plane.cross()
    text_line.share()
    add_sums(image, 0)
    rest_lines[0].join()
    rest_lines[1].join()
    project(text)
    rest_lines[2].join()
    input_grad(text)
    image.qkv_plane.arrived()
    for line in image.qkv_sums:
        line.gather()
    text.qkv_plane.cross()
    add_sums(image, 1)
    add_sums(text, 0)
    rest_lines[0].share()
    text.qkv_plane.arrived()
    text.qkv_sums[0].gather()
    add_sums(text, 1)
    rest_lines[1].share()
    rest_lines[3].join()
    image.qkv_sums[0].join()
    rest_lines[2].share()
    image.qkv_sums[1].join()
    text.qkv_sums[0].join()
    rest_lines[3].share()
    for line in image.qkv_sums + text.qkv_sums:
        line.share()
    for s in streams:
        end_sums(s)
    for line in [text_line] + rest_lines + image.qkv_sums + text.qkv_sums:
        line.finish()
    plane.sent()
    for s in streams:
        s.qkv_plane.sent()
        for copy in s.sums_done:
            copy.wait_send()
        s.write.wait()


def last(streams):
    vmem, hbm = pl.BlockSpec(memory_space=pltpu.VMEM), pl.BlockSpec(memory_space=pl.ANY)
    out_shape, scratch = [], []
    for messages, do, o, lse, seg, first, x, small, weight, dmid, rest, sums in streams:
        tokens, width = x.shape
        own = weight.shape[2]
        rest_shape, qkv_shape = (width // 4, rest.shape[1]), (width // 4, 3 * own)
        out_shape += [
            jax.ShapeDtypeStruct((tokens, width), F32),
            jax.ShapeDtypeStruct(small.shape, F32),
            jax.ShapeDtypeStruct(rest_shape, BF16),
            jax.ShapeDtypeStruct(qkv_shape, BF16),
        ]
        scratch += [
            pltpu.VMEM(messages.shape, BF16),
            pltpu.VMEM(do.shape, BF16),
            pltpu.VMEM(do.shape, BF16),
            pltpu.VMEM((4 * tokens, LANES), BF16),
            pltpu.VMEM((4 * tokens, LANES), BF16),
            pltpu.VMEM((1 if own == 4 * HD else 2, 4 * tokens, LANES), BF16),
            pltpu.VMEM((tokens, width), F32),
            pltpu.VMEM((1 if own == 4 * HD else 2, 4 * tokens, LANES), F32),
            pltpu.VMEM(messages.shape, BF16),
            pltpu.VMEM(messages.shape, BF16),
            pltpu.VMEM((tokens, 3 * own), BF16),
            pltpu.VMEM(weight.shape, BF16),
            pltpu.VMEM(first.shape, BF16),
            pltpu.VMEM((tokens, width), BF16),
            pltpu.VMEM((tokens, width), F32),
            pltpu.VMEM((tokens, width), F32),
            pltpu.VMEM((tokens, width), F32),
            pltpu.VMEM((width, 3 * own), BF16),
            pltpu.VMEM(small.shape, F32),
            pltpu.VMEM(small.shape, F32),
            pltpu.VMEM((2,) + small.shape, F32),
            pltpu.VMEM((4,) + small.shape, F32),
        ]
        scratch += LineSum.scratch(*rest_shape) + LineSum.scratch(*qkv_shape)
        scratch += PlaneSum.arrivals(*qkv_shape)
    scratch += PlaneSum.arrivals(*rest_shape) + PlaneSum.loads_scratch(*rest_shape)
    scratch += [pltpu.VMEM(streams[0][10].shape, F32)]
    specs = [hbm, hbm, hbm, vmem, vmem, hbm, hbm, vmem, hbm, hbm, hbm, vmem]
    specs += specs[:10] + [hbm, vmem]
    results = pl.pallas_call(
        last_kernel,
        out_shape=out_shape,
        in_specs=specs,
        out_specs=[hbm, vmem, vmem, vmem] * 2,
        scratch_shapes=scratch + copy_sems(2 * (3 + 1 + 5 + 6) + 3 + 6 + 3 * 8, 2 * (1 + 7 + 1) + 3 + 2),
        compiler_params=pltpu.CompilerParams(
            collective_id=2, has_side_effects=True, vmem_limit_bytes=64 * 1024 * 1000
        ),
        name="last",
    )(*streams[0], *streams[1])
    return results[:4], results[4:]


def take_own(group, row):
    columns = row.shape[1] // 4
    return pltpu.roll(row, (4 - group) % 4 * columns, 1)[:, :columns]


FINISH_IN, FINISH_OUT = 5, 9


def finish_kernel(*refs):
    ins = [refs[:FINISH_IN], refs[FINISH_IN : 2 * FINISH_IN]]
    refs = refs[2 * FINISH_IN :]
    outs = [refs[:FINISH_OUT], refs[FINISH_OUT : 2 * FINISH_OUT]]
    refs = refs[2 * FINISH_OUT :]
    count = FINISH_IN + FINISH_OUT - 2
    scratch = [refs[:count], refs[count : 2 * count]]
    reads, writes = refs[2 * count :]
    streams, written = [], []

    def write(src, dst):
        copy = pltpu.make_async_copy(src, dst, writes.at[len(written)])
        copy.start()
        written.append(copy)

    for which, (in_refs, own) in enumerate(zip(ins, scratch)):
        streams.append([])
        for index in range(FINISH_IN):
            copy = pltpu.make_async_copy(
                in_refs[index], own[index], reads.at[which * FINISH_IN + index]
            )
            copy.start()
            streams[which].append(copy)
    for copies, out, own in reversed(list(zip(streams, outs, scratch))):
        sums, rest, qkv, y, grad, gains, shifts, bias, qkv_out, proj, up, down = own
        copies[1].wait()
        width = qkv.shape[1] // 3
        hidden = up.shape[1]
        up[...] = rest[:, width : width + hidden].astype(F32)
        write(up, out[5])
        if down.shape[0] > down.shape[1]:
            down[...] = jnp.transpose(rest[:, width + hidden :].astype(F32))
            proj[...] = jnp.transpose(rest[:, :width].astype(F32))
        else:
            down[...] = rest[:, width + hidden :].astype(F32)
            proj[...] = rest[:, :width].astype(F32)
        write(down, out[6])
        write(proj, out[4])
        copies[2].wait()
        for index in range(3):
            qkv_out[index] = qkv[:, index * width : (index + 1) * width].astype(F32)
        write(qkv_out, out[3])
        copies[3].wait()
        write(y, out[7])
        copies[4].wait()
        write(grad, out[8])
        copies[0].wait()
        group = lax.axis_index(FSDP)
        rows = take_own(group, sums[0:8])
        gains[...] = rows[0:2]
        shifts[...] = rows[2:6]
        line = jnp.concatenate([sums[6:7], sums[7:8], sums[8:9]], axis=1)
        bias[...] = take_own(group, jnp.broadcast_to(line, (8, line.shape[1])))[0:1]
        write(gains, out[0])
        write(shifts, out[1])
        write(bias, out[2])
    for copy in written:
        copy.wait()


def finish(streams):
    hbm = pl.BlockSpec(memory_space=pl.ANY)
    out_shape, scratch = [], []
    for sums, rest, qkv, y, grad, flip in streams:
        rows, own = qkv.shape[0], qkv.shape[1] // 3
        hidden = (rest.shape[1] - own) // 2
        shapes = [(2, rows), (4, rows), (1, 3 * rows), (3, rows, own)]
        shapes += [(own, rows), (rows, hidden), (hidden, rows)] if flip else [
            (rows, own), (rows, hidden), (rows, hidden)
        ]
        out_shape += [jax.ShapeDtypeStruct(shape, F32) for shape in shapes]
        out_shape += [jax.ShapeDtypeStruct(a.shape, a.dtype) for a in (y, grad)]
        scratch += [pltpu.VMEM(a.shape, a.dtype) for a in (sums, rest, qkv, y, grad)]
        scratch += [pltpu.VMEM(shape, F32) for shape in shapes]
    results = pl.pallas_call(
        finish_kernel,
        out_shape=out_shape,
        in_specs=[hbm] * (2 * FINISH_IN),
        out_specs=[hbm] * (2 * FINISH_OUT),
        scratch_shapes=scratch
        + [
            pltpu.SemaphoreType.DMA((2 * FINISH_IN,)),
            pltpu.SemaphoreType.DMA((2 * FINISH_OUT,)),
        ],
        compiler_params=pltpu.CompilerParams(vmem_limit_bytes=64 * 1024 * 1000),
        name="finish",
    )(*streams[0][:FINISH_IN], *streams[1][:FINISH_IN])
    return results[:FINISH_OUT], results[FINISH_OUT:]


def on_device(*args):
    streams = []
    for item, causal in ((args[10:], True), (args[:10], False)):
        s = Bag()
        rows, s.seg, cotangent, s.gains, s.shifts, s.head_bias, s.qkv, proj, s.up, down = item
        s.flip, s.x, s.dy = causal, rows[0], cotangent[0]
        s.down, s.proj = (down, proj) if causal else (down.T, proj.T)
        streams.append(s)
    started = front(
        [(s.x, s.seg, s.gains, s.shifts, s.head_bias, s.qkv, s.up, s.down, s.proj) for s in streams]
    )
    for s, (weight, small, first, messages, proj, up, down, o, lse, o_got) in zip(streams, started):
        s.weight, s.small, s.first, s.messages, s.o, s.lse = weight, small, first, messages, o, lse
        s.weights, s.o_got = (proj, up, down), o_got
    done = middle([(s.o_got, s.x, s.dy, s.small, *s.weights) for s in streams])
    ended = last(
        [
            (s.messages, do, s.o, s.lse, s.seg, s.first, s.x, s.small, s.weight, dmid, rest, sums)
            for s, (y, dmid, do, rest, sums) in zip(streams, done)
        ]
    )
    final = finish(
        [
            (sums, rest, qkv, y, grad, s.flip)
            for s, (y, *_), (grad, sums, rest, qkv) in zip(streams, done, ended)
        ]
    )
    outputs = []
    for s, (gains, shifts, bias, qkv, proj, up, down, y, grad_rows) in zip(streams, final):
        if not s.flip:
            proj, down = proj.T, down.T
        outputs.append((y[None], grad_rows[None], gains, shifts, bias, qkv, proj, up, down))
    return outputs[1] + outputs[0]


def layer_stats(rows):
    row_mean = jnp.mean(rows, axis=-1, keepdims=True)
    centred = rows - row_mean
    inv_std = lax.rsqrt(jnp.mean(centred * centred, axis=-1, keepdims=True) + 1e-05)
    return (centred * inv_std, inv_std)


def norm_back(grad_normed_out, normed, inv_std, gain):
    scaled = grad_normed_out * gain
    return inv_std * (
        scaled
        - jnp.mean(scaled, axis=-1, keepdims=True)
        - normed * jnp.mean(scaled * normed, axis=-1, keepdims=True)
    )


def tensor_psum(partial_rows):
    return lax.psum(partial_rows, TP)


def any_mesh_block(
    rows_in,
    seg_row,
    cotangent,
    gains,
    shifts,
    head_bias,
    qkv_weight,
    proj_weight,
    up_weight,
    down_weight,
    causal,
):
    gain_full, shift_full, bias_full, qkv_full, proj_full, up_full, down_full = (
        lax.all_gather(gains, FSDP, axis=1, tiled=True),
        lax.all_gather(shifts, FSDP, axis=1, tiled=True),
        lax.all_gather(head_bias, FSDP, axis=1, tiled=True),
        lax.all_gather(qkv_weight, FSDP, axis=1, tiled=True),
        lax.all_gather(proj_weight, FSDP, axis=1, tiled=True),
        lax.all_gather(up_weight, FSDP, axis=0, tiled=True),
        lax.all_gather(down_weight, FSDP, axis=1, tiled=True),
    )
    gain_vals = gain_full.astype(jnp.float32)
    shift_vals = shift_full.astype(jnp.float32)
    bias_vals = bias_full[0].astype(jnp.float32)
    tp_width = qkv_full.shape[2]
    local_rows = rows_in.shape[1]
    seq_length = seg_row.shape[1]
    head_local = tp_width // HD
    rows = rows_in[0].astype(jnp.float32)
    row_start = lax.axis_index(CTX) * local_rows
    seg_all = seg_row[0]
    seg_query = lax.dynamic_slice_in_dim(seg_all, row_start, local_rows)
    query_pos = row_start + jnp.arange(local_rows, dtype=jnp.int32)
    key_pos = jnp.arange(seq_length, dtype=jnp.int32)
    allowed = seg_query[:, None] == seg_all[None, :]
    if causal:
        allowed = jnp.logical_and(allowed, key_pos[None, :] <= query_pos[:, None])

    def to_heads(matrix):
        return matrix.reshape(matrix.shape[0], head_local, HD).transpose(1, 0, 2)

    def from_heads(stacked):
        return stacked.transpose(1, 0, 2).reshape(stacked.shape[1], head_local * HD)

    normed_one, inv_one = layer_stats(rows)
    first_in = (normed_one * gain_vals[0] + shift_vals[0]).astype(jnp.bfloat16)
    queries = (
        jnp.dot(first_in, qkv_full[0], preferred_element_type=jnp.float32) + bias_vals[:tp_width]
    ).astype(jnp.bfloat16)
    key_rows = jnp.dot(first_in, qkv_full[1], preferred_element_type=jnp.float32).astype(
        jnp.bfloat16
    )
    values = (
        jnp.dot(first_in, qkv_full[2], preferred_element_type=jnp.float32)
        + bias_vals[tp_width : 2 * tp_width]
    ).astype(jnp.bfloat16)
    key_all, value_all = (
        lax.all_gather(key_rows, CTX, axis=0, tiled=True),
        lax.all_gather(values, CTX, axis=0, tiled=True),
    )
    query_heads = to_heads(queries)
    key_heads = to_heads(key_all)
    value_heads = to_heads(value_all)

    def attend(head_items):
        query_h, key_h, value_h = head_items
        scores = dot(query_h, key_h, ((1,), (1,))) * 0.125
        scores = jnp.where(allowed, scores, -1e30)
        row_top = jnp.max(scores, axis=-1, keepdims=True)
        weights = jnp.exp(scores - row_top)
        row_total = jnp.sum(weights, axis=-1, keepdims=True)
        weights_low = (weights / row_total).astype(jnp.bfloat16)
        mixed_h = dot(weights_low, value_h, ((1,), (0,)))
        return (mixed_h.astype(jnp.bfloat16), row_top[:, 0] + jnp.log(row_total[:, 0]))

    mixed_heads, log_totals = lax.map(attend, (query_heads, key_heads, value_heads))
    mixed = from_heads(mixed_heads)
    middle = (
        rows
        + tensor_psum(jnp.dot(mixed, proj_full, preferred_element_type=jnp.float32))
        + shift_vals[1]
    )
    normed_two, inv_two = layer_stats(middle)
    second_in = (normed_two * gain_vals[1] + shift_vals[2]).astype(jnp.bfloat16)
    hidden = (
        jnp.dot(second_in, up_full, preferred_element_type=jnp.float32) + bias_vals[2 * tp_width :]
    )
    sigma = jax.nn.sigmoid(1.702 * hidden)
    activated = (hidden * sigma).astype(jnp.bfloat16)
    output = (
        middle
        + tensor_psum(jnp.dot(activated, down_full, preferred_element_type=jnp.float32))
        + shift_vals[3]
    )
    grad_out = cotangent[0].astype(jnp.float32)
    grad_down_bias = jnp.sum(grad_out, axis=0)
    grad_branch = grad_out.astype(jnp.bfloat16)
    grad_down = dot(activated, grad_branch, ((0,), (0,)))
    grad_act = dot(grad_branch, down_full, ((1,), (1,)))
    grad_hidden = (grad_act * (sigma + 1.702 * hidden * sigma * (1.0 - sigma))).astype(jnp.bfloat16)
    grad_up_bias = jnp.sum(grad_hidden.astype(jnp.float32), axis=0)
    grad_up = dot(second_in, grad_hidden, ((0,), (0,)))
    grad_second = tensor_psum(
        dot(grad_hidden, up_full, ((1,), (1,)))
    )
    grad_gain_two = jnp.sum(grad_second * normed_two, axis=0)
    grad_shift_two = jnp.sum(grad_second, axis=0)
    grad_middle = grad_out + norm_back(grad_second, normed_two, inv_two, gain_vals[1])
    grad_proj_bias = jnp.sum(grad_middle, axis=0)
    grad_attn = grad_middle.astype(jnp.bfloat16)
    grad_proj = dot(mixed, grad_attn, ((0,), (0,)))
    grad_mixed = dot(grad_attn, proj_full, ((1,), (1,))).astype(jnp.bfloat16)

    def attend_back(head_items):
        query_h, key_h, value_h, grad_h, log_total = head_items
        scores = dot(query_h, key_h, ((1,), (1,))) * 0.125
        weights = jnp.where(allowed, jnp.exp(scores - log_total[:, None]), 0.0)
        grad_weights = dot(grad_h, value_h, ((1,), (1,)))
        row_delta = jnp.sum(weights * grad_weights, axis=-1, keepdims=True)
        grad_scores = (weights * (grad_weights - row_delta)).astype(jnp.bfloat16)
        grad_query_h = (
            dot(grad_scores, key_h, ((1,), (0,))) * 0.125
        )
        grad_key_h = (
            dot(grad_scores, query_h, ((0,), (0,)))
            * 0.125
        )
        grad_value_h = dot(weights.astype(jnp.bfloat16), grad_h, ((0,), (0,)))
        return (grad_query_h, grad_key_h, grad_value_h)

    query_parts, key_parts, value_parts = lax.map(
        attend_back, (query_heads, key_heads, value_heads, to_heads(grad_mixed), log_totals)
    )
    key_sum, value_sum = (
        lax.psum_scatter(from_heads(key_parts), CTX, scatter_dimension=0, tiled=True),
        lax.psum_scatter(from_heads(value_parts), CTX, scatter_dimension=0, tiled=True),
    )
    grad_query = from_heads(query_parts).astype(jnp.bfloat16)
    grad_key = key_sum.astype(jnp.bfloat16)
    grad_value = value_sum.astype(jnp.bfloat16)
    grad_qkv = jnp.stack(
        [
            dot(first_in, grad_query, ((0,), (0,))),
            dot(first_in, grad_key, ((0,), (0,))),
            dot(first_in, grad_value, ((0,), (0,))),
        ]
    )
    grad_head = jnp.concatenate(
        [
            jnp.sum(grad_query.astype(jnp.float32), axis=0),
            jnp.sum(grad_value.astype(jnp.float32), axis=0),
            grad_up_bias,
        ]
    )[None, :]
    grad_first_part = dot(grad_query, qkv_full[0], ((1,), (1,)))
    grad_first_part = grad_first_part + dot(grad_key, qkv_full[1], ((1,), (1,)))
    grad_first_part = grad_first_part + dot(grad_value, qkv_full[2], ((1,), (1,)))
    grad_first = tensor_psum(grad_first_part)
    grad_gain_one = jnp.sum(grad_first * normed_one, axis=0)
    grad_shift_one = jnp.sum(grad_first, axis=0)
    grad_rows = grad_middle + norm_back(grad_first, normed_one, inv_one, gain_vals[0])
    grad_gains = jnp.stack([grad_gain_one, grad_gain_two])
    grad_shifts = jnp.stack([grad_shift_one, grad_proj_bias, grad_shift_two, grad_down_bias])
    share_gains, share_shifts, share_head, share_qkv, share_proj, share_up, share_down = (
        lax.psum_scatter(grad_gains, FSDP, scatter_dimension=1, tiled=True),
        lax.psum_scatter(grad_shifts, FSDP, scatter_dimension=1, tiled=True),
        lax.psum_scatter(grad_head, FSDP, scatter_dimension=1, tiled=True),
        lax.psum_scatter(grad_qkv, FSDP, scatter_dimension=1, tiled=True),
        lax.psum_scatter(grad_proj, FSDP, scatter_dimension=1, tiled=True),
        lax.psum_scatter(grad_up, FSDP, scatter_dimension=0, tiled=True),
        lax.psum_scatter(grad_down, FSDP, scatter_dimension=1, tiled=True),
    )
    owned = lax.psum(
        (share_gains, share_shifts, share_head, share_qkv, share_proj, share_up, share_down), CTX
    )
    return (output.astype(jnp.bfloat16)[None], grad_rows[None]) + tuple(owned)


def on_any_mesh(
    image_input,
    image_segments,
    image_cotangent,
    image_gains,
    image_shifts,
    image_head_bias,
    image_qkv_weight,
    image_proj_weight,
    image_up_weight,
    image_down_weight,
    text_input,
    text_segments,
    text_cotangent,
    text_gains,
    text_shifts,
    text_head_bias,
    text_qkv_weight,
    text_proj_weight,
    text_up_weight,
    text_down_weight,
):
    image_results = any_mesh_block(
        image_input,
        image_segments,
        image_cotangent,
        image_gains,
        image_shifts,
        image_head_bias,
        image_qkv_weight,
        image_proj_weight,
        image_up_weight,
        image_down_weight,
        False,
    )
    text_results = any_mesh_block(
        text_input,
        text_segments,
        text_cotangent,
        text_gains,
        text_shifts,
        text_head_bias,
        text_qkv_weight,
        text_proj_weight,
        text_up_weight,
        text_down_weight,
        True,
    )
    return image_results + text_results


def stream_specs():
    return (
        P(FSDP, CTX, None),
        P(FSDP, None),
        P(FSDP, CTX, None),
        P(None, FSDP),
        P(None, FSDP),
        P(TP, FSDP),
        P(None, FSDP, TP),
        P(TP, FSDP),
        P(FSDP, TP),
        P(TP, FSDP),
    )


def solution(mesh):
    one = stream_specs()
    grads = (one[0], one[0]) + one[3:]
    body = on_device
    if (mesh.shape[FSDP], mesh.shape[CTX], mesh.shape[TP]) != (4, 4, 2):
        body = on_any_mesh
    return jax.shard_map(
        body, mesh=mesh, in_specs=one + one, out_specs=grads + grads, check_vma=False
    )
```
